32 devices in a mesh: ctx: 8 (over z, core), dp: 2 (over x), ws: 2 (over y).
Axes of the slice: x: 2, y: 2, z: 4, core: 2. Of those that a mesh axis runs over, the one named last changes fastest.
Arguments:
- byte_ids: int32 [4, 8064], P(('dp', 'ws'), 'ctx'), may hold values from 0 to 258
- segments: int32 [4, 8064], P(('dp', 'ws'), 'ctx'), may hold values from 0 to 15, as said below
- embed: bfloat16 [259, 768], P(None, 'ws'), may hold values from -6 to 6
- conv_kernel: bfloat16 [5, 768], replicated, may hold values from -2.6875 to 2.6875
- score_weight: bfloat16 [768], replicated, may hold values from -0.21875 to 0.21875
- attn_gain: float32 [768], replicated, may hold values from 0.5 to 1.5
- w_q: bfloat16 [768, 768], P('ws'), may hold values from -0.0546875 to 0.0546875
- w_k: bfloat16 [768, 768], P('ws'), may hold values from -0.21875 to 0.21875
- w_v: bfloat16 [768, 768], P('ws'), may hold values from -0.21875 to 0.21875
- w_o: bfloat16 [768, 768], P('ws'), may hold values from -0.625 to 0.625
- rel_bias: float32 [32, 12], replicated, may hold values from -4 to 4
- ff_gain: float32 [768], replicated, may hold values from 0.5 to 1.5
- w_gate: bfloat16 [768, 2048], P('ws'), may hold values from -0.21875 to 0.21875
- w_up: bfloat16 [768, 2048], P('ws'), may hold values from -0.21875 to 0.21875
- w_down: bfloat16 [2048, 768], P('ws'), may hold values from -0.125 to 0.125
- cotangent: bfloat16 [4, 4032, 768], P(('dp', 'ws'), 'ctx'), may hold values from -6 to 6
Outputs:
- output: bfloat16 [4, 4032, 768], P(('dp', 'ws'), 'ctx')
- byte_grad: float32 [4, 8064, 768], P(('dp', 'ws'), 'ctx')
- embed_grad: float32 [259, 768], P(None, 'ws')
- conv_grad: float32 [5, 768], replicated
- score_grad: float32 [768], replicated
- attn_gain_grad: float32 [768], replicated
- q_grad: float32 [768, 768], P('ws')
- k_grad: float32 [768, 768], P('ws')
- v_grad: float32 [768, 768], P('ws')
- o_grad: float32 [768, 768], P('ws')
- bias_grad: float32 [32, 12], replicated
- ff_gain_grad: float32 [768], replicated
- gate_grad: float32 [768, 2048], P('ws')
- up_grad: float32 [768, 2048], P('ws')
- down_grad: float32 [2048, 768], P('ws')
The draws below stay inside these ranges and needn't reach their ends.
Inputs may be any that keep to these rules, and one draw needn't show every extreme that they name: `segments`: in each sequence the document numbers start at 0 and rise by one at each document's first byte; documents begin at multiples of 4 bytes and hold 124 to 1008 bytes, except the last one, which the sequence's end may cut short; some document of each sequence holds exactly 1008 bytes; every sequence has the same number of documents.
All inputs are finite; a program needn't handle non-finite values.
Results may differ from the reference program's by a relative error of at most 0.02.
Values may be sent and summed in bfloat16 or wider, within the bound.
No kernel may reach another device: no remote copies, remote signals or barrier semaphores. Data moves between devices by JAX's collectives and lax.ppermute only.
A program may use at most 192 MiB of HBM per device.

```python
import math
import jax
import jax.numpy as jnp
import numpy as np
from jax import lax

D = 768
H = 12
DH = 64
FF = 2048
VOCAB = 259
NB = 32
KW = 5
BYTE_DEV = 1008
ROW_DEV = 504
BYTES = 8064
ROWS = 4032
SEQS = 4
DOC_MIN = 124


def draw_segments(key, part):
    block_units = BYTE_DEV // 4
    low_units = DOC_MIN // 4
    block_total = BYTES // BYTE_DEV
    edge_key = jax.random.fold_in(key, 11)
    first_key = jax.random.fold_in(key, 12)
    block_index = jnp.arange(block_total, dtype=jnp.int32)[None, :]
    edge_draw = jax.random.randint(edge_key, (SEQS, block_total), 1, low_units + 1)
    edge_off = jnp.where(block_index == 0, 0, jnp.where(block_index == 1, low_units, edge_draw))
    first_draw = jax.random.randint(first_key, (SEQS, block_total), low_units, block_units // 2 + 1)
    first_len = jnp.where(block_index == 0, low_units, first_draw)
    first_start = block_index * block_units + edge_off
    second_start = first_start + first_len
    starts = jnp.stack([first_start, second_start], axis=2).reshape(SEQS, 2 * block_total)
    units = jnp.arange(BYTES, dtype=jnp.int32) // 4
    numbers = jax.vmap(lambda start_row: jnp.searchsorted(start_row, units, side='right'))(starts) - 1
    return numbers.astype(jnp.int32)


def place_ends(entries, stream_key, low, largest):
    longest = entries.shape.index(max(entries.shape))
    spots = []
    for shift in (0, 1):
        where = [jax.random.randint(jax.random.fold_in(stream_key, axis), (), 0, length) for axis, length in enumerate(entries.shape)]
        where[longest] = (where[longest] + shift) % entries.shape[longest]
        spots.append(tuple(where))
    return entries.at[spots[0]].set(low).at[spots[1]].set(largest)


def level_of(stream_key, extent, cuts, least, top_value):
    level, own = 1.0, jax.random.fold_in(stream_key, 6)
    for position, shards_of in cuts:
        steps = jnp.exp(jax.random.uniform(jax.random.fold_in(own, position), (shards_of,), jnp.float32, least / len(cuts), top_value / len(cuts)))
        level = level * jnp.repeat(steps, extent[position] // shards_of).reshape([-1 if axis == position else 1 for axis in range(len(extent))])
    return level


def rank_table(count, lean):
    weights = [(1 << 20) // math.isqrt(grade ** lean) + 1 for grade in range(1, count + 1)]
    scale = 1 + sum(weights) // (1 << 30)
    return np.cumsum(np.array([max(1, weight // scale) for weight in weights]))


def ranked(key, dims, count, slope):
    table = rank_table(count, slope)
    ticket = jax.random.randint(jax.random.fold_in(key, 1), dims, 0, int(table[count - 1]))
    standing = jnp.searchsorted(jnp.asarray(table, jnp.int32), ticket, side="right")
    return jax.random.permutation(jax.random.fold_in(key, 2), count)[standing].astype(jnp.int32)


def gaussian(key, shape, scale, reach, cuts=(), kind=jnp.bfloat16):
    factor_of = level_of(key, shape, cuts, -0.22, 0.18) if cuts else 1.0
    values = jax.random.normal(key, shape, jnp.float32) * scale * factor_of
    return jnp.minimum(jnp.maximum(values, -reach), reach).astype(kind)


def setup_inputs(seed: int = 0) -> dict:
    streams_of = jax.random.split(jax.random.key(seed), 17)
    return {
        "byte_ids": place_ends(ranked(streams_of[0], (SEQS, BYTES), VOCAB, 2), jax.random.fold_in(streams_of[0], 3), 0, VOCAB - 1).astype(jnp.int32),
        "segments": draw_segments(jax.random.fold_in(streams_of[16], 71), 0),
        "embed": gaussian(streams_of[2], (VOCAB, D), 1.0, 6.0, ((1, 2),)),
        "conv_kernel": gaussian(streams_of[3], (KW, D), 0.45, 2.6875),
        "score_weight": gaussian(streams_of[4], (D,), D ** -0.5, 0.21875),
        "attn_gain": jnp.clip(1.0 + 0.1 * jax.random.normal(streams_of[5], (D,), jnp.float32), 0.5, 1.5),
        "w_q": gaussian(streams_of[6], (D, D), (16 * D) ** -0.5, 0.0546875, ((0, 2),)),
        "w_k": gaussian(streams_of[7], (D, D), D ** -0.5, 0.21875, ((0, 2),)),
        "w_v": gaussian(streams_of[8], (D, D), D ** -0.5, 0.21875, ((0, 2),)),
        "w_o": gaussian(streams_of[9], (D, D), (D // 8) ** -0.5, 0.625, ((0, 2),)),
        "rel_bias": gaussian(streams_of[10], (NB, H), 1.0, 4.0, (), jnp.float32),
        "ff_gain": jnp.clip(1.0 + 0.1 * jax.random.normal(streams_of[11], (D,), jnp.float32), 0.5, 1.5),
        "w_gate": gaussian(streams_of[12], (D, FF), D ** -0.5, 0.21875, ((0, 2),)),
        "w_up": gaussian(streams_of[13], (D, FF), D ** -0.5, 0.21875, ((0, 2),)),
        "w_down": gaussian(streams_of[14], (FF, D), FF ** -0.5, 0.125, ((0, 2),)),
        "cotangent": gaussian(streams_of[15], (SEQS, ROWS, D), 1.0, 6.0, ((0, 4), (1, 8))),
    }


thresholds = (12, 16, 23, 32, 46, 64, 91)
negative = -1e+30
epsilon = 1e-06
highest = lax.Precision.HIGHEST

@jax.custom_vjp
def low(v):
    return lax.optimization_barrier(v.astype(jnp.bfloat16)).astype(jnp.float32)

@jax.custom_vjp
def low_back(v):
    return v

def low_keep(v):
    return (low(v), None)

def low_pass(kept, grad):
    return (grad,)

def back_keep(v):
    return (v, None)

def back_low(kept, grad):
    return (low(grad),)
low.defvjp(low_keep, low_pass)
low_back.defvjp(back_keep, back_low)

def bucket_of(relative):
    distance = jnp.abs(relative)
    far_bucket = 8 + sum(((distance >= threshold).astype(jnp.int32) for threshold in thresholds))
    near_bucket = jnp.where(distance < 8, distance, far_bucket)
    return near_bucket + 16 * (relative > 0).astype(jnp.int32)

def product(left_side, right_side):
    return jnp.dot(left_side, right_side, precision=highest)

def rms_norm(values, gain_vec):
    return values * lax.rsqrt(lax.optimization_barrier(jnp.mean(values * values, axis=-1, keepdims=True)) + epsilon) * gain_vec

def gbst(embedded, conv_kernel, score_weight):
    length = embedded.shape[0]
    half_width = (KW - 1) // 2
    padded = jnp.pad(embedded, ((half_width, half_width), (0, 0)))
    conv_out = conv_kernel[0] * padded[0:length]
    for offset in range(1, KW):
        conv_out = conv_out + conv_kernel[offset] * padded[offset:offset + length]
    pooled = []
    for block_size in (1, 2, 3, 4):
        block_means = lax.optimization_barrier(jnp.mean(conv_out.reshape(length // block_size, block_size, D), axis=1))
        pooled.append(jnp.repeat(block_means, block_size, axis=0))
    block_scores = jnp.stack([product(pooled_part, score_weight) for pooled_part in pooled], axis=1)
    block_weight = jax.nn.softmax(block_scores, axis=1)
    latent = block_weight[:, 0:1] * pooled[0]
    for number in range(1, 4):
        latent = latent + block_weight[:, number:number + 1] * pooled[number]
    return lax.optimization_barrier(jnp.mean(latent.reshape(length // 2, 2, D), axis=1))

def attend(queries, key_rows, values, row_segs, rel_bias):
    row_total = queries.shape[0]
    key_pad = jnp.pad(key_rows, ((ROW_DEV, ROW_DEV), (0, 0)))
    value_pad = jnp.pad(values, ((ROW_DEV, ROW_DEV), (0, 0)))
    seg_pad = jnp.pad(row_segs, (ROW_DEV, ROW_DEV), constant_values=-1)
    window = jnp.arange(3 * ROW_DEV, dtype=jnp.int32)
    own_range = jnp.arange(ROW_DEV, dtype=jnp.int32)
    bucket = bucket_of(window[None, :] - ROW_DEV - own_range[:, None])

    def one_block(block_number):
        block_start = (block_number * ROW_DEV).astype(jnp.int32)
        query_block = lax.dynamic_slice_in_dim(queries, block_start, ROW_DEV, 0).reshape(ROW_DEV, H, DH)
        key_block = lax.dynamic_slice_in_dim(key_pad, block_start, 3 * ROW_DEV, 0).reshape(3 * ROW_DEV, H, DH)
        value_block = lax.dynamic_slice_in_dim(value_pad, block_start, 3 * ROW_DEV, 0).reshape(3 * ROW_DEV, H, DH)
        query_segs = lax.dynamic_slice_in_dim(row_segs, block_start, ROW_DEV, 0)
        key_segs = lax.dynamic_slice_in_dim(seg_pad, block_start, 3 * ROW_DEV, 0)
        allowed = query_segs[:, None] == key_segs[None, :]
        raw_scores = low_back(jnp.einsum('qhd,khd->hqk', query_block, key_block, precision=highest))
        bias_grid = jnp.transpose(rel_bias[bucket], (2, 0, 1))
        scores = jnp.where(allowed[None], raw_scores + bias_grid, negative)
        attn_probs = low(jax.nn.softmax(scores, axis=-1))
        mixed_rows = jnp.einsum('hqk,khd->qhd', attn_probs, value_block, precision=highest)
        return mixed_rows.reshape(ROW_DEV, D)
    blocks = lax.map(jax.checkpoint(one_block), jnp.arange(row_total // ROW_DEV, dtype=jnp.int32))
    return blocks.reshape(row_total, D)

def block(embedded, row_segs, weights):
    conv_kernel, score_weight, attn_gain, w_q, w_k, w_v, w_o, rel_bias, ff_gain, w_gate, w_up, w_down = weights
    start_rows = gbst(embedded, conv_kernel, score_weight)
    first_in = low(rms_norm(start_rows, attn_gain))
    queries = low(low_back(product(first_in, w_q)))
    key_rows = low(low_back(product(first_in, w_k)))
    values = low(low_back(product(first_in, w_v)))
    attended = low(low_back(attend(queries, key_rows, values, row_segs, rel_bias)))
    middle = start_rows + low_back(product(attended, w_o))
    second_in = low(rms_norm(middle, ff_gain))
    gate_pre = low_back(product(second_in, w_gate))
    up_pre = low_back(product(second_in, w_up))
    hidden = low(jax.nn.gelu(gate_pre, approximate=True) * up_pre)
    return middle + low_back(product(hidden, w_down))

def reference(byte_ids, segments, embed, conv_kernel, score_weight, attn_gain, w_q, w_k, w_v, w_o, rel_bias, ff_gain, w_gate, w_up, w_down, cotangent):
    weights = tuple((array_in.astype(jnp.float32) for array_in in (embed, conv_kernel, score_weight, attn_gain, w_q, w_k, w_v, w_o, rel_bias, ff_gain, w_gate, w_up, w_down)))

    def one_sequence(totals, seq_items):
        ids_row, seg_row, cot_row = seq_items

        def whole_layer(byte_shift, params):
            embedded = params[0][ids_row] + byte_shift
            return block(embedded, seg_row[::2], params[1:])
        result, pull_back = jax.vjp(whole_layer, jnp.zeros((BYTES, D), jnp.float32), weights)
        byte_grad, weight_grads = pull_back(cot_row.astype(jnp.float32))
        totals = tuple((first_term + second_term for first_term, second_term in zip(totals, weight_grads)))
        return (totals, (result.astype(jnp.bfloat16), byte_grad))
    zeros_init = tuple((jnp.zeros_like(array_in) for array_in in weights))
    totals, (outputs, byte_grads) = lax.scan(one_sequence, zeros_init, (byte_ids, segments, cotangent))
    return (outputs, byte_grads, totals[0], totals[1], totals[2], totals[3], totals[4], totals[5], totals[6], totals[7], totals[8], totals[9], totals[10], totals[11], totals[12])
```

```python
import functools

import jax
import jax.numpy as jnp
from jax import lax
from jax.experimental import pallas as pl
from jax.experimental.pallas import tpu as pltpu
from jax.sharding import PartitionSpec as P

thresholds = (12, 16, 23, 32, 46, 64, 91)
negative = -1e30
epsilon = 1e-06
highest = lax.Precision.HIGHEST
tile = 128
near_bases = (-128, -120, 0, 120, 128)
class_count = len(near_bases) + 2


def bucket_of(relative):
    distance = jnp.abs(relative)
    far_bucket = 8 + sum(((distance >= threshold).astype(jnp.int32) for threshold in thresholds))
    near_bucket = jnp.where(distance < 8, distance, far_bucket)
    return near_bucket + 16 * (relative > 0).astype(jnp.int32)


def matmul(left, right, left_dim, right_dim):
    return lax.dot_general(
        left, right, (((left_dim,), (right_dim,)), ((), ())), preferred_element_type=jnp.float32
    )


def split_pair(values):
    high = values.astype(jnp.bfloat16)
    return high, (values - high.astype(jnp.float32)).astype(jnp.bfloat16)


def tile_class(query_tile, key_tile):
    step = key_tile - query_tile - 4
    own = jnp.where(
        step <= -2, 0, jnp.where(step == -1, 1, jnp.where(step == 0, 3, jnp.where(step == 1, 5, 6)))
    )
    before = jnp.where(step == -1, 2, 0)
    after = jnp.where(step == 1, 4, 6)
    return jnp.where(key_tile < 4, before, jnp.where(key_tile < 8, own, after))


def key_range(seg_ref, query_tile, row_count, tiles_per_block):
    first_seg = seg_ref[1, query_tile * tile]
    last_seg = seg_ref[1, jnp.minimum(query_tile * tile + tile, row_count) - 1]
    low = jnp.int32(0)
    high = jnp.int32(0)
    for block in range(3):
        for part in range(tiles_per_block):
            key_first = seg_ref[block, part * tile]
            key_last = seg_ref[block, min(part * tile + tile, row_count) - 1]
            low = low + (key_last < first_seg).astype(jnp.int32)
            high = high + (key_first <= last_seg).astype(jnp.int32)
    return low, high


def make_bias(line_ref, bias_ref, pair_count):
    for kind in range(class_count):
        for pair in range(pair_count):
            for half in range(2):
                head = 2 * pair + half
                line = line_ref[kind, head : head + 1, :]
                grid = jnp.broadcast_to(line, (tile, 2 * tile))
                if 0 < kind < class_count - 1:
                    grid = pltpu.roll(grid, 0, 1, stride=1, stride_axis=0)
                bias_ref[kind, pair, :, half * tile : (half + 1) * tile] = grid[:, :tile]


def stack_heads(block):
    lane = lax.broadcasted_iota(jnp.int32, block.shape, 1)
    zero = jnp.zeros_like(block)
    return jnp.concatenate(
        [jnp.where(lane < tile // 2, block, zero), jnp.where(lane < tile // 2, zero, block)], axis=0
    )


def fold_rows(values, combine):
    pieces = [values[8 * i : 8 * i + 8] for i in range(values.shape[0] // 8)]
    while len(pieces) > 1:
        joined = [combine(pieces[i], pieces[i + 1]) for i in range(0, len(pieces) - 1, 2)]
        if len(pieces) % 2:
            joined.append(pieces[-1])
        pieces = joined
    return pieces[0]


def key_columns(segs_ref, column_ref, key_tile):
    row = segs_ref[key_tile, 0:1, :]
    column_ref[key_tile] = jnp.transpose(jnp.broadcast_to(row, (tile, tile)))


def start_copies(sources, window_ref, sems):
    rows = sources[0].shape[0]
    copies = [
        pltpu.make_async_copy(source, window_ref.at[pl.ds(rows * i, rows)], sems.at[i])
        for i, source in enumerate(sources)
    ]
    for copy in copies:
        copy.start()
    return copies


def forward_kernel(
    seg_ref, q_ref, before_ref, own_ref, after_ref, segs_ref, qsegs_ref, line_ref,
    out_ref, lse_ref,
    window_ref, bias_ref, column_ref, mask_ref, flipped_ref, score_ref, mixed_ref, sems, *, row_count
):
    width = q_ref.shape[1]
    pair_count = width // tile
    query_tiles = q_ref.shape[0] // tile
    copies = start_copies((before_ref, own_ref, after_ref), window_ref, sems)
    make_bias(line_ref, bias_ref, pair_count)
    first = key_range(seg_ref, 0, row_count, query_tiles)[0]
    last = key_range(seg_ref, query_tiles - 1, row_count, query_tiles)[1]
    for copy in copies:
        copy.wait()

    def prepare(key_tile, carry):
        key_columns(segs_ref, column_ref, key_tile)
        at = pl.multiple_of(key_tile * tile, tile)
        flipped_ref[key_tile] = jnp.transpose(window_ref[pl.ds(at, tile), width:])
        return carry

    lax.fori_loop(first, last, prepare, 0)

    def query_step(query_tile, carry):
        low, high = key_range(seg_ref, query_tile, row_count, query_tiles)
        rows = pl.ds(pl.multiple_of(query_tile * tile, tile), tile)
        stacked = [
            stack_heads(q_ref[rows, pair * tile : (pair + 1) * tile]) for pair in range(pair_count)
        ]
        query_seg = qsegs_ref[query_tile, 0:1, :]

        def score_step(key_tile, tops):
            keys = pl.ds(pl.multiple_of(key_tile * tile, tile), tile)
            hide = jnp.where(column_ref[key_tile] == query_seg, 0.0, negative)
            hide = jnp.concatenate([hide, hide], axis=1)
            kind = tile_class(query_tile, key_tile)
            fresh = []
            for pair in range(pair_count):
                scores = matmul(
                    window_ref[keys, pair * tile : (pair + 1) * tile], stacked[pair], 1, 1
                )
                scores = scores + bias_ref[kind, pair] + hide
                score_ref[key_tile, pair] = scores
                fresh.append(jnp.maximum(tops[pair], fold_rows(scores, jnp.maximum)))
            return tuple(fresh)

        tops = lax.fori_loop(
            low, high, score_step,
            tuple(jnp.full((8, 2 * tile), negative, jnp.float32) for _ in range(pair_count)),
        )
        tops = [jnp.max(top, axis=0, keepdims=True) for top in tops]
        for pair in range(pair_count):
            mixed_ref[pair] = jnp.zeros((tile, tile), jnp.float32)

        def mix_step(key_tile, totals):
            fresh = []
            for pair in range(pair_count):
                exponent = jnp.exp(score_ref[key_tile, pair] - tops[pair])
                fresh.append(totals[pair] + fold_rows(exponent, jnp.add))
                mixed = matmul(
                    flipped_ref[key_tile, pair * tile : (pair + 1) * tile, :],
                    exponent.astype(jnp.bfloat16), 1, 0,
                )
                half = tile // 2
                mixed_ref[pair, :half] += mixed[:half, :tile]
                mixed_ref[pair, half:] += mixed[half:, tile:]
            return tuple(fresh)

        totals = lax.fori_loop(
            low, high, mix_step,
            tuple(jnp.zeros((8, 2 * tile), jnp.float32) for _ in range(pair_count)),
        )
        for pair in range(pair_count):
            total = jnp.sum(totals[pair], axis=0, keepdims=True)
            lse_ref[query_tile, pair : pair + 1, :] = tops[pair] + jnp.log(total)
            inverse = 1.0 / total
            half = tile // 2
            scaled = jnp.concatenate(
                [
                    mixed_ref[pair, :half] * inverse[:, :tile],
                    mixed_ref[pair, half:] * inverse[:, tile:],
                ],
                axis=0,
            )
            out_ref[rows, pair * tile : (pair + 1) * tile] = jnp.transpose(scaled).astype(
                jnp.bfloat16
            )
        return carry

    lax.fori_loop(0, query_tiles, query_step, 0)


def backward_kernel(
    seg_ref, q_ref, do_ref, o_ref, before_ref, own_ref, after_ref, segs_ref, qsegs_ref, line_ref, lse_ref,
    dq_ref, dbefore_ref, down_ref, dafter_ref, bias_out_ref,
    window_ref, bias_ref, column_ref, flipped_ref, dbias_ref, dwindow_ref, dq_acc_ref, delta_ref, sems,
    *, row_count
):
    width = q_ref.shape[1]
    pair_count = width // tile
    query_tiles = q_ref.shape[0] // tile
    block_rows = q_ref.shape[0]
    half = tile // 2
    copies = start_copies((before_ref, own_ref, after_ref), window_ref, sems)
    make_bias(line_ref, bias_ref, pair_count)
    dwindow_ref[...] = jnp.zeros(dwindow_ref.shape, jnp.float32)
    dbias_ref[...] = jnp.zeros(dbias_ref.shape, jnp.float32)
    product = do_ref[...].astype(jnp.float32) * o_ref[...].astype(jnp.float32)
    product_high, product_low = split_pair(product)
    member = (
        lax.broadcasted_iota(jnp.int32, (16, width), 1) // half
        == lax.broadcasted_iota(jnp.int32, (16, width), 0)
    ).astype(jnp.bfloat16)
    delta_ref[...] = matmul(member, product_high, 1, 1) + matmul(member, product_low, 1, 1)
    first = key_range(seg_ref, 0, row_count, query_tiles)[0]
    last = key_range(seg_ref, query_tiles - 1, row_count, query_tiles)[1]
    for copy in copies:
        copy.wait()

    def prepare(key_tile, carry):
        key_columns(segs_ref, column_ref, key_tile)
        at = pl.multiple_of(key_tile * tile, tile)
        flipped_ref[key_tile] = jnp.transpose(window_ref[pl.ds(at, tile), :width])
        return carry

    lax.fori_loop(first, last, prepare, 0)

    def query_step(query_tile, carry):
        low, high = key_range(seg_ref, query_tile, row_count, query_tiles)
        at = pl.multiple_of(query_tile * tile, tile)
        rows = pl.ds(at, tile)
        lanes = [slice(pair * tile, (pair + 1) * tile) for pair in range(pair_count)]
        queries = [stack_heads(q_ref[rows, lane]) for lane in lanes]
        grads = [stack_heads(do_ref[rows, lane]) for lane in lanes]
        query_seg = qsegs_ref[query_tile, 0:1, :]
        deltas = [
            jnp.concatenate(
                [delta_ref[2 * pair : 2 * pair + 1, rows], delta_ref[2 * pair + 1 : 2 * pair + 2, rows]],
                axis=1,
            )
            for pair in range(pair_count)
        ]
        norms = [lse_ref[query_tile, pair : pair + 1, :] for pair in range(pair_count)]
        for pair in range(pair_count):
            dq_acc_ref[pair] = jnp.zeros((tile, tile), jnp.float32)

        def key_step(key_tile, carry):
            keys = pl.ds(pl.multiple_of(key_tile * tile, tile), tile)
            hide = jnp.where(column_ref[key_tile] == query_seg, 0.0, negative)
            hide = jnp.concatenate([hide, hide], axis=1)
            kind = tile_class(query_tile, key_tile)
            for pair in range(pair_count):
                lane = lanes[pair]
                value_lane = slice(width + pair * tile, width + (pair + 1) * tile)
                scores = matmul(window_ref[keys, lane], queries[pair], 1, 1)
                probs = jnp.exp(scores + bias_ref[kind, pair] + hide - norms[pair])
                dprobs = matmul(window_ref[keys, value_lane], grads[pair], 1, 1)
                dscores = probs * (dprobs - deltas[pair])
                dbias_ref[kind, pair] += dscores
                dscores_low = dscores.astype(jnp.bfloat16)
                dwindow_ref[keys, lane] += matmul(dscores_low, queries[pair], 1, 0)
                dwindow_ref[keys, value_lane] += matmul(
                    probs.astype(jnp.bfloat16), grads[pair], 1, 0
                )
                dquery = matmul(flipped_ref[key_tile, lane, :], dscores_low, 1, 0)
                dq_acc_ref[pair, :half] += dquery[:half, :tile]
                dq_acc_ref[pair, half:] += dquery[half:, tile:]
            return carry

        lax.fori_loop(low, high, key_step, 0)
        for pair in range(pair_count):
            dq_ref[rows, lanes[pair]] = jnp.transpose(dq_acc_ref[pair]).astype(jnp.bfloat16)
        return carry

    lax.fori_loop(0, query_tiles, query_step, 0)
    dbefore_ref[...] = dwindow_ref[:block_rows].astype(jnp.bfloat16)
    down_ref[...] = dwindow_ref[block_rows : 2 * block_rows]
    dafter_ref[...] = dwindow_ref[2 * block_rows :].astype(jnp.bfloat16)
    turn = (
        lax.broadcasted_iota(jnp.int32, (tile, tile), 0)
        + lax.broadcasted_iota(jnp.int32, (tile, tile), 1)
        == tile - 1
    ).astype(jnp.bfloat16)
    zero_half = jnp.zeros((tile, tile), jnp.float32)
    bias_out_ref[...] = jnp.zeros(bias_out_ref.shape, jnp.float32)
    for kind in range(class_count):
        for pair in range(pair_count):
            grid = dbias_ref[kind, pair]
            near = 0 < kind < class_count - 1
            if near:
                grid_high, grid_low = split_pair(grid)
                grid = matmul(turn, grid_high, 1, 0) + matmul(turn, grid_low, 1, 0)
            for side in range(2):
                part = jnp.concatenate([grid[:, side * tile : (side + 1) * tile], zero_half], axis=1)
                if near:
                    part = pltpu.roll(part, tile + 1, 1, stride=1, stride_axis=0)
                head = 2 * pair + side
                bias_out_ref[kind, head : head + 1, :] = jnp.sum(
                    fold_rows(part, jnp.add), axis=0, keepdims=True
                )


def line_offsets():
    place = jnp.arange(2 * tile, dtype=jnp.int32)
    swing = jnp.where(place < tile, place, place - 2 * tile)
    far = jnp.full((1, 2 * tile), 4 * tile, jnp.int32)
    near = jnp.stack([base - swing for base in near_bases])
    return jnp.concatenate([-far, near, far])


def bias_lines(rel_bias):
    bucket_count, head_count = rel_bias.shape
    buckets = bucket_of(line_offsets())
    lines = jnp.take(rel_bias, buckets.reshape(-1), axis=0).reshape(class_count, 2 * tile, head_count)
    lines = jnp.transpose(lines, (0, 2, 1))
    return jnp.pad(lines, ((0, 0), (0, 16 - head_count), (0, 0)))


def bias_collect(sums, bucket_count, head_count):
    onehot = (bucket_of(line_offsets())[:, :, None] == jnp.arange(bucket_count)).astype(jnp.float32)
    return jnp.einsum(
        "chx,cxb->bh", sums[:, :head_count], onehot, precision=lax.Precision.HIGHEST
    )


def specs(count, space=pltpu.VMEM):
    return [pl.BlockSpec(memory_space=space) for _ in range(count)]


def attention_forward(segs, q, before, own, after, lines, row_count):
    rows, width = q.shape
    tiles = rows // tile
    pairs = width // tile
    seg_rows = segs.reshape(3 * tiles, 1, tile)
    query_segs = mark_queries(segs, row_count).reshape(tiles, 1, tile)
    return pl.pallas_call(
        functools.partial(forward_kernel, row_count=row_count),
        out_shape=(
            jax.ShapeDtypeStruct((rows, width), jnp.bfloat16),
            jax.ShapeDtypeStruct((tiles, 8, 2 * tile), jnp.float32),
        ),
        in_specs=specs(1, pltpu.SMEM) + specs(1) + specs(3, pl.ANY) + specs(3),
        out_specs=tuple(specs(2)),
        scratch_shapes=[
            pltpu.VMEM((3 * rows, 2 * width), jnp.bfloat16),
            pltpu.VMEM((class_count, pairs, tile, 2 * tile), jnp.float32),
            pltpu.VMEM((3 * tiles, tile, tile), jnp.int32),
            pltpu.VMEM((8, 128), jnp.float32),
            pltpu.VMEM((3 * tiles, width, tile), jnp.bfloat16),
            pltpu.VMEM((3 * tiles, pairs, tile, 2 * tile), jnp.float32),
            pltpu.VMEM((pairs, tile, tile), jnp.float32),
            pltpu.SemaphoreType.DMA((3,)),
        ],
        compiler_params=pltpu.CompilerParams(vmem_limit_bytes=60 << 20),
        name="attention_forward",
    )(segs, q, before, own, after, seg_rows, query_segs, lines)


def mark_queries(segs, row_count):
    place = jnp.arange(segs.shape[1], dtype=jnp.int32)
    return jnp.where(place < row_count, segs[1], -1)


def attention_backward(segs, q, do, o, before, own, after, lines, lse, row_count):
    rows, width = q.shape
    tiles = rows // tile
    pairs = width // tile
    seg_rows = segs.reshape(3 * tiles, 1, tile)
    query_segs = mark_queries(segs, row_count).reshape(tiles, 1, tile)
    return pl.pallas_call(
        functools.partial(backward_kernel, row_count=row_count),
        out_shape=(
            jax.ShapeDtypeStruct((rows, width), jnp.bfloat16),
            jax.ShapeDtypeStruct((rows, 2 * width), jnp.bfloat16),
            jax.ShapeDtypeStruct((rows, 2 * width), jnp.float32),
            jax.ShapeDtypeStruct((rows, 2 * width), jnp.bfloat16),
            jax.ShapeDtypeStruct((class_count, 16, 2 * tile), jnp.float32),
        ),
        in_specs=specs(1, pltpu.SMEM) + specs(3) + specs(3, pl.ANY) + specs(4),
        out_specs=tuple(specs(5)),
        scratch_shapes=[
            pltpu.VMEM((3 * rows, 2 * width), jnp.bfloat16),
            pltpu.VMEM((class_count, pairs, tile, 2 * tile), jnp.float32),
            pltpu.VMEM((3 * tiles, tile, tile), jnp.int32),
            pltpu.VMEM((3 * tiles, width, tile), jnp.bfloat16),
            pltpu.VMEM((class_count, pairs, tile, 2 * tile), jnp.float32),
            pltpu.VMEM((3 * rows, 2 * width), jnp.float32),
            pltpu.VMEM((pairs, tile, tile), jnp.float32),
            pltpu.VMEM((16, rows), jnp.float32),
            pltpu.SemaphoreType.DMA((3,)),
        ],
        compiler_params=pltpu.CompilerParams(vmem_limit_bytes=60 << 20),
        name="attention_backward",
    )(segs, q, do, o, before, own, after, seg_rows, query_segs, lines, lse)


def neighbours(block, axis):
    count = lax.axis_size(axis)
    forward = [(i, i + 1) for i in range(count - 1)]
    backward = [(target, source) for source, target in forward]
    return lax.ppermute(block, axis, forward), lax.ppermute(block, axis, backward)


def pad_rows(block):
    return jnp.pad(block, ((0, -block.shape[0] % tile), (0, 0)))


def extended(block, sides, width):
    for axis, dim in sides:
        count = lax.axis_size(axis)
        forward = [(i, i + 1) for i in range(count - 1)]
        backward = [(target, source) for source, target in forward]
        low = lax.ppermute(
            lax.slice_in_dim(block, block.shape[dim] - width, None, axis=dim), axis, forward
        )
        high = lax.ppermute(lax.slice_in_dim(block, 0, width, axis=dim), axis, backward)
        block = jnp.concatenate([low, block, high], axis=dim)
    return block


def contract(left_side, right_side, left_axis, right_axis):
    return lax.dot_general(
        left_side,
        right_side,
        (((left_axis,), (right_axis,)), ((), ())),
        preferred_element_type=jnp.float32,
    )


def inverse_rms(values):
    return lax.rsqrt(jnp.mean(values * values, axis=-1, keepdims=True) + epsilon)


def pool_blocks(conv_out):
    byte_count, channels = conv_out.shape
    pooled = []
    for block_size in (1, 2, 3, 4):
        block_means = jnp.mean(
            conv_out.reshape(byte_count // block_size, block_size, channels), axis=1
        )
        pooled.append(jnp.repeat(block_means, block_size, axis=0))
    return pooled


def unpool_blocks(grad_list):
    byte_count, channels = grad_list[0].shape
    summed = jnp.zeros((byte_count, channels), jnp.float32)
    for block_size, grad_part in zip((1, 2, 3, 4), grad_list):
        block_sums = (
            jnp.sum(grad_part.reshape(byte_count // block_size, block_size, channels), axis=1)
            / block_size
        )
        summed = summed + jnp.repeat(block_sums, block_size, axis=0)
    return summed


def per_device(
    byte_ids,
    segments,
    embed,
    conv_kernel,
    score_weight,
    attn_gain,
    w_q,
    w_k,
    w_v,
    w_o,
    rel_bias,
    ff_gain,
    w_gate,
    w_up,
    w_down,
    cotangent,
):
    byte_count = byte_ids.shape[1]
    row_count = byte_count // 2
    cycle_count = lax.axis_size("ctx")
    cycle_place = lax.axis_index("ctx")
    head_count = rel_bias.shape[1]
    bucket_count = rel_bias.shape[0]
    kernel_width = conv_kernel.shape[0]
    half_width = (kernel_width - 1) // 2
    id_stack = jnp.stack([byte_ids[0], segments[0]])
    id_rim = extended(id_stack, (("ctx", 1),), byte_count)
    byte_place = (cycle_place - 1) * byte_count + jnp.arange(3 * byte_count, dtype=jnp.int32)
    byte_valid = (byte_place >= 0) & (byte_place < cycle_count * byte_count)
    gathered = (
        lax.all_gather(embed, "ws", axis=1, tiled=True),
        lax.all_gather(w_q, "ws", axis=0, tiled=True),
        lax.all_gather(w_k, "ws", axis=0, tiled=True),
        lax.all_gather(w_v, "ws", axis=0, tiled=True),
        lax.all_gather(w_o, "ws", axis=0, tiled=True),
        lax.all_gather(w_gate, "ws", axis=0, tiled=True),
        lax.all_gather(w_up, "ws", axis=0, tiled=True),
        lax.all_gather(w_down, "ws", axis=0, tiled=True),
    )
    embed_table, query_w, key_w, value_w, out_w, gate_w, up_w, down_w = gathered
    lookup_ids = id_rim[0, byte_count - half_width : 2 * byte_count + half_width]
    lookup_valid = byte_valid[byte_count - half_width : 2 * byte_count + half_width]
    vocab_range = jnp.arange(embed_table.shape[0], dtype=jnp.int32)
    one_hot = ((lookup_ids[:, None] == vocab_range[None, :]) & lookup_valid[:, None]).astype(
        jnp.bfloat16
    )
    embedded = jnp.dot(one_hot, embed_table, preferred_element_type=jnp.float32)
    kernel = conv_kernel.astype(jnp.float32)
    conv_out = kernel[0] * embedded[0:byte_count]
    for offset in range(1, kernel_width):
        conv_out = conv_out + kernel[offset] * embedded[offset : offset + byte_count]
    pooled = pool_blocks(conv_out)
    score_vec = score_weight.astype(jnp.float32)
    block_scores = jnp.stack(
        [jnp.dot(pooled_part, score_vec, precision=highest) for pooled_part in pooled], axis=1
    )
    block_weight = jax.nn.softmax(block_scores, axis=1)
    latent = block_weight[:, 0:1] * pooled[0]
    for number in range(1, 4):
        latent = latent + block_weight[:, number : number + 1] * pooled[number]
    start_rows = jnp.mean(latent.reshape(row_count, 2, -1), axis=1)
    inverse_one = inverse_rms(start_rows)
    normed_one = start_rows * inverse_one
    first_in = (normed_one * attn_gain).astype(jnp.bfloat16)
    queries = jnp.dot(first_in, query_w, preferred_element_type=jnp.float32).astype(jnp.bfloat16)
    keys_own = jnp.dot(first_in, key_w, preferred_element_type=jnp.float32).astype(jnp.bfloat16)
    values_own = jnp.dot(first_in, value_w, preferred_element_type=jnp.float32).astype(jnp.bfloat16)
    own_kv = pad_rows(jnp.concatenate([keys_own, values_own], axis=1))
    before_kv, after_kv = neighbours(own_kv, "ctx")
    row_segs = segments[0, ::2]
    before_seg, after_seg = neighbours(row_segs, "ctx")
    segs = jnp.stack(
        [
            jnp.where(cycle_place > 0, before_seg, -2),
            row_segs,
            jnp.where(cycle_place < cycle_count - 1, after_seg, 1 << 20),
        ]
    )
    segs = jnp.pad(segs, ((0, 0), (0, -row_count % tile)), constant_values=-3)
    lines = bias_lines(rel_bias)
    queries = pad_rows(queries)
    attended_wide, log_norm = attention_forward(
        segs, queries, before_kv, own_kv, after_kv, lines, row_count
    )
    attended = attended_wide[:row_count]
    middle = start_rows + jnp.dot(attended, out_w, preferred_element_type=jnp.float32)
    inverse_two = inverse_rms(middle)
    normed_two = middle * inverse_two
    second_in = (normed_two * ff_gain).astype(jnp.bfloat16)
    gate_pre = jnp.dot(second_in, gate_w, preferred_element_type=jnp.float32)
    up_pre = jnp.dot(second_in, up_w, preferred_element_type=jnp.float32)
    gelu_gate, gelu_pull = jax.vjp(
        lambda pre_values: jax.nn.gelu(pre_values, approximate=True), gate_pre
    )
    hidden = (gelu_gate * up_pre).astype(jnp.bfloat16)
    output = (middle + jnp.dot(hidden, down_w, preferred_element_type=jnp.float32)).astype(
        jnp.bfloat16
    )
    back_weights = (
        lax.all_gather(w_q, "ws", axis=0, tiled=True),
        lax.all_gather(w_k, "ws", axis=0, tiled=True),
        lax.all_gather(w_v, "ws", axis=0, tiled=True),
        lax.all_gather(w_o, "ws", axis=0, tiled=True),
        lax.all_gather(w_gate, "ws", axis=0, tiled=True),
        lax.all_gather(w_up, "ws", axis=0, tiled=True),
        lax.all_gather(w_down, "ws", axis=0, tiled=True),
    )
    query_w, key_w, value_w, out_w, gate_w, up_w, down_w = back_weights
    grad_low = cotangent[0]
    grad_out = grad_low.astype(jnp.float32)
    down_grad = contract(hidden, grad_low, 0, 0)
    d_hidden = contract(grad_low, down_w, 1, 1)
    d_gate = gelu_pull(d_hidden * up_pre)[0].astype(jnp.bfloat16)
    d_up = (d_hidden * gelu_gate).astype(jnp.bfloat16)
    gate_grad = contract(second_in, d_gate, 0, 0)
    up_grad = contract(second_in, d_up, 0, 0)
    d_second = contract(d_gate, gate_w, 1, 1) + contract(d_up, up_w, 1, 1)
    ff_gain_grad = jnp.sum(d_second * normed_two, axis=0)
    d_normed_two = d_second * ff_gain
    d_middle = grad_out + inverse_two * (
        d_normed_two - normed_two * jnp.mean(d_normed_two * normed_two, axis=-1, keepdims=True)
    )
    d_branch = d_middle.astype(jnp.bfloat16)
    out_grad = contract(attended, d_branch, 0, 0)
    d_attended = contract(d_branch, out_w, 1, 1).astype(jnp.bfloat16)
    d_queries, d_before, d_own, d_after, bias_sums = attention_backward(
        segs, queries, pad_rows(d_attended), attended_wide, before_kv, own_kv, after_kv, lines,
        log_norm, row_count,
    )
    from_after, from_before = (
        lax.ppermute(d_before, "ctx", [(i + 1, i) for i in range(cycle_count - 1)]),
        lax.ppermute(d_after, "ctx", [(i, i + 1) for i in range(cycle_count - 1)]),
    )
    d_keyval = d_own + from_after.astype(jnp.float32) + from_before.astype(jnp.float32)
    d_keyval = d_keyval[:row_count].astype(jnp.bfloat16)
    d_queries = d_queries[:row_count]
    width = d_queries.shape[1]
    d_keys = d_keyval[:, :width]
    d_values = d_keyval[:, width:]
    bias_grad = bias_collect(bias_sums, bucket_count, head_count)
    q_grad = contract(first_in, d_queries, 0, 0)
    k_grad = contract(first_in, d_keys, 0, 0)
    v_grad = contract(first_in, d_values, 0, 0)
    d_first = (
        contract(d_queries, query_w, 1, 1)
        + contract(d_keys, key_w, 1, 1)
        + contract(d_values, value_w, 1, 1)
    )
    attn_gain_grad = jnp.sum(d_first * normed_one, axis=0)
    d_normed_one = d_first * attn_gain
    d_start = d_middle + inverse_one * (
        d_normed_one - normed_one * jnp.mean(d_normed_one * normed_one, axis=-1, keepdims=True)
    )
    d_latent = jnp.repeat(d_start * 0.5, 2, axis=0)
    d_block = jnp.stack([jnp.sum(d_latent * pooled_part, axis=1) for pooled_part in pooled], axis=1)
    d_block_scores = block_weight * (
        d_block - jnp.sum(block_weight * d_block, axis=1, keepdims=True)
    )
    score_grad = jnp.dot(d_block_scores[:, 0], pooled[0], precision=highest)
    for number in range(1, 4):
        score_grad = score_grad + jnp.dot(
            d_block_scores[:, number], pooled[number], precision=highest
        )
    d_pooled = [
        block_weight[:, number : number + 1] * d_latent
        + d_block_scores[:, number : number + 1] * score_vec[None, :]
        for number in range(4)
    ]
    d_conv = unpool_blocks(d_pooled)
    conv_rim = extended(d_conv.astype(jnp.bfloat16), (("ctx", 0),), half_width).astype(d_conv.dtype)
    conv_grad = jnp.stack(
        [
            jnp.sum(d_conv * embedded[offset : offset + byte_count], axis=0)
            for offset in range(kernel_width)
        ]
    )
    byte_grad = kernel[0] * conv_rim[2 * half_width : 2 * half_width + byte_count]
    for offset in range(1, kernel_width):
        byte_grad = (
            byte_grad
            + kernel[offset]
            * conv_rim[2 * half_width - offset : 2 * half_width - offset + byte_count]
        )
    own_hot = one_hot[half_width : half_width + byte_count].astype(jnp.float32)
    embed_full = lax.dot_general(
        own_hot,
        byte_grad,
        (((0,), (0,)), ((), ())),
        precision=highest,
        preferred_element_type=jnp.float32,
    )
    large_sums = (
        lax.psum_scatter(
            embed_full.astype(jnp.bfloat16), "ws", scatter_dimension=1, tiled=True
        ).astype(jnp.float32),
        lax.psum_scatter(q_grad.astype(jnp.bfloat16), "ws", scatter_dimension=0, tiled=True).astype(
            jnp.float32
        ),
        lax.psum_scatter(k_grad.astype(jnp.bfloat16), "ws", scatter_dimension=0, tiled=True).astype(
            jnp.float32
        ),
        lax.psum_scatter(v_grad.astype(jnp.bfloat16), "ws", scatter_dimension=0, tiled=True).astype(
            jnp.float32
        ),
        lax.psum_scatter(
            out_grad.astype(jnp.bfloat16), "ws", scatter_dimension=0, tiled=True
        ).astype(jnp.float32),
        lax.psum_scatter(
            gate_grad.astype(jnp.bfloat16), "ws", scatter_dimension=0, tiled=True
        ).astype(jnp.float32),
        lax.psum_scatter(
            up_grad.astype(jnp.bfloat16), "ws", scatter_dimension=0, tiled=True
        ).astype(jnp.float32),
        lax.psum_scatter(
            down_grad.astype(jnp.bfloat16), "ws", scatter_dimension=0, tiled=True
        ).astype(jnp.float32),
    )
    large_sums = (
        lax.psum(large_sums[0].astype(jnp.bfloat16), ("ctx", "dp")).astype(jnp.float32),
        lax.psum(large_sums[1].astype(jnp.bfloat16), ("ctx", "dp")).astype(jnp.float32),
        lax.psum(large_sums[2].astype(jnp.bfloat16), ("ctx", "dp")).astype(jnp.float32),
        lax.psum(large_sums[3].astype(jnp.bfloat16), ("ctx", "dp")).astype(jnp.float32),
        lax.psum(large_sums[4].astype(jnp.bfloat16), ("ctx", "dp")).astype(jnp.float32),
        lax.psum(large_sums[5].astype(jnp.bfloat16), ("ctx", "dp")).astype(jnp.float32),
        lax.psum(large_sums[6].astype(jnp.bfloat16), ("ctx", "dp")).astype(jnp.float32),
        lax.psum(large_sums[7].astype(jnp.bfloat16), ("ctx", "dp")).astype(jnp.float32),
    )
    small_sums = lax.psum(
        (conv_grad, score_grad, attn_gain_grad, bias_grad, ff_gain_grad), ("ctx", "dp", "ws")
    )
    return (
        output[None],
        byte_grad[None],
        large_sums[0],
        small_sums[0],
        small_sums[1],
        small_sums[2],
        large_sums[1],
        large_sums[2],
        large_sums[3],
        large_sums[4],
        small_sums[3],
        small_sums[4],
        large_sums[5],
        large_sums[6],
        large_sums[7],
    )


def solution(mesh):
    in_specs = (
        P(("dp", "ws"), "ctx"),
        P(("dp", "ws"), "ctx"),
        P(None, "ws"),
        P(),
        P(),
        P(),
        P("ws", None),
        P("ws", None),
        P("ws", None),
        P("ws", None),
        P(),
        P(),
        P("ws", None),
        P("ws", None),
        P("ws", None),
        P(("dp", "ws"), "ctx", None),
    )
    out_specs = (
        P(("dp", "ws"), "ctx", None),
        P(("dp", "ws"), "ctx", None),
        P(None, "ws"),
        P(),
        P(),
        P(),
        P("ws", None),
        P("ws", None),
        P("ws", None),
        P("ws", None),
        P(),
        P(),
        P("ws", None),
        P("ws", None),
        P("ws", None),
    )
    return jax.shard_map(
        per_device, mesh=mesh, in_specs=in_specs, out_specs=out_specs, check_vma=False
    )
```

```python
import functools

import jax
import jax.numpy as jnp
from jax import lax
from jax.experimental import pallas as pl
from jax.experimental.pallas import tpu as pltpu
from jax.sharding import Mesh
from jax.sharding import PartitionSpec as P

thresholds = (12, 16, 23, 32, 46, 64, 91)
negative = -1e30
epsilon = 1e-06
conv_width = 5
tile = 128
near_bases = (-128, -120, 0, 120, 128)
class_count = len(near_bases) + 2


def bucket_of(relative):
    distance = jnp.abs(relative)
    far_bucket = 8 + sum(((distance >= threshold).astype(jnp.int32) for threshold in thresholds))
    near_bucket = jnp.where(distance < 8, distance, far_bucket)
    return near_bucket + 16 * (relative > 0).astype(jnp.int32)


def matmul(left, right, left_dim, right_dim):
    return lax.dot_general(
        left, right, (((left_dim,), (right_dim,)), ((), ())), preferred_element_type=jnp.float32
    )


def split_pair(values):
    high = values.astype(jnp.bfloat16)
    return high, (values - high.astype(jnp.float32)).astype(jnp.bfloat16)


def tile_class(query_tile, key_tile):
    step = key_tile - query_tile - 4
    own = jnp.where(
        step <= -2, 0, jnp.where(step == -1, 1, jnp.where(step == 0, 3, jnp.where(step == 1, 5, 6)))
    )
    before = jnp.where(step == -1, 2, 0)
    after = jnp.where(step == 1, 4, 6)
    return jnp.where(key_tile < 4, before, jnp.where(key_tile < 8, own, after))


def key_range(seg_ref, query_tile, row_count, tiles_per_block):
    first_seg = seg_ref[1, query_tile * tile]
    last_seg = seg_ref[1, jnp.minimum(query_tile * tile + tile, row_count) - 1]
    low = jnp.int32(0)
    high = jnp.int32(0)
    for block in range(3):
        for part in range(tiles_per_block):
            key_first = seg_ref[block, part * tile]
            key_last = seg_ref[block, min(part * tile + tile, row_count) - 1]
            low = low + (key_last < first_seg).astype(jnp.int32)
            high = high + (key_first <= last_seg).astype(jnp.int32)
    return low, high


def class_buckets(kind, shape, dim):
    place = lax.broadcasted_iota(jnp.int32, shape, dim)
    swing = jnp.where(place < tile, place, place - 2 * tile)
    if kind == 0:
        return jnp.full(shape, bucket_of(jnp.int32(-4 * tile)))
    if kind == class_count - 1:
        return jnp.full(shape, bucket_of(jnp.int32(4 * tile)))
    return bucket_of(near_bases[kind - 1] - swing)


def make_bias(rel_ref, bias_ref, first_pair, pair_count):
    bucket_count = rel_ref.shape[0]
    for kind in range(class_count):
        shape = (bucket_count, 2 * tile)
        hot = class_buckets(kind, shape, 1) == lax.broadcasted_iota(jnp.int32, shape, 0)
        lines = lax.dot_general(
            rel_ref[...], hot.astype(jnp.float32), (((0,), (0,)), ((), ())),
            precision=lax.Precision.HIGHEST, preferred_element_type=jnp.float32,
        )
        for pair in range(pair_count):
            for half in range(2):
                head = 2 * (first_pair + pair) + half
                grid = jnp.broadcast_to(lines[head : head + 1], (tile, 2 * tile))
                if 0 < kind < class_count - 1:
                    grid = pltpu.roll(grid, 0, 1, stride=1, stride_axis=0)
                bias_ref[kind, pair, :, half * tile : (half + 1) * tile] = grid[:, :tile]


def cost(microseconds):
    return pl.CostEstimate(
        flops=int(microseconds * 1e7), transcendentals=0, bytes_accessed=int(microseconds * 3e4)
    )


def stack_heads(block):
    lane = lax.broadcasted_iota(jnp.int32, block.shape, 1)
    zero = jnp.zeros_like(block)
    return jnp.concatenate(
        [jnp.where(lane < tile // 2, block, zero), jnp.where(lane < tile // 2, zero, block)], axis=0
    )


def fold_rows(values, combine):
    pieces = [values[8 * i : 8 * i + 8] for i in range(values.shape[0] // 8)]
    while len(pieces) > 1:
        joined = [combine(pieces[i], pieces[i + 1]) for i in range(0, len(pieces) - 1, 2)]
        if len(pieces) % 2:
            joined.append(pieces[-1])
        pieces = joined
    return pieces[0]


def key_columns(segs_ref, column_ref, key_tile):
    row = segs_ref[key_tile, 0:1, :]
    column_ref[key_tile] = jnp.transpose(jnp.broadcast_to(row, (tile, tile)))


def start_copies(sources, window_ref, sems, first_pair):
    rows, full_width = sources[0].shape
    width = window_ref.shape[1] // 2
    copies = []
    for i, source in enumerate(sources):
        for side in range(2):
            copies.append(
                pltpu.make_async_copy(
                    source.at[:, pl.ds(side * (full_width // 2) + first_pair * tile, width)],
                    window_ref.at[pl.ds(rows * i, rows), pl.ds(side * width, width)],
                    sems.at[2 * i + side],
                )
            )
    for copy in copies:
        copy.start()
    return copies


def forward_kernel(seg_ref, q_ref, *refs, row_count, near):
    if near:
        source_refs, refs = refs[:1], refs[1:]
    else:
        source_refs, refs = refs[:2], refs[2:]
        (mixed_in_ref, top_in_ref, total_in_ref), refs = refs[:3], refs[3:]
    segs_ref, qsegs_ref, rel_ref = refs[:3]
    if near:
        mixed_ref, top_ref, total_ref = refs[3:6]
    else:
        out_ref, lse_ref = refs[3:5]
    window_ref, bias_ref, column_ref, flipped_ref, score_ref = refs[-6 if near else -7 :][:5]
    sems = refs[-1]
    if not near:
        mixed_ref = refs[-2]
    width = q_ref.shape[1]
    pair_count = width // tile
    query_tiles = q_ref.shape[0] // tile
    half = tile // 2
    middle = query_tiles // 2
    copies = start_copies(source_refs, window_ref, sems, 0)
    make_bias(rel_ref, bias_ref, 0, pair_count)

    def key_span(query_tile):
        low, high = key_range(seg_ref, query_tile, row_count, query_tiles)
        if near:
            low = jnp.maximum(low - query_tiles, 0)
            high = jnp.minimum(high - query_tiles, query_tiles)
            return low // 2, (high + 1) // 2
        return jnp.minimum(low // 2, middle), jnp.maximum((high + 1) // 2 - middle, middle)

    def global_tile(key_pair, part):
        key_tile = 2 * key_pair + part
        if near:
            return key_tile + query_tiles
        return key_tile + jnp.where(key_pair >= middle, query_tiles, 0)

    first = key_span(0)[0]
    last = key_span(query_tiles - 1)[1]
    for copy in copies:
        copy.wait()

    def prepare(key_pair, carry):
        for part in range(2):
            row = segs_ref[global_tile(key_pair, part), 0:1, :]
            column_ref[2 * key_pair + part] = jnp.transpose(jnp.broadcast_to(row, (tile, tile)))
        at = pl.multiple_of(key_pair * 2 * tile, 2 * tile)
        flipped_ref[key_pair] = jnp.transpose(window_ref[pl.ds(at, 2 * tile), width:])
        return carry

    lax.fori_loop(first, last, prepare, 0)

    def query_step(query_tile, carry):
        low, high = key_span(query_tile)
        rows = pl.ds(pl.multiple_of(query_tile * tile, tile), tile)
        lanes = [slice(pair * tile, (pair + 1) * tile) for pair in range(pair_count)]
        stacked = [stack_heads(q_ref[rows, lane]) for lane in lanes]
        query_seg = qsegs_ref[query_tile, 0:1, :]
        slot = query_tile if near else 0

        def score_step(key_pair, tops):
            keys = pl.ds(pl.multiple_of(key_pair * 2 * tile, 2 * tile), 2 * tile)
            hides = []
            kinds = []
            for part in range(2):
                hide = jnp.where(column_ref[2 * key_pair + part] == query_seg, 0.0, negative)
                hides.append(jnp.concatenate([hide, hide], axis=1))
                kinds.append(tile_class(query_tile, global_tile(key_pair, part)))
            fresh = []
            for pair in range(pair_count):
                scores = matmul(window_ref[keys, lanes[pair]], stacked[pair], 1, 1)
                top = tops[pair]
                for part in range(2):
                    cut = slice(part * tile, (part + 1) * tile)
                    piece = scores[cut] + bias_ref[kinds[part], pair] + hides[part]
                    score_ref[key_pair, pair, cut] = piece
                    top = jnp.maximum(top, fold_rows(piece, jnp.maximum))
                fresh.append(top)
            return tuple(fresh)

        tops = lax.fori_loop(
            low, high, score_step,
            tuple(jnp.full((8, 2 * tile), negative, jnp.float32) for _ in range(pair_count)),
        )
        tops = [jnp.max(top, axis=0, keepdims=True) for top in tops]
        scales = []
        for pair in range(pair_count):
            if near:
                mixed_ref[slot, pair] = jnp.zeros((tile, tile), jnp.float32)
            else:
                before = top_in_ref[query_tile, pair : pair + 1, :]
                tops[pair] = jnp.maximum(tops[pair], before)
                scale = jnp.exp(before - tops[pair])
                scales.append(scale)
                mixed_ref[slot, pair, :half] = mixed_in_ref[query_tile, pair, :half] * scale[:, :tile]
                mixed_ref[slot, pair, half:] = mixed_in_ref[query_tile, pair, half:] * scale[:, tile:]

        def mix_step(key_pair, totals):
            fresh = []
            for pair in range(pair_count):
                exponent = jnp.exp(score_ref[key_pair, pair] - tops[pair])
                fresh.append(totals[pair] + fold_rows(exponent, jnp.add))
                mixed = matmul(
                    flipped_ref[key_pair, lanes[pair], :], exponent.astype(jnp.bfloat16), 1, 0
                )
                mixed_ref[slot, pair, :half] += mixed[:half, :tile]
                mixed_ref[slot, pair, half:] += mixed[half:, tile:]
            return tuple(fresh)

        totals = lax.fori_loop(
            low, high, mix_step,
            tuple(jnp.zeros((8, 2 * tile), jnp.float32) for _ in range(pair_count)),
        )
        for pair in range(pair_count):
            total = jnp.sum(totals[pair], axis=0, keepdims=True)
            if near:
                top_ref[query_tile, pair : pair + 1, :] = tops[pair]
                total_ref[query_tile, pair : pair + 1, :] = total
                continue
            total = total + total_in_ref[query_tile, pair : pair + 1, :] * scales[pair]
            lse_ref[query_tile, pair : pair + 1, :] = tops[pair] + jnp.log(total)
            inverse = 1.0 / total
            scaled = jnp.concatenate(
                [
                    mixed_ref[slot, pair, :half] * inverse[:, :tile],
                    mixed_ref[slot, pair, half:] * inverse[:, tile:],
                ],
                axis=0,
            )
            out_ref[rows, lanes[pair]] = jnp.transpose(scaled).astype(jnp.bfloat16)
        return carry

    lax.fori_loop(0, query_tiles, query_step, 0)


def backward_kernel(
    seg_ref, q_ref, do_ref, o_ref, before_ref, own_ref, after_ref, segs_ref, qsegs_ref, rel_ref, lse_ref,
    dq_ref, dbefore_ref, down_ref, dafter_ref, bias_out_ref,
    window_ref, bias_ref, column_ref, flipped_ref, dbias_ref, dwindow_ref, dq_acc_ref, delta_ref, sems,
    *, row_count, first_pair
):
    width = dq_ref.shape[1]
    pair_count = width // tile
    query_tiles = q_ref.shape[0] // tile
    block_rows = q_ref.shape[0]
    half = tile // 2
    copies = start_copies((before_ref, own_ref, after_ref), window_ref, sems, first_pair)
    make_bias(rel_ref, bias_ref, first_pair, pair_count)
    dwindow_ref[...] = jnp.zeros(dwindow_ref.shape, jnp.float32)
    dbias_ref[...] = jnp.zeros(dbias_ref.shape, jnp.float32)
    product = do_ref[...].astype(jnp.float32) * o_ref[...].astype(jnp.float32)
    product_high, product_low = split_pair(product)
    member = (
        lax.broadcasted_iota(jnp.int32, (16, width), 1) // half
        == lax.broadcasted_iota(jnp.int32, (16, width), 0)
    ).astype(jnp.bfloat16)
    delta_ref[...] = matmul(member, product_high, 1, 1) + matmul(member, product_low, 1, 1)
    first = key_range(seg_ref, 0, row_count, query_tiles)[0]
    last = key_range(seg_ref, query_tiles - 1, row_count, query_tiles)[1]
    for copy in copies:
        copy.wait()

    def prepare(key_pair, carry):
        for part in range(2):
            key_columns(segs_ref, column_ref, 2 * key_pair + part)
        at = pl.multiple_of(key_pair * 2 * tile, 2 * tile)
        flipped_ref[key_pair] = jnp.transpose(window_ref[pl.ds(at, 2 * tile), :width])
        return carry

    lax.fori_loop(first // 2, (last + 1) // 2, prepare, 0)

    def query_step(query_tile, carry):
        low, high = key_range(seg_ref, query_tile, row_count, query_tiles)
        at = pl.multiple_of(query_tile * tile, tile)
        rows = pl.ds(at, tile)
        lanes = [slice(pair * tile, (pair + 1) * tile) for pair in range(pair_count)]
        queries = [stack_heads(q_ref[rows, lane]) for lane in lanes]
        grads = [stack_heads(do_ref[rows, lane]) for lane in lanes]
        query_seg = qsegs_ref[query_tile, 0:1, :]
        deltas = [
            jnp.concatenate(
                [delta_ref[2 * pair : 2 * pair + 1, rows], delta_ref[2 * pair + 1 : 2 * pair + 2, rows]],
                axis=1,
            )
            for pair in range(pair_count)
        ]
        norms = [
            lse_ref[query_tile, first_pair + pair : first_pair + pair + 1, :]
            for pair in range(pair_count)
        ]
        for pair in range(pair_count):
            dq_acc_ref[pair] = jnp.zeros((tile, tile), jnp.float32)

        def key_step(key_pair, carry):
            keys = pl.ds(pl.multiple_of(key_pair * 2 * tile, 2 * tile), 2 * tile)
            hides = []
            kinds = []
            for part in range(2):
                key_tile = 2 * key_pair + part
                hide = jnp.where(column_ref[key_tile] == query_seg, 0.0, negative)
                hides.append(jnp.concatenate([hide, hide], axis=1))
                kinds.append(tile_class(query_tile, key_tile))
            for pair in range(pair_count):
                lane = lanes[pair]
                value_lane = slice(width + pair * tile, width + (pair + 1) * tile)
                scores = matmul(window_ref[keys, lane], queries[pair], 1, 1)
                dprobs = matmul(window_ref[keys, value_lane], grads[pair], 1, 1)
                probs_low, dscores_low = [], []
                for part in range(2):
                    cut = slice(part * tile, (part + 1) * tile)
                    probs = jnp.exp(
                        scores[cut] + bias_ref[kinds[part], pair] + hides[part] - norms[pair]
                    )
                    dscores = probs * (dprobs[cut] - deltas[pair])
                    dbias_ref[kinds[part], pair] += dscores
                    probs_low.append(probs.astype(jnp.bfloat16))
                    dscores_low.append(dscores.astype(jnp.bfloat16))
                probs_low = jnp.concatenate(probs_low, axis=0)
                dscores_low = jnp.concatenate(dscores_low, axis=0)
                dwindow_ref[keys, lane] += matmul(dscores_low, queries[pair], 1, 0)
                dwindow_ref[keys, value_lane] += matmul(probs_low, grads[pair], 1, 0)
                dquery = matmul(flipped_ref[key_pair, lane, :], dscores_low, 1, 0)
                dq_acc_ref[pair, :half] += dquery[:half, :tile]
                dq_acc_ref[pair, half:] += dquery[half:, tile:]
            return carry

        lax.fori_loop(low // 2, (high + 1) // 2, key_step, 0)
        for pair in range(pair_count):
            dq_ref[rows, lanes[pair]] = jnp.transpose(dq_acc_ref[pair]).astype(jnp.bfloat16)
        return carry

    lax.fori_loop(0, query_tiles, query_step, 0)
    dbefore_ref[...] = dwindow_ref[:block_rows].astype(jnp.bfloat16)
    down_ref[...] = dwindow_ref[block_rows : 2 * block_rows]
    dafter_ref[...] = dwindow_ref[2 * block_rows :].astype(jnp.bfloat16)
    turn = (
        lax.broadcasted_iota(jnp.int32, (tile, tile), 0)
        + lax.broadcasted_iota(jnp.int32, (tile, tile), 1)
        == tile - 1
    ).astype(jnp.bfloat16)
    zero_half = jnp.zeros((tile, tile), jnp.float32)
    bucket_count = rel_ref.shape[0]
    total = jnp.zeros(bias_out_ref.shape, jnp.float32)
    for kind in range(class_count):
        lines = []
        for pair in range(pair_count):
            grid = dbias_ref[kind, pair]
            near = 0 < kind < class_count - 1
            if near:
                grid_high, grid_low = split_pair(grid)
                grid = matmul(turn, grid_high, 1, 0) + matmul(turn, grid_low, 1, 0)
            for side in range(2):
                part = jnp.concatenate([grid[:, side * tile : (side + 1) * tile], zero_half], axis=1)
                if near:
                    part = pltpu.roll(part, tile + 1, 1, stride=1, stride_axis=0)
                lines.append(jnp.sum(fold_rows(part, jnp.add), axis=0, keepdims=True))
        lines.append(jnp.zeros((bias_out_ref.shape[0] - len(lines), 2 * tile), jnp.float32))
        shape = (2 * tile, tile)
        hot = class_buckets(kind, shape, 0) == lax.broadcasted_iota(jnp.int32, shape, 1)
        total = total + jnp.dot(
            jnp.concatenate(lines, axis=0), hot.astype(jnp.float32),
            precision=lax.Precision.HIGHEST, preferred_element_type=jnp.float32,
        )
    bias_out_ref[...] = total


def specs(count, space=pltpu.VMEM):
    return [pl.BlockSpec(memory_space=space) for _ in range(count)]


def attention_forward(segs, q, sources, state, rel_bias, row_count):
    rows, width = q.shape
    tiles = rows // tile
    pairs = width // tile
    near = state is None
    seg_rows = segs.reshape(3 * tiles, 1, tile)
    query_segs = mark_queries(segs, row_count).reshape(tiles, 1, tile)
    f32 = jnp.float32
    norm = jax.ShapeDtypeStruct((tiles, 8, 2 * tile), f32)
    mixed = jax.ShapeDtypeStruct((tiles, pairs, tile, tile), f32)
    count = len(sources)
    blocks = count * tiles // 2
    scratch = [
        pltpu.VMEM((count * rows, 2 * width), jnp.bfloat16),
        pltpu.VMEM((class_count, pairs, tile, 2 * tile), f32),
        pltpu.VMEM((count * tiles, tile, tile), jnp.int32),
        pltpu.VMEM((blocks, width, 2 * tile), jnp.bfloat16),
        pltpu.VMEM((blocks, pairs, 2 * tile, 2 * tile), f32),
    ]
    if not near:
        scratch.append(pltpu.VMEM((1, pairs, tile, tile), f32))
    return pl.pallas_call(
        functools.partial(forward_kernel, row_count=row_count, near=near),
        out_shape=(mixed, norm, norm)
        if near
        else (jax.ShapeDtypeStruct((rows, width), jnp.bfloat16), norm),
        in_specs=specs(1, pltpu.SMEM) + specs(1) + specs(count, pl.ANY)
        + specs(3 if near else 6),
        out_specs=tuple(specs(3 if near else 2)),
        scratch_shapes=scratch + [pltpu.SemaphoreType.DMA((2 * count,))],
        compiler_params=pltpu.CompilerParams(vmem_limit_bytes=(22 if near else 30) << 20),
        cost_estimate=cost(12),
        name="attention_near" if near else "attention_rim",
    )(segs, q, *sources, *(state or ()), seg_rows, query_segs, rel_bias)


def mark_queries(segs, row_count):
    place = jnp.arange(segs.shape[1], dtype=jnp.int32)
    return jnp.where(place < row_count, segs[1], -1)


def attention_backward(
    segs, q, do, o, before, own, after, rel_bias, lse, row_count, first_pair, pairs
):
    rows, full_width = q.shape
    tiles = rows // tile
    width = pairs * tile
    seg_rows = segs.reshape(3 * tiles, 1, tile)
    query_segs = mark_queries(segs, row_count).reshape(tiles, 1, tile)
    part = pl.BlockSpec((rows, width), lambda i: (0, first_pair // pairs))
    return pl.pallas_call(
        functools.partial(backward_kernel, row_count=row_count, first_pair=first_pair),
        grid=(1,),
        out_shape=(
            jax.ShapeDtypeStruct((rows, width), jnp.bfloat16),
            jax.ShapeDtypeStruct((rows, 2 * width), jnp.bfloat16),
            jax.ShapeDtypeStruct((rows, 2 * width), jnp.float32),
            jax.ShapeDtypeStruct((rows, 2 * width), jnp.bfloat16),
            jax.ShapeDtypeStruct((8, tile), jnp.float32),
        ),
        in_specs=specs(1, pltpu.SMEM) + [part, part, part] + specs(3, pl.ANY) + specs(4),
        out_specs=tuple(specs(5)),
        scratch_shapes=[
            pltpu.VMEM((3 * rows, 2 * width), jnp.bfloat16),
            pltpu.VMEM((class_count, pairs, tile, 2 * tile), jnp.float32),
            pltpu.VMEM((3 * tiles, tile, tile), jnp.int32),
            pltpu.VMEM((3 * tiles // 2, width, 2 * tile), jnp.bfloat16),
            pltpu.VMEM((class_count, pairs, tile, 2 * tile), jnp.float32),
            pltpu.VMEM((3 * rows, 2 * width), jnp.float32),
            pltpu.VMEM((pairs, tile, tile), jnp.float32),
            pltpu.VMEM((16, rows), jnp.float32),
            pltpu.SemaphoreType.DMA((6,)),
        ],
        compiler_params=pltpu.CompilerParams(vmem_limit_bytes=30 << 20),
        cost_estimate=cost(20),
        name="attention_backward",
    )(segs, q, do, o, before, own, after, seg_rows, query_segs, rel_bias, lse)


span = 96
id_pad = 128


def dot3(left, right, left_dim, right_dim):
    left_high, left_low = split_pair(left)
    right_high, right_low = split_pair(right)
    return (
        matmul(left_high, right_high, left_dim, right_dim)
        + matmul(left_low, right_high, left_dim, right_dim)
        + matmul(left_high, right_low, left_dim, right_dim)
    )


def block_means_grid(block_size):
    row = lax.broadcasted_iota(jnp.int32, (span, tile), 0)
    lane = lax.broadcasted_iota(jnp.int32, (span, tile), 1)
    same = (row // block_size == lane // block_size) & (lane < span)
    return jnp.where(same, 1.0 / block_size, 0.0)


def row_to_column(row):
    lane = lax.broadcasted_iota(jnp.int32, (span, tile), 1)
    place = lax.broadcasted_iota(jnp.int32, (span, tile), 0)
    return jnp.sum(jnp.where(lane == place, row, 0.0), axis=1, keepdims=True)


def column_to_row(column):
    lane = lax.broadcasted_iota(jnp.int32, (span, tile), 1)
    place = lax.broadcasted_iota(jnp.int32, (span, tile), 0)
    return jnp.sum(jnp.where(lane == place, column, 0.0), axis=0, keepdims=True)


def conv_tile(x_ref, conv_ref, base, lanes):
    taps = range(conv_width)
    return [
        sum(
            conv_ref[tap : tap + 1, i * tile : (i + 1) * tile]
            * x_ref[i, pl.ds(base + tap - conv_width // 2, span), :]
            for tap in taps
        )
        for i in range(lanes)
    ]


def gbst_forward_kernel(
    ids_ref, embed_ref, conv_ref, score_ref,
    start_ref, x_ref, mix_ref, weight_ref,
    table_ref, square_ref, wide_ref,
):
    vocab, width = embed_ref.shape
    lanes = width // tile
    id_tiles = ids_ref.shape[0]
    rows = start_ref.shape[0]
    table_ref[...] = jnp.zeros(table_ref.shape, jnp.bfloat16)
    table_ref[:vocab] = embed_ref[...]
    table_rows = table_ref.shape[0]
    rest = x_ref.shape[1] - id_tiles * tile
    for i in range(lanes):
        x_ref[i, id_tiles * tile :, :] = jnp.zeros((rest, tile), jnp.float32)

    def lookup(step, carry):
        ids = jnp.transpose(jnp.broadcast_to(ids_ref[step, 0:1, :], (tile, tile)))
        lane = lax.broadcasted_iota(jnp.int32, (tile, tile), 1)
        hot = jnp.concatenate(
            [(ids == lane + tile * i).astype(jnp.bfloat16) for i in range(table_rows // tile)], axis=1
        )
        found = matmul(hot, table_ref[...], 1, 0)
        at = pl.ds(pl.multiple_of(step * tile, tile), tile)
        for i in range(lanes):
            x_ref[i, at, :] = found[:, i * tile : (i + 1) * tile]
        return carry

    lax.fori_loop(0, id_tiles, lookup, 0)
    means = [block_means_grid(size) for size in (1, 2, 3, 4)]

    def pool(step, carry):
        base = pl.multiple_of(step * span, 8)
        conv = conv_tile(x_ref, conv_ref, base + id_pad, lanes)
        total = sum(conv[i] * score_ref[0:1, i * tile : (i + 1) * tile] for i in range(lanes))
        row = column_to_row(jnp.sum(total, axis=1, keepdims=True))
        scores = [jnp.sum(mean * row, axis=1, keepdims=True) for mean in means]
        top = functools.reduce(jnp.maximum, scores)
        exponents = [jnp.exp(score - top) for score in scores]
        inverse = 1.0 / sum(exponents)
        weights = [exponent * inverse for exponent in exponents]
        square_ref[...] = sum(weight * mean for weight, mean in zip(weights, means))
        mix = 0.5 * (
            square_ref[pl.ds(0, span // 2, stride=2), :] + square_ref[pl.ds(1, span // 2, stride=2), :]
        )
        half = pl.ds(pl.multiple_of(step * (span // 2), 8), span // 2)
        mix_ref[half, :] = mix
        lane = lax.broadcasted_iota(jnp.int32, (span, tile), 1)
        packed = jnp.zeros((span, tile), jnp.float32)
        for i in range(4):
            packed = jnp.where(lane == i, weights[i], packed)
        weight_ref[pl.ds(base, span), :] = packed
        wide_ref[half, :] = dot3(mix[:, :span], jnp.concatenate(conv, axis=1), 1, 0)
        return carry

    lax.fori_loop(0, mix_ref.shape[0] * 2 // span, pool, 0)
    start_ref[...] = wide_ref[:rows]


def gbst_forward(ids, embed, conv, score, row_count):
    vocab, width = embed.shape
    rows = -(-row_count // tile) * tile
    steps = -(-2 * row_count // span)
    x_rows = max(ids.shape[0] * tile, id_pad + steps * span) + 8
    f32 = jnp.float32
    return pl.pallas_call(
        gbst_forward_kernel,
        out_shape=(
            jax.ShapeDtypeStruct((rows, width), f32),
            jax.ShapeDtypeStruct((width // tile, x_rows, tile), f32),
            jax.ShapeDtypeStruct((steps * span // 2, tile), f32),
            jax.ShapeDtypeStruct((steps * span, tile), f32),
        ),
        in_specs=specs(4),
        out_specs=tuple(specs(4)),
        scratch_shapes=[
            pltpu.VMEM((-(-vocab // tile) * tile, width), jnp.bfloat16),
            pltpu.VMEM((span, tile), f32),
            pltpu.VMEM((steps * span // 2, width), f32),
        ],
        compiler_params=pltpu.CompilerParams(vmem_limit_bytes=18 << 20),
        cost_estimate=cost(12),
        name="gbst_forward",
    )(ids, embed, conv, score)


def weight_copies(place_ref, parts, pieces, full_ref, sems):
    copies = []
    rows = parts[0].shape[0]
    for i, part in enumerate(parts):
        at = pl.multiple_of(place_ref[0] * rows, rows)
        copies.append(
            pltpu.make_async_copy(part, full_ref.at[i, pl.ds(at, rows)], sems.at[len(copies)])
        )
    for number, piece in enumerate(pieces):
        share = piece.shape[1]
        at = pl.multiple_of((1 - place_ref[0]) * rows + place_ref[1 + number] * share, share)
        copies.append(
            pltpu.make_async_copy(piece, full_ref.at[:, pl.ds(at, share)], sems.at[len(copies)])
        )
    for copy in copies:
        copy.start()
    return copies


def project_kernel(place_ref, start_ref, gain_ref, *refs):
    pieces = refs[3:-5]
    first_ref, q_ref, kv_ref, weight_ref, sems = refs[-5:]
    copies = weight_copies(place_ref, refs[:3], pieces, weight_ref, sems)
    width = q_ref.shape[1]
    start = start_ref[...]
    inverse = lax.rsqrt(jnp.mean(start * start, axis=-1, keepdims=True) + epsilon)
    first = (start * inverse * gain_ref[...]).astype(jnp.bfloat16)
    first_ref[...] = first
    for copy in copies:
        copy.wait()
    q_ref[...] = matmul(first, weight_ref[0], 1, 0).astype(jnp.bfloat16)
    kv_ref[:, :width] = matmul(first, weight_ref[1], 1, 0).astype(jnp.bfloat16)
    kv_ref[:, width:] = matmul(first, weight_ref[2], 1, 0).astype(jnp.bfloat16)


def project(place, start, gain, own, pieces):
    rows, width = start.shape
    b16 = jnp.bfloat16
    return pl.pallas_call(
        project_kernel,
        out_shape=(
            jax.ShapeDtypeStruct((rows, width), b16),
            jax.ShapeDtypeStruct((rows, width), b16),
            jax.ShapeDtypeStruct((rows, 2 * width), b16),
        ),
        in_specs=specs(1, pltpu.SMEM) + specs(2) + specs(3 + len(pieces), pl.ANY),
        out_specs=tuple(specs(3)),
        scratch_shapes=[
            pltpu.VMEM((3, width, width), b16),
            pltpu.SemaphoreType.DMA((3 + len(pieces),)),
        ],
        compiler_params=pltpu.CompilerParams(vmem_limit_bytes=60 << 20),
        cost_estimate=cost(6),
        name="project",
    )(place, start, gain, *own, *pieces)


def feed_kernel(place_ref, order_ref, bits_ref, mixed_ref, start_ref, cot_ref, gain_ref, *refs, piece_count):
    (wo_ref, wg_ref, wu_ref, wd_ref), refs = refs[:4], refs[4:]
    gate_pieces, refs = refs[:piece_count], refs[piece_count:]
    tail_pieces, refs = refs[:piece_count], refs[piece_count:]
    (
        out_ref, downg_ref, gateup_ref, extra_ref, dmid_ref, dmixed_ref, outg_ref, gaing_ref,
        second_ref, turned_ref, middle_ref, scale_ref, total_ref, dsecond_ref, grad_ref,
        fullo_ref, fullg_ref, fullu_ref, fulld_ref,
    ) = refs
    step = pl.program_id(0)
    last = pl.num_programs(0) - 1
    row_count = out_ref.shape[0]
    chunk = fulld_ref.shape[0]

    def fill(full_ref, own_ref, pieces, pick):
        rows = own_ref.shape[0]
        full_ref[pl.ds(pl.multiple_of(place_ref[0] * rows, rows), rows), :] = own_ref[...]
        for number, piece in enumerate(pieces):
            block = pick(piece)
            share = block.shape[0]
            at = (1 - place_ref[0]) * rows + place_ref[1 + number] * share
            full_ref[pl.ds(pl.multiple_of(at, share), share), :] = block

    @pl.when(step == 0)
    def _():
        fill(fullo_ref, wo_ref, tail_pieces, lambda piece: piece[chunk:])
        middle = start_ref[...] + matmul(mixed_ref[...], fullo_ref[...], 1, 0)
        middle_ref[...] = middle
        inverse = lax.rsqrt(jnp.mean(middle * middle, axis=-1, keepdims=True) + epsilon)
        scale_ref[...] = jnp.broadcast_to(inverse, scale_ref.shape)
        second = (middle * inverse * gain_ref[...]).astype(jnp.bfloat16)
        second_ref[...] = second
        turned_ref[...] = jnp.transpose(second)
        total_ref[...] = jnp.zeros(total_ref.shape, jnp.float32)
        dsecond_ref[...] = jnp.zeros(dsecond_ref.shape, jnp.float32)
        grad_ref[:row_count] = cot_ref[...]
        grad_ref[row_count:] = jnp.zeros((grad_ref.shape[0] - row_count, grad_ref.shape[1]), jnp.bfloat16)

    fill(fullg_ref, wg_ref, gate_pieces, lambda piece: piece[0])
    fill(fullu_ref, wu_ref, gate_pieces, lambda piece: piece[1])
    own_steps = pl.num_programs(0) - piece_count

    @pl.when(step < own_steps)
    def _():
        fulld_ref[...] = wd_ref[...]

    for number in range(piece_count):

        @pl.when(step == own_steps + number)
        def _():
            fulld_ref[...] = tail_pieces[number][:chunk]

    second = second_ref[...]
    cot = grad_ref[...]
    gate = matmul(second, fullg_ref[...], 1, 0)
    up = matmul(second, fullu_ref[...], 1, 0)
    dhidden = matmul(cot, fulld_ref[...], 1, 1)
    root = 0.7978845608028654
    square = gate * gate
    bend = jnp.tanh(root * (gate + 0.044715 * (square * gate)))
    rise = 0.5 * (1.0 + bend)
    gelu = gate * rise
    slope = rise + 0.5 * gate * (1.0 - bend * bend) * (root * (1.0 + 3 * 0.044715 * square))
    hidden = (gelu * up).astype(jnp.bfloat16)
    dgate = (dhidden * up * slope).astype(jnp.bfloat16)
    dup = (dhidden * gelu).astype(jnp.bfloat16)
    total_ref[...] += matmul(hidden, fulld_ref[...], 1, 0)
    downg = matmul(jnp.transpose(hidden), cot, 1, 0).astype(jnp.bfloat16)
    gateg = matmul(turned_ref[...], dgate, 1, 0).astype(jnp.bfloat16)
    upg = matmul(turned_ref[...], dup, 1, 0).astype(jnp.bfloat16)
    side = downg.shape[1] // 2
    if piece_count:
        bit_core, bit_ws, bit_dp = bits_ref[0], bits_ref[1], bits_ref[2]
        for first in range(2):
            for second in range(2):
                rows = slice(first * (chunk // 2), (first + 1) * (chunk // 2))
                downg_ref[first ^ bit_core, second ^ bit_dp, 0, 0, 0] = downg[
                    rows, second * side : (second + 1) * side
                ]

        def store_gate(target_ref):
            for first in range(2):
                rows = slice(first * side, (first + 1) * side)
                target_ref[first ^ bit_ws, 0 ^ bit_dp, 0, 0] = gateg[rows]
                target_ref[first ^ bit_ws, 1 ^ bit_dp, 0, 0] = upg[rows]

        @pl.when((step >> 1) & 1 == 0)
        def _():
            store_gate(gateup_ref)

        @pl.when((step >> 1) & 1 == 1)
        def _():
            store_gate(extra_ref)

    else:
        downg_ref[...] = downg
        extra_ref[...] = jnp.zeros(extra_ref.shape, jnp.bfloat16)
        gateup_ref[0, 0] = gateg
        gateup_ref[0, 1] = upg
    dsecond_ref[...] += matmul(dgate, fullg_ref[...], 1, 1) + matmul(dup, fullu_ref[...], 1, 1)

    @pl.when(step == last)
    def _():
        middle = middle_ref[...]
        inverse = scale_ref[:, 0:1]
        out_ref[...] = (middle + total_ref[...])[:row_count].astype(jnp.bfloat16)
        normed = middle * inverse
        dsecond = dsecond_ref[...]
        gaing_ref[...] = jnp.sum(dsecond * normed, axis=0, keepdims=True)
        dnormed = dsecond * gain_ref[...]
        dmid = grad_ref[...].astype(jnp.float32) + inverse * (
            dnormed - normed * jnp.mean(dnormed * normed, axis=-1, keepdims=True)
        )
        dmid_ref[...] = dmid
        dbranch = dmid.astype(jnp.bfloat16)
        dmixed_ref[...] = matmul(dbranch, fullo_ref[...], 1, 1).astype(jnp.bfloat16)
        outg = matmul(jnp.transpose(mixed_ref[...]), dbranch, 1, 0).astype(jnp.bfloat16)
        if piece_count:
            store_relative(outg_ref, outg, bits_ref, 0, True)
        else:
            outg_ref[...] = outg


def store_relative(out_ref, grad, bits_ref, at, group_last):
    rows = grad.shape[0] // 16
    width = grad.shape[1] // 2
    bits = [bits_ref[i] for i in range(5)]
    for number in range(16):
        group, high, low, core = number >> 3, (number >> 2) & 1, (number >> 1) & 1, number & 1
        for side in range(2):
            place = (side ^ bits[2], low ^ bits[3], high ^ bits[4])
            own_group = (group ^ bits[1],)
            place = place + own_group if group_last else own_group + place
            out_ref[(core ^ bits[0],) + place + (slice(at, at + rows),)] = grad[
                number * rows : (number + 1) * rows, side * width : (side + 1) * width
            ]


def feed_forward(place, order, bits, mixed, start, cot, gain, own, gate_pieces, tail_pieces):
    rows, width = start.shape
    row_count = cot.shape[0]
    wo, wg, wu, wd = own
    hidden = wg.shape[1]
    steps = order.shape[0]
    chunk = hidden // steps
    count = len(gate_pieces)
    own_blocks = wd.shape[0] // chunk
    f32, b16 = jnp.float32, jnp.bfloat16

    def whole(array):
        return pl.BlockSpec(array.shape, lambda f, *refs: (0,) * len(array.shape))

    def columns(array):
        if array.ndim == 3:
            shape = array.shape[:2] + (chunk,)
            return pl.BlockSpec(shape, lambda f, place, order, bits: (0, 0, order[f]))
        return pl.BlockSpec((array.shape[0], chunk), lambda f, place, order, bits: (0, order[f]))

    if count:
        relative = (2,) * 5
        gate_shape = (2,) * 4 + (width // 2, chunk)
        grad_shapes = (relative + (chunk // 2, width // 2), gate_shape, gate_shape)
        out_grad_shape = relative + (width // 16, width // 2)

        def down_index(f, place, order, bits):
            return (
                0, 0, (order[f] & 1) ^ bits[3], ((order[f] >> 1) & 1) ^ bits[4],
                (order[f] >> 2) ^ bits[1], 0, 0,
            )

        def gate_spec(steps_of):
            def index(f, place, order, bits):
                held = jnp.int32(steps_of[-1])
                for number in range(len(steps_of) - 2, -1, -1):
                    held = jnp.where(f <= number, steps_of[number], held)
                chosen = order[held]
                return 0, 0, ((chosen >> 1) & 1) ^ bits[3], (chosen >> 2) ^ bits[4], 0, 0

            return pl.BlockSpec((2, 2, 1, 1, width // 2, chunk), index)

        grad_specs = [
            pl.BlockSpec((2, 2, 1, 1, 1, chunk // 2, width // 2), down_index),
            gate_spec((0, 1, 1, 1, 4, 5, 5, 5)),
            gate_spec((2, 2, 2, 3, 3, 3, 6, 7)),
        ]
    else:
        grad_shapes = ((hidden, width), (steps, 2, width, chunk), (8, tile))
        out_grad_shape = (width, width)
        grad_specs = [
            pl.BlockSpec((chunk, width), lambda f, place, order, bits: (order[f], 0)),
            pl.BlockSpec((1, 2, width, chunk), lambda f, place, order, bits: (order[f], 0, 0, 0)),
            pl.BlockSpec((8, tile), lambda f, place, order, bits: (0, 0)),
        ]
    shapes = (
        jax.ShapeDtypeStruct((row_count, width), b16),
        jax.ShapeDtypeStruct(grad_shapes[0], b16),
        jax.ShapeDtypeStruct(grad_shapes[1], b16),
        jax.ShapeDtypeStruct(grad_shapes[2], b16),
        jax.ShapeDtypeStruct((rows, width), f32),
        jax.ShapeDtypeStruct((rows, width), b16),
        jax.ShapeDtypeStruct(out_grad_shape, b16),
        jax.ShapeDtypeStruct((1, width), f32),
    )
    return pl.pallas_call(
        functools.partial(feed_kernel, piece_count=count),
        out_shape=shapes,
        grid_spec=pltpu.PrefetchScalarGridSpec(
            num_scalar_prefetch=3,
            grid=(steps,),
            in_specs=[whole(mixed), whole(start), whole(cot), whole(gain), whole(wo)]
            + [
                columns(wg), columns(wu),
                pl.BlockSpec(
                    (chunk, width),
                    lambda f, place, order, bits: (
                        order[jnp.minimum(f, own_blocks - 1)] & (own_blocks - 1), 0
                    ),
                ),
            ]
            + [columns(piece) for piece in gate_pieces]
            + [whole(piece) for piece in tail_pieces],
            out_specs=(
                whole(shapes[0]),
                *grad_specs,
                whole(shapes[4]), whole(shapes[5]), whole(shapes[6]), whole(shapes[7]),
            ),
            scratch_shapes=[
                pltpu.VMEM((rows, width), b16),
                pltpu.VMEM((width, rows), b16),
                pltpu.VMEM((rows, width), f32),
                pltpu.VMEM((rows, tile), f32),
                pltpu.VMEM((rows, width), f32),
                pltpu.VMEM((rows, width), f32),
                pltpu.VMEM((rows, width), b16),
                pltpu.VMEM((width, width), b16),
                pltpu.VMEM((width, chunk), b16),
                pltpu.VMEM((width, chunk), b16),
                pltpu.VMEM((chunk, width), b16),
            ],
        ),
        compiler_params=pltpu.CompilerParams(vmem_limit_bytes=46 << 20),
        cost_estimate=cost(26),
        name="feed_forward",
    )(place, order, bits, mixed, start, cot, gain, *own, *gate_pieces, *tail_pieces)


def project_grads_kernel(
    bits_ref, dq0_ref, dq1_ref, own0_ref, own1_ref, after0_ref, after1_ref, before0_ref, before1_ref,
    first_ref, grads_ref, total_ref, *, relative
):
    width = first_ref.shape[1]
    half = width // 2

    def total(own_ref, after_ref, before_ref):
        return (
            own_ref[...] + after_ref[...].astype(jnp.float32) + before_ref[...].astype(jnp.float32)
        ).astype(jnp.bfloat16)

    sides = (total(own0_ref, after0_ref, before0_ref), total(own1_ref, after1_ref, before1_ref))
    grads = (
        jnp.concatenate([dq0_ref[...], dq1_ref[...]], axis=1),
        jnp.concatenate([side[:, :half] for side in sides], axis=1),
        jnp.concatenate([side[:, half:] for side in sides], axis=1),
    )
    turned = jnp.transpose(first_ref[...])
    for i, grad in enumerate(grads):
        total_ref[i] = grad
        product = matmul(turned, grad, 1, 0).astype(jnp.bfloat16)
        if relative:
            store_relative(grads_ref, product, bits_ref, i * (width // 16), False)
        else:
            grads_ref[i] = product


def project_grads(bits, halves, first, relative):
    rows, width = first.shape
    shape = (2,) * 5 + (3 * (width // 16), width // 2) if relative else (3, width, width)
    return pl.pallas_call(
        functools.partial(project_grads_kernel, relative=relative),
        out_shape=(
            jax.ShapeDtypeStruct(shape, jnp.bfloat16),
            jax.ShapeDtypeStruct((3, rows, width), jnp.bfloat16),
        ),
        in_specs=specs(1, pltpu.SMEM) + specs(9),
        out_specs=tuple(specs(2)),
        compiler_params=pltpu.CompilerParams(vmem_limit_bytes=24 << 20),
        cost_estimate=cost(5),
        name="project_grads",
    )(bits, *halves, first)


def project_back_kernel(place_ref, grads_ref, start_ref, dmid_ref, gain_ref, *refs):
    dstart_ref, gaing_ref, weight_ref, sems = refs[-4:]
    copies = weight_copies(place_ref, refs[:3], refs[3:-4], weight_ref, sems)
    start = start_ref[...]
    inverse = lax.rsqrt(jnp.mean(start * start, axis=-1, keepdims=True) + epsilon)
    normed = start * inverse
    for copy in copies:
        copy.wait()
    dfirst = sum(matmul(grads_ref[i], weight_ref[i], 1, 1) for i in range(3))
    gaing_ref[...] = jnp.sum(dfirst * normed, axis=0, keepdims=True)
    dnormed = dfirst * gain_ref[...]
    dstart_ref[...] = dmid_ref[...] + inverse * (
        dnormed - normed * jnp.mean(dnormed * normed, axis=-1, keepdims=True)
    )


def project_back(place, grads, start, dmid, gain, own, pieces):
    rows, width = start.shape
    return pl.pallas_call(
        project_back_kernel,
        out_shape=(
            jax.ShapeDtypeStruct((rows, width), jnp.float32),
            jax.ShapeDtypeStruct((1, width), jnp.float32),
        ),
        in_specs=specs(1, pltpu.SMEM) + specs(4) + specs(3 + len(pieces), pl.ANY),
        out_specs=tuple(specs(2)),
        scratch_shapes=[
            pltpu.VMEM((3, width, width), jnp.bfloat16),
            pltpu.SemaphoreType.DMA((3 + len(pieces),)),
        ],
        compiler_params=pltpu.CompilerParams(vmem_limit_bytes=60 << 20),
        cost_estimate=cost(6),
        name="project_back",
    )(place, grads, start, dmid, gain, *own, *pieces)


def unpool_kernel(
    x_ref, mix_ref, weight_ref, dstart_ref, conv_ref, score_ref,
    dconv_ref, left_ref, right_ref, convg_ref, scoreg_ref,
    wide_ref, square_ref, sums_ref, *, byte_count
):
    lanes = x_ref.shape[0]
    width = lanes * tile
    rows = dstart_ref.shape[0]
    steps = mix_ref.shape[0] * 2 // span
    lead = id_pad + 8
    wide_ref[:rows] = dstart_ref[...]
    wide_ref[rows:] = jnp.zeros((wide_ref.shape[0] - rows, width), jnp.float32)
    for i in range(lanes):
        dconv_ref[i, :lead] = jnp.zeros((lead, tile), jnp.float32)
    sums_ref[...] = jnp.zeros(sums_ref.shape, jnp.float32)
    means = [block_means_grid(size) for size in (1, 2, 3, 4)]

    def unpool(step, carry):
        base = pl.multiple_of(step * span, 8)
        half = pl.ds(pl.multiple_of(step * (span // 2), 8), span // 2)
        conv = jnp.concatenate(conv_tile(x_ref, conv_ref, base + id_pad, lanes), axis=1)
        dstart = wide_ref[half, :]
        dstart_high, dstart_low = split_pair(dstart)
        conv_high, conv_low = split_pair(conv)
        inner = (
            matmul(dstart_high, conv_high, 1, 1)
            + matmul(dstart_low, conv_high, 1, 1)
            + matmul(dstart_high, conv_low, 1, 1)
        )
        inner = jnp.concatenate([inner, jnp.zeros((span // 2, tile - span), jnp.float32)], axis=1)
        square_ref[pl.ds(0, span // 2, stride=2), :] = inner
        square_ref[pl.ds(1, span // 2, stride=2), :] = inner
        inner = square_ref[...]
        weights = [weight_ref[pl.ds(base, span), i : i + 1] for i in range(4)]
        dweights = [0.5 * jnp.sum(mean * inner, axis=1, keepdims=True) for mean in means]
        common = sum(weight * dweight for weight, dweight in zip(weights, dweights))
        dscores = [weight * (dweight - common) for weight, dweight in zip(weights, dweights)]
        row = jnp.sum(
            sum(dscore * mean for dscore, mean in zip(dscores, means)), axis=0, keepdims=True
        )
        column = row_to_column(row)
        mix_high, mix_low = split_pair(mix_ref[half, :][:, :span])
        dconv = (
            matmul(mix_high, dstart_high, 0, 0)
            + matmul(mix_low, dstart_high, 0, 0)
            + matmul(mix_high, dstart_low, 0, 0)
            + column * score_ref[...]
        )
        for i in range(lanes):
            part = dconv[:, i * tile : (i + 1) * tile]
            dconv_ref[i, pl.ds(base + lead, span), :] = part
            for tap in range(conv_width):
                moved = x_ref[i, pl.ds(base + id_pad + tap - conv_width // 2, span), :]
                sums_ref[tap, :, i * tile : (i + 1) * tile] += fold_rows(part * moved, jnp.add)
        sums_ref[conv_width] += fold_rows(column * conv, jnp.add)
        return carry

    lax.fori_loop(0, steps, unpool, 0)
    for tap in range(conv_width):
        convg_ref[tap : tap + 1, :] = jnp.sum(sums_ref[tap], axis=0, keepdims=True)
    scoreg_ref[...] = jnp.sum(sums_ref[conv_width], axis=0, keepdims=True)
    left_ref[...] = spread(dconv_ref, conv_ref, lead - 8, 8)
    right_ref[...] = spread(dconv_ref, conv_ref, lead + byte_count, 8)


def spread(dconv_ref, conv_ref, base, count):
    lanes = dconv_ref.shape[0]
    parts = [
        sum(
            conv_ref[tap : tap + 1, i * tile : (i + 1) * tile]
            * dconv_ref[i, pl.ds(base + conv_width // 2 - tap, count), :]
            for tap in range(conv_width)
        )
        for i in range(lanes)
    ]
    return jnp.concatenate(parts, axis=1)


def unpool(x, mix, weight, dstart, conv, score, byte_count):
    lanes = x.shape[0]
    width = lanes * tile
    f32 = jnp.float32
    half_rows = mix.shape[0]
    return pl.pallas_call(
        functools.partial(unpool_kernel, byte_count=byte_count),
        out_shape=(
            jax.ShapeDtypeStruct((lanes, 2 * half_rows + id_pad + 8, tile), f32),
            jax.ShapeDtypeStruct((8, width), f32),
            jax.ShapeDtypeStruct((8, width), f32),
            jax.ShapeDtypeStruct((conv_width, width), f32),
            jax.ShapeDtypeStruct((1, width), f32),
        ),
        in_specs=specs(6),
        out_specs=tuple(specs(5)),
        scratch_shapes=[
            pltpu.VMEM((half_rows, width), f32),
            pltpu.VMEM((span, tile), f32),
            pltpu.VMEM((conv_width + 1, 8, width), f32),
        ],
        compiler_params=pltpu.CompilerParams(vmem_limit_bytes=20 << 20),
        cost_estimate=cost(13),
        name="unpool",
    )(x, mix, weight, dstart, conv, score)


def scatter_kernel(ids_ref, dconv_ref, conv_ref, left_ref, right_ref, byteg_ref, embedg_ref, total_ref):
    byte_count = byteg_ref.shape[0]
    total_ref[...] = jnp.zeros(total_ref.shape, jnp.float32)

    def scatter(step):
        grads = spread(dconv_ref, conv_ref, step * tile + 8, tile)
        ids = ids_ref[step, 0:1, :]
        place = lax.broadcasted_iota(jnp.int32, (total_ref.shape[0], tile), 0)
        hot = (place == ids).astype(jnp.bfloat16)
        grads_high, grads_low = split_pair(grads)
        total_ref[...] += matmul(hot, grads_high, 1, 0) + matmul(hot, grads_low, 1, 0)
        return grads

    scatter(0)

    def whole_tile(step, carry):
        byteg_ref[pl.ds(pl.multiple_of((step - 1) * tile, tile), tile), :] = scatter(step)
        return carry

    full = byte_count // tile
    lax.fori_loop(1, full + 1, whole_tile, 0)
    byteg_ref[full * tile :, :] = scatter(full + 1)[: byte_count - full * tile]
    byteg_ref[:8] += left_ref[...]
    byteg_ref[byte_count - 8 :] += right_ref[...]
    embedg_ref[...] = total_ref[...].astype(jnp.bfloat16)


def scatter_bytes(ids, dconv, conv, left, right, byte_count, vocab):
    width = conv.shape[1]
    table_rows = -(-vocab // 32) * 32
    return pl.pallas_call(
        scatter_kernel,
        out_shape=(
            jax.ShapeDtypeStruct((byte_count, width), jnp.float32),
            jax.ShapeDtypeStruct((table_rows, width), jnp.bfloat16),
        ),
        in_specs=specs(5),
        out_specs=tuple(specs(2)),
        scratch_shapes=[pltpu.VMEM((table_rows, width), jnp.float32)],
        compiler_params=pltpu.CompilerParams(vmem_limit_bytes=16 << 20),
        cost_estimate=cost(10),
        name="scatter_bytes",
    )(ids, dconv, conv, left, right)


def finish_kernel(bits_ref, near_ref, across_ref, core_ref, both_ref, *out_refs, columns):
    flip = bits_ref[2] == 0
    for number in range(8):
        high, low, core = number >> 2, (number >> 1) & 1, number & 1
        place = (low ^ bits_ref[3], high ^ bits_ref[4])
        same = (core ^ bits_ref[0]) == 0
        near = jnp.where(same, near_ref[place], core_ref[place]).astype(jnp.float32)
        across = jnp.where(same, across_ref[place], both_ref[place]).astype(jnp.float32)
        first, second = jnp.where(flip, near, across), jnp.where(flip, across, near)
        if columns:
            width = first.shape[1]
            out_refs[0][:, number * width : (number + 1) * width] = first
            out_refs[1][:, number * width : (number + 1) * width] = second
            continue
        half = first.shape[1]
        at = 0
        for out_ref in out_refs:
            rows = out_ref.shape[0] // 8
            out_ref[number * rows : (number + 1) * rows, :half] = first[at : at + rows]
            out_ref[number * rows : (number + 1) * rows, half:] = second[at : at + rows]
            at += rows


def finish(bits, parts, shapes, columns):
    return pl.pallas_call(
        functools.partial(finish_kernel, columns=columns),
        out_shape=tuple(jax.ShapeDtypeStruct(shape, jnp.float32) for shape in shapes),
        in_specs=specs(1, pltpu.SMEM) + specs(4),
        out_specs=tuple(specs(len(shapes))),
        compiler_params=pltpu.CompilerParams(vmem_limit_bytes=20 << 20),
        cost_estimate=cost(3),
        name="finish_gate" if columns else "finish_square",
    )(bits, *parts)


def finish_rows_kernel(sum_ref, *out_refs):
    at = 0
    for out_ref in out_refs:
        blocks = sum_ref.shape[0]
        rows, width = out_ref.shape[0] // blocks, out_ref.shape[1]
        for number in range(blocks):
            for side in range(2):
                block = sum_ref[number, side, at : at + rows].astype(jnp.float32)
                out_ref[
                    number * rows : (number + 1) * rows, side * (width // 2) : (side + 1) * (width // 2)
                ] = block
        at += rows


def finish_rows(total, rows):
    steps, _, height, half = total.shape
    return pl.pallas_call(
        finish_rows_kernel,
        out_shape=tuple(jax.ShapeDtypeStruct((steps * n, 2 * half), jnp.float32) for n in rows),
        in_specs=specs(1),
        out_specs=tuple(specs(len(rows))),
        compiler_params=pltpu.CompilerParams(vmem_limit_bytes=20 << 20),
        cost_estimate=cost(3),
        name="finish_rows",
    )(total)


sequence_axes = ("z", "core")
copy_axes = ("z", "core", "dp")
all_axes = ("z", "core", "dp", "ws")


def neighbours(block, axes):
    count = 1
    for axis in axes:
        count *= lax.axis_size(axis)
    forward = [(i, i + 1) for i in range(count - 1)]
    backward = [(target, source) for source, target in forward]
    return lax.ppermute(block, axes, forward), lax.ppermute(block, axes, backward)


def pad_rows(block):
    return jnp.pad(block, ((0, -block.shape[0] % tile), (0, 0)))


def swap(block, axis, distance=1):
    pairs = [(i, i ^ distance) for i in range(lax.axis_size(axis))]
    return lax.ppermute(block, axis, pairs)


def ordered(near, far, place, axis):
    first = place == 0
    return jnp.concatenate([jnp.where(first, near, far), jnp.where(first, far, near)], axis=axis)


def pack(block, small):
    high, low = split_pair(small)
    rest = jnp.zeros((-2 * small.shape[0] % 16, small.shape[1]), jnp.bfloat16)
    return jnp.concatenate([block, high, low, rest])


def unpack(sent, small):
    count = small.shape[0]
    rows = sent.shape[0] - (2 * count + -2 * count % 16)
    high, low = sent[rows : rows + count], sent[rows + count : rows + 2 * count]
    return sent[:rows], small + high.astype(jnp.float32) + low.astype(jnp.float32)


def gather_columns(shard):
    axis = shard.ndim - 1
    if lax.axis_size("ws") != 2:
        return lax.all_gather(shard, "ws", axis=axis, tiled=True)
    return ordered(shard, swap(shard, "ws"), lax.axis_index("ws"), axis)


def own_share(shard, axis):
    share = shard.shape[axis] // 4
    place = lax.axis_index("dp") * 2 + lax.axis_index("core")
    return lax.dynamic_slice_in_dim(shard, place * share, share, axis)


def spread_pieces(first):
    second = swap(first, "dp")
    return first, second, swap(first, "core"), swap(second, "core")


def special_mesh():
    return lax.axis_size("ws") == 2 and lax.axis_size("dp") == 2 and lax.axis_size("z") == 4


def add(*parts):
    return sum(part.astype(jnp.float32) for part in parts).astype(parts[0].dtype)


def swap_high(block, place):
    return swap(block, "z", place[0] + 2 * place[1])


others = ((1, 0), (0, 1), (1, 1))


class Chain:
    def __init__(self, sent, kept, order):
        self.sent, self.kept = (sent,), kept
        self.order = order

    def join(self):
        axis, rest = self.order[0], self.order[1:]
        if axis == "z":
            received = [swap_high(part, place) for part, place in zip(self.sent, others)]
        else:
            received = [swap(self.sent[0], axis)]
        parts = [self.kept] + received
        self.order = rest
        if not rest:
            self.sent, self.kept = (), add(*parts)
            return
        places = others if rest[0] == "z" else ((1,),)
        self.sent = tuple(add(*(part[place] for part in parts)) for place in places)
        own = (0,) * len(places[0])
        self.kept = add(*(part[own] for part in parts))

    def state(self):
        return (self.sent, self.kept)

    def set_state(self, state):
        self.sent, self.kept = state


def gather_high(part):
    return jnp.stack(
        [
            jnp.stack([part, swap_high(part, (0, 1))]),
            jnp.stack([swap_high(part, (1, 0)), swap_high(part, (1, 1))]),
        ]
    )


def collect(part):
    return lax.all_gather(part, copy_axes, axis=0).reshape((8, 2) + part.shape)


def reduce_plain(grad):
    part = lax.psum_scatter(grad, "ws", scatter_dimension=grad.ndim - 2, tiled=True)
    return lax.psum(part, copy_axes).astype(jnp.float32)


def after(value, chains):
    if not special_mesh():
        return value
    value, kept = lax.optimization_barrier((value, [chain.kept for chain in chains]))
    for chain, part in zip(chains, kept):
        chain.kept = part
    return value


def hold(value, chains=()):
    if not special_mesh():
        return value
    value, states = lax.optimization_barrier((value, [chain.state() for chain in chains]))
    for chain, state in zip(chains, states):
        chain.set_state(state)
    return value


def per_device(
    byte_ids,
    segments,
    embed,
    conv_kernel,
    score_weight,
    attn_gain,
    w_q,
    w_k,
    w_v,
    w_o,
    rel_bias,
    ff_gain,
    w_gate,
    w_up,
    w_down,
    cotangent,
):
    byte_count = byte_ids.shape[1]
    row_count = byte_count // 2
    width = w_q.shape[1]
    group_count = lax.axis_size("ws")
    cycle_count = lax.axis_size("z") * lax.axis_size("core")
    cycle_place = lax.axis_index("z") * lax.axis_size("core") + lax.axis_index("core")
    bucket_count, head_count = rel_bias.shape
    rim = conv_width // 2
    has_before = cycle_place > 0
    has_after = cycle_place < cycle_count - 1

    ids = byte_ids[0]
    row_segs = segments[0, ::2]
    note = jnp.concatenate([row_segs, ids[:rim], ids[byte_count - rim :]])
    before_note, after_note = neighbours(note, sequence_axes)
    embed_table = gather_columns(embed)
    if special_mesh():
        core, dp = lax.axis_index("core"), lax.axis_index("dp")
        place = jnp.stack(
            [lax.axis_index("ws"), dp * 2 + core, 2 - dp * 2 + core, dp * 2 + 1 - core, 3 - dp * 2 - core]
        ).astype(jnp.int32)
        own_order = jnp.stack([core, core + 2, 1 - core, 3 - core])
        order = jnp.concatenate([place[0] * 4 + own_order, (1 - place[0]) * 4 + place[1:]])
        order = order.astype(jnp.int32)
        z = lax.axis_index("z")
        bits = jnp.stack([core, place[0], dp, z & 1, z >> 1]).astype(jnp.int32)
        square_share = jnp.stack([own_share(weight, 0) for weight in (w_q, w_k, w_v)])
        gate_share = jnp.stack([own_share(weight, 0) for weight in (w_gate, w_up)])
        tail_share = jnp.concatenate([own_share(weight, 0) for weight in (w_down, w_o)])
        square_first = swap(square_share, "ws")
        (gate_share, square_first, embed_table, before_note, after_note) = lax.optimization_barrier(
            (gate_share, square_first, embed_table, before_note, after_note)
        )
        square_second, square_third = swap(square_first, "dp"), swap(square_first, "core")
        gate_first = swap(gate_share, "ws")
        own_square, own_feed = (w_q, w_k, w_v), (w_o, w_gate, w_up, w_down)
    else:
        place = jnp.zeros((1,), jnp.int32)
        order = jnp.arange(8, dtype=jnp.int32)
        bits = jnp.zeros((5,), jnp.int32)
        square_pieces = gate_pieces = tail_pieces = ()
        own_square, own_feed = (
            tuple(lax.all_gather(weight, "ws", axis=0, tiled=True) for weight in weights)
            for weights in ((w_q, w_k, w_v), (w_o, w_gate, w_up, w_down))
        )
    segs = jnp.stack(
        [
            jnp.where(has_before, before_note[:row_count], -2),
            row_segs,
            jnp.where(has_after, after_note[:row_count], 1 << 20),
        ]
    )
    segs = jnp.pad(segs, ((0, 0), (0, -row_count % tile)), constant_values=-3)
    left_ids = jnp.where(has_before, before_note[row_count + rim :], -1)
    right_ids = jnp.where(has_after, after_note[row_count : row_count + rim], -1)
    id_rows = -(-(byte_count + rim) // tile) * tile
    id_line = jnp.concatenate(
        [
            jnp.full((tile - rim,), -1, jnp.int32),
            left_ids,
            ids,
            right_ids,
            jnp.full((id_rows - byte_count - rim,), -1, jnp.int32),
        ]
    ).reshape(-1, 1, tile)
    conv = jnp.pad(conv_kernel.astype(jnp.float32), ((0, 8 - conv_width), (0, 0)))
    score = score_weight.astype(jnp.float32)[None]
    gain_one = attn_gain[None]
    gain_two = ff_gain[None]

    special = special_mesh()
    half_pairs = width // tile // 2
    start, x_rows, mix, block_weight = gbst_forward(id_line, embed_table, conv, score, row_count)
    if special:
        start, square_second, tail_share = lax.optimization_barrier((start, square_second, tail_share))
        square_pieces = (square_first, square_second, square_third, swap(square_second, "core"))
        tail_first = swap(tail_share, "ws")
    first_in, queries, own_kv = project(place, start, gain_one, own_square, square_pieces)
    if special:
        own_kv, gate_first = lax.optimization_barrier((own_kv, gate_first))
        gate_second, gate_third = swap(gate_first, "dp"), swap(gate_first, "core")
    before_kv, after_kv = neighbours(own_kv, sequence_axes)
    near_state = attention_forward(segs, queries, (own_kv,), None, rel_bias, row_count)
    if special:
        near_state, tail_first = lax.optimization_barrier((near_state, tail_first))
        tail_second, tail_third = swap(tail_first, "dp"), swap(tail_first, "core")
        near_state, before_kv, after_kv, gate_second = lax.optimization_barrier(
            (near_state, before_kv, after_kv, gate_second)
        )
        gate_pieces = (gate_first, gate_second, gate_third, swap(gate_second, "core"))
    attended, log_norm = attention_forward(
        segs, queries, (before_kv, after_kv), near_state, rel_bias, row_count
    )
    if special:
        attended, tail_second = lax.optimization_barrier((attended, tail_second))
        tail_pieces = (tail_first, tail_second, tail_third, swap(tail_second, "core"))
    output, down_grad, gate_up_grad, gate_up_sent, d_middle, d_attended, out_grad, ff_gain_grad = feed_forward(
        place, order, bits, attended, start, cotangent[0], gain_two, own_feed, gate_pieces, tail_pieces
    )
    chains = []
    if special:
        gate_chain = Chain(gate_up_sent, gate_up_grad, ("core", "ws", "dp", "z"))
        tail_chain = Chain(
            jnp.concatenate([down_grad[1], out_grad[1]], axis=4),
            jnp.concatenate([down_grad[0], out_grad[0]], axis=4),
            ("core", "dp", "z", "ws"),
        )
        tail_chain.join()
        gate_chain.join()
        chains = [gate_chain, tail_chain]
    d_attended = hold(d_attended, chains)
    halves = []
    bias_parts = []
    for part in range(2):
        d_queries, d_before, d_own, d_after, bias_sums = attention_backward(
            segs, queries, d_attended, attended, before_kv, own_kv, after_kv, rel_bias,
            log_norm,            row_count, part * half_pairs, half_pairs,
        )
        if part == 0:
            d_attended, d_before, d_after = hold((d_attended, d_before, d_after))
        else:
            d_before, d_after = after((d_before, d_after), chains)
            for chain in chains:
                chain.join()
            d_before, d_after, halves = hold((d_before, d_after, halves), chains)
        from_after = lax.ppermute(
            d_before, sequence_axes, [(i + 1, i) for i in range(cycle_count - 1)]
        )
        from_before = lax.ppermute(
            d_after, sequence_axes, [(i, i + 1) for i in range(cycle_count - 1)]
        )
        halves.append((d_queries, d_own, from_after, from_before))
        bias_parts.append(jnp.transpose(bias_sums[: 2 * half_pairs, :bucket_count]))
    square_grads, projected = project_grads(
        bits, [part[i] for i in range(4) for part in halves], first_in, special
    )
    if special:
        square_chain = Chain(square_grads[1], square_grads[0], ("core", "ws", "dp", "z"))
        projected = after(projected, chains)
        for chain in chains:
            chain.join()
        projected = hold(projected, [square_chain] + chains)
    d_start, attn_gain_grad = project_back(
        place, projected, start, d_middle, gain_one, own_square, square_pieces
    )
    if special:
        d_start = after(d_start, [square_chain])
        square_chain.join()
        d_start = hold(d_start, [square_chain])
        chains = [square_chain, gate_chain, tail_chain]
    d_conv, left_grad, right_grad, conv_grad, score_grad = unpool(
        x_rows, mix, block_weight, d_start, conv, score, byte_count
    )
    bias_grad = jnp.concatenate(bias_parts, axis=1)
    bias_rows = jnp.pad(bias_grad.reshape(1, -1), ((0, 0), (0, width - bucket_count * head_count)))
    small = jnp.concatenate(
        [conv_grad, score_grad, attn_gain_grad, ff_gain_grad, bias_rows], axis=0
    )
    left_grad, right_grad = after((left_grad, right_grad), chains)
    for chain in chains:
        chain.join()
    if special:
        gate_part, tail_part = gate_chain.kept, tail_chain.kept
        left_grad, right_grad, small, gate_part, tail_part = hold(
            (left_grad, right_grad, small, gate_part, tail_part), [square_chain]
        )
        tail_sum = collect(tail_part)
        gate_part = gather_high(gate_part)
    from_right = lax.ppermute(
        left_grad, sequence_axes, [(i + 1, i) for i in range(cycle_count - 1)]
    )
    from_left = lax.ppermute(
        right_grad, sequence_axes, [(i, i + 1) for i in range(cycle_count - 1)]
    )
    byte_grad, embed_part = scatter_bytes(
        id_line, d_conv, conv, from_left, from_right, byte_count, embed.shape[0]
    )
    if special:
        rows = embed_part.shape[0] // 2
        columns = width // 2
        embed_part = after(embed_part, [square_chain])
        square_chain.join()
        small = small.reshape(-1, columns)
        core_rows = lax.dynamic_slice_in_dim(embed_part, bits[0] * rows, rows, 0)
        sent_rows = lax.dynamic_slice_in_dim(embed_part, (1 - bits[0]) * rows, rows, 0)
        sent = pack(sent_rows.reshape(2 * rows, columns), small)
        core_rows, small, sent, gate_part = hold((core_rows, small, sent, gate_part), [square_chain])
        received, small = unpack(swap(sent, "core"), small)
        embed_part = add(core_rows, received.reshape(rows, width))
        across = swap(gate_part, "dp")
        square_chain.join()
        square_part = square_chain.kept
        own_columns = lax.dynamic_slice_in_dim(embed_part, bits[1] * columns, columns, 1)
        sent_columns = lax.dynamic_slice_in_dim(embed_part, (1 - bits[1]) * columns, columns, 1)
        sent = pack(sent_columns, small)
        own_columns, small, sent, square_part, gate_part, across = hold(
            (own_columns, small, sent, square_part, gate_part, across)
        )
        received, small = unpack(swap(sent, "ws"), small)
        embed_part = add(own_columns, received)
        square_part = gather_high(square_part)
        gate_parts = (gate_part, across, swap(gate_part, "core"), swap(across, "core"))
        sent = pack(embed_part, small)
        embed_part, small, sent, gate_parts, square_part = hold(
            (embed_part, small, sent, gate_parts, square_part)
        )
        received, small = unpack(swap(sent, "dp"), small)
        embed_part = add(embed_part, received)
        square_across = swap(square_part, "dp")
        square_core = swap(square_part, "core")
        gate_sum, up_sum = finish(
            bits, gate_parts, ((columns, gate_parts[0].shape[3] * 8),) * 2, True
        )
        sent = pack(embed_part, small)
        embed_part, small, sent, square_across, square_core, gate_sum, up_sum = hold(
            (embed_part, small, sent, square_across, square_core, gate_sum, up_sum)
        )
        parts = [embed_part]
        for place in others:
            received, small = unpack(swap_high(sent, place), small)
            parts.append(received)
        embed_part = add(*parts)
        square_both = swap(square_across, "core")
        piece = width // 16
        down_sum, out_sum = finish_rows(tail_sum, (tail_sum.shape[2] - piece, piece))
        square_both, embed_part, small, down_sum, out_sum = hold(
            (square_both, embed_part, small, down_sum, out_sum)
        )
        embed_part = ordered(embed_part, swap(embed_part, "core"), bits[0], 0)
        query_sum, key_sum, value_sum = finish(
            bits, (square_part, square_across, square_core, square_both),
            ((columns, width),) * 3, False,
        )
        small = small.reshape(-1, width)
    else:
        small = lax.psum(small, all_axes)
        embed_part = lax.psum_scatter(embed_part, "ws", scatter_dimension=1, tiled=True)
        embed_part = lax.psum(embed_part, copy_axes)
    embed_sum = embed_part[: embed.shape[0]].astype(jnp.float32)
    if not special:
        gate_sum, up_sum = jnp.transpose(reduce_plain(gate_up_grad), (1, 2, 0, 3)).reshape(
            2, width // group_count, -1
        )
        down_sum, out_sum = reduce_plain(down_grad), reduce_plain(out_grad)
        query_sum, key_sum, value_sum = reduce_plain(square_grads)
    return (
        output[None],
        byte_grad[None],
        embed_sum,
        small[:conv_width],
        small[conv_width],
        small[conv_width + 1],
        query_sum,
        key_sum,
        value_sum,
        out_sum,
        small[conv_width + 3, : bucket_count * head_count].reshape(bucket_count, head_count),
        small[conv_width + 2],
        gate_sum,
        up_sum,
        down_sum,
    )


def solution(mesh):
    devices = mesh.devices
    fine = Mesh(devices.reshape((devices.shape[0] // 2, 2) + devices.shape[1:]), all_axes)
    rows = P(("dp", "ws"), sequence_axes)
    split = P("ws", None)
    in_specs = (
        rows, rows, P(None, "ws"), P(), P(), P(), split, split, split, split, P(), P(),
        split, split, split, P(("dp", "ws"), sequence_axes, None),
    )
    wide = P(("dp", "ws"), sequence_axes, None)
    out_specs = (
        wide, wide, P(None, "ws"), P(), P(), P(), split, split, split, split, P(), P(),
        split, split, split,
    )
    return jax.shard_map(
        per_device, mesh=fine, in_specs=in_specs, out_specs=out_specs, check_vma=False
    )
```

```python
import functools

import jax
import jax.numpy as jnp
from jax import lax
from jax.experimental import pallas as pl
from jax.experimental.pallas import tpu as pltpu
from jax.sharding import Mesh
from jax.sharding import PartitionSpec as P

thresholds = (12, 16, 23, 32, 46, 64, 91)
negative = -1e30
epsilon = 1e-06
conv_width = 5
tile = 128
near_bases = (-128, -120, 0, 120, 128)
class_count = len(near_bases) + 2


def bucket_of(relative):
    distance = jnp.abs(relative)
    far_bucket = 8 + sum(((distance >= threshold).astype(jnp.int32) for threshold in thresholds))
    near_bucket = jnp.where(distance < 8, distance, far_bucket)
    return near_bucket + 16 * (relative > 0).astype(jnp.int32)


def matmul(left, right, left_dim, right_dim):
    return lax.dot_general(
        left, right, (((left_dim,), (right_dim,)), ((), ())), preferred_element_type=jnp.float32
    )


def split_pair(values):
    high = values.astype(jnp.bfloat16)
    return high, (values - high.astype(jnp.float32)).astype(jnp.bfloat16)


def tile_class(query_tile, key_tile):
    step = key_tile - query_tile - 4
    own = jnp.where(
        step <= -2, 0, jnp.where(step == -1, 1, jnp.where(step == 0, 3, jnp.where(step == 1, 5, 6)))
    )
    before = jnp.where(step == -1, 2, 0)
    after = jnp.where(step == 1, 4, 6)
    return jnp.where(key_tile < 4, before, jnp.where(key_tile < 8, own, after))


def key_range(seg_ref, query_tile, row_count, tiles_per_block):
    first_seg = seg_ref[1, query_tile * tile]
    last_seg = seg_ref[1, jnp.minimum(query_tile * tile + tile, row_count) - 1]
    low = jnp.int32(0)
    high = jnp.int32(0)
    for block in range(3):
        for part in range(tiles_per_block):
            key_first = seg_ref[block, part * tile]
            key_last = seg_ref[block, min(part * tile + tile, row_count) - 1]
            low = low + (key_last < first_seg).astype(jnp.int32)
            high = high + (key_first <= last_seg).astype(jnp.int32)
    return low, high


def class_buckets(kind, shape, dim):
    place = lax.broadcasted_iota(jnp.int32, shape, dim)
    swing = jnp.where(place < tile, place, place - 2 * tile)
    if kind == 0:
        return jnp.full(shape, bucket_of(jnp.int32(-4 * tile)))
    if kind == class_count - 1:
        return jnp.full(shape, bucket_of(jnp.int32(4 * tile)))
    return bucket_of(near_bases[kind - 1] - swing)


def make_bias(rel_ref, bias_ref, first_pair, pair_count):
    bucket_count = rel_ref.shape[0]
    for kind in range(class_count):
        shape = (bucket_count, 2 * tile)
        hot = class_buckets(kind, shape, 1) == lax.broadcasted_iota(jnp.int32, shape, 0)
        lines = lax.dot_general(
            rel_ref[...], hot.astype(jnp.float32), (((0,), (0,)), ((), ())),
            precision=lax.Precision.HIGHEST, preferred_element_type=jnp.float32,
        )
        for pair in range(pair_count):
            for half in range(2):
                head = 2 * (first_pair + pair) + half
                grid = jnp.broadcast_to(lines[head : head + 1], (tile, 2 * tile))
                if 0 < kind < class_count - 1:
                    grid = pltpu.roll(grid, 0, 1, stride=1, stride_axis=0)
                bias_ref[kind, pair, :, half * tile : (half + 1) * tile] = grid[:, :tile]


def cost(microseconds):
    return pl.CostEstimate(
        flops=int(microseconds * 1e7), transcendentals=0, bytes_accessed=int(microseconds * 3e4)
    )


def stack_heads(block):
    lane = lax.broadcasted_iota(jnp.int32, block.shape, 1)
    zero = jnp.zeros_like(block)
    return jnp.concatenate(
        [jnp.where(lane < tile // 2, block, zero), jnp.where(lane < tile // 2, zero, block)], axis=0
    )


def fold_rows(values, combine):
    pieces = [values[8 * i : 8 * i + 8] for i in range(values.shape[0] // 8)]
    while len(pieces) > 1:
        joined = [combine(pieces[i], pieces[i + 1]) for i in range(0, len(pieces) - 1, 2)]
        if len(pieces) % 2:
            joined.append(pieces[-1])
        pieces = joined
    return pieces[0]


def key_columns(segs_ref, column_ref, key_tile):
    row = segs_ref[key_tile, 0:1, :]
    column_ref[key_tile] = jnp.transpose(jnp.broadcast_to(row, (tile, tile)))


def start_copies(sources, window_ref, sems, first_pair):
    rows, full_width = sources[0].shape
    width = window_ref.shape[1] // 2
    copies = []
    for i, source in enumerate(sources):
        for side in range(2):
            copies.append(
                pltpu.make_async_copy(
                    source.at[:, pl.ds(side * (full_width // 2) + first_pair * tile, width)],
                    window_ref.at[pl.ds(rows * i, rows), pl.ds(side * width, width)],
                    sems.at[2 * i + side],
                )
            )
    for copy in copies:
        copy.start()
    return copies


def forward_kernel(seg_ref, q_ref, *refs, row_count, near):
    if near:
        source_refs, refs = refs[:1], refs[1:]
    else:
        source_refs, refs = refs[:2], refs[2:]
        (mixed_in_ref, top_in_ref, total_in_ref), refs = refs[:3], refs[3:]
    segs_ref, qsegs_ref, rel_ref = refs[:3]
    if near:
        mixed_ref, top_ref, total_ref = refs[3:6]
    else:
        out_ref, lse_ref = refs[3:5]
    window_ref, bias_ref, column_ref, flipped_ref, score_ref = refs[-6 if near else -7 :][:5]
    sems = refs[-1]
    if not near:
        mixed_ref = refs[-2]
    width = q_ref.shape[1]
    pair_count = width // tile
    query_tiles = q_ref.shape[0] // tile
    half = tile // 2
    middle = query_tiles // 2
    copies = start_copies(source_refs, window_ref, sems, 0)
    make_bias(rel_ref, bias_ref, 0, pair_count)

    def key_span(query_tile):
        low, high = key_range(seg_ref, query_tile, row_count, query_tiles)
        if near:
            low = jnp.maximum(low - query_tiles, 0)
            high = jnp.minimum(high - query_tiles, query_tiles)
            return low // 2, (high + 1) // 2
        return jnp.minimum(low // 2, middle), jnp.maximum((high + 1) // 2 - middle, middle)

    def global_tile(key_pair, part):
        key_tile = 2 * key_pair + part
        if near:
            return key_tile + query_tiles
        return key_tile + jnp.where(key_pair >= middle, query_tiles, 0)

    first = key_span(0)[0]
    last = key_span(query_tiles - 1)[1]
    for copy in copies:
        copy.wait()

    def prepare(key_pair, carry):
        for part in range(2):
            row = segs_ref[global_tile(key_pair, part), 0:1, :]
            column_ref[2 * key_pair + part] = jnp.transpose(jnp.broadcast_to(row, (tile, tile)))
        at = pl.multiple_of(key_pair * 2 * tile, 2 * tile)
        flipped_ref[key_pair] = jnp.transpose(window_ref[pl.ds(at, 2 * tile), width:])
        return carry

    lax.fori_loop(first, last, prepare, 0)

    def query_step(query_tile, carry):
        low, high = key_span(query_tile)
        rows = pl.ds(pl.multiple_of(query_tile * tile, tile), tile)
        lanes = [slice(pair * tile, (pair + 1) * tile) for pair in range(pair_count)]
        stacked = [stack_heads(q_ref[rows, lane]) for lane in lanes]
        query_seg = qsegs_ref[query_tile, 0:1, :]
        slot = query_tile if near else 0

        def score_step(key_pair, tops):
            keys = pl.ds(pl.multiple_of(key_pair * 2 * tile, 2 * tile), 2 * tile)
            hides = []
            kinds = []
            for part in range(2):
                hide = jnp.where(column_ref[2 * key_pair + part] == query_seg, 0.0, negative)
                hides.append(jnp.concatenate([hide, hide], axis=1))
                kinds.append(tile_class(query_tile, global_tile(key_pair, part)))
            fresh = []
            for pair in range(pair_count):
                scores = matmul(window_ref[keys, lanes[pair]], stacked[pair], 1, 1)
                top = tops[pair]
                for part in range(2):
                    cut = slice(part * tile, (part + 1) * tile)
                    piece = scores[cut] + bias_ref[kinds[part], pair] + hides[part]
                    score_ref[key_pair, pair, cut] = piece
                    top = jnp.maximum(top, fold_rows(piece, jnp.maximum))
                fresh.append(top)
            return tuple(fresh)

        tops = lax.fori_loop(
            low, high, score_step,
            tuple(jnp.full((8, 2 * tile), negative, jnp.float32) for _ in range(pair_count)),
        )
        tops = [jnp.max(top, axis=0, keepdims=True) for top in tops]
        scales = []
        for pair in range(pair_count):
            if near:
                mixed_ref[slot, pair] = jnp.zeros((tile, tile), jnp.float32)
            else:
                before = top_in_ref[query_tile, pair : pair + 1, :]
                tops[pair] = jnp.maximum(tops[pair], before)
                scale = jnp.exp(before - tops[pair])
                scales.append(scale)
                mixed_ref[slot, pair, :half] = mixed_in_ref[query_tile, pair, :half] * scale[:, :tile]
                mixed_ref[slot, pair, half:] = mixed_in_ref[query_tile, pair, half:] * scale[:, tile:]

        def mix_step(key_pair, totals):
            fresh = []
            for pair in range(pair_count):
                exponent = jnp.exp(score_ref[key_pair, pair] - tops[pair])
                fresh.append(totals[pair] + fold_rows(exponent, jnp.add))
                mixed = matmul(
                    flipped_ref[key_pair, lanes[pair], :], exponent.astype(jnp.bfloat16), 1, 0
                )
                mixed_ref[slot, pair, :half] += mixed[:half, :tile]
                mixed_ref[slot, pair, half:] += mixed[half:, tile:]
            return tuple(fresh)

        totals = lax.fori_loop(
            low, high, mix_step,
            tuple(jnp.zeros((8, 2 * tile), jnp.float32) for _ in range(pair_count)),
        )
        for pair in range(pair_count):
            total = jnp.sum(totals[pair], axis=0, keepdims=True)
            if near:
                top_ref[query_tile, pair : pair + 1, :] = tops[pair]
                total_ref[query_tile, pair : pair + 1, :] = total
                continue
            total = total + total_in_ref[query_tile, pair : pair + 1, :] * scales[pair]
            lse_ref[query_tile, pair : pair + 1, :] = tops[pair] + jnp.log(total)
            inverse = 1.0 / total
            scaled = jnp.concatenate(
                [
                    mixed_ref[slot, pair, :half] * inverse[:, :tile],
                    mixed_ref[slot, pair, half:] * inverse[:, tile:],
                ],
                axis=0,
            )
            out_ref[rows, lanes[pair]] = jnp.transpose(scaled).astype(jnp.bfloat16)
        return carry

    lax.fori_loop(0, query_tiles, query_step, 0)


def backward_kernel(
    seg_ref, q_ref, do_ref, o_ref, before_ref, own_ref, after_ref, segs_ref, qsegs_ref, rel_ref, lse_ref,
    dq_ref, dbefore_ref, down_ref, dafter_ref, bias_out_ref,
    window_ref, bias_ref, column_ref, flipped_ref, dbias_ref, dwindow_ref, dq_acc_ref, delta_ref, sems,
    *, row_count, first_pair
):
    width = dq_ref.shape[1]
    pair_count = width // tile
    query_tiles = q_ref.shape[0] // tile
    block_rows = q_ref.shape[0]
    half = tile // 2
    copies = start_copies((before_ref, own_ref, after_ref), window_ref, sems, first_pair)
    make_bias(rel_ref, bias_ref, first_pair, pair_count)
    dwindow_ref[...] = jnp.zeros(dwindow_ref.shape, jnp.float32)
    dbias_ref[...] = jnp.zeros(dbias_ref.shape, jnp.float32)
    product = do_ref[...].astype(jnp.float32) * o_ref[...].astype(jnp.float32)
    product_high, product_low = split_pair(product)
    member = (
        lax.broadcasted_iota(jnp.int32, (16, width), 1) // half
        == lax.broadcasted_iota(jnp.int32, (16, width), 0)
    ).astype(jnp.bfloat16)
    delta_ref[...] = matmul(member, product_high, 1, 1) + matmul(member, product_low, 1, 1)
    first = key_range(seg_ref, 0, row_count, query_tiles)[0]
    last = key_range(seg_ref, query_tiles - 1, row_count, query_tiles)[1]
    for copy in copies:
        copy.wait()

    def prepare(key_pair, carry):
        for part in range(2):
            key_columns(segs_ref, column_ref, 2 * key_pair + part)
        at = pl.multiple_of(key_pair * 2 * tile, 2 * tile)
        flipped_ref[key_pair] = jnp.transpose(window_ref[pl.ds(at, 2 * tile), :width])
        return carry

    lax.fori_loop(first // 2, (last + 1) // 2, prepare, 0)

    def query_step(query_tile, carry):
        low, high = key_range(seg_ref, query_tile, row_count, query_tiles)
        at = pl.multiple_of(query_tile * tile, tile)
        rows = pl.ds(at, tile)
        lanes = [slice(pair * tile, (pair + 1) * tile) for pair in range(pair_count)]
        queries = [stack_heads(q_ref[rows, lane]) for lane in lanes]
        grads = [stack_heads(do_ref[rows, lane]) for lane in lanes]
        query_seg = qsegs_ref[query_tile, 0:1, :]
        deltas = [
            jnp.concatenate(
                [delta_ref[2 * pair : 2 * pair + 1, rows], delta_ref[2 * pair + 1 : 2 * pair + 2, rows]],
                axis=1,
            )
            for pair in range(pair_count)
        ]
        norms = [
            lse_ref[query_tile, first_pair + pair : first_pair + pair + 1, :]
            for pair in range(pair_count)
        ]
        for pair in range(pair_count):
            dq_acc_ref[pair] = jnp.zeros((tile, tile), jnp.float32)

        def key_step(key_pair, carry):
            keys = pl.ds(pl.multiple_of(key_pair * 2 * tile, 2 * tile), 2 * tile)
            hides = []
            kinds = []
            for part in range(2):
                key_tile = 2 * key_pair + part
                hide = jnp.where(column_ref[key_tile] == query_seg, 0.0, negative)
                hides.append(jnp.concatenate([hide, hide], axis=1))
                kinds.append(tile_class(query_tile, key_tile))
            for pair in range(pair_count):
                lane = lanes[pair]
                value_lane = slice(width + pair * tile, width + (pair + 1) * tile)
                scores = matmul(window_ref[keys, lane], queries[pair], 1, 1)
                dprobs = matmul(window_ref[keys, value_lane], grads[pair], 1, 1)
                probs_low, dscores_low = [], []
                for part in range(2):
                    cut = slice(part * tile, (part + 1) * tile)
                    probs = jnp.exp(
                        scores[cut] + bias_ref[kinds[part], pair] + hides[part] - norms[pair]
                    )
                    dscores = probs * (dprobs[cut] - deltas[pair])
                    dbias_ref[kinds[part], pair] += dscores
                    probs_low.append(probs.astype(jnp.bfloat16))
                    dscores_low.append(dscores.astype(jnp.bfloat16))
                probs_low = jnp.concatenate(probs_low, axis=0)
                dscores_low = jnp.concatenate(dscores_low, axis=0)
                dwindow_ref[keys, lane] += matmul(dscores_low, queries[pair], 1, 0)
                dwindow_ref[keys, value_lane] += matmul(probs_low, grads[pair], 1, 0)
                dquery = matmul(flipped_ref[key_pair, lane, :], dscores_low, 1, 0)
                dq_acc_ref[pair, :half] += dquery[:half, :tile]
                dq_acc_ref[pair, half:] += dquery[half:, tile:]
            return carry

        lax.fori_loop(low // 2, (high + 1) // 2, key_step, 0)
        for pair in range(pair_count):
            dq_ref[rows, lanes[pair]] = jnp.transpose(dq_acc_ref[pair]).astype(jnp.bfloat16)
        return carry

    lax.fori_loop(0, query_tiles, query_step, 0)
    dbefore_ref[...] = dwindow_ref[:block_rows].astype(jnp.bfloat16)
    down_ref[...] = dwindow_ref[block_rows : 2 * block_rows]
    dafter_ref[...] = dwindow_ref[2 * block_rows :].astype(jnp.bfloat16)
    turn = (
        lax.broadcasted_iota(jnp.int32, (tile, tile), 0)
        + lax.broadcasted_iota(jnp.int32, (tile, tile), 1)
        == tile - 1
    ).astype(jnp.bfloat16)
    zero_half = jnp.zeros((tile, tile), jnp.float32)
    bucket_count = rel_ref.shape[0]
    total = jnp.zeros(bias_out_ref.shape, jnp.float32)
    for kind in range(class_count):
        lines = []
        for pair in range(pair_count):
            grid = dbias_ref[kind, pair]
            near = 0 < kind < class_count - 1
            if near:
                grid_high, grid_low = split_pair(grid)
                grid = matmul(turn, grid_high, 1, 0) + matmul(turn, grid_low, 1, 0)
            for side in range(2):
                part = jnp.concatenate([grid[:, side * tile : (side + 1) * tile], zero_half], axis=1)
                if near:
                    part = pltpu.roll(part, tile + 1, 1, stride=1, stride_axis=0)
                lines.append(jnp.sum(fold_rows(part, jnp.add), axis=0, keepdims=True))
        lines.append(jnp.zeros((bias_out_ref.shape[0] - len(lines), 2 * tile), jnp.float32))
        shape = (2 * tile, tile)
        hot = class_buckets(kind, shape, 0) == lax.broadcasted_iota(jnp.int32, shape, 1)
        total = total + jnp.dot(
            jnp.concatenate(lines, axis=0), hot.astype(jnp.float32),
            precision=lax.Precision.HIGHEST, preferred_element_type=jnp.float32,
        )
    bias_out_ref[...] = total


def specs(count, space=pltpu.VMEM):
    return [pl.BlockSpec(memory_space=space) for _ in range(count)]


def attention_forward(segs, q, sources, state, rel_bias, row_count):
    rows, width = q.shape
    tiles = rows // tile
    pairs = width // tile
    near = state is None
    seg_rows = segs.reshape(3 * tiles, 1, tile)
    query_segs = mark_queries(segs, row_count).reshape(tiles, 1, tile)
    f32 = jnp.float32
    norm = jax.ShapeDtypeStruct((tiles, 8, 2 * tile), f32)
    mixed = jax.ShapeDtypeStruct((tiles, pairs, tile, tile), f32)
    count = len(sources)
    blocks = count * tiles // 2
    scratch = [
        pltpu.VMEM((count * rows, 2 * width), jnp.bfloat16),
        pltpu.VMEM((class_count, pairs, tile, 2 * tile), f32),
        pltpu.VMEM((count * tiles, tile, tile), jnp.int32),
        pltpu.VMEM((blocks, width, 2 * tile), jnp.bfloat16),
        pltpu.VMEM((blocks, pairs, 2 * tile, 2 * tile), f32),
    ]
    if not near:
        scratch.append(pltpu.VMEM((1, pairs, tile, tile), f32))
    return pl.pallas_call(
        functools.partial(forward_kernel, row_count=row_count, near=near),
        out_shape=(mixed, norm, norm)
        if near
        else (jax.ShapeDtypeStruct((rows, width), jnp.bfloat16), norm),
        in_specs=specs(1, pltpu.SMEM) + specs(1) + specs(count, pl.ANY)
        + specs(3 if near else 6),
        out_specs=tuple(specs(3 if near else 2)),
        scratch_shapes=scratch + [pltpu.SemaphoreType.DMA((2 * count,))],
        compiler_params=pltpu.CompilerParams(vmem_limit_bytes=(22 if near else 30) << 20),
        cost_estimate=cost(12),
        name="attention_near" if near else "attention_rim",
    )(segs, q, *sources, *(state or ()), seg_rows, query_segs, rel_bias)


def mark_queries(segs, row_count):
    place = jnp.arange(segs.shape[1], dtype=jnp.int32)
    return jnp.where(place < row_count, segs[1], -1)


def attention_backward(
    segs, q, do, o, before, own, after, rel_bias, lse, row_count, first_pair, pairs
):
    rows, full_width = q.shape
    tiles = rows // tile
    width = pairs * tile
    seg_rows = segs.reshape(3 * tiles, 1, tile)
    query_segs = mark_queries(segs, row_count).reshape(tiles, 1, tile)
    part = pl.BlockSpec((rows, width), lambda i: (0, first_pair // pairs))
    return pl.pallas_call(
        functools.partial(backward_kernel, row_count=row_count, first_pair=first_pair),
        grid=(1,),
        out_shape=(
            jax.ShapeDtypeStruct((rows, width), jnp.bfloat16),
            jax.ShapeDtypeStruct((rows, 2 * width), jnp.bfloat16),
            jax.ShapeDtypeStruct((rows, 2 * width), jnp.float32),
            jax.ShapeDtypeStruct((rows, 2 * width), jnp.bfloat16),
            jax.ShapeDtypeStruct((8, tile), jnp.float32),
        ),
        in_specs=specs(1, pltpu.SMEM) + [part, part, part] + specs(3, pl.ANY) + specs(4),
        out_specs=tuple(specs(5)),
        scratch_shapes=[
            pltpu.VMEM((3 * rows, 2 * width), jnp.bfloat16),
            pltpu.VMEM((class_count, pairs, tile, 2 * tile), jnp.float32),
            pltpu.VMEM((3 * tiles, tile, tile), jnp.int32),
            pltpu.VMEM((3 * tiles // 2, width, 2 * tile), jnp.bfloat16),
            pltpu.VMEM((class_count, pairs, tile, 2 * tile), jnp.float32),
            pltpu.VMEM((3 * rows, 2 * width), jnp.float32),
            pltpu.VMEM((pairs, tile, tile), jnp.float32),
            pltpu.VMEM((16, rows), jnp.float32),
            pltpu.SemaphoreType.DMA((6,)),
        ],
        compiler_params=pltpu.CompilerParams(vmem_limit_bytes=30 << 20),
        cost_estimate=cost(20),
        name="attention_backward",
    )(segs, q, do, o, before, own, after, seg_rows, query_segs, rel_bias, lse)


span = 96
id_pad = 128


def dot3(left, right, left_dim, right_dim):
    left_high, left_low = split_pair(left)
    right_high, right_low = split_pair(right)
    return (
        matmul(left_high, right_high, left_dim, right_dim)
        + matmul(left_low, right_high, left_dim, right_dim)
        + matmul(left_high, right_low, left_dim, right_dim)
    )


def block_means_grid(block_size):
    row = lax.broadcasted_iota(jnp.int32, (span, tile), 0)
    lane = lax.broadcasted_iota(jnp.int32, (span, tile), 1)
    same = (row // block_size == lane // block_size) & (lane < span)
    return jnp.where(same, 1.0 / block_size, 0.0)


def row_to_column(row):
    lane = lax.broadcasted_iota(jnp.int32, (span, tile), 1)
    place = lax.broadcasted_iota(jnp.int32, (span, tile), 0)
    return jnp.sum(jnp.where(lane == place, row, 0.0), axis=1, keepdims=True)


def column_to_row(column):
    lane = lax.broadcasted_iota(jnp.int32, (span, tile), 1)
    place = lax.broadcasted_iota(jnp.int32, (span, tile), 0)
    return jnp.sum(jnp.where(lane == place, column, 0.0), axis=0, keepdims=True)


def conv_tile(x_ref, conv_ref, base, lanes):
    taps = range(conv_width)
    return [
        sum(
            conv_ref[tap : tap + 1, i * tile : (i + 1) * tile]
            * x_ref[i, pl.ds(base + tap - conv_width // 2, span), :]
            for tap in taps
        )
        for i in range(lanes)
    ]


def gbst_forward_kernel(
    ids_ref, embed_ref, conv_ref, score_ref,
    start_ref, x_ref, mix_ref, weight_ref,
    table_ref, square_ref, wide_ref,
):
    vocab, width = embed_ref.shape
    lanes = width // tile
    id_tiles = ids_ref.shape[0]
    rows = start_ref.shape[0]
    table_ref[...] = jnp.zeros(table_ref.shape, jnp.bfloat16)
    table_ref[:vocab] = embed_ref[...]
    table_rows = table_ref.shape[0]
    rest = x_ref.shape[1] - id_tiles * tile
    for i in range(lanes):
        x_ref[i, id_tiles * tile :, :] = jnp.zeros((rest, tile), jnp.float32)

    def lookup(step, carry):
        ids = jnp.transpose(jnp.broadcast_to(ids_ref[step, 0:1, :], (tile, tile)))
        lane = lax.broadcasted_iota(jnp.int32, (tile, tile), 1)
        hot = jnp.concatenate(
            [(ids == lane + tile * i).astype(jnp.bfloat16) for i in range(table_rows // tile)], axis=1
        )
        found = matmul(hot, table_ref[...], 1, 0)
        at = pl.ds(pl.multiple_of(step * tile, tile), tile)
        for i in range(lanes):
            x_ref[i, at, :] = found[:, i * tile : (i + 1) * tile]
        return carry

    lax.fori_loop(0, id_tiles, lookup, 0)
    means = [block_means_grid(size) for size in (1, 2, 3, 4)]

    def pool(step, carry):
        base = pl.multiple_of(step * span, 8)
        conv = conv_tile(x_ref, conv_ref, base + id_pad, lanes)
        total = sum(conv[i] * score_ref[0:1, i * tile : (i + 1) * tile] for i in range(lanes))
        row = column_to_row(jnp.sum(total, axis=1, keepdims=True))
        scores = [jnp.sum(mean * row, axis=1, keepdims=True) for mean in means]
        top = functools.reduce(jnp.maximum, scores)
        exponents = [jnp.exp(score - top) for score in scores]
        inverse = 1.0 / sum(exponents)
        weights = [exponent * inverse for exponent in exponents]
        square_ref[...] = sum(weight * mean for weight, mean in zip(weights, means))
        mix = 0.5 * (
            square_ref[pl.ds(0, span // 2, stride=2), :] + square_ref[pl.ds(1, span // 2, stride=2), :]
        )
        half = pl.ds(pl.multiple_of(step * (span // 2), 8), span // 2)
        mix_ref[half, :] = mix
        lane = lax.broadcasted_iota(jnp.int32, (span, tile), 1)
        packed = jnp.zeros((span, tile), jnp.float32)
        for i in range(4):
            packed = jnp.where(lane == i, weights[i], packed)
        weight_ref[pl.ds(base, span), :] = packed
        wide_ref[half, :] = dot3(mix[:, :span], jnp.concatenate(conv, axis=1), 1, 0)
        return carry

    lax.fori_loop(0, mix_ref.shape[0] * 2 // span, pool, 0)
    start_ref[...] = wide_ref[:rows]


def gbst_forward(ids, embed, conv, score, row_count):
    vocab, width = embed.shape
    rows = -(-row_count // tile) * tile
    steps = -(-2 * row_count // span)
    x_rows = max(ids.shape[0] * tile, id_pad + steps * span) + 8
    f32 = jnp.float32
    return pl.pallas_call(
        gbst_forward_kernel,
        out_shape=(
            jax.ShapeDtypeStruct((rows, width), f32),
            jax.ShapeDtypeStruct((width // tile, x_rows, tile), f32),
            jax.ShapeDtypeStruct((steps * span // 2, tile), f32),
            jax.ShapeDtypeStruct((steps * span, tile), f32),
        ),
        in_specs=specs(4),
        out_specs=tuple(specs(4)),
        scratch_shapes=[
            pltpu.VMEM((-(-vocab // tile) * tile, width), jnp.bfloat16),
            pltpu.VMEM((span, tile), f32),
            pltpu.VMEM((steps * span // 2, width), f32),
        ],
        compiler_params=pltpu.CompilerParams(vmem_limit_bytes=18 << 20),
        cost_estimate=cost(12),
        name="gbst_forward",
    )(ids, embed, conv, score)


def weight_copies(place_ref, parts, pieces, full_ref, sems):
    copies = []
    rows = parts[0].shape[0]
    for i, part in enumerate(parts):
        at = pl.multiple_of(place_ref[0] * rows, rows)
        copies.append(
            pltpu.make_async_copy(part, full_ref.at[i, pl.ds(at, rows)], sems.at[len(copies)])
        )
    for number, piece in enumerate(pieces):
        share = piece.shape[1]
        at = pl.multiple_of((1 - place_ref[0]) * rows + place_ref[1 + number] * share, share)
        copies.append(
            pltpu.make_async_copy(piece, full_ref.at[:, pl.ds(at, share)], sems.at[len(copies)])
        )
    for copy in copies:
        copy.start()
    return copies


def project_kernel(place_ref, start_ref, gain_ref, *refs):
    pieces = refs[3:-5]
    first_ref, q_ref, kv_ref, weight_ref, sems = refs[-5:]
    copies = weight_copies(place_ref, refs[:3], pieces, weight_ref, sems)
    width = q_ref.shape[1]
    start = start_ref[...]
    inverse = lax.rsqrt(jnp.mean(start * start, axis=-1, keepdims=True) + epsilon)
    first = (start * inverse * gain_ref[...]).astype(jnp.bfloat16)
    first_ref[...] = first
    for copy in copies:
        copy.wait()
    q_ref[...] = matmul(first, weight_ref[0], 1, 0).astype(jnp.bfloat16)
    kv_ref[:, :width] = matmul(first, weight_ref[1], 1, 0).astype(jnp.bfloat16)
    kv_ref[:, width:] = matmul(first, weight_ref[2], 1, 0).astype(jnp.bfloat16)


def project(place, start, gain, own, pieces):
    rows, width = start.shape
    b16 = jnp.bfloat16
    return pl.pallas_call(
        project_kernel,
        out_shape=(
            jax.ShapeDtypeStruct((rows, width), b16),
            jax.ShapeDtypeStruct((rows, width), b16),
            jax.ShapeDtypeStruct((rows, 2 * width), b16),
        ),
        in_specs=specs(1, pltpu.SMEM) + specs(2) + specs(3 + len(pieces), pl.ANY),
        out_specs=tuple(specs(3)),
        scratch_shapes=[
            pltpu.VMEM((3, width, width), b16),
            pltpu.SemaphoreType.DMA((3 + len(pieces),)),
        ],
        compiler_params=pltpu.CompilerParams(vmem_limit_bytes=60 << 20),
        cost_estimate=cost(6),
        name="project",
    )(place, start, gain, *own, *pieces)


def feed_kernel(
    place_ref, order_ref, bits_ref, mixed_ref, start_ref, cot_ref, gain_ref, *refs, piece_count, tail_count
):
    (wo_ref, wg_ref, wu_ref, wd_ref), refs = refs[:4], refs[4:]
    gate_pieces, refs = refs[:piece_count], refs[piece_count:]
    tail_pieces, refs = refs[:tail_count], refs[tail_count:]
    (
        out_ref, downg_ref, gateup_ref, extra_ref, dmid_ref, dmixed_ref, outg_ref, gaing_ref,
        second_ref, turned_ref, middle_ref, scale_ref, total_ref, dsecond_ref, grad_ref,
        fullo_ref, fullg_ref, fullu_ref, fulld_ref,
    ) = refs
    step = pl.program_id(0)
    last = pl.num_programs(0) - 1
    row_count = out_ref.shape[0]
    chunk = fulld_ref.shape[0]

    def fill(full_ref, own_ref, pieces, pick, base=1):
        rows = own_ref.shape[0]
        full_ref[pl.ds(pl.multiple_of(place_ref[0] * rows, rows), rows), :] = own_ref[...]
        for number, piece in enumerate(pieces):
            block = pick(piece)
            share = block.shape[0]
            at = (1 - place_ref[0]) * rows + place_ref[base + number] * share
            full_ref[pl.ds(pl.multiple_of(at, share), share), :] = block

    @pl.when(step == 0)
    def _():
        fill(fullo_ref, wo_ref, tail_pieces, lambda piece: piece[2 * chunk :], 5)
        middle = start_ref[...] + matmul(mixed_ref[...], fullo_ref[...], 1, 0)
        middle_ref[...] = middle
        inverse = lax.rsqrt(jnp.mean(middle * middle, axis=-1, keepdims=True) + epsilon)
        scale_ref[...] = jnp.broadcast_to(inverse, scale_ref.shape)
        second = (middle * inverse * gain_ref[...]).astype(jnp.bfloat16)
        second_ref[...] = second
        turned_ref[...] = jnp.transpose(second)
        total_ref[...] = jnp.zeros(total_ref.shape, jnp.float32)
        dsecond_ref[...] = jnp.zeros(dsecond_ref.shape, jnp.float32)
        grad_ref[:row_count] = cot_ref[...]
        grad_ref[row_count:] = jnp.zeros((grad_ref.shape[0] - row_count, grad_ref.shape[1]), jnp.bfloat16)

    fill(fullg_ref, wg_ref, gate_pieces, lambda piece: piece[0])
    fill(fullu_ref, wu_ref, gate_pieces, lambda piece: piece[1])
    own_steps = pl.num_programs(0) - piece_count

    @pl.when(step < own_steps)
    def _():
        fulld_ref[...] = wd_ref[...]

    for number in range(tail_count):

        @pl.when((step >= own_steps) & ((step - own_steps) >> 1 == number))
        def _():
            at = pl.multiple_of((order_ref[step] & 1) * chunk, chunk)
            fulld_ref[...] = tail_pieces[number][pl.ds(at, chunk), :]

    second = second_ref[...]
    cot = grad_ref[...]
    gate = matmul(second, fullg_ref[...], 1, 0)
    up = matmul(second, fullu_ref[...], 1, 0)
    dhidden = matmul(cot, fulld_ref[...], 1, 1)
    root = 0.7978845608028654
    square = gate * gate
    bend = jnp.tanh(root * (gate + 0.044715 * (square * gate)))
    rise = 0.5 * (1.0 + bend)
    gelu = gate * rise
    slope = rise + 0.5 * gate * (1.0 - bend * bend) * (root * (1.0 + 3 * 0.044715 * square))
    hidden = (gelu * up).astype(jnp.bfloat16)
    dgate = (dhidden * up * slope).astype(jnp.bfloat16)
    dup = (dhidden * gelu).astype(jnp.bfloat16)
    total_ref[...] += matmul(hidden, fulld_ref[...], 1, 0)
    downg = matmul(jnp.transpose(hidden), cot, 1, 0).astype(jnp.bfloat16)
    gateg = matmul(turned_ref[...], dgate, 1, 0).astype(jnp.bfloat16)
    upg = matmul(turned_ref[...], dup, 1, 0).astype(jnp.bfloat16)
    side = downg.shape[1] // 2
    if piece_count:
        bit_core, bit_ws, bit_dp = bits_ref[0], bits_ref[1], bits_ref[2]
        number = order_ref[step]
        low, high = (number & 1) ^ bits_ref[3], ((number >> 1) & 1) ^ bits_ref[4]
        straight = bit_core == 0
        first_rows, second_rows = downg[: chunk // 2], downg[chunk // 2 :]
        kept = jnp.where(straight, first_rows, second_rows)
        sent = jnp.where(straight, second_rows, first_rows)
        for second in range(2):
            cut = slice(second * side, (second + 1) * side)
            place = (second ^ bit_dp, (number >> 2) ^ bit_ws, low, high, slice(0, chunk // 2))
            downg_ref[place] = kept[:, cut]
            outg_ref[place] = sent[:, cut]

        def store_gate(target_ref):
            for first in range(2):
                rows = slice(first * side, (first + 1) * side)
                target_ref[first ^ bit_ws, 0 ^ bit_dp, 0, 0] = gateg[rows]
                target_ref[first ^ bit_ws, 1 ^ bit_dp, 0, 0] = upg[rows]

        turn = jnp.where(step < own_steps, step >> 1, step & 1) & 1

        @pl.when(turn == 0)
        def _():
            store_gate(gateup_ref)

        @pl.when(turn == 1)
        def _():
            store_gate(extra_ref)

    else:
        downg_ref[...] = downg
        extra_ref[...] = jnp.zeros(extra_ref.shape, jnp.bfloat16)
        gateup_ref[0, 0] = gateg
        gateup_ref[0, 1] = upg
    dsecond_ref[...] += matmul(dgate, fullg_ref[...], 1, 1) + matmul(dup, fullu_ref[...], 1, 1)

    @pl.when(step == last)
    def _():
        middle = middle_ref[...]
        inverse = scale_ref[:, 0:1]
        out_ref[...] = (middle + total_ref[...])[:row_count].astype(jnp.bfloat16)
        normed = middle * inverse
        dsecond = dsecond_ref[...]
        gaing_ref[...] = jnp.sum(dsecond * normed, axis=0, keepdims=True)
        dnormed = dsecond * gain_ref[...]
        dmid = grad_ref[...].astype(jnp.float32) + inverse * (
            dnormed - normed * jnp.mean(dnormed * normed, axis=-1, keepdims=True)
        )
        dmid_ref[...] = dmid
        dbranch = dmid.astype(jnp.bfloat16)
        dmixed_ref[...] = matmul(dbranch, fullo_ref[...], 1, 1).astype(jnp.bfloat16)
        outg = matmul(jnp.transpose(mixed_ref[...]), dbranch, 1, 0).astype(jnp.bfloat16)
        if piece_count:
            store_relative(downg_ref, outg_ref, outg, bits_ref, chunk // 2, True)
        else:
            outg_ref[...] = outg


def store_relative(kept_ref, sent_ref, grad, bits_ref, at, dp_first):
    rows = grad.shape[0] // 16
    width = grad.shape[1] // 2
    bits = [bits_ref[i] for i in range(5)]
    straight = bits[0] == 0
    for number in range(8):
        group, high, low = number >> 2, (number >> 1) & 1, number & 1
        first = grad[2 * number * rows : (2 * number + 1) * rows]
        second = grad[(2 * number + 1) * rows : (2 * number + 2) * rows]
        kept = jnp.where(straight, first, second)
        sent = jnp.where(straight, second, first)
        for side in range(2):
            pair = (side ^ bits[2], group ^ bits[1])
            pair = pair if dp_first else pair[::-1]
            place = pair + (low ^ bits[3], high ^ bits[4], slice(at, at + rows))
            cut = slice(side * width, (side + 1) * width)
            kept_ref[place] = kept[:, cut]
            sent_ref[place] = sent[:, cut]


def feed_forward(place, order, bits, mixed, start, cot, gain, own, gate_pieces, tail_pieces):
    rows, width = start.shape
    row_count = cot.shape[0]
    wo, wg, wu, wd = own
    hidden = wg.shape[1]
    steps = order.shape[0]
    chunk = hidden // steps
    count = len(gate_pieces)
    own_blocks = wd.shape[0] // chunk
    f32, b16 = jnp.float32, jnp.bfloat16

    def whole(array):
        return pl.BlockSpec(array.shape, lambda f, *refs: (0,) * len(array.shape))

    def columns(array):
        if array.ndim == 3:
            shape = array.shape[:2] + (chunk,)
            return pl.BlockSpec(shape, lambda f, place, order, bits: (0, 0, order[f]))
        return pl.BlockSpec((array.shape[0], chunk), lambda f, place, order, bits: (0, order[f]))

    if count:
        gate_shape = (2,) * 4 + (width // 2, chunk)
        tail_shape = (2,) * 4 + (chunk // 2 + width // 16, width // 2)
        grad_shapes = (tail_shape, gate_shape, gate_shape)
        out_grad_shape = tail_shape

        def gate_spec(steps_of):
            def index(f, place, order, bits):
                held = jnp.int32(steps_of[-1])
                for number in range(len(steps_of) - 2, -1, -1):
                    held = jnp.where(f <= number, steps_of[number], held)
                chosen = order[held]
                return 0, 0, ((chosen >> 1) & 1) ^ bits[3], (chosen >> 2) ^ bits[4], 0, 0

            return pl.BlockSpec((2, 2, 1, 1, width // 2, chunk), index)

        grad_specs = [
            pl.BlockSpec(tail_shape, lambda f, *refs: (0,) * len(tail_shape)),
            gate_spec((0, 1, 1, 1, 4, 4, 6, 6)),
            gate_spec((2, 2, 2, 3, 3, 5, 5, 7)),
        ]
    else:
        grad_shapes = ((hidden, width), (steps, 2, width, chunk), (8, tile))
        out_grad_shape = (width, width)
        grad_specs = [
            pl.BlockSpec((chunk, width), lambda f, place, order, bits: (order[f], 0)),
            pl.BlockSpec((1, 2, width, chunk), lambda f, place, order, bits: (order[f], 0, 0, 0)),
            pl.BlockSpec((8, tile), lambda f, place, order, bits: (0, 0)),
        ]
    shapes = (
        jax.ShapeDtypeStruct((row_count, width), b16),
        jax.ShapeDtypeStruct(grad_shapes[0], b16),
        jax.ShapeDtypeStruct(grad_shapes[1], b16),
        jax.ShapeDtypeStruct(grad_shapes[2], b16),
        jax.ShapeDtypeStruct((rows, width), f32),
        jax.ShapeDtypeStruct((rows, width), b16),
        jax.ShapeDtypeStruct(out_grad_shape, b16),
        jax.ShapeDtypeStruct((1, width), f32),
    )
    return pl.pallas_call(
        functools.partial(feed_kernel, piece_count=count, tail_count=len(tail_pieces)),
        out_shape=shapes,
        grid_spec=pltpu.PrefetchScalarGridSpec(
            num_scalar_prefetch=3,
            grid=(steps,),
            in_specs=[whole(mixed), whole(start), whole(cot), whole(gain), whole(wo)]
            + [
                columns(wg), columns(wu),
                pl.BlockSpec(
                    (chunk, width),
                    lambda f, place, order, bits: (
                        order[jnp.minimum(f, own_blocks - 1)] & (own_blocks - 1), 0
                    ),
                ),
            ]
            + [columns(piece) for piece in gate_pieces]
            + [whole(piece) for piece in tail_pieces],
            out_specs=(
                whole(shapes[0]),
                *grad_specs,
                whole(shapes[4]), whole(shapes[5]), whole(shapes[6]), whole(shapes[7]),
            ),
            scratch_shapes=[
                pltpu.VMEM((rows, width), b16),
                pltpu.VMEM((width, rows), b16),
                pltpu.VMEM((rows, width), f32),
                pltpu.VMEM((rows, tile), f32),
                pltpu.VMEM((rows, width), f32),
                pltpu.VMEM((rows, width), f32),
                pltpu.VMEM((rows, width), b16),
                pltpu.VMEM((width, width), b16),
                pltpu.VMEM((width, chunk), b16),
                pltpu.VMEM((width, chunk), b16),
                pltpu.VMEM((chunk, width), b16),
            ],
        ),
        compiler_params=pltpu.CompilerParams(vmem_limit_bytes=46 << 20),
        cost_estimate=cost(26),
        name="feed_forward",
    )(place, order, bits, mixed, start, cot, gain, *own, *gate_pieces, *tail_pieces)


def project_back_kernel(
    place_ref, bits_ref, dq0_ref, dq1_ref, own0_ref, own1_ref, after0_ref, after1_ref, before0_ref,
    before1_ref, first_ref, start_ref, dmid_ref, gain_ref, *refs
):
    pieces = refs[3:-6]
    grads_ref, sent_ref, dstart_ref, gaing_ref, weight_ref, sems = refs[-6:]
    copies = weight_copies(place_ref, refs[:3], pieces, weight_ref, sems)
    width = first_ref.shape[1]
    half = width // 2

    def total(own_ref, after_ref, before_ref):
        return (
            own_ref[...] + after_ref[...].astype(jnp.float32) + before_ref[...].astype(jnp.float32)
        ).astype(jnp.bfloat16)

    sides = (total(own0_ref, after0_ref, before0_ref), total(own1_ref, after1_ref, before1_ref))
    grads = (
        jnp.concatenate([dq0_ref[...], dq1_ref[...]], axis=1),
        jnp.concatenate([side[:, :half] for side in sides], axis=1),
        jnp.concatenate([side[:, half:] for side in sides], axis=1),
    )
    turned = jnp.transpose(first_ref[...])
    for i, grad in enumerate(grads):
        product = matmul(turned, grad, 1, 0).astype(jnp.bfloat16)
        if pieces:
            store_relative(grads_ref, sent_ref, product, bits_ref, i * (width // 16), False)
        else:
            grads_ref[i] = product
    if not pieces:
        sent_ref[...] = jnp.zeros(sent_ref.shape, jnp.bfloat16)
    start = start_ref[...]
    inverse = lax.rsqrt(jnp.mean(start * start, axis=-1, keepdims=True) + epsilon)
    normed = start * inverse
    for copy in copies:
        copy.wait()
    dfirst = sum(matmul(grad, weight_ref[i], 1, 1) for i, grad in enumerate(grads))
    gaing_ref[...] = jnp.sum(dfirst * normed, axis=0, keepdims=True)
    dnormed = dfirst * gain_ref[...]
    dstart_ref[...] = dmid_ref[...] + inverse * (
        dnormed - normed * jnp.mean(dnormed * normed, axis=-1, keepdims=True)
    )


def project_back(place, bits, halves, first, start, dmid, gain, own, pieces):
    rows, width = first.shape
    shape = (2,) * 4 + (3 * (width // 16), width // 2) if pieces else (3, width, width)
    return pl.pallas_call(
        project_back_kernel,
        out_shape=(
            jax.ShapeDtypeStruct(shape, jnp.bfloat16),
            jax.ShapeDtypeStruct(shape if pieces else (8, tile), jnp.bfloat16),
            jax.ShapeDtypeStruct((rows, width), jnp.float32),
            jax.ShapeDtypeStruct((1, width), jnp.float32),
        ),
        in_specs=specs(2, pltpu.SMEM) + specs(12) + specs(3 + len(pieces), pl.ANY),
        out_specs=tuple(specs(4)),
        scratch_shapes=[
            pltpu.VMEM((3, width, width), jnp.bfloat16),
            pltpu.SemaphoreType.DMA((3 + len(pieces),)),
        ],
        compiler_params=pltpu.CompilerParams(vmem_limit_bytes=26 << 20),
        cost_estimate=cost(10),
        name="project_back",
    )(place, bits, *halves, first, start, dmid, gain, *own, *pieces)


def unpool_kernel(
    x_ref, mix_ref, weight_ref, dstart_ref, conv_ref, score_ref,
    dconv_ref, left_ref, right_ref, convg_ref, scoreg_ref,
    wide_ref, square_ref, sums_ref, *, byte_count
):
    lanes = x_ref.shape[0]
    width = lanes * tile
    rows = dstart_ref.shape[0]
    steps = mix_ref.shape[0] * 2 // span
    lead = id_pad + 8
    wide_ref[:rows] = dstart_ref[...]
    wide_ref[rows:] = jnp.zeros((wide_ref.shape[0] - rows, width), jnp.float32)
    for i in range(lanes):
        dconv_ref[i, :lead] = jnp.zeros((lead, tile), jnp.float32)
    sums_ref[...] = jnp.zeros(sums_ref.shape, jnp.float32)
    means = [block_means_grid(size) for size in (1, 2, 3, 4)]

    def unpool(step, carry):
        base = pl.multiple_of(step * span, 8)
        half = pl.ds(pl.multiple_of(step * (span // 2), 8), span // 2)
        conv = jnp.concatenate(conv_tile(x_ref, conv_ref, base + id_pad, lanes), axis=1)
        dstart = wide_ref[half, :]
        dstart_high, dstart_low = split_pair(dstart)
        conv_high, conv_low = split_pair(conv)
        inner = (
            matmul(dstart_high, conv_high, 1, 1)
            + matmul(dstart_low, conv_high, 1, 1)
            + matmul(dstart_high, conv_low, 1, 1)
        )
        inner = jnp.concatenate([inner, jnp.zeros((span // 2, tile - span), jnp.float32)], axis=1)
        square_ref[pl.ds(0, span // 2, stride=2), :] = inner
        square_ref[pl.ds(1, span // 2, stride=2), :] = inner
        inner = square_ref[...]
        weights = [weight_ref[pl.ds(base, span), i : i + 1] for i in range(4)]
        dweights = [0.5 * jnp.sum(mean * inner, axis=1, keepdims=True) for mean in means]
        common = sum(weight * dweight for weight, dweight in zip(weights, dweights))
        dscores = [weight * (dweight - common) for weight, dweight in zip(weights, dweights)]
        row = jnp.sum(
            sum(dscore * mean for dscore, mean in zip(dscores, means)), axis=0, keepdims=True
        )
        column = row_to_column(row)
        mix_high, mix_low = split_pair(mix_ref[half, :][:, :span])
        dconv = (
            matmul(mix_high, dstart_high, 0, 0)
            + matmul(mix_low, dstart_high, 0, 0)
            + matmul(mix_high, dstart_low, 0, 0)
            + column * score_ref[...]
        )
        for i in range(lanes):
            part = dconv[:, i * tile : (i + 1) * tile]
            dconv_ref[i, pl.ds(base + lead, span), :] = part
            for tap in range(conv_width):
                moved = x_ref[i, pl.ds(base + id_pad + tap - conv_width // 2, span), :]
                sums_ref[tap, :, i * tile : (i + 1) * tile] += fold_rows(part * moved, jnp.add)
        sums_ref[conv_width] += fold_rows(column * conv, jnp.add)
        return carry

    lax.fori_loop(0, steps, unpool, 0)
    for tap in range(conv_width):
        convg_ref[tap : tap + 1, :] = jnp.sum(sums_ref[tap], axis=0, keepdims=True)
    scoreg_ref[...] = jnp.sum(sums_ref[conv_width], axis=0, keepdims=True)
    left_ref[...] = spread(dconv_ref, conv_ref, lead - 8, 8)
    right_ref[...] = spread(dconv_ref, conv_ref, lead + byte_count, 8)


def spread(dconv_ref, conv_ref, base, count):
    lanes = dconv_ref.shape[0]
    parts = [
        sum(
            conv_ref[tap : tap + 1, i * tile : (i + 1) * tile]
            * dconv_ref[i, pl.ds(base + conv_width // 2 - tap, count), :]
            for tap in range(conv_width)
        )
        for i in range(lanes)
    ]
    return jnp.concatenate(parts, axis=1)


def unpool(x, mix, weight, dstart, conv, score, byte_count):
    lanes = x.shape[0]
    width = lanes * tile
    f32 = jnp.float32
    half_rows = mix.shape[0]
    return pl.pallas_call(
        functools.partial(unpool_kernel, byte_count=byte_count),
        out_shape=(
            jax.ShapeDtypeStruct((lanes, 2 * half_rows + id_pad + 8, tile), f32),
            jax.ShapeDtypeStruct((8, width), f32),
            jax.ShapeDtypeStruct((8, width), f32),
            jax.ShapeDtypeStruct((conv_width, width), f32),
            jax.ShapeDtypeStruct((1, width), f32),
        ),
        in_specs=specs(6),
        out_specs=tuple(specs(5)),
        scratch_shapes=[
            pltpu.VMEM((half_rows, width), f32),
            pltpu.VMEM((span, tile), f32),
            pltpu.VMEM((conv_width + 1, 8, width), f32),
        ],
        compiler_params=pltpu.CompilerParams(vmem_limit_bytes=20 << 20),
        cost_estimate=cost(13),
        name="unpool",
    )(x, mix, weight, dstart, conv, score)


def scatter_kernel(ids_ref, dconv_ref, conv_ref, byteg_ref, embedg_ref, total_ref):
    byte_count = byteg_ref.shape[0]
    total_ref[...] = jnp.zeros(total_ref.shape, jnp.float32)

    def scatter(step):
        grads = spread(dconv_ref, conv_ref, step * tile + 8, tile)
        ids = ids_ref[step, 0:1, :]
        place = lax.broadcasted_iota(jnp.int32, (total_ref.shape[0], tile), 0)
        hot = (place == ids).astype(jnp.bfloat16)
        grads_high, grads_low = split_pair(grads)
        total_ref[...] += matmul(hot, grads_high, 1, 0) + matmul(hot, grads_low, 1, 0)
        return grads

    scatter(0)

    def whole_tile(step, carry):
        byteg_ref[pl.ds(pl.multiple_of((step - 1) * tile, tile), tile), :] = scatter(step)
        return carry

    full = byte_count // tile
    lax.fori_loop(1, full + 1, whole_tile, 0)
    byteg_ref[full * tile :, :] = scatter(full + 1)[: byte_count - full * tile]
    embedg_ref[...] = total_ref[...].astype(jnp.bfloat16)


def scatter_bytes(ids, dconv, conv, byte_count, vocab):
    width = conv.shape[1]
    table_rows = -(-vocab // 32) * 32
    return pl.pallas_call(
        scatter_kernel,
        out_shape=(
            jax.ShapeDtypeStruct((byte_count, width), jnp.float32),
            jax.ShapeDtypeStruct((table_rows, width), jnp.bfloat16),
        ),
        in_specs=specs(3),
        out_specs=tuple(specs(2)),
        scratch_shapes=[pltpu.VMEM((table_rows, width), jnp.float32)],
        compiler_params=pltpu.CompilerParams(vmem_limit_bytes=16 << 20),
        cost_estimate=cost(10),
        name="scatter_bytes",
    )(ids, dconv, conv)


def edge_kernel(bytes_ref, left_ref, right_ref, out_ref, edge_ref, sems):
    places = (pl.ds(0, 8), pl.ds(out_ref.shape[0] - 8, 8))
    loads = [
        pltpu.make_async_copy(bytes_ref.at[place], edge_ref.at[i], sems.at[i])
        for i, place in enumerate(places)
    ]
    for load in loads:
        load.start()
    for load in loads:
        load.wait()
    edge_ref[0] += left_ref[...]
    edge_ref[1] += right_ref[...]
    stores = [
        pltpu.make_async_copy(edge_ref.at[i], out_ref.at[place], sems.at[i])
        for i, place in enumerate(places)
    ]
    for store in stores:
        store.start()
    for store in stores:
        store.wait()


def add_edges(grads, left, right):
    return pl.pallas_call(
        edge_kernel,
        out_shape=jax.ShapeDtypeStruct(grads.shape, grads.dtype),
        in_specs=specs(1, pl.ANY) + specs(2),
        out_specs=specs(1, pl.ANY)[0],
        scratch_shapes=[
            pltpu.VMEM((2, 8, grads.shape[1]), jnp.float32),
            pltpu.SemaphoreType.DMA((2,)),
        ],
        input_output_aliases={0: 0},
        cost_estimate=cost(1),
        name="add_edges",
    )(grads, left, right)


def finish_kernel(bits_ref, near_ref, across_ref, core_ref, both_ref, *out_refs):
    flip = bits_ref[2] == 0
    for number in range(8):
        high, low, core = number >> 2, (number >> 1) & 1, number & 1
        place = (low ^ bits_ref[3], high ^ bits_ref[4])
        same = (core ^ bits_ref[0]) == 0
        near = jnp.where(same, near_ref[place], core_ref[place]).astype(jnp.float32)
        across = jnp.where(same, across_ref[place], both_ref[place]).astype(jnp.float32)
        first, second = jnp.where(flip, near, across), jnp.where(flip, across, near)
        half = first.shape[1]
        at = 0
        for out_ref in out_refs:
            rows = out_ref.shape[0] // 8
            out_ref[number * rows : (number + 1) * rows, :half] = first[at : at + rows]
            out_ref[number * rows : (number + 1) * rows, half:] = second[at : at + rows]
            at += rows


def finish_square(bits, parts, shapes):
    return pl.pallas_call(
        finish_kernel,
        out_shape=tuple(jax.ShapeDtypeStruct(shape, jnp.float32) for shape in shapes),
        in_specs=specs(1, pltpu.SMEM) + specs(4),
        out_specs=tuple(specs(len(shapes))),
        compiler_params=pltpu.CompilerParams(vmem_limit_bytes=20 << 20),
        cost_estimate=cost(3),
        name="finish_square",
    )(bits, *parts)


def finish_feed_kernel(sum_ref, gate_ref, up_ref, down_ref, out_ref):
    gate_rows = gate_ref.shape[0]
    chunk = gate_ref.shape[1] // 8
    down_rows, out_rows = down_ref.shape[0] // 8, out_ref.shape[0] // 8
    half = down_ref.shape[1] // 2
    for number in range(8):
        at = 0
        for strip in range(chunk // tile):
            cut = slice(number * chunk + strip * tile, number * chunk + (strip + 1) * tile)
            gate_ref[:, cut] = sum_ref[number, 0, at : at + gate_rows].astype(jnp.float32)
            up_ref[:, cut] = sum_ref[number, 1, at : at + gate_rows].astype(jnp.float32)
            at += gate_rows
        for strip in range(half // tile):
            for side in range(2):
                cut = slice(side * half + strip * tile, side * half + (strip + 1) * tile)
                middle = at + down_rows
                down = sum_ref[number, side, at:middle]
                out = sum_ref[number, side, middle : middle + out_rows]
                down_ref[number * down_rows : (number + 1) * down_rows, cut] = down.astype(jnp.float32)
                out_ref[number * out_rows : (number + 1) * out_rows, cut] = out.astype(jnp.float32)
            at += down_rows + out_rows


def finish_feed(total, shapes):
    return pl.pallas_call(
        finish_feed_kernel,
        out_shape=tuple(jax.ShapeDtypeStruct(shape, jnp.float32) for shape in shapes),
        in_specs=specs(1),
        out_specs=tuple(specs(4)),
        compiler_params=pltpu.CompilerParams(vmem_limit_bytes=28 << 20),
        cost_estimate=cost(5),
        name="finish_feed",
    )(total)


def join_feed_kernel(gate_ref, gate_in_ref, tail_ref, tail_in_ref, *out_refs):
    for number, out_ref in enumerate(out_refs):
        place = (number >> 1, number & 1)
        at = 0
        for kept_ref, in_ref in ((gate_ref, gate_in_ref), (tail_ref, tail_in_ref)):
            rows, width = kept_ref.shape[2:]
            total = kept_ref[place].astype(jnp.float32) + in_ref[place].astype(jnp.float32)
            total = total.astype(jnp.bfloat16)
            for strip in range(width // tile):
                out_ref[at : at + rows] = total[:, strip * tile : (strip + 1) * tile]
                at += rows


def join_feed(gate, gate_in, tail, tail_in):
    rows = sum(block.shape[2] * block.shape[3] // tile for block in (gate, tail))
    shape = jax.ShapeDtypeStruct((rows, tile), jnp.bfloat16)
    return pl.pallas_call(
        join_feed_kernel,
        out_shape=(shape,) * 4,
        in_specs=specs(4),
        out_specs=tuple(specs(4)),
        compiler_params=pltpu.CompilerParams(vmem_limit_bytes=20 << 20),
        cost_estimate=cost(2),
        name="join_feed",
    )(gate, gate_in, tail, tail_in)


sequence_axes = ("z", "core")
copy_axes = ("z", "core", "dp")
all_axes = ("z", "core", "dp", "ws")


def neighbours(block, axes):
    count = 1
    for axis in axes:
        count *= lax.axis_size(axis)
    forward = [(i, i + 1) for i in range(count - 1)]
    backward = [(target, source) for source, target in forward]
    return lax.ppermute(block, axes, forward), lax.ppermute(block, axes, backward)


def pad_rows(block):
    return jnp.pad(block, ((0, -block.shape[0] % tile), (0, 0)))


def send_edges(left, right, count):
    from_right = lax.ppermute(left, sequence_axes, [(i + 1, i) for i in range(count - 1)])
    from_left = lax.ppermute(right, sequence_axes, [(i, i + 1) for i in range(count - 1)])
    return from_right, from_left


def swap(block, axis, distance=1):
    pairs = [(i, i ^ distance) for i in range(lax.axis_size(axis))]
    return lax.ppermute(block, axis, pairs)


def ordered(near, far, place, axis):
    first = place == 0
    return jnp.concatenate([jnp.where(first, near, far), jnp.where(first, far, near)], axis=axis)


def pack(block, small):
    high, low = split_pair(small)
    rest = jnp.zeros((-2 * small.shape[0] % 16, small.shape[1]), jnp.bfloat16)
    return jnp.concatenate([block, high, low, rest])


def unpack(sent, small):
    count = small.shape[0]
    rows = sent.shape[0] - (2 * count + -2 * count % 16)
    high, low = sent[rows : rows + count], sent[rows + count : rows + 2 * count]
    return sent[:rows], small + high.astype(jnp.float32) + low.astype(jnp.float32)


def gather_columns(shard):
    axis = shard.ndim - 1
    if lax.axis_size("ws") != 2:
        return lax.all_gather(shard, "ws", axis=axis, tiled=True)
    return ordered(shard, swap(shard, "ws"), lax.axis_index("ws"), axis)


def own_share(shard, axis):
    share = shard.shape[axis] // 4
    place = lax.axis_index("dp") * 2 + lax.axis_index("core")
    return lax.dynamic_slice_in_dim(shard, place * share, share, axis)


def spread_pieces(first):
    second = swap(first, "dp")
    return first, second, swap(first, "core"), swap(second, "core")


def special_mesh():
    return lax.axis_size("ws") == 2 and lax.axis_size("dp") == 2 and lax.axis_size("z") == 4


def add(*parts):
    return sum(part.astype(jnp.float32) for part in parts).astype(parts[0].dtype)


def swap_high(block, place):
    return swap(block, "z", place[0] + 2 * place[1])


others = ((1, 0), (0, 1), (1, 1))


class Chain:
    def __init__(self, sent, kept, order):
        self.sent, self.kept = (sent,), kept
        self.order = order

    def join(self):
        axis, rest = self.order[0], self.order[1:]
        if axis == "z":
            received = [swap_high(part, place) for part, place in zip(self.sent, others)]
        else:
            received = [swap(self.sent[0], axis)]
        parts = [self.kept] + received
        self.order = rest
        if not rest:
            self.sent, self.kept = (), add(*parts)
            return
        places = others if rest[0] == "z" else ((1,),)
        self.sent = tuple(add(*(part[place] for part in parts)) for place in places)
        own = (0,) * len(places[0])
        self.kept = add(*(part[own] for part in parts))

    def state(self):
        return (self.sent, self.kept)

    def set_state(self, state):
        self.sent, self.kept = state


def gather_high(part):
    return jnp.stack(
        [
            jnp.stack([part, swap_high(part, (0, 1))]),
            jnp.stack([swap_high(part, (1, 0)), swap_high(part, (1, 1))]),
        ]
    )


def collect(part):
    return lax.all_gather(part, copy_axes, axis=0).reshape((8, 2) + part.shape)


def reduce_plain(grad):
    part = lax.psum_scatter(grad, "ws", scatter_dimension=grad.ndim - 2, tiled=True)
    return lax.psum(part, copy_axes).astype(jnp.float32)


def after(value, chains):
    if not special_mesh():
        return value
    value, kept = lax.optimization_barrier((value, [chain.kept for chain in chains]))
    for chain, part in zip(chains, kept):
        chain.kept = part
    return value


def hold(value, chains=()):
    if not special_mesh():
        return value
    value, states = lax.optimization_barrier((value, [chain.state() for chain in chains]))
    for chain, state in zip(chains, states):
        chain.set_state(state)
    return value


def per_device(
    byte_ids,
    segments,
    embed,
    conv_kernel,
    score_weight,
    attn_gain,
    w_q,
    w_k,
    w_v,
    w_o,
    rel_bias,
    ff_gain,
    w_gate,
    w_up,
    w_down,
    cotangent,
):
    byte_count = byte_ids.shape[1]
    row_count = byte_count // 2
    width = w_q.shape[1]
    group_count = lax.axis_size("ws")
    cycle_count = lax.axis_size("z") * lax.axis_size("core")
    cycle_place = lax.axis_index("z") * lax.axis_size("core") + lax.axis_index("core")
    bucket_count, head_count = rel_bias.shape
    rim = conv_width // 2
    has_before = cycle_place > 0
    has_after = cycle_place < cycle_count - 1

    ids = byte_ids[0]
    row_segs = segments[0, ::2]
    note = jnp.concatenate([row_segs, ids[:rim], ids[byte_count - rim :]])
    before_note, after_note = neighbours(note, sequence_axes)
    embed_table = gather_columns(embed)
    if special_mesh():
        core, dp = lax.axis_index("core"), lax.axis_index("dp")
        place = jnp.stack(
            [
                lax.axis_index("ws"), dp * 2 + core, 2 - dp * 2 + core, dp * 2 + 1 - core,
                3 - dp * 2 - core, core, 1 - core,
            ]
        ).astype(jnp.int32)
        own_order = jnp.stack([core, core + 2, 1 - core, 3 - core])
        peer_order = jnp.stack([3 * core, 1 + core, 2 - core, 3 - 3 * core])
        order = jnp.concatenate([place[0] * 4 + own_order, (1 - place[0]) * 4 + peer_order])
        order = order.astype(jnp.int32)
        z = lax.axis_index("z")
        bits = jnp.stack([core, place[0], dp, z & 1, z >> 1]).astype(jnp.int32)
        half = w_q.shape[0] // 2
        square_share = jnp.stack(
            [lax.dynamic_slice_in_dim(weight, core * half, half, 0) for weight in (w_q, w_k, w_v)]
        )
        gate_share = jnp.stack([own_share(weight, 0) for weight in (w_gate, w_up)])
        tail_share = jnp.concatenate(
            [
                lax.dynamic_slice_in_dim(weight, core * (weight.shape[0] // 2), weight.shape[0] // 2, 0)
                for weight in (w_down, w_o)
            ]
        )
        square_first = swap(square_share, "ws")
        square_share, embed_table, before_note, after_note = lax.optimization_barrier(
            (square_share, embed_table, before_note, after_note)
        )
        square_first = swap(square_share, "ws")
        square_place = jnp.stack([place[0], core, 1 - core]).astype(jnp.int32)
        own_square, own_feed = (w_q, w_k, w_v), (w_o, w_gate, w_up, w_down)
    else:
        place = square_place = jnp.zeros((1,), jnp.int32)
        order = jnp.arange(8, dtype=jnp.int32)
        bits = jnp.zeros((5,), jnp.int32)
        square_pieces = gate_pieces = tail_pieces = ()
        own_square, own_feed = (
            tuple(lax.all_gather(weight, "ws", axis=0, tiled=True) for weight in weights)
            for weights in ((w_q, w_k, w_v), (w_o, w_gate, w_up, w_down))
        )
    segs = jnp.stack(
        [
            jnp.where(has_before, before_note[:row_count], -2),
            row_segs,
            jnp.where(has_after, after_note[:row_count], 1 << 20),
        ]
    )
    segs = jnp.pad(segs, ((0, 0), (0, -row_count % tile)), constant_values=-3)
    left_ids = jnp.where(has_before, before_note[row_count + rim :], -1)
    right_ids = jnp.where(has_after, after_note[row_count : row_count + rim], -1)
    id_rows = -(-(byte_count + rim) // tile) * tile
    id_line = jnp.concatenate(
        [
            jnp.full((tile - rim,), -1, jnp.int32),
            left_ids,
            ids,
            right_ids,
            jnp.full((id_rows - byte_count - rim,), -1, jnp.int32),
        ]
    ).reshape(-1, 1, tile)
    conv = jnp.pad(conv_kernel.astype(jnp.float32), ((0, 8 - conv_width), (0, 0)))
    score = score_weight.astype(jnp.float32)[None]
    gain_one = attn_gain[None]
    gain_two = ff_gain[None]

    special = special_mesh()
    half_pairs = width // tile // 2
    start, x_rows, mix, block_weight = gbst_forward(id_line, embed_table, conv, score, row_count)
    if special:
        start, square_first, gate_share = lax.optimization_barrier((start, square_first, gate_share))
        square_pieces = (square_first, swap(square_first, "core"))
        gate_first = swap(gate_share, "ws")
    first_in, queries, own_kv = project(square_place, start, gain_one, own_square, square_pieces)
    if special:
        queries, gate_first, tail_share = lax.optimization_barrier((queries, gate_first, tail_share))
        tail_first = swap(tail_share, "ws")
        gate_second, gate_third = swap(gate_first, "dp"), swap(gate_first, "core")
    before_kv, after_kv = neighbours(own_kv, sequence_axes)
    near_state = attention_forward(segs, queries, (own_kv,), None, rel_bias, row_count)
    if special:
        near_state, before_kv, after_kv, gate_second = lax.optimization_barrier(
            (near_state, before_kv, after_kv, gate_second)
        )
        gate_pieces = (gate_first, gate_second, gate_third, swap(gate_second, "core"))
    attended, log_norm = attention_forward(
        segs, queries, (before_kv, after_kv), near_state, rel_bias, row_count
    )
    if special:
        attended, tail_first = lax.optimization_barrier((attended, tail_first))
        tail_pieces = (tail_first, swap(tail_first, "core"))
    output, down_grad, gate_up_grad, gate_up_sent, d_middle, d_attended, out_grad, ff_gain_grad = feed_forward(
        place, order, bits, attended, start, cotangent[0], gain_two, own_feed, gate_pieces, tail_pieces
    )
    chains = []
    if special:
        gate_chain = Chain(gate_up_sent, gate_up_grad, ("core", "ws", "dp", "z"))
        tail_chain = Chain(out_grad, down_grad, ("core", "dp", "ws", "z"))
        tail_chain.join()
        gate_chain.join()
        chains = [gate_chain, tail_chain]
    d_attended = hold(d_attended, chains)
    halves = []
    bias_parts = []
    for part in range(2):
        d_queries, d_before, d_own, d_after, bias_sums = attention_backward(
            segs, queries, d_attended, attended, before_kv, own_kv, after_kv, rel_bias,
            log_norm,            row_count, part * half_pairs, half_pairs,
        )
        if part == 0:
            d_attended, d_before, d_after = hold((d_attended, d_before, d_after))
        else:
            d_before, d_after = after((d_before, d_after), chains)
            for chain in chains:
                chain.join()
            d_before, d_after, halves = hold((d_before, d_after, halves), chains)
        from_after = lax.ppermute(
            d_before, sequence_axes, [(i + 1, i) for i in range(cycle_count - 1)]
        )
        from_before = lax.ppermute(
            d_after, sequence_axes, [(i, i + 1) for i in range(cycle_count - 1)]
        )
        halves.append((d_queries, d_own, from_after, from_before))
        bias_parts.append(jnp.transpose(bias_sums[: 2 * half_pairs, :bucket_count]))
    square_grads, square_sent, d_start, attn_gain_grad = project_back(
        square_place, bits, [part[i] for i in range(4) for part in halves], first_in, start,
        d_middle, gain_one, own_square, square_pieces,
    )
    if special:
        square_chain = Chain(square_sent, square_grads, ("core", "ws", "dp", "z"))
        d_start = after(d_start, chains)
        kept, high, low, both = join_feed(
            gate_chain.kept, swap(gate_chain.sent[0], "dp"),
            tail_chain.kept, swap(tail_chain.sent[0], "ws"),
        )
        feed_chain = Chain(None, kept, ("z",))
        feed_chain.sent = (low, high, both)
        d_start = hold(d_start, [square_chain, feed_chain])
        square_chain.join()
        d_start = hold(d_start, [square_chain])
    d_conv, left_grad, right_grad, conv_grad, score_grad = unpool(
        x_rows, mix, block_weight, d_start, conv, score, byte_count
    )
    bias_grad = jnp.concatenate(bias_parts, axis=1)
    bias_rows = jnp.pad(bias_grad.reshape(1, -1), ((0, 0), (0, width - bucket_count * head_count)))
    small = jnp.concatenate(
        [conv_grad, score_grad, attn_gain_grad, ff_gain_grad, bias_rows], axis=0
    )
    if special:
        d_conv, small = after((d_conv, small), [square_chain])
        square_chain.join()
        d_conv, small = hold((d_conv, small), [square_chain])
    byte_grad, embed_part = scatter_bytes(id_line, d_conv, conv, byte_count, embed.shape[0])
    if special:
        rows = embed_part.shape[0] // 2
        columns = width // 2
        small = small.reshape(-1, columns)
        embed_part = after(embed_part, [feed_chain, square_chain])
        feed_chain.join()
        square_chain.join()
        embed_part, feed_part = hold((embed_part, feed_chain.kept), [square_chain])
        feed_sum = collect(feed_part)
        core_rows = lax.dynamic_slice_in_dim(embed_part, bits[0] * rows, rows, 0)
        sent_rows = lax.dynamic_slice_in_dim(embed_part, (1 - bits[0]) * rows, rows, 0)
        sent = pack(sent_rows.reshape(2 * rows, columns), small)
        received, small = unpack(swap(sent, "core"), small)
        embed_part = add(core_rows, received.reshape(rows, width))
        square_chain.join()
        square_part = square_chain.kept
        own_columns = lax.dynamic_slice_in_dim(embed_part, bits[1] * columns, columns, 1)
        sent_columns = lax.dynamic_slice_in_dim(embed_part, (1 - bits[1]) * columns, columns, 1)
        sent = pack(sent_columns, small)
        own_columns, small, sent, square_part = hold((own_columns, small, sent, square_part))
        received, small = unpack(swap(sent, "ws"), small)
        embed_part = add(own_columns, received)
        square_part = gather_high(square_part)
        sent = pack(embed_part, small)
        embed_part, small, sent, square_part, left_grad, right_grad = hold(
            (embed_part, small, sent, square_part, left_grad, right_grad)
        )
        received, small = unpack(swap(sent, "dp"), small)
        embed_part = add(embed_part, received)
        square_across = swap(square_part, "dp")
        square_core = swap(square_part, "core")
        from_right, from_left = send_edges(left_grad, right_grad, cycle_count)
        sent = pack(embed_part, small)
        embed_part, small, sent, square_across, square_core, from_right, from_left = hold(
            (embed_part, small, sent, square_across, square_core, from_right, from_left)
        )
        parts = [embed_part]
        for place in others:
            received, small = unpack(swap_high(sent, place), small)
            parts.append(received)
        embed_part = add(*parts)
        square_both = swap(square_across, "core")
        byte_grad = add_edges(byte_grad, from_left, from_right)
        embed_part, small, square_both, byte_grad = hold((embed_part, small, square_both, byte_grad))
        embed_part = ordered(embed_part, swap(embed_part, "core"), bits[0], 0)
        query_sum, key_sum, value_sum = finish_square(
            bits, (square_part, square_across, square_core, square_both), ((columns, width),) * 3
        )
        embed_part, query_sum = hold((embed_part, query_sum))
        gate_sum, up_sum, down_sum, out_sum = finish_feed(
            feed_sum,
            (
                (columns, w_gate.shape[1]), (columns, w_gate.shape[1]),
                (w_down.shape[0], width), (columns, width),
            ),
        )
        small = small.reshape(-1, width)
    else:
        small = lax.psum(small, all_axes)
        embed_part = lax.psum_scatter(embed_part, "ws", scatter_dimension=1, tiled=True)
        embed_part = lax.psum(embed_part, copy_axes)
    embed_sum = embed_part[: embed.shape[0]].astype(jnp.float32)
    if not special:
        from_right, from_left = send_edges(left_grad, right_grad, cycle_count)
        byte_grad = add_edges(byte_grad, from_left, from_right)
        gate_sum, up_sum = jnp.transpose(reduce_plain(gate_up_grad), (1, 2, 0, 3)).reshape(
            2, width // group_count, -1
        )
        down_sum, out_sum = reduce_plain(down_grad), reduce_plain(out_grad)
        query_sum, key_sum, value_sum = reduce_plain(square_grads)
    return (
        output[None],
        byte_grad[None],
        embed_sum,
        small[:conv_width],
        small[conv_width],
        small[conv_width + 1],
        query_sum,
        key_sum,
        value_sum,
        out_sum,
        small[conv_width + 3, : bucket_count * head_count].reshape(bucket_count, head_count),
        small[conv_width + 2],
        gate_sum,
        up_sum,
        down_sum,
    )


def solution(mesh):
    devices = mesh.devices
    fine = Mesh(devices.reshape((devices.shape[0] // 2, 2) + devices.shape[1:]), all_axes)
    rows = P(("dp", "ws"), sequence_axes)
    split = P("ws", None)
    in_specs = (
        rows, rows, P(None, "ws"), P(), P(), P(), split, split, split, split, P(), P(),
        split, split, split, P(("dp", "ws"), sequence_axes, None),
    )
    wide = P(("dp", "ws"), sequence_axes, None)
    out_specs = (
        wide, wide, P(None, "ws"), P(), P(), P(), split, split, split, split, P(), P(),
        split, split, split,
    )
    return jax.shard_map(
        per_device, mesh=fine, in_specs=in_specs, out_specs=out_specs, check_vma=False
    )
```

```python
import functools

import jax
import jax.numpy as jnp
from jax import lax
from jax.experimental import pallas as pl
from jax.experimental.pallas import tpu as pltpu
from jax.sharding import Mesh
from jax.sharding import PartitionSpec as P

thresholds = (12, 16, 23, 32, 46, 64, 91)
negative = -1e30
epsilon = 1e-06
conv_width = 5
tile = 128
near_bases = (-128, -120, 0, 120, 128)
class_count = len(near_bases) + 2


def bucket_of(relative):
    distance = jnp.abs(relative)
    far_bucket = 8 + sum(((distance >= threshold).astype(jnp.int32) for threshold in thresholds))
    near_bucket = jnp.where(distance < 8, distance, far_bucket)
    return near_bucket + 16 * (relative > 0).astype(jnp.int32)


def matmul(left, right, left_dim, right_dim):
    return lax.dot_general(
        left, right, (((left_dim,), (right_dim,)), ((), ())), preferred_element_type=jnp.float32
    )


def split_pair(values):
    high = values.astype(jnp.bfloat16)
    return high, (values - high.astype(jnp.float32)).astype(jnp.bfloat16)


def tile_class(query_tile, key_tile):
    step = key_tile - query_tile - 4
    own = jnp.where(
        step <= -2, 0, jnp.where(step == -1, 1, jnp.where(step == 0, 3, jnp.where(step == 1, 5, 6)))
    )
    before = jnp.where(step == -1, 2, 0)
    after = jnp.where(step == 1, 4, 6)
    return jnp.where(key_tile < 4, before, jnp.where(key_tile < 8, own, after))


def key_range(seg_ref, query_tile, row_count, tiles_per_block):
    first_seg = seg_ref[1, query_tile * tile]
    last_seg = seg_ref[1, jnp.minimum(query_tile * tile + tile, row_count) - 1]
    low = jnp.int32(0)
    high = jnp.int32(0)
    for block in range(3):
        for part in range(tiles_per_block):
            key_first = seg_ref[block, part * tile]
            key_last = seg_ref[block, min(part * tile + tile, row_count) - 1]
            low = low + (key_last < first_seg).astype(jnp.int32)
            high = high + (key_first <= last_seg).astype(jnp.int32)
    return low, high


def class_buckets(kind, shape, dim):
    place = lax.broadcasted_iota(jnp.int32, shape, dim)
    swing = jnp.where(place < tile, place, place - 2 * tile)
    if kind == 0:
        return jnp.full(shape, bucket_of(jnp.int32(-4 * tile)))
    if kind == class_count - 1:
        return jnp.full(shape, bucket_of(jnp.int32(4 * tile)))
    return bucket_of(near_bases[kind - 1] - swing)


def make_bias(rel_ref, bias_ref, first_pair, pair_count):
    bucket_count = rel_ref.shape[0]
    for kind in range(class_count):
        shape = (bucket_count, 2 * tile)
        hot = class_buckets(kind, shape, 1) == lax.broadcasted_iota(jnp.int32, shape, 0)
        lines = lax.dot_general(
            rel_ref[...], hot.astype(jnp.float32), (((0,), (0,)), ((), ())),
            precision=lax.Precision.HIGHEST, preferred_element_type=jnp.float32,
        )
        for pair in range(pair_count):
            for half in range(2):
                head = 2 * (first_pair + pair) + half
                grid = jnp.broadcast_to(lines[head : head + 1], (tile, 2 * tile))
                if 0 < kind < class_count - 1:
                    grid = pltpu.roll(grid, 0, 1, stride=1, stride_axis=0)
                bias_ref[kind, pair, :, half * tile : (half + 1) * tile] = grid[:, :tile]


def cost(microseconds):
    return pl.CostEstimate(
        flops=int(microseconds * 1e7), transcendentals=0, bytes_accessed=int(microseconds * 3e4)
    )


def stack_heads(block):
    lane = lax.broadcasted_iota(jnp.int32, block.shape, 1)
    zero = jnp.zeros_like(block)
    return jnp.concatenate(
        [jnp.where(lane < tile // 2, block, zero), jnp.where(lane < tile // 2, zero, block)], axis=0
    )


def fold_rows(values, combine):
    pieces = [values[8 * i : 8 * i + 8] for i in range(values.shape[0] // 8)]
    while len(pieces) > 1:
        joined = [combine(pieces[i], pieces[i + 1]) for i in range(0, len(pieces) - 1, 2)]
        if len(pieces) % 2:
            joined.append(pieces[-1])
        pieces = joined
    return pieces[0]


def key_columns(segs_ref, column_ref, key_tile):
    row = segs_ref[key_tile, 0:1, :]
    column_ref[key_tile] = jnp.transpose(jnp.broadcast_to(row, (tile, tile)))


def start_copies(sources, window_ref, sems, first_pair):
    rows, full_width = sources[0].shape
    width = window_ref.shape[1] // 2
    copies = []
    for i, source in enumerate(sources):
        for side in range(2):
            copies.append(
                pltpu.make_async_copy(
                    source.at[:, pl.ds(side * (full_width // 2) + first_pair * tile, width)],
                    window_ref.at[pl.ds(rows * i, rows), pl.ds(side * width, width)],
                    sems.at[2 * i + side],
                )
            )
    for copy in copies:
        copy.start()
    return copies


def forward_kernel(seg_ref, q_ref, *refs, row_count, near):
    if near:
        source_refs, refs = refs[:1], refs[1:]
    else:
        source_refs, refs = refs[:2], refs[2:]
        (mixed_in_ref, top_in_ref, total_in_ref), refs = refs[:3], refs[3:]
    segs_ref, qsegs_ref, rel_ref = refs[:3]
    if near:
        mixed_ref, top_ref, total_ref = refs[3:6]
    else:
        out_ref, lse_ref = refs[3:5]
    window_ref, bias_ref, column_ref, flipped_ref, score_ref = refs[-6 if near else -7 :][:5]
    sems = refs[-1]
    if not near:
        mixed_ref = refs[-2]
    width = q_ref.shape[1]
    pair_count = width // tile
    query_tiles = q_ref.shape[0] // tile
    half = tile // 2
    middle = query_tiles // 2
    copies = start_copies(source_refs, window_ref, sems, 0)
    make_bias(rel_ref, bias_ref, 0, pair_count)

    def key_span(query_tile):
        low, high = key_range(seg_ref, query_tile, row_count, query_tiles)
        if near:
            low = jnp.maximum(low - query_tiles, 0)
            high = jnp.minimum(high - query_tiles, query_tiles)
            return low // 2, (high + 1) // 2
        return jnp.minimum(low // 2, middle), jnp.maximum((high + 1) // 2 - middle, middle)

    def global_tile(key_pair, part):
        key_tile = 2 * key_pair + part
        if near:
            return key_tile + query_tiles
        return key_tile + jnp.where(key_pair >= middle, query_tiles, 0)

    first = key_span(0)[0]
    last = key_span(query_tiles - 1)[1]
    for copy in copies:
        copy.wait()

    def prepare(key_pair, carry):
        for part in range(2):
            row = segs_ref[global_tile(key_pair, part), 0:1, :]
            column_ref[2 * key_pair + part] = jnp.transpose(jnp.broadcast_to(row, (tile, tile)))
        at = pl.multiple_of(key_pair * 2 * tile, 2 * tile)
        flipped_ref[key_pair] = jnp.transpose(window_ref[pl.ds(at, 2 * tile), width:])
        return carry

    lax.fori_loop(first, last, prepare, 0)

    def query_step(query_tile, carry):
        low, high = key_span(query_tile)
        rows = pl.ds(pl.multiple_of(query_tile * tile, tile), tile)
        lanes = [slice(pair * tile, (pair + 1) * tile) for pair in range(pair_count)]
        stacked = [stack_heads(q_ref[rows, lane]) for lane in lanes]
        query_seg = qsegs_ref[query_tile, 0:1, :]
        slot = query_tile if near else 0

        def score_step(key_pair, tops):
            keys = pl.ds(pl.multiple_of(key_pair * 2 * tile, 2 * tile), 2 * tile)
            hides = []
            kinds = []
            for part in range(2):
                hide = jnp.where(column_ref[2 * key_pair + part] == query_seg, 0.0, negative)
                hides.append(jnp.concatenate([hide, hide], axis=1))
                kinds.append(tile_class(query_tile, global_tile(key_pair, part)))
            fresh = []
            for pair in range(pair_count):
                scores = matmul(window_ref[keys, lanes[pair]], stacked[pair], 1, 1)
                top = tops[pair]
                for part in range(2):
                    cut = slice(part * tile, (part + 1) * tile)
                    piece = scores[cut] + bias_ref[kinds[part], pair] + hides[part]
                    score_ref[key_pair, pair, cut] = piece
                    top = jnp.maximum(top, fold_rows(piece, jnp.maximum))
                fresh.append(top)
            return tuple(fresh)

        tops = lax.fori_loop(
            low, high, score_step,
            tuple(jnp.full((8, 2 * tile), negative, jnp.float32) for _ in range(pair_count)),
        )
        tops = [jnp.max(top, axis=0, keepdims=True) for top in tops]
        scales = []
        for pair in range(pair_count):
            if near:
                mixed_ref[slot, pair] = jnp.zeros((tile, tile), jnp.float32)
            else:
                before = top_in_ref[query_tile, pair : pair + 1, :]
                tops[pair] = jnp.maximum(tops[pair], before)
                scale = jnp.exp(before - tops[pair])
                scales.append(scale)
                mixed_ref[slot, pair, :half] = mixed_in_ref[query_tile, pair, :half] * scale[:, :tile]
                mixed_ref[slot, pair, half:] = mixed_in_ref[query_tile, pair, half:] * scale[:, tile:]

        def mix_step(key_pair, totals):
            fresh = []
            for pair in range(pair_count):
                exponent = jnp.exp(score_ref[key_pair, pair] - tops[pair])
                fresh.append(totals[pair] + fold_rows(exponent, jnp.add))
                mixed = matmul(
                    flipped_ref[key_pair, lanes[pair], :], exponent.astype(jnp.bfloat16), 1, 0
                )
                mixed_ref[slot, pair, :half] += mixed[:half, :tile]
                mixed_ref[slot, pair, half:] += mixed[half:, tile:]
            return tuple(fresh)

        totals = lax.fori_loop(
            low, high, mix_step,
            tuple(jnp.zeros((8, 2 * tile), jnp.float32) for _ in range(pair_count)),
        )
        for pair in range(pair_count):
            total = jnp.sum(totals[pair], axis=0, keepdims=True)
            if near:
                top_ref[query_tile, pair : pair + 1, :] = tops[pair]
                total_ref[query_tile, pair : pair + 1, :] = total
                continue
            total = total + total_in_ref[query_tile, pair : pair + 1, :] * scales[pair]
            lse_ref[query_tile, pair : pair + 1, :] = tops[pair] + jnp.log(total)
            inverse = 1.0 / total
            scaled = jnp.concatenate(
                [
                    mixed_ref[slot, pair, :half] * inverse[:, :tile],
                    mixed_ref[slot, pair, half:] * inverse[:, tile:],
                ],
                axis=0,
            )
            out_ref[rows, lanes[pair]] = jnp.transpose(scaled).astype(jnp.bfloat16)
        return carry

    lax.fori_loop(0, query_tiles, query_step, 0)


def backward_kernel(
    seg_ref, q_ref, do_ref, o_ref, before_ref, own_ref, after_ref, segs_ref, qsegs_ref, rel_ref, lse_ref,
    dq_ref, dbefore_ref, down_ref, dafter_ref, bias_out_ref,
    window_ref, bias_ref, column_ref, flipped_ref, dbias_ref, dwindow_ref, dq_acc_ref, delta_ref, sems,
    *, row_count, first_pair
):
    width = dq_ref.shape[1]
    pair_count = width // tile
    query_tiles = q_ref.shape[0] // tile
    block_rows = q_ref.shape[0]
    half = tile // 2
    copies = start_copies((before_ref, own_ref, after_ref), window_ref, sems, first_pair)
    make_bias(rel_ref, bias_ref, first_pair, pair_count)
    dwindow_ref[...] = jnp.zeros(dwindow_ref.shape, jnp.float32)
    dbias_ref[...] = jnp.zeros(dbias_ref.shape, jnp.float32)
    product = do_ref[...].astype(jnp.float32) * o_ref[...].astype(jnp.float32)
    product_high, product_low = split_pair(product)
    member = (
        lax.broadcasted_iota(jnp.int32, (16, width), 1) // half
        == lax.broadcasted_iota(jnp.int32, (16, width), 0)
    ).astype(jnp.bfloat16)
    delta_ref[...] = matmul(member, product_high, 1, 1) + matmul(member, product_low, 1, 1)
    first = key_range(seg_ref, 0, row_count, query_tiles)[0]
    last = key_range(seg_ref, query_tiles - 1, row_count, query_tiles)[1]
    for copy in copies:
        copy.wait()

    def prepare(key_pair, carry):
        for part in range(2):
            key_columns(segs_ref, column_ref, 2 * key_pair + part)
        at = pl.multiple_of(key_pair * 2 * tile, 2 * tile)
        flipped_ref[key_pair] = jnp.transpose(window_ref[pl.ds(at, 2 * tile), :width])
        return carry

    lax.fori_loop(first // 2, (last + 1) // 2, prepare, 0)

    def query_step(query_tile, carry):
        low, high = key_range(seg_ref, query_tile, row_count, query_tiles)
        at = pl.multiple_of(query_tile * tile, tile)
        rows = pl.ds(at, tile)
        lanes = [slice(pair * tile, (pair + 1) * tile) for pair in range(pair_count)]
        queries = [stack_heads(q_ref[rows, lane]) for lane in lanes]
        grads = [stack_heads(do_ref[rows, lane]) for lane in lanes]
        query_seg = qsegs_ref[query_tile, 0:1, :]
        deltas = [
            jnp.concatenate(
                [delta_ref[2 * pair : 2 * pair + 1, rows], delta_ref[2 * pair + 1 : 2 * pair + 2, rows]],
                axis=1,
            )
            for pair in range(pair_count)
        ]
        norms = [
            lse_ref[query_tile, first_pair + pair : first_pair + pair + 1, :]
            for pair in range(pair_count)
        ]
        for pair in range(pair_count):
            dq_acc_ref[pair] = jnp.zeros((tile, tile), jnp.float32)

        def key_step(key_pair, carry):
            keys = pl.ds(pl.multiple_of(key_pair * 2 * tile, 2 * tile), 2 * tile)
            hides = []
            kinds = []
            for part in range(2):
                key_tile = 2 * key_pair + part
                hide = jnp.where(column_ref[key_tile] == query_seg, 0.0, negative)
                hides.append(jnp.concatenate([hide, hide], axis=1))
                kinds.append(tile_class(query_tile, key_tile))
            for pair in range(pair_count):
                lane = lanes[pair]
                value_lane = slice(width + pair * tile, width + (pair + 1) * tile)
                scores = matmul(window_ref[keys, lane], queries[pair], 1, 1)
                dprobs = matmul(window_ref[keys, value_lane], grads[pair], 1, 1)
                probs_low, dscores_low = [], []
                for part in range(2):
                    cut = slice(part * tile, (part + 1) * tile)
                    probs = jnp.exp(
                        scores[cut] + bias_ref[kinds[part], pair] + hides[part] - norms[pair]
                    )
                    dscores = probs * (dprobs[cut] - deltas[pair])
                    dbias_ref[kinds[part], pair] += dscores
                    probs_low.append(probs.astype(jnp.bfloat16))
                    dscores_low.append(dscores.astype(jnp.bfloat16))
                probs_low = jnp.concatenate(probs_low, axis=0)
                dscores_low = jnp.concatenate(dscores_low, axis=0)
                dwindow_ref[keys, lane] += matmul(dscores_low, queries[pair], 1, 0)
                dwindow_ref[keys, value_lane] += matmul(probs_low, grads[pair], 1, 0)
                dquery = matmul(flipped_ref[key_pair, lane, :], dscores_low, 1, 0)
                dq_acc_ref[pair, :half] += dquery[:half, :tile]
                dq_acc_ref[pair, half:] += dquery[half:, tile:]
            return carry

        lax.fori_loop(low // 2, (high + 1) // 2, key_step, 0)
        for pair in range(pair_count):
            dq_ref[rows, lanes[pair]] = jnp.transpose(dq_acc_ref[pair]).astype(jnp.bfloat16)
        return carry

    lax.fori_loop(0, query_tiles, query_step, 0)
    dbefore_ref[...] = dwindow_ref[:block_rows].astype(jnp.bfloat16)
    down_ref[...] = dwindow_ref[block_rows : 2 * block_rows]
    dafter_ref[...] = dwindow_ref[2 * block_rows :].astype(jnp.bfloat16)
    turn = (
        lax.broadcasted_iota(jnp.int32, (tile, tile), 0)
        + lax.broadcasted_iota(jnp.int32, (tile, tile), 1)
        == tile - 1
    ).astype(jnp.bfloat16)
    zero_half = jnp.zeros((tile, tile), jnp.float32)
    bucket_count = rel_ref.shape[0]
    total = jnp.zeros(bias_out_ref.shape, jnp.float32)
    for kind in range(class_count):
        lines = []
        for pair in range(pair_count):
            grid = dbias_ref[kind, pair]
            near = 0 < kind < class_count - 1
            if near:
                grid_high, grid_low = split_pair(grid)
                grid = matmul(turn, grid_high, 1, 0) + matmul(turn, grid_low, 1, 0)
            for side in range(2):
                part = jnp.concatenate([grid[:, side * tile : (side + 1) * tile], zero_half], axis=1)
                if near:
                    part = pltpu.roll(part, tile + 1, 1, stride=1, stride_axis=0)
                lines.append(jnp.sum(fold_rows(part, jnp.add), axis=0, keepdims=True))
        lines.append(jnp.zeros((bias_out_ref.shape[0] - len(lines), 2 * tile), jnp.float32))
        shape = (2 * tile, tile)
        hot = class_buckets(kind, shape, 0) == lax.broadcasted_iota(jnp.int32, shape, 1)
        total = total + jnp.dot(
            jnp.concatenate(lines, axis=0), hot.astype(jnp.float32),
            precision=lax.Precision.HIGHEST, preferred_element_type=jnp.float32,
        )
    bias_out_ref[...] = total


def specs(count, space=pltpu.VMEM):
    return [pl.BlockSpec(memory_space=space) for _ in range(count)]


def attention_forward(segs, q, sources, state, rel_bias, row_count):
    rows, width = q.shape
    tiles = rows // tile
    pairs = width // tile
    near = state is None
    seg_rows = segs.reshape(3 * tiles, 1, tile)
    query_segs = mark_queries(segs, row_count).reshape(tiles, 1, tile)
    f32 = jnp.float32
    norm = jax.ShapeDtypeStruct((tiles, 8, 2 * tile), f32)
    mixed = jax.ShapeDtypeStruct((tiles, pairs, tile, tile), f32)
    count = len(sources)
    blocks = count * tiles // 2
    scratch = [
        pltpu.VMEM((count * rows, 2 * width), jnp.bfloat16),
        pltpu.VMEM((class_count, pairs, tile, 2 * tile), f32),
        pltpu.VMEM((count * tiles, tile, tile), jnp.int32),
        pltpu.VMEM((blocks, width, 2 * tile), jnp.bfloat16),
        pltpu.VMEM((blocks, pairs, 2 * tile, 2 * tile), f32),
    ]
    if not near:
        scratch.append(pltpu.VMEM((1, pairs, tile, tile), f32))
    return pl.pallas_call(
        functools.partial(forward_kernel, row_count=row_count, near=near),
        out_shape=(mixed, norm, norm)
        if near
        else (jax.ShapeDtypeStruct((rows, width), jnp.bfloat16), norm),
        in_specs=specs(1, pltpu.SMEM) + specs(1) + specs(count, pl.ANY)
        + specs(3 if near else 6),
        out_specs=tuple(specs(3 if near else 2)),
        scratch_shapes=scratch + [pltpu.SemaphoreType.DMA((2 * count,))],
        compiler_params=pltpu.CompilerParams(vmem_limit_bytes=(22 if near else 30) << 20),
        cost_estimate=cost(12),
        name="attention_near" if near else "attention_rim",
    )(segs, q, *sources, *(state or ()), seg_rows, query_segs, rel_bias)


def mark_queries(segs, row_count):
    place = jnp.arange(segs.shape[1], dtype=jnp.int32)
    return jnp.where(place < row_count, segs[1], -1)


def attention_backward(
    segs, q, do, o, before, own, after, rel_bias, lse, row_count, first_pair, pairs
):
    rows, full_width = q.shape
    tiles = rows // tile
    width = pairs * tile
    seg_rows = segs.reshape(3 * tiles, 1, tile)
    query_segs = mark_queries(segs, row_count).reshape(tiles, 1, tile)
    part = pl.BlockSpec((rows, width), lambda i: (0, first_pair // pairs))
    return pl.pallas_call(
        functools.partial(backward_kernel, row_count=row_count, first_pair=first_pair),
        grid=(1,),
        out_shape=(
            jax.ShapeDtypeStruct((rows, width), jnp.bfloat16),
            jax.ShapeDtypeStruct((rows, 2 * width), jnp.bfloat16),
            jax.ShapeDtypeStruct((rows, 2 * width), jnp.float32),
            jax.ShapeDtypeStruct((rows, 2 * width), jnp.bfloat16),
            jax.ShapeDtypeStruct((8, tile), jnp.float32),
        ),
        in_specs=specs(1, pltpu.SMEM) + [part, part, part] + specs(3, pl.ANY) + specs(4),
        out_specs=tuple(specs(5)),
        scratch_shapes=[
            pltpu.VMEM((3 * rows, 2 * width), jnp.bfloat16),
            pltpu.VMEM((class_count, pairs, tile, 2 * tile), jnp.float32),
            pltpu.VMEM((3 * tiles, tile, tile), jnp.int32),
            pltpu.VMEM((3 * tiles // 2, width, 2 * tile), jnp.bfloat16),
            pltpu.VMEM((class_count, pairs, tile, 2 * tile), jnp.float32),
            pltpu.VMEM((3 * rows, 2 * width), jnp.float32),
            pltpu.VMEM((pairs, tile, tile), jnp.float32),
            pltpu.VMEM((16, rows), jnp.float32),
            pltpu.SemaphoreType.DMA((6,)),
        ],
        compiler_params=pltpu.CompilerParams(vmem_limit_bytes=30 << 20),
        cost_estimate=cost(20),
        name="attention_backward",
    )(segs, q, do, o, before, own, after, seg_rows, query_segs, rel_bias, lse)


span = 96
id_pad = 128


def dot3(left, right, left_dim, right_dim):
    left_high, left_low = split_pair(left)
    right_high, right_low = split_pair(right)
    return (
        matmul(left_high, right_high, left_dim, right_dim)
        + matmul(left_low, right_high, left_dim, right_dim)
        + matmul(left_high, right_low, left_dim, right_dim)
    )


def block_means_grid(block_size):
    row = lax.broadcasted_iota(jnp.int32, (span, tile), 0)
    lane = lax.broadcasted_iota(jnp.int32, (span, tile), 1)
    same = (row // block_size == lane // block_size) & (lane < span)
    return jnp.where(same, 1.0 / block_size, 0.0)


def row_to_column(row):
    lane = lax.broadcasted_iota(jnp.int32, (span, tile), 1)
    place = lax.broadcasted_iota(jnp.int32, (span, tile), 0)
    return jnp.sum(jnp.where(lane == place, row, 0.0), axis=1, keepdims=True)


def column_to_row(column):
    lane = lax.broadcasted_iota(jnp.int32, (span, tile), 1)
    place = lax.broadcasted_iota(jnp.int32, (span, tile), 0)
    return jnp.sum(jnp.where(lane == place, column, 0.0), axis=0, keepdims=True)


def conv_tile(x_ref, conv_ref, base, lanes):
    taps = range(conv_width)
    return [
        sum(
            conv_ref[tap : tap + 1, i * tile : (i + 1) * tile]
            * x_ref[i, pl.ds(base + tap - conv_width // 2, span), :]
            for tap in taps
        )
        for i in range(lanes)
    ]


def gbst_forward_kernel(
    ids_ref, embed_ref, conv_ref, score_ref,
    start_ref, x_ref, mix_ref, weight_ref,
    table_ref, square_ref, wide_ref,
):
    vocab, width = embed_ref.shape
    lanes = width // tile
    id_tiles = ids_ref.shape[0]
    rows = start_ref.shape[0]
    table_ref[...] = jnp.zeros(table_ref.shape, jnp.bfloat16)
    table_ref[:vocab] = embed_ref[...]
    table_rows = table_ref.shape[0]
    rest = x_ref.shape[1] - id_tiles * tile
    for i in range(lanes):
        x_ref[i, id_tiles * tile :, :] = jnp.zeros((rest, tile), jnp.float32)

    def lookup(step, carry):
        ids = jnp.transpose(jnp.broadcast_to(ids_ref[step, 0:1, :], (tile, tile)))
        lane = lax.broadcasted_iota(jnp.int32, (tile, tile), 1)
        hot = jnp.concatenate(
            [(ids == lane + tile * i).astype(jnp.bfloat16) for i in range(table_rows // tile)], axis=1
        )
        found = matmul(hot, table_ref[...], 1, 0)
        at = pl.ds(pl.multiple_of(step * tile, tile), tile)
        for i in range(lanes):
            x_ref[i, at, :] = found[:, i * tile : (i + 1) * tile]
        return carry

    lax.fori_loop(0, id_tiles, lookup, 0)
    means = [block_means_grid(size) for size in (1, 2, 3, 4)]

    def pool(step, carry):
        base = pl.multiple_of(step * span, 8)
        conv = conv_tile(x_ref, conv_ref, base + id_pad, lanes)
        total = sum(conv[i] * score_ref[0:1, i * tile : (i + 1) * tile] for i in range(lanes))
        row = column_to_row(jnp.sum(total, axis=1, keepdims=True))
        scores = [jnp.sum(mean * row, axis=1, keepdims=True) for mean in means]
        top = functools.reduce(jnp.maximum, scores)
        exponents = [jnp.exp(score - top) for score in scores]
        inverse = 1.0 / sum(exponents)
        weights = [exponent * inverse for exponent in exponents]
        square_ref[...] = sum(weight * mean for weight, mean in zip(weights, means))
        mix = 0.5 * (
            square_ref[pl.ds(0, span // 2, stride=2), :] + square_ref[pl.ds(1, span // 2, stride=2), :]
        )
        half = pl.ds(pl.multiple_of(step * (span // 2), 8), span // 2)
        mix_ref[half, :] = mix
        lane = lax.broadcasted_iota(jnp.int32, (span, tile), 1)
        packed = jnp.zeros((span, tile), jnp.float32)
        for i in range(4):
            packed = jnp.where(lane == i, weights[i], packed)
        weight_ref[pl.ds(base, span), :] = packed
        wide_ref[half, :] = dot3(mix[:, :span], jnp.concatenate(conv, axis=1), 1, 0)
        return carry

    lax.fori_loop(0, mix_ref.shape[0] * 2 // span, pool, 0)
    start_ref[...] = wide_ref[:rows]


def gbst_forward(ids, embed, conv, score, row_count):
    vocab, width = embed.shape
    rows = -(-row_count // tile) * tile
    steps = -(-2 * row_count // span)
    x_rows = max(ids.shape[0] * tile, id_pad + steps * span) + 8
    f32 = jnp.float32
    return pl.pallas_call(
        gbst_forward_kernel,
        out_shape=(
            jax.ShapeDtypeStruct((rows, width), f32),
            jax.ShapeDtypeStruct((width // tile, x_rows, tile), f32),
            jax.ShapeDtypeStruct((steps * span // 2, tile), f32),
            jax.ShapeDtypeStruct((steps * span, tile), f32),
        ),
        in_specs=specs(4),
        out_specs=tuple(specs(4)),
        scratch_shapes=[
            pltpu.VMEM((-(-vocab // tile) * tile, width), jnp.bfloat16),
            pltpu.VMEM((span, tile), f32),
            pltpu.VMEM((steps * span // 2, width), f32),
        ],
        compiler_params=pltpu.CompilerParams(vmem_limit_bytes=18 << 20),
        cost_estimate=cost(12),
        name="gbst_forward",
    )(ids, embed, conv, score)


def weight_copies(place_ref, parts, pieces, full_ref, sems):
    copies = []
    rows = parts[0].shape[0]
    for i, part in enumerate(parts):
        at = pl.multiple_of(place_ref[0] * rows, rows)
        copies.append(
            pltpu.make_async_copy(part, full_ref.at[i, pl.ds(at, rows)], sems.at[len(copies)])
        )
    for number, piece in enumerate(pieces):
        share = piece.shape[1]
        at = pl.multiple_of((1 - place_ref[0]) * rows + place_ref[1 + number] * share, share)
        copies.append(
            pltpu.make_async_copy(piece, full_ref.at[:, pl.ds(at, share)], sems.at[len(copies)])
        )
    for copy in copies:
        copy.start()
    return copies


def project_kernel(place_ref, start_ref, gain_ref, *refs):
    pieces = refs[3:-5]
    first_ref, q_ref, kv_ref, weight_ref, sems = refs[-5:]
    copies = weight_copies(place_ref, refs[:3], pieces, weight_ref, sems)
    width = q_ref.shape[1]
    start = start_ref[...]
    inverse = lax.rsqrt(jnp.mean(start * start, axis=-1, keepdims=True) + epsilon)
    first = (start * inverse * gain_ref[...]).astype(jnp.bfloat16)
    first_ref[...] = first
    for copy in copies:
        copy.wait()
    q_ref[...] = matmul(first, weight_ref[0], 1, 0).astype(jnp.bfloat16)
    kv_ref[:, :width] = matmul(first, weight_ref[1], 1, 0).astype(jnp.bfloat16)
    kv_ref[:, width:] = matmul(first, weight_ref[2], 1, 0).astype(jnp.bfloat16)


def project(place, start, gain, own, pieces):
    rows, width = start.shape
    b16 = jnp.bfloat16
    return pl.pallas_call(
        project_kernel,
        out_shape=(
            jax.ShapeDtypeStruct((rows, width), b16),
            jax.ShapeDtypeStruct((rows, width), b16),
            jax.ShapeDtypeStruct((rows, 2 * width), b16),
        ),
        in_specs=specs(1, pltpu.SMEM) + specs(2) + specs(3 + len(pieces), pl.ANY),
        out_specs=tuple(specs(3)),
        scratch_shapes=[
            pltpu.VMEM((3, width, width), b16),
            pltpu.SemaphoreType.DMA((3 + len(pieces),)),
        ],
        compiler_params=pltpu.CompilerParams(vmem_limit_bytes=60 << 20),
        cost_estimate=cost(6),
        name="project",
    )(place, start, gain, *own, *pieces)


def feed_kernel(
    place_ref, order_ref, bits_ref, mixed_ref, start_ref, cot_ref, gain_ref, *refs, piece_count, tail_count
):
    (wo_ref, wg_ref, wu_ref, wd_ref), refs = refs[:4], refs[4:]
    gate_pieces, refs = refs[:piece_count], refs[piece_count:]
    tail_pieces, refs = refs[:tail_count], refs[tail_count:]
    (
        out_ref, downg_ref, gateup_ref, extra_ref, dmid_ref, dmixed_ref, outg_ref, gaing_ref,
        second_ref, turned_ref, middle_ref, scale_ref, total_ref, dsecond_ref, grad_ref,
        fullo_ref, fullg_ref, fullu_ref, fulld_ref,
    ) = refs
    step = pl.program_id(0)
    last = pl.num_programs(0) - 1
    row_count = out_ref.shape[0]
    chunk = fulld_ref.shape[0]

    def fill(full_ref, own_ref, pieces, pick, base=1):
        rows = own_ref.shape[0]
        full_ref[pl.ds(pl.multiple_of(place_ref[0] * rows, rows), rows), :] = own_ref[...]
        for number, piece in enumerate(pieces):
            block = pick(piece)
            share = block.shape[0]
            at = (1 - place_ref[0]) * rows + place_ref[base + number] * share
            full_ref[pl.ds(pl.multiple_of(at, share), share), :] = block

    @pl.when(step == 0)
    def _():
        fill(fullo_ref, wo_ref, tail_pieces, lambda piece: piece[2 * chunk :], 5)
        middle = start_ref[...] + matmul(mixed_ref[...], fullo_ref[...], 1, 0)
        middle_ref[...] = middle
        inverse = lax.rsqrt(jnp.mean(middle * middle, axis=-1, keepdims=True) + epsilon)
        scale_ref[...] = jnp.broadcast_to(inverse, scale_ref.shape)
        second = (middle * inverse * gain_ref[...]).astype(jnp.bfloat16)
        second_ref[...] = second
        turned_ref[...] = jnp.transpose(second)
        total_ref[...] = jnp.zeros(total_ref.shape, jnp.float32)
        dsecond_ref[...] = jnp.zeros(dsecond_ref.shape, jnp.float32)
        grad_ref[:row_count] = cot_ref[...]
        grad_ref[row_count:] = jnp.zeros((grad_ref.shape[0] - row_count, grad_ref.shape[1]), jnp.bfloat16)

    fill(fullg_ref, wg_ref, gate_pieces, lambda piece: piece[0])
    fill(fullu_ref, wu_ref, gate_pieces, lambda piece: piece[1])
    own_steps = pl.num_programs(0) - piece_count

    @pl.when(step < own_steps)
    def _():
        fulld_ref[...] = wd_ref[...]

    for number in range(tail_count):

        @pl.when((step >= own_steps) & ((step - own_steps) >> 1 == number))
        def _():
            at = pl.multiple_of((order_ref[step] & 1) * chunk, chunk)
            fulld_ref[...] = tail_pieces[number][pl.ds(at, chunk), :]

    second = second_ref[...]
    cot = grad_ref[...]
    gate = matmul(second, fullg_ref[...], 1, 0)
    up = matmul(second, fullu_ref[...], 1, 0)
    dhidden = matmul(cot, fulld_ref[...], 1, 1)
    root = 0.7978845608028654
    square = gate * gate
    bend = jnp.tanh(root * (gate + 0.044715 * (square * gate)))
    rise = 0.5 * (1.0 + bend)
    gelu = gate * rise
    slope = rise + 0.5 * gate * (1.0 - bend * bend) * (root * (1.0 + 3 * 0.044715 * square))
    hidden = (gelu * up).astype(jnp.bfloat16)
    dgate = (dhidden * up * slope).astype(jnp.bfloat16)
    dup = (dhidden * gelu).astype(jnp.bfloat16)
    total_ref[...] += matmul(hidden, fulld_ref[...], 1, 0)
    downg = matmul(jnp.transpose(hidden), cot, 1, 0).astype(jnp.bfloat16)
    gateg = matmul(turned_ref[...], dgate, 1, 0).astype(jnp.bfloat16)
    upg = matmul(turned_ref[...], dup, 1, 0).astype(jnp.bfloat16)
    side = downg.shape[1] // 2
    if piece_count:
        bit_core, bit_ws, bit_dp = bits_ref[0], bits_ref[1], bits_ref[2]
        number = order_ref[step]
        low, high = (number & 1) ^ bits_ref[3], ((number >> 1) & 1) ^ bits_ref[4]
        straight = bit_core == 0
        first_rows, second_rows = downg[: chunk // 2], downg[chunk // 2 :]
        kept = jnp.where(straight, first_rows, second_rows)
        sent = jnp.where(straight, second_rows, first_rows)
        for second in range(2):
            cut = slice(second * side, (second + 1) * side)
            place = (second ^ bit_dp, (number >> 2) ^ bit_ws, low, high, slice(0, chunk // 2))
            downg_ref[place] = kept[:, cut]
            outg_ref[place] = sent[:, cut]

        def store_gate(target_ref):
            for first in range(2):
                rows = slice(first * side, (first + 1) * side)
                target_ref[first ^ bit_ws, 0 ^ bit_dp, 0, 0] = gateg[rows]
                target_ref[first ^ bit_ws, 1 ^ bit_dp, 0, 0] = upg[rows]

        turn = jnp.where(step < own_steps, step >> 1, step & 1) & 1

        @pl.when(turn == 0)
        def _():
            store_gate(gateup_ref)

        @pl.when(turn == 1)
        def _():
            store_gate(extra_ref)

    else:
        downg_ref[...] = downg
        extra_ref[...] = jnp.zeros(extra_ref.shape, jnp.bfloat16)
        gateup_ref[0, 0] = gateg
        gateup_ref[0, 1] = upg
    dsecond_ref[...] += matmul(dgate, fullg_ref[...], 1, 1) + matmul(dup, fullu_ref[...], 1, 1)

    @pl.when(step == last)
    def _():
        middle = middle_ref[...]
        inverse = scale_ref[:, 0:1]
        out_ref[...] = (middle + total_ref[...])[:row_count].astype(jnp.bfloat16)
        normed = middle * inverse
        dsecond = dsecond_ref[...]
        gaing_ref[...] = jnp.sum(dsecond * normed, axis=0, keepdims=True)
        dnormed = dsecond * gain_ref[...]
        dmid = grad_ref[...].astype(jnp.float32) + inverse * (
            dnormed - normed * jnp.mean(dnormed * normed, axis=-1, keepdims=True)
        )
        dmid_ref[...] = dmid
        dbranch = dmid.astype(jnp.bfloat16)
        dmixed_ref[...] = matmul(dbranch, fullo_ref[...], 1, 1).astype(jnp.bfloat16)
        outg = matmul(jnp.transpose(mixed_ref[...]), dbranch, 1, 0).astype(jnp.bfloat16)
        if piece_count:
            store_relative(downg_ref, outg_ref, outg, bits_ref, chunk // 2, True)
        else:
            outg_ref[...] = outg


def store_relative(kept_ref, sent_ref, grad, bits_ref, at, dp_first):
    rows = grad.shape[0] // 16
    width = grad.shape[1] // 2
    bits = [bits_ref[i] for i in range(5)]
    straight = bits[0] == 0
    for number in range(8):
        group, high, low = number >> 2, (number >> 1) & 1, number & 1
        first = grad[2 * number * rows : (2 * number + 1) * rows]
        second = grad[(2 * number + 1) * rows : (2 * number + 2) * rows]
        kept = jnp.where(straight, first, second)
        sent = jnp.where(straight, second, first)
        for side in range(2):
            pair = (side ^ bits[2], group ^ bits[1])
            pair = pair if dp_first else pair[::-1]
            place = pair + (low ^ bits[3], high ^ bits[4], slice(at, at + rows))
            cut = slice(side * width, (side + 1) * width)
            kept_ref[place] = kept[:, cut]
            sent_ref[place] = sent[:, cut]


def feed_forward(place, order, bits, mixed, start, cot, gain, own, gate_pieces, tail_pieces):
    rows, width = start.shape
    row_count = cot.shape[0]
    wo, wg, wu, wd = own
    hidden = wg.shape[1]
    steps = order.shape[0]
    chunk = hidden // steps
    count = len(gate_pieces)
    own_blocks = wd.shape[0] // chunk
    f32, b16 = jnp.float32, jnp.bfloat16

    def whole(array):
        return pl.BlockSpec(array.shape, lambda f, *refs: (0,) * len(array.shape))

    def columns(array):
        if array.ndim == 3:
            shape = array.shape[:2] + (chunk,)
            return pl.BlockSpec(shape, lambda f, place, order, bits: (0, 0, order[f]))
        return pl.BlockSpec((array.shape[0], chunk), lambda f, place, order, bits: (0, order[f]))

    if count:
        gate_shape = (2,) * 4 + (width // 2, chunk)
        tail_shape = (2,) * 4 + (chunk // 2 + width // 16, width // 2)
        grad_shapes = (tail_shape, gate_shape, gate_shape)
        out_grad_shape = tail_shape

        def gate_spec(steps_of):
            def index(f, place, order, bits):
                held = jnp.int32(steps_of[-1])
                for number in range(len(steps_of) - 2, -1, -1):
                    held = jnp.where(f <= number, steps_of[number], held)
                chosen = order[held]
                return 0, 0, ((chosen >> 1) & 1) ^ bits[3], (chosen >> 2) ^ bits[4], 0, 0

            return pl.BlockSpec((2, 2, 1, 1, width // 2, chunk), index)

        grad_specs = [
            pl.BlockSpec(tail_shape, lambda f, *refs: (0,) * len(tail_shape)),
            gate_spec((0, 1, 1, 1, 4, 4, 6, 6)),
            gate_spec((2, 2, 2, 3, 3, 5, 5, 7)),
        ]
    else:
        grad_shapes = ((hidden, width), (steps, 2, width, chunk), (8, tile))
        out_grad_shape = (width, width)
        grad_specs = [
            pl.BlockSpec((chunk, width), lambda f, place, order, bits: (order[f], 0)),
            pl.BlockSpec((1, 2, width, chunk), lambda f, place, order, bits: (order[f], 0, 0, 0)),
            pl.BlockSpec((8, tile), lambda f, place, order, bits: (0, 0)),
        ]
    shapes = (
        jax.ShapeDtypeStruct((row_count, width), b16),
        jax.ShapeDtypeStruct(grad_shapes[0], b16),
        jax.ShapeDtypeStruct(grad_shapes[1], b16),
        jax.ShapeDtypeStruct(grad_shapes[2], b16),
        jax.ShapeDtypeStruct((rows, width), f32),
        jax.ShapeDtypeStruct((rows, width), b16),
        jax.ShapeDtypeStruct(out_grad_shape, b16),
        jax.ShapeDtypeStruct((1, width), f32),
    )
    return pl.pallas_call(
        functools.partial(feed_kernel, piece_count=count, tail_count=len(tail_pieces)),
        out_shape=shapes,
        grid_spec=pltpu.PrefetchScalarGridSpec(
            num_scalar_prefetch=3,
            grid=(steps,),
            in_specs=[whole(mixed), whole(start), whole(cot), whole(gain), whole(wo)]
            + [
                columns(wg), columns(wu),
                pl.BlockSpec(
                    (chunk, width),
                    lambda f, place, order, bits: (
                        order[jnp.minimum(f, own_blocks - 1)] & (own_blocks - 1), 0
                    ),
                ),
            ]
            + [columns(piece) for piece in gate_pieces]
            + [whole(piece) for piece in tail_pieces],
            out_specs=(
                whole(shapes[0]),
                *grad_specs,
                whole(shapes[4]), whole(shapes[5]), whole(shapes[6]), whole(shapes[7]),
            ),
            scratch_shapes=[
                pltpu.VMEM((rows, width), b16),
                pltpu.VMEM((width, rows), b16),
                pltpu.VMEM((rows, width), f32),
                pltpu.VMEM((rows, tile), f32),
                pltpu.VMEM((rows, width), f32),
                pltpu.VMEM((rows, width), f32),
                pltpu.VMEM((rows, width), b16),
                pltpu.VMEM((width, width), b16),
                pltpu.VMEM((width, chunk), b16),
                pltpu.VMEM((width, chunk), b16),
                pltpu.VMEM((chunk, width), b16),
            ],
        ),
        compiler_params=pltpu.CompilerParams(vmem_limit_bytes=46 << 20),
        cost_estimate=cost(26),
        name="feed_forward",
    )(place, order, bits, mixed, start, cot, gain, *own, *gate_pieces, *tail_pieces)


def project_back_kernel(
    place_ref, bits_ref, dq0_ref, dq1_ref, own0_ref, own1_ref, after0_ref, after1_ref, before0_ref,
    before1_ref, first_ref, start_ref, dmid_ref, gain_ref, *refs
):
    pieces = refs[3:-6]
    grads_ref, sent_ref, dstart_ref, gaing_ref, weight_ref, sems = refs[-6:]
    copies = weight_copies(place_ref, refs[:3], pieces, weight_ref, sems)
    width = first_ref.shape[1]
    half = width // 2

    def total(own_ref, after_ref, before_ref):
        return (
            own_ref[...] + after_ref[...].astype(jnp.float32) + before_ref[...].astype(jnp.float32)
        ).astype(jnp.bfloat16)

    sides = (total(own0_ref, after0_ref, before0_ref), total(own1_ref, after1_ref, before1_ref))
    grads = (
        jnp.concatenate([dq0_ref[...], dq1_ref[...]], axis=1),
        jnp.concatenate([side[:, :half] for side in sides], axis=1),
        jnp.concatenate([side[:, half:] for side in sides], axis=1),
    )
    turned = jnp.transpose(first_ref[...])
    for i, grad in enumerate(grads):
        product = matmul(turned, grad, 1, 0).astype(jnp.bfloat16)
        if pieces:
            store_relative(grads_ref, sent_ref, product, bits_ref, i * (width // 16), False)
        else:
            grads_ref[i] = product
    if not pieces:
        sent_ref[...] = jnp.zeros(sent_ref.shape, jnp.bfloat16)
    start = start_ref[...]
    inverse = lax.rsqrt(jnp.mean(start * start, axis=-1, keepdims=True) + epsilon)
    normed = start * inverse
    for copy in copies:
        copy.wait()
    dfirst = sum(matmul(grad, weight_ref[i], 1, 1) for i, grad in enumerate(grads))
    gaing_ref[...] = jnp.sum(dfirst * normed, axis=0, keepdims=True)
    dnormed = dfirst * gain_ref[...]
    dstart_ref[...] = dmid_ref[...] + inverse * (
        dnormed - normed * jnp.mean(dnormed * normed, axis=-1, keepdims=True)
    )


def project_back(place, bits, halves, first, start, dmid, gain, own, pieces):
    rows, width = first.shape
    shape = (2,) * 4 + (3 * (width // 16), width // 2) if pieces else (3, width, width)
    return pl.pallas_call(
        project_back_kernel,
        out_shape=(
            jax.ShapeDtypeStruct(shape, jnp.bfloat16),
            jax.ShapeDtypeStruct(shape if pieces else (8, tile), jnp.bfloat16),
            jax.ShapeDtypeStruct((rows, width), jnp.float32),
            jax.ShapeDtypeStruct((1, width), jnp.float32),
        ),
        in_specs=specs(2, pltpu.SMEM) + specs(12) + specs(3 + len(pieces), pl.ANY),
        out_specs=tuple(specs(4)),
        scratch_shapes=[
            pltpu.VMEM((3, width, width), jnp.bfloat16),
            pltpu.SemaphoreType.DMA((3 + len(pieces),)),
        ],
        compiler_params=pltpu.CompilerParams(vmem_limit_bytes=26 << 20),
        cost_estimate=cost(10),
        name="project_back",
    )(place, bits, *halves, first, start, dmid, gain, *own, *pieces)


def unpool_kernel(
    x_ref, mix_ref, weight_ref, dstart_ref, conv_ref, score_ref,
    dconv_ref, left_ref, right_ref, convg_ref, scoreg_ref,
    wide_ref, square_ref, sums_ref, *, byte_count
):
    lanes = x_ref.shape[0]
    width = lanes * tile
    rows = dstart_ref.shape[0]
    steps = mix_ref.shape[0] * 2 // span
    lead = id_pad + 8
    wide_ref[:rows] = dstart_ref[...]
    wide_ref[rows:] = jnp.zeros((wide_ref.shape[0] - rows, width), jnp.float32)
    for i in range(lanes):
        dconv_ref[i, :lead] = jnp.zeros((lead, tile), jnp.float32)
    sums_ref[...] = jnp.zeros(sums_ref.shape, jnp.float32)
    means = [block_means_grid(size) for size in (1, 2, 3, 4)]

    def unpool(step, carry):
        base = pl.multiple_of(step * span, 8)
        half = pl.ds(pl.multiple_of(step * (span // 2), 8), span // 2)
        conv = jnp.concatenate(conv_tile(x_ref, conv_ref, base + id_pad, lanes), axis=1)
        dstart = wide_ref[half, :]
        dstart_high, dstart_low = split_pair(dstart)
        conv_high, conv_low = split_pair(conv)
        inner = (
            matmul(dstart_high, conv_high, 1, 1)
            + matmul(dstart_low, conv_high, 1, 1)
            + matmul(dstart_high, conv_low, 1, 1)
        )
        inner = jnp.concatenate([inner, jnp.zeros((span // 2, tile - span), jnp.float32)], axis=1)
        square_ref[pl.ds(0, span // 2, stride=2), :] = inner
        square_ref[pl.ds(1, span // 2, stride=2), :] = inner
        inner = square_ref[...]
        weights = [weight_ref[pl.ds(base, span), i : i + 1] for i in range(4)]
        dweights = [0.5 * jnp.sum(mean * inner, axis=1, keepdims=True) for mean in means]
        common = sum(weight * dweight for weight, dweight in zip(weights, dweights))
        dscores = [weight * (dweight - common) for weight, dweight in zip(weights, dweights)]
        row = jnp.sum(
            sum(dscore * mean for dscore, mean in zip(dscores, means)), axis=0, keepdims=True
        )
        column = row_to_column(row)
        mix_high, mix_low = split_pair(mix_ref[half, :][:, :span])
        dconv = (
            matmul(mix_high, dstart_high, 0, 0)
            + matmul(mix_low, dstart_high, 0, 0)
            + matmul(mix_high, dstart_low, 0, 0)
            + column * score_ref[...]
        )
        for i in range(lanes):
            part = dconv[:, i * tile : (i + 1) * tile]
            dconv_ref[i, pl.ds(base + lead, span), :] = part
            for tap in range(conv_width):
                moved = x_ref[i, pl.ds(base + id_pad + tap - conv_width // 2, span), :]
                sums_ref[tap, :, i * tile : (i + 1) * tile] += fold_rows(part * moved, jnp.add)
        sums_ref[conv_width] += fold_rows(column * conv, jnp.add)
        return carry

    lax.fori_loop(0, steps, unpool, 0)
    for tap in range(conv_width):
        convg_ref[tap : tap + 1, :] = jnp.sum(sums_ref[tap], axis=0, keepdims=True)
    scoreg_ref[...] = jnp.sum(sums_ref[conv_width], axis=0, keepdims=True)
    left_ref[...] = spread(dconv_ref, conv_ref, lead - 8, 8)
    right_ref[...] = spread(dconv_ref, conv_ref, lead + byte_count, 8)


def spread(dconv_ref, conv_ref, base, count):
    lanes = dconv_ref.shape[0]
    parts = [
        sum(
            conv_ref[tap : tap + 1, i * tile : (i + 1) * tile]
            * dconv_ref[i, pl.ds(base + conv_width // 2 - tap, count), :]
            for tap in range(conv_width)
        )
        for i in range(lanes)
    ]
    return jnp.concatenate(parts, axis=1)


def unpool(x, mix, weight, dstart, conv, score, byte_count):
    lanes = x.shape[0]
    width = lanes * tile
    f32 = jnp.float32
    half_rows = mix.shape[0]
    return pl.pallas_call(
        functools.partial(unpool_kernel, byte_count=byte_count),
        out_shape=(
            jax.ShapeDtypeStruct((lanes, 2 * half_rows + id_pad + 8, tile), f32),
            jax.ShapeDtypeStruct((8, width), f32),
            jax.ShapeDtypeStruct((8, width), f32),
            jax.ShapeDtypeStruct((conv_width, width), f32),
            jax.ShapeDtypeStruct((1, width), f32),
        ),
        in_specs=specs(6),
        out_specs=tuple(specs(5)),
        scratch_shapes=[
            pltpu.VMEM((half_rows, width), f32),
            pltpu.VMEM((span, tile), f32),
            pltpu.VMEM((conv_width + 1, 8, width), f32),
        ],
        compiler_params=pltpu.CompilerParams(vmem_limit_bytes=20 << 20),
        cost_estimate=cost(13),
        name="unpool",
    )(x, mix, weight, dstart, conv, score)


def scatter_kernel(ids_ref, dconv_ref, conv_ref, byteg_ref, embedg_ref, total_ref):
    byte_count = byteg_ref.shape[0]
    total_ref[...] = jnp.zeros(total_ref.shape, jnp.float32)

    def scatter(step):
        grads = spread(dconv_ref, conv_ref, step * tile + 8, tile)
        ids = ids_ref[step, 0:1, :]
        place = lax.broadcasted_iota(jnp.int32, (total_ref.shape[0], tile), 0)
        hot = (place == ids).astype(jnp.bfloat16)
        grads_high, grads_low = split_pair(grads)
        total_ref[...] += matmul(hot, grads_high, 1, 0) + matmul(hot, grads_low, 1, 0)
        return grads

    scatter(0)

    def whole_tile(step, carry):
        byteg_ref[pl.ds(pl.multiple_of((step - 1) * tile, tile), tile), :] = scatter(step)
        return carry

    full = byte_count // tile
    lax.fori_loop(1, full + 1, whole_tile, 0)
    byteg_ref[full * tile :, :] = scatter(full + 1)[: byte_count - full * tile]
    embedg_ref[...] = total_ref[...].astype(jnp.bfloat16)


def scatter_bytes(ids, dconv, conv, byte_count, vocab):
    width = conv.shape[1]
    table_rows = -(-vocab // 32) * 32
    return pl.pallas_call(
        scatter_kernel,
        out_shape=(
            jax.ShapeDtypeStruct((byte_count, width), jnp.float32),
            jax.ShapeDtypeStruct((table_rows, width), jnp.bfloat16),
        ),
        in_specs=specs(3),
        out_specs=tuple(specs(2)),
        scratch_shapes=[pltpu.VMEM((table_rows, width), jnp.float32)],
        compiler_params=pltpu.CompilerParams(vmem_limit_bytes=16 << 20),
        cost_estimate=cost(10),
        name="scatter_bytes",
    )(ids, dconv, conv)


def edge_kernel(bytes_ref, left_ref, right_ref, out_ref, edge_ref, sems):
    places = (pl.ds(0, 8), pl.ds(out_ref.shape[0] - 8, 8))
    loads = [
        pltpu.make_async_copy(bytes_ref.at[place], edge_ref.at[i], sems.at[i])
        for i, place in enumerate(places)
    ]
    for load in loads:
        load.start()
    for load in loads:
        load.wait()
    edge_ref[0] += left_ref[...]
    edge_ref[1] += right_ref[...]
    stores = [
        pltpu.make_async_copy(edge_ref.at[i], out_ref.at[place], sems.at[i])
        for i, place in enumerate(places)
    ]
    for store in stores:
        store.start()
    for store in stores:
        store.wait()


def add_edges(grads, left, right):
    return pl.pallas_call(
        edge_kernel,
        out_shape=jax.ShapeDtypeStruct(grads.shape, grads.dtype),
        in_specs=specs(1, pl.ANY) + specs(2),
        out_specs=specs(1, pl.ANY)[0],
        scratch_shapes=[
            pltpu.VMEM((2, 8, grads.shape[1]), jnp.float32),
            pltpu.SemaphoreType.DMA((2,)),
        ],
        input_output_aliases={0: 0},
        cost_estimate=cost(1),
        name="add_edges",
    )(grads, left, right)


def finish_kernel(bits_ref, near_ref, across_ref, core_ref, both_ref, *out_refs):
    flip = bits_ref[2] == 0
    for number in range(8):
        high, low, core = number >> 2, (number >> 1) & 1, number & 1
        place = (low ^ bits_ref[3], high ^ bits_ref[4])
        same = (core ^ bits_ref[0]) == 0
        near = jnp.where(same, near_ref[place], core_ref[place]).astype(jnp.float32)
        across = jnp.where(same, across_ref[place], both_ref[place]).astype(jnp.float32)
        first, second = jnp.where(flip, near, across), jnp.where(flip, across, near)
        half = first.shape[1]
        at = 0
        for out_ref in out_refs:
            rows = out_ref.shape[0] // 8
            out_ref[number * rows : (number + 1) * rows, :half] = first[at : at + rows]
            out_ref[number * rows : (number + 1) * rows, half:] = second[at : at + rows]
            at += rows


def finish_square(bits, parts, shapes):
    return pl.pallas_call(
        finish_kernel,
        out_shape=tuple(jax.ShapeDtypeStruct(shape, jnp.float32) for shape in shapes),
        in_specs=specs(1, pltpu.SMEM) + specs(4),
        out_specs=tuple(specs(len(shapes))),
        compiler_params=pltpu.CompilerParams(vmem_limit_bytes=20 << 20),
        cost_estimate=cost(3),
        name="finish_square",
    )(bits, *parts)


def finish_feed_kernel(sum_ref, gate_ref, up_ref, down_ref, out_ref):
    gate_rows, chunk = gate_ref.shape
    down_rows, out_rows = down_ref.shape[0], out_ref.shape[0]
    half = down_ref.shape[1] // 2
    at = 0
    for strip in range(chunk // tile):
        cut = slice(strip * tile, (strip + 1) * tile)
        gate_ref[:, cut] = sum_ref[0, 0, at : at + gate_rows].astype(jnp.float32)
        up_ref[:, cut] = sum_ref[0, 1, at : at + gate_rows].astype(jnp.float32)
        at += gate_rows
    for strip in range(half // tile):
        for side in range(2):
            cut = slice(side * half + strip * tile, side * half + (strip + 1) * tile)
            middle = at + down_rows
            down_ref[:, cut] = sum_ref[0, side, at:middle].astype(jnp.float32)
            out_ref[:, cut] = sum_ref[0, side, middle : middle + out_rows].astype(jnp.float32)
        at += down_rows + out_rows


def finish_feed(total, shapes):
    gate, up, down, out = shapes
    block = pl.BlockSpec((gate[0], gate[1] // 8), lambda f: (0, f))
    return pl.pallas_call(
        finish_feed_kernel,
        grid=(8,),
        out_shape=tuple(jax.ShapeDtypeStruct(shape, jnp.float32) for shape in shapes),
        in_specs=[pl.BlockSpec((1,) + total.shape[1:], lambda f: (f, 0, 0, 0))],
        out_specs=(
            block, block,
            pl.BlockSpec((down[0] // 8, down[1]), lambda f: (f, 0)),
            pl.BlockSpec((out[0] // 8, out[1]), lambda f: (f, 0)),
        ),
        compiler_params=pltpu.CompilerParams(vmem_limit_bytes=60 << 20),
        cost_estimate=cost(5),
        name="finish_feed",
    )(total)


def join_feed_kernel(gate_ref, gate_in_ref, tail_ref, tail_in_ref, *out_refs):
    for number, out_ref in enumerate(out_refs):
        place = (number >> 1, number & 1)
        at = 0
        for kept_ref, in_ref in ((gate_ref, gate_in_ref), (tail_ref, tail_in_ref)):
            rows, width = kept_ref.shape[2:]
            total = kept_ref[place].astype(jnp.float32) + in_ref[place].astype(jnp.float32)
            total = total.astype(jnp.bfloat16)
            for strip in range(width // tile):
                out_ref[at : at + rows] = total[:, strip * tile : (strip + 1) * tile]
                at += rows


def join_feed(gate, gate_in, tail, tail_in):
    rows = sum(block.shape[2] * block.shape[3] // tile for block in (gate, tail))
    shape = jax.ShapeDtypeStruct((rows, tile), jnp.bfloat16)
    return pl.pallas_call(
        join_feed_kernel,
        out_shape=(shape,) * 4,
        in_specs=specs(4),
        out_specs=tuple(specs(4)),
        compiler_params=pltpu.CompilerParams(vmem_limit_bytes=20 << 20),
        cost_estimate=cost(2),
        name="join_feed",
    )(gate, gate_in, tail, tail_in)


sequence_axes = ("z", "core")
copy_axes = ("z", "core", "dp")
all_axes = ("z", "core", "dp", "ws")


def neighbours(block, axes):
    count = 1
    for axis in axes:
        count *= lax.axis_size(axis)
    forward = [(i, i + 1) for i in range(count - 1)]
    backward = [(target, source) for source, target in forward]
    return lax.ppermute(block, axes, forward), lax.ppermute(block, axes, backward)


def pad_rows(block):
    return jnp.pad(block, ((0, -block.shape[0] % tile), (0, 0)))


def send_left(block, count):
    return lax.ppermute(block, sequence_axes, [(i + 1, i) for i in range(count - 1)])


def send_right(block, count):
    return lax.ppermute(block, sequence_axes, [(i, i + 1) for i in range(count - 1)])


def swap(block, axis, distance=1):
    pairs = [(i, i ^ distance) for i in range(lax.axis_size(axis))]
    return lax.ppermute(block, axis, pairs)


def ordered(near, far, place, axis):
    first = place == 0
    return jnp.concatenate([jnp.where(first, near, far), jnp.where(first, far, near)], axis=axis)


def pack(block, small):
    high, low = split_pair(small)
    rest = jnp.zeros((-2 * small.shape[0] % 16, small.shape[1]), jnp.bfloat16)
    return jnp.concatenate([block, high, low, rest])


def unpack(sent, small):
    count = small.shape[0]
    rows = sent.shape[0] - (2 * count + -2 * count % 16)
    high, low = sent[rows : rows + count], sent[rows + count : rows + 2 * count]
    return sent[:rows], small + high.astype(jnp.float32) + low.astype(jnp.float32)


def gather_columns(shard):
    axis = shard.ndim - 1
    if lax.axis_size("ws") != 2:
        return lax.all_gather(shard, "ws", axis=axis, tiled=True)
    return ordered(shard, swap(shard, "ws"), lax.axis_index("ws"), axis)


def own_share(shard, axis):
    share = shard.shape[axis] // 4
    place = lax.axis_index("dp") * 2 + lax.axis_index("core")
    return lax.dynamic_slice_in_dim(shard, place * share, share, axis)


def spread_pieces(first):
    second = swap(first, "dp")
    return first, second, swap(first, "core"), swap(second, "core")


def special_mesh():
    return lax.axis_size("ws") == 2 and lax.axis_size("dp") == 2 and lax.axis_size("z") == 4


def add(*parts):
    return sum(part.astype(jnp.float32) for part in parts).astype(parts[0].dtype)


def swap_high(block, place):
    return swap(block, "z", place[0] + 2 * place[1])


others = ((1, 0), (0, 1), (1, 1))


class Chain:
    def __init__(self, sent, kept, order):
        self.sent, self.kept = (sent,), kept
        self.order = order

    def join(self):
        axis, rest = self.order[0], self.order[1:]
        if axis == "z":
            received = [swap_high(part, place) for part, place in zip(self.sent, others)]
        else:
            received = [swap(self.sent[0], axis)]
        parts = [self.kept] + received
        self.order = rest
        if not rest:
            self.sent, self.kept = (), add(*parts)
            return
        places = others if rest[0] == "z" else ((1,),)
        self.sent = tuple(add(*(part[place] for part in parts)) for place in places)
        own = (0,) * len(places[0])
        self.kept = add(*(part[own] for part in parts))

    def state(self):
        return (self.sent, self.kept)

    def set_state(self, state):
        self.sent, self.kept = state


def gather_high(part):
    return jnp.stack(
        [
            jnp.stack([part, swap_high(part, (0, 1))]),
            jnp.stack([swap_high(part, (1, 0)), swap_high(part, (1, 1))]),
        ]
    )


def collect(part):
    return lax.all_gather(part, copy_axes, axis=0).reshape((8, 2) + part.shape)


def reduce_plain(grad):
    part = lax.psum_scatter(grad, "ws", scatter_dimension=grad.ndim - 2, tiled=True)
    return lax.psum(part, copy_axes).astype(jnp.float32)


def after(value, chains):
    if not special_mesh():
        return value
    value, kept = lax.optimization_barrier((value, [chain.kept for chain in chains]))
    for chain, part in zip(chains, kept):
        chain.kept = part
    return value


def hold(value, chains=()):
    if not special_mesh():
        return value
    value, states = lax.optimization_barrier((value, [chain.state() for chain in chains]))
    for chain, state in zip(chains, states):
        chain.set_state(state)
    return value


def per_device(
    byte_ids,
    segments,
    embed,
    conv_kernel,
    score_weight,
    attn_gain,
    w_q,
    w_k,
    w_v,
    w_o,
    rel_bias,
    ff_gain,
    w_gate,
    w_up,
    w_down,
    cotangent,
):
    byte_count = byte_ids.shape[1]
    row_count = byte_count // 2
    width = w_q.shape[1]
    group_count = lax.axis_size("ws")
    cycle_count = lax.axis_size("z") * lax.axis_size("core")
    cycle_place = lax.axis_index("z") * lax.axis_size("core") + lax.axis_index("core")
    bucket_count, head_count = rel_bias.shape
    rim = conv_width // 2
    has_before = cycle_place > 0
    has_after = cycle_place < cycle_count - 1

    ids = byte_ids[0]
    row_segs = segments[0, ::2]
    note = jnp.concatenate([row_segs, ids[:rim], ids[byte_count - rim :]])
    before_note, after_note = neighbours(note, sequence_axes)
    embed_table = gather_columns(embed)
    if special_mesh():
        core, dp = lax.axis_index("core"), lax.axis_index("dp")
        place = jnp.stack(
            [
                lax.axis_index("ws"), dp * 2 + core, 2 - dp * 2 + core, dp * 2 + 1 - core,
                3 - dp * 2 - core, core, 1 - core,
            ]
        ).astype(jnp.int32)
        own_order = jnp.stack([core, core + 2, 1 - core, 3 - core])
        peer_order = jnp.stack([3 * core, 1 + core, 2 - core, 3 - 3 * core])
        order = jnp.concatenate([place[0] * 4 + own_order, (1 - place[0]) * 4 + peer_order])
        order = order.astype(jnp.int32)
        z = lax.axis_index("z")
        bits = jnp.stack([core, place[0], dp, z & 1, z >> 1]).astype(jnp.int32)
        half = w_q.shape[0] // 2
        square_share = jnp.stack(
            [lax.dynamic_slice_in_dim(weight, core * half, half, 0) for weight in (w_q, w_k, w_v)]
        )
        gate_share = jnp.stack([own_share(weight, 0) for weight in (w_gate, w_up)])
        tail_share = jnp.concatenate(
            [
                lax.dynamic_slice_in_dim(weight, core * (weight.shape[0] // 2), weight.shape[0] // 2, 0)
                for weight in (w_down, w_o)
            ]
        )
        square_first = swap(square_share, "ws")
        square_share, embed_table, before_note, after_note = lax.optimization_barrier(
            (square_share, embed_table, before_note, after_note)
        )
        square_first = swap(square_share, "ws")
        square_place = jnp.stack([place[0], core, 1 - core]).astype(jnp.int32)
        own_square, own_feed = (w_q, w_k, w_v), (w_o, w_gate, w_up, w_down)
    else:
        place = square_place = jnp.zeros((1,), jnp.int32)
        order = jnp.arange(8, dtype=jnp.int32)
        bits = jnp.zeros((5,), jnp.int32)
        square_pieces = gate_pieces = tail_pieces = ()
        own_square, own_feed = (
            tuple(lax.all_gather(weight, "ws", axis=0, tiled=True) for weight in weights)
            for weights in ((w_q, w_k, w_v), (w_o, w_gate, w_up, w_down))
        )
    segs = jnp.stack(
        [
            jnp.where(has_before, before_note[:row_count], -2),
            row_segs,
            jnp.where(has_after, after_note[:row_count], 1 << 20),
        ]
    )
    segs = jnp.pad(segs, ((0, 0), (0, -row_count % tile)), constant_values=-3)
    left_ids = jnp.where(has_before, before_note[row_count + rim :], -1)
    right_ids = jnp.where(has_after, after_note[row_count : row_count + rim], -1)
    id_rows = -(-(byte_count + rim) // tile) * tile
    id_line = jnp.concatenate(
        [
            jnp.full((tile - rim,), -1, jnp.int32),
            left_ids,
            ids,
            right_ids,
            jnp.full((id_rows - byte_count - rim,), -1, jnp.int32),
        ]
    ).reshape(-1, 1, tile)
    conv = jnp.pad(conv_kernel.astype(jnp.float32), ((0, 8 - conv_width), (0, 0)))
    score = score_weight.astype(jnp.float32)[None]
    gain_one = attn_gain[None]
    gain_two = ff_gain[None]

    special = special_mesh()
    half_pairs = width // tile // 2
    start, x_rows, mix, block_weight = gbst_forward(id_line, embed_table, conv, score, row_count)
    if special:
        start, square_first, gate_share = lax.optimization_barrier((start, square_first, gate_share))
        square_pieces = (square_first, swap(square_first, "core"))
        gate_first = swap(gate_share, "ws")
    first_in, queries, own_kv = project(square_place, start, gain_one, own_square, square_pieces)
    if special:
        queries, gate_first, tail_share = lax.optimization_barrier((queries, gate_first, tail_share))
        tail_first = swap(tail_share, "ws")
        gate_second, gate_third = swap(gate_first, "dp"), swap(gate_first, "core")
    before_kv, after_kv = neighbours(own_kv, sequence_axes)
    near_state = attention_forward(segs, queries, (own_kv,), None, rel_bias, row_count)
    if special:
        near_state, before_kv, after_kv, gate_second = lax.optimization_barrier(
            (near_state, before_kv, after_kv, gate_second)
        )
        gate_pieces = (gate_first, gate_second, gate_third, swap(gate_second, "core"))
    attended, log_norm = attention_forward(
        segs, queries, (before_kv, after_kv), near_state, rel_bias, row_count
    )
    if special:
        attended, tail_first = lax.optimization_barrier((attended, tail_first))
        tail_pieces = (tail_first, swap(tail_first, "core"))
    output, down_grad, gate_up_grad, gate_up_sent, d_middle, d_attended, out_grad, ff_gain_grad = feed_forward(
        place, order, bits, attended, start, cotangent[0], gain_two, own_feed, gate_pieces, tail_pieces
    )
    chains = []
    if special:
        gate_chain = Chain(gate_up_sent, gate_up_grad, ("core", "ws", "dp", "z"))
        tail_chain = Chain(out_grad, down_grad, ("core", "dp", "ws", "z"))
        gate_chain.join()
        chains = [gate_chain, tail_chain]
    d_attended = hold(d_attended, chains)
    halves = []
    bias_parts = []
    for part in range(2):
        d_queries, d_before, d_own, d_after, bias_sums = attention_backward(
            segs, queries, d_attended, attended, before_kv, own_kv, after_kv, rel_bias,
            log_norm,            row_count, part * half_pairs, half_pairs,
        )
        active = chains if part else chains[1:]
        d_before, d_after = after((d_before, d_after), active)
        for chain in active:
            chain.join()
        d_attended, d_before, d_after, halves = hold((d_attended, d_before, d_after, halves), active)
        from_after = lax.ppermute(
            d_before, sequence_axes, [(i + 1, i) for i in range(cycle_count - 1)]
        )
        from_before = lax.ppermute(
            d_after, sequence_axes, [(i, i + 1) for i in range(cycle_count - 1)]
        )
        halves.append((d_queries, d_own, from_after, from_before))
        bias_parts.append(jnp.transpose(bias_sums[: 2 * half_pairs, :bucket_count]))
    square_grads, square_sent, d_start, attn_gain_grad = project_back(
        square_place, bits, [part[i] for i in range(4) for part in halves], first_in, start,
        d_middle, gain_one, own_square, square_pieces,
    )
    if special:
        square_chain = Chain(square_sent, square_grads, ("core", "ws", "dp", "z"))
        d_start = after(d_start, chains)
        kept, high, low, both = join_feed(
            gate_chain.kept, swap(gate_chain.sent[0], "dp"),
            tail_chain.kept, swap(tail_chain.sent[0], "ws"),
        )
        feed_chain = Chain(None, kept, ("z",))
        feed_chain.sent = (low, high, both)
        d_start = hold(d_start, [square_chain, feed_chain])
        square_chain.join()
        d_start = hold(d_start, [square_chain])
    d_conv, left_grad, right_grad, conv_grad, score_grad = unpool(
        x_rows, mix, block_weight, d_start, conv, score, byte_count
    )
    bias_grad = jnp.concatenate(bias_parts, axis=1)
    bias_rows = jnp.pad(bias_grad.reshape(1, -1), ((0, 0), (0, width - bucket_count * head_count)))
    small = jnp.concatenate(
        [conv_grad, score_grad, attn_gain_grad, ff_gain_grad, bias_rows], axis=0
    )
    if special:
        d_conv, small = after((d_conv, small), [square_chain])
        square_chain.join()
        d_conv, small = hold((d_conv, small), [square_chain])
    byte_grad, embed_part = scatter_bytes(id_line, d_conv, conv, byte_count, embed.shape[0])
    if special:
        rows = embed_part.shape[0] // 2
        columns = width // 2
        small = small.reshape(-1, columns)
        embed_part = after(embed_part, [feed_chain, square_chain])
        feed_chain.join()
        feed_sum = collect(feed_chain.kept)
        core_rows = lax.dynamic_slice_in_dim(embed_part, bits[0] * rows, rows, 0)
        sent_rows = lax.dynamic_slice_in_dim(embed_part, (1 - bits[0]) * rows, rows, 0)
        sent = pack(sent_rows.reshape(2 * rows, columns), small)
        received, small = unpack(swap(sent, "core"), small)
        embed_part = add(core_rows, received.reshape(rows, width))
        square_chain.join()
        own_columns = lax.dynamic_slice_in_dim(embed_part, bits[1] * columns, columns, 1)
        sent_columns = lax.dynamic_slice_in_dim(embed_part, (1 - bits[1]) * columns, columns, 1)
        sent = pack(sent_columns, small)
        own_columns, small, sent, left_grad = hold(
            (own_columns, small, sent, left_grad), [square_chain]
        )
        from_right = send_left(left_grad, cycle_count)
        received, small = unpack(swap(sent, "ws"), small)
        embed_part = add(own_columns, received)
        square_chain.join()
        square_part = square_chain.kept
        sent = pack(embed_part, small)
        embed_part, small, sent, square_part, from_right, right_grad = hold(
            (embed_part, small, sent, square_part, from_right, right_grad)
        )
        from_left = send_right(right_grad, cycle_count)
        received, small = unpack(swap(sent, "dp"), small)
        embed_part = add(embed_part, received)
        square_part = gather_high(square_part)
        sent = pack(embed_part, small)
        embed_part, small, sent, square_part, from_left = hold(
            (embed_part, small, sent, square_part, from_left)
        )
        byte_grad = add_edges(byte_grad, from_left, from_right)
        parts = [embed_part]
        for place in others:
            received, small = unpack(swap_high(sent, place), small)
            parts.append(received)
        embed_part = add(*parts)
        square_across = swap(square_part, "dp")
        square_core = swap(square_part, "core")
        embed_part, small, square_across, square_core, byte_grad = hold(
            (embed_part, small, square_across, square_core, byte_grad)
        )
        square_both = swap(square_across, "core")
        embed_part = ordered(embed_part, swap(embed_part, "core"), bits[0], 0)
        square_both, embed_part, small = hold((square_both, embed_part, small))
        query_sum, key_sum, value_sum = finish_square(
            bits, (square_part, square_across, square_core, square_both), ((columns, width),) * 3
        )
        embed_part, query_sum = hold((embed_part, query_sum))
        gate_sum, up_sum, down_sum, out_sum = finish_feed(
            feed_sum,
            (
                (columns, w_gate.shape[1]), (columns, w_gate.shape[1]),
                (w_down.shape[0], width), (columns, width),
            ),
        )
        small = small.reshape(-1, width)
    else:
        small = lax.psum(small, all_axes)
        embed_part = lax.psum_scatter(embed_part, "ws", scatter_dimension=1, tiled=True)
        embed_part = lax.psum(embed_part, copy_axes)
    embed_sum = embed_part[: embed.shape[0]].astype(jnp.float32)
    if not special:
        from_right = send_left(left_grad, cycle_count)
        from_left = send_right(right_grad, cycle_count)
        byte_grad = add_edges(byte_grad, from_left, from_right)
        gate_sum, up_sum = jnp.transpose(reduce_plain(gate_up_grad), (1, 2, 0, 3)).reshape(
            2, width // group_count, -1
        )
        down_sum, out_sum = reduce_plain(down_grad), reduce_plain(out_grad)
        query_sum, key_sum, value_sum = reduce_plain(square_grads)
    return (
        output[None],
        byte_grad[None],
        embed_sum,
        small[:conv_width],
        small[conv_width],
        small[conv_width + 1],
        query_sum,
        key_sum,
        value_sum,
        out_sum,
        small[conv_width + 3, : bucket_count * head_count].reshape(bucket_count, head_count),
        small[conv_width + 2],
        gate_sum,
        up_sum,
        down_sum,
    )


def solution(mesh):
    devices = mesh.devices
    fine = Mesh(devices.reshape((devices.shape[0] // 2, 2) + devices.shape[1:]), all_axes)
    rows = P(("dp", "ws"), sequence_axes)
    split = P("ws", None)
    in_specs = (
        rows, rows, P(None, "ws"), P(), P(), P(), split, split, split, split, P(), P(),
        split, split, split, P(("dp", "ws"), sequence_axes, None),
    )
    wide = P(("dp", "ws"), sequence_axes, None)
    out_specs = (
        wide, wide, P(None, "ws"), P(), P(), P(), split, split, split, split, P(), P(),
        split, split, split,
    )
    return jax.shard_map(
        per_device, mesh=fine, in_specs=in_specs, out_specs=out_specs, check_vma=False
    )
```

```python
import functools

import jax
import jax.numpy as jnp
from jax import lax
from jax.experimental import pallas as pl
from jax.experimental.pallas import tpu as pltpu
from jax.sharding import Mesh
from jax.sharding import PartitionSpec as P

thresholds = (12, 16, 23, 32, 46, 64, 91)
negative = -1e30
epsilon = 1e-06
conv_width = 5
tile = 128
near_bases = (-128, -120, 0, 120, 128)
class_count = len(near_bases) + 2


def bucket_of(relative):
    distance = jnp.abs(relative)
    far_bucket = 8 + sum(((distance >= threshold).astype(jnp.int32) for threshold in thresholds))
    near_bucket = jnp.where(distance < 8, distance, far_bucket)
    return near_bucket + 16 * (relative > 0).astype(jnp.int32)


def matmul(left, right, left_dim, right_dim):
    return lax.dot_general(
        left, right, (((left_dim,), (right_dim,)), ((), ())), preferred_element_type=jnp.float32
    )


def split_pair(values):
    high = values.astype(jnp.bfloat16)
    return high, (values - high.astype(jnp.float32)).astype(jnp.bfloat16)


def tile_class(query_tile, key_tile):
    step = key_tile - query_tile - 4
    own = jnp.where(
        step <= -2, 0, jnp.where(step == -1, 1, jnp.where(step == 0, 3, jnp.where(step == 1, 5, 6)))
    )
    before = jnp.where(step == -1, 2, 0)
    after = jnp.where(step == 1, 4, 6)
    return jnp.where(key_tile < 4, before, jnp.where(key_tile < 8, own, after))


def key_range(seg_ref, query_tile, row_count, tiles_per_block):
    first_seg = seg_ref[1, query_tile * tile]
    last_seg = seg_ref[1, jnp.minimum(query_tile * tile + tile, row_count) - 1]
    low = jnp.int32(0)
    high = jnp.int32(0)
    for block in range(3):
        for part in range(tiles_per_block):
            key_first = seg_ref[block, part * tile]
            key_last = seg_ref[block, min(part * tile + tile, row_count) - 1]
            low = low + (key_last < first_seg).astype(jnp.int32)
            high = high + (key_first <= last_seg).astype(jnp.int32)
    return low, high


def class_buckets(kind, shape, dim):
    place = lax.broadcasted_iota(jnp.int32, shape, dim)
    swing = jnp.where(place < tile, place, place - 2 * tile)
    if kind == 0:
        return jnp.full(shape, bucket_of(jnp.int32(-4 * tile)))
    if kind == class_count - 1:
        return jnp.full(shape, bucket_of(jnp.int32(4 * tile)))
    return bucket_of(near_bases[kind - 1] - swing)


def make_bias(rel_ref, bias_ref, first_pair, pair_count):
    bucket_count = rel_ref.shape[0]
    for kind in range(class_count):
        shape = (bucket_count, 2 * tile)
        hot = class_buckets(kind, shape, 1) == lax.broadcasted_iota(jnp.int32, shape, 0)
        lines = lax.dot_general(
            rel_ref[...], hot.astype(jnp.float32), (((0,), (0,)), ((), ())),
            precision=lax.Precision.HIGHEST, preferred_element_type=jnp.float32,
        )
        for pair in range(pair_count):
            for half in range(2):
                head = 2 * (first_pair + pair) + half
                grid = jnp.broadcast_to(lines[head : head + 1], (tile, 2 * tile))
                if 0 < kind < class_count - 1:
                    grid = pltpu.roll(grid, 0, 1, stride=1, stride_axis=0)
                bias_ref[kind, pair, :, half * tile : (half + 1) * tile] = grid[:, :tile]


def cost(microseconds):
    return pl.CostEstimate(
        flops=int(microseconds * 1e7), transcendentals=0, bytes_accessed=int(microseconds * 3e4)
    )


def stack_heads(block):
    lane = lax.broadcasted_iota(jnp.int32, block.shape, 1)
    zero = jnp.zeros_like(block)
    return jnp.concatenate(
        [jnp.where(lane < tile // 2, block, zero), jnp.where(lane < tile // 2, zero, block)], axis=0
    )


def fold_rows(values, combine):
    pieces = [values[8 * i : 8 * i + 8] for i in range(values.shape[0] // 8)]
    while len(pieces) > 1:
        joined = [combine(pieces[i], pieces[i + 1]) for i in range(0, len(pieces) - 1, 2)]
        if len(pieces) % 2:
            joined.append(pieces[-1])
        pieces = joined
    return pieces[0]


def key_columns(segs_ref, column_ref, key_tile):
    row = segs_ref[key_tile, 0:1, :]
    column_ref[key_tile] = jnp.transpose(jnp.broadcast_to(row, (tile, tile)))


def start_copies(sources, window_ref, sems, first_pair):
    rows, full_width = sources[0].shape
    width = window_ref.shape[1] // 2
    copies = []
    for i, source in enumerate(sources):
        for side in range(2):
            copies.append(
                pltpu.make_async_copy(
                    source.at[:, pl.ds(side * (full_width // 2) + first_pair * tile, width)],
                    window_ref.at[pl.ds(rows * i, rows), pl.ds(side * width, width)],
                    sems.at[2 * i + side],
                )
            )
    for copy in copies:
        copy.start()
    return copies


def forward_kernel(seg_ref, q_ref, *refs, row_count, near):
    if near:
        source_refs, refs = refs[:1], refs[1:]
    else:
        source_refs, refs = refs[:2], refs[2:]
        (mixed_in_ref, top_in_ref, total_in_ref), refs = refs[:3], refs[3:]
    segs_ref, qsegs_ref, rel_ref = refs[:3]
    if near:
        mixed_ref, top_ref, total_ref = refs[3:6]
    else:
        out_ref, lse_ref = refs[3:5]
    window_ref, bias_ref, column_ref, flipped_ref, score_ref = refs[-6 if near else -7 :][:5]
    sems = refs[-1]
    if not near:
        mixed_ref = refs[-2]
    width = q_ref.shape[1]
    pair_count = width // tile
    query_tiles = q_ref.shape[0] // tile
    half = tile // 2
    middle = query_tiles // 2
    copies = start_copies(source_refs, window_ref, sems, 0)
    make_bias(rel_ref, bias_ref, 0, pair_count)

    def key_span(query_tile):
        low, high = key_range(seg_ref, query_tile, row_count, query_tiles)
        if near:
            low = jnp.maximum(low - query_tiles, 0)
            high = jnp.minimum(high - query_tiles, query_tiles)
            return low // 2, (high + 1) // 2
        return jnp.minimum(low // 2, middle), jnp.maximum((high + 1) // 2 - middle, middle)

    def global_tile(key_pair, part):
        key_tile = 2 * key_pair + part
        if near:
            return key_tile + query_tiles
        return key_tile + jnp.where(key_pair >= middle, query_tiles, 0)

    first = key_span(0)[0]
    last = key_span(query_tiles - 1)[1]
    for copy in copies:
        copy.wait()

    def prepare(key_pair, carry):
        for part in range(2):
            row = segs_ref[global_tile(key_pair, part), 0:1, :]
            column_ref[2 * key_pair + part] = jnp.transpose(jnp.broadcast_to(row, (tile, tile)))
        at = pl.multiple_of(key_pair * 2 * tile, 2 * tile)
        flipped_ref[key_pair] = jnp.transpose(window_ref[pl.ds(at, 2 * tile), width:])
        return carry

    lax.fori_loop(first, last, prepare, 0)

    def query_step(query_tile, carry):
        low, high = key_span(query_tile)
        rows = pl.ds(pl.multiple_of(query_tile * tile, tile), tile)
        lanes = [slice(pair * tile, (pair + 1) * tile) for pair in range(pair_count)]
        stacked = [stack_heads(q_ref[rows, lane]) for lane in lanes]
        query_seg = qsegs_ref[query_tile, 0:1, :]
        slot = query_tile if near else 0

        def score_step(key_pair, tops):
            keys = pl.ds(pl.multiple_of(key_pair * 2 * tile, 2 * tile), 2 * tile)
            hides = []
            kinds = []
            for part in range(2):
                hide = jnp.where(column_ref[2 * key_pair + part] == query_seg, 0.0, negative)
                hides.append(jnp.concatenate([hide, hide], axis=1))
                kinds.append(tile_class(query_tile, global_tile(key_pair, part)))
            fresh = []
            for pair in range(pair_count):
                scores = matmul(window_ref[keys, lanes[pair]], stacked[pair], 1, 1)
                top = tops[pair]
                for part in range(2):
                    cut = slice(part * tile, (part + 1) * tile)
                    piece = scores[cut] + bias_ref[kinds[part], pair] + hides[part]
                    score_ref[key_pair, pair, cut] = piece
                    top = jnp.maximum(top, fold_rows(piece, jnp.maximum))
                fresh.append(top)
            return tuple(fresh)

        tops = lax.fori_loop(
            low, high, score_step,
            tuple(jnp.full((8, 2 * tile), negative, jnp.float32) for _ in range(pair_count)),
        )
        tops = [jnp.max(top, axis=0, keepdims=True) for top in tops]
        scales = []
        for pair in range(pair_count):
            if near:
                mixed_ref[slot, pair] = jnp.zeros((tile, tile), jnp.float32)
            else:
                before = top_in_ref[query_tile, pair : pair + 1, :]
                tops[pair] = jnp.maximum(tops[pair], before)
                scale = jnp.exp(before - tops[pair])
                scales.append(scale)
                mixed_ref[slot, pair, :half] = mixed_in_ref[query_tile, pair, :half] * scale[:, :tile]
                mixed_ref[slot, pair, half:] = mixed_in_ref[query_tile, pair, half:] * scale[:, tile:]

        def mix_step(key_pair, totals):
            fresh = []
            for pair in range(pair_count):
                exponent = jnp.exp(score_ref[key_pair, pair] - tops[pair])
                fresh.append(totals[pair] + fold_rows(exponent, jnp.add))
                mixed = matmul(
                    flipped_ref[key_pair, lanes[pair], :], exponent.astype(jnp.bfloat16), 1, 0
                )
                mixed_ref[slot, pair, :half] += mixed[:half, :tile]
                mixed_ref[slot, pair, half:] += mixed[half:, tile:]
            return tuple(fresh)

        totals = lax.fori_loop(
            low, high, mix_step,
            tuple(jnp.zeros((8, 2 * tile), jnp.float32) for _ in range(pair_count)),
        )
        for pair in range(pair_count):
            total = jnp.sum(totals[pair], axis=0, keepdims=True)
            if near:
                top_ref[query_tile, pair : pair + 1, :] = tops[pair]
                total_ref[query_tile, pair : pair + 1, :] = total
                continue
            total = total + total_in_ref[query_tile, pair : pair + 1, :] * scales[pair]
            lse_ref[query_tile, pair : pair + 1, :] = tops[pair] + jnp.log(total)
            inverse = 1.0 / total
            scaled = jnp.concatenate(
                [
                    mixed_ref[slot, pair, :half] * inverse[:, :tile],
                    mixed_ref[slot, pair, half:] * inverse[:, tile:],
                ],
                axis=0,
            )
            out_ref[rows, lanes[pair]] = jnp.transpose(scaled).astype(jnp.bfloat16)
        return carry

    lax.fori_loop(0, query_tiles, query_step, 0)


def backward_kernel(
    seg_ref, q_ref, do_ref, o_ref, before_ref, own_ref, after_ref, segs_ref, qsegs_ref, rel_ref, lse_ref,
    dq_ref, dbefore_ref, down_ref, dafter_ref, bias_out_ref,
    window_ref, bias_ref, column_ref, flipped_ref, dbias_ref, dwindow_ref, dq_acc_ref, delta_ref, sems,
    *, row_count, first_pair
):
    width = dq_ref.shape[1]
    pair_count = width // tile
    query_tiles = q_ref.shape[0] // tile
    block_rows = q_ref.shape[0]
    half = tile // 2
    copies = start_copies((before_ref, own_ref, after_ref), window_ref, sems, first_pair)
    make_bias(rel_ref, bias_ref, first_pair, pair_count)
    dwindow_ref[...] = jnp.zeros(dwindow_ref.shape, jnp.float32)
    dbias_ref[...] = jnp.zeros(dbias_ref.shape, jnp.float32)
    product = do_ref[...].astype(jnp.float32) * o_ref[...].astype(jnp.float32)
    product_high, product_low = split_pair(product)
    member = (
        lax.broadcasted_iota(jnp.int32, (16, width), 1) // half
        == lax.broadcasted_iota(jnp.int32, (16, width), 0)
    ).astype(jnp.bfloat16)
    delta_ref[...] = matmul(member, product_high, 1, 1) + matmul(member, product_low, 1, 1)
    first = key_range(seg_ref, 0, row_count, query_tiles)[0]
    last = key_range(seg_ref, query_tiles - 1, row_count, query_tiles)[1]
    for copy in copies:
        copy.wait()

    def prepare(key_pair, carry):
        for part in range(2):
            key_columns(segs_ref, column_ref, 2 * key_pair + part)
        at = pl.multiple_of(key_pair * 2 * tile, 2 * tile)
        flipped_ref[key_pair] = jnp.transpose(window_ref[pl.ds(at, 2 * tile), :width])
        return carry

    lax.fori_loop(first // 2, (last + 1) // 2, prepare, 0)

    def query_step(query_tile, carry):
        low, high = key_range(seg_ref, query_tile, row_count, query_tiles)
        at = pl.multiple_of(query_tile * tile, tile)
        rows = pl.ds(at, tile)
        lanes = [slice(pair * tile, (pair + 1) * tile) for pair in range(pair_count)]
        queries = [stack_heads(q_ref[rows, lane]) for lane in lanes]
        grads = [stack_heads(do_ref[rows, lane]) for lane in lanes]
        query_seg = qsegs_ref[query_tile, 0:1, :]
        deltas = [
            jnp.concatenate(
                [delta_ref[2 * pair : 2 * pair + 1, rows], delta_ref[2 * pair + 1 : 2 * pair + 2, rows]],
                axis=1,
            )
            for pair in range(pair_count)
        ]
        norms = [
            lse_ref[query_tile, first_pair + pair : first_pair + pair + 1, :]
            for pair in range(pair_count)
        ]
        for pair in range(pair_count):
            dq_acc_ref[pair] = jnp.zeros((tile, tile), jnp.float32)

        def key_step(key_pair, carry):
            keys = pl.ds(pl.multiple_of(key_pair * 2 * tile, 2 * tile), 2 * tile)
            hides = []
            kinds = []
            for part in range(2):
                key_tile = 2 * key_pair + part
                hide = jnp.where(column_ref[key_tile] == query_seg, 0.0, negative)
                hides.append(jnp.concatenate([hide, hide], axis=1))
                kinds.append(tile_class(query_tile, key_tile))
            for pair in range(pair_count):
                lane = lanes[pair]
                value_lane = slice(width + pair * tile, width + (pair + 1) * tile)
                scores = matmul(window_ref[keys, lane], queries[pair], 1, 1)
                dprobs = matmul(window_ref[keys, value_lane], grads[pair], 1, 1)
                probs_low, dscores_low = [], []
                for part in range(2):
                    cut = slice(part * tile, (part + 1) * tile)
                    probs = jnp.exp(
                        scores[cut] + bias_ref[kinds[part], pair] + hides[part] - norms[pair]
                    )
                    dscores = probs * (dprobs[cut] - deltas[pair])
                    dbias_ref[kinds[part], pair] += dscores
                    probs_low.append(probs.astype(jnp.bfloat16))
                    dscores_low.append(dscores.astype(jnp.bfloat16))
                probs_low = jnp.concatenate(probs_low, axis=0)
                dscores_low = jnp.concatenate(dscores_low, axis=0)
                dwindow_ref[keys, lane] += matmul(dscores_low, queries[pair], 1, 0)
                dwindow_ref[keys, value_lane] += matmul(probs_low, grads[pair], 1, 0)
                dquery = matmul(flipped_ref[key_pair, lane, :], dscores_low, 1, 0)
                dq_acc_ref[pair, :half] += dquery[:half, :tile]
                dq_acc_ref[pair, half:] += dquery[half:, tile:]
            return carry

        lax.fori_loop(low // 2, (high + 1) // 2, key_step, 0)
        for pair in range(pair_count):
            dq_ref[rows, lanes[pair]] = jnp.transpose(dq_acc_ref[pair]).astype(jnp.bfloat16)
        return carry

    lax.fori_loop(0, query_tiles, query_step, 0)
    dbefore_ref[...] = dwindow_ref[:block_rows].astype(jnp.bfloat16)
    down_ref[...] = dwindow_ref[block_rows : 2 * block_rows]
    dafter_ref[...] = dwindow_ref[2 * block_rows :].astype(jnp.bfloat16)
    turn = (
        lax.broadcasted_iota(jnp.int32, (tile, tile), 0)
        + lax.broadcasted_iota(jnp.int32, (tile, tile), 1)
        == tile - 1
    ).astype(jnp.bfloat16)
    zero_half = jnp.zeros((tile, tile), jnp.float32)
    bucket_count = rel_ref.shape[0]
    total = jnp.zeros(bias_out_ref.shape, jnp.float32)
    for kind in range(class_count):
        lines = []
        for pair in range(pair_count):
            grid = dbias_ref[kind, pair]
            near = 0 < kind < class_count - 1
            if near:
                grid_high, grid_low = split_pair(grid)
                grid = matmul(turn, grid_high, 1, 0) + matmul(turn, grid_low, 1, 0)
            for side in range(2):
                part = jnp.concatenate([grid[:, side * tile : (side + 1) * tile], zero_half], axis=1)
                if near:
                    part = pltpu.roll(part, tile + 1, 1, stride=1, stride_axis=0)
                lines.append(jnp.sum(fold_rows(part, jnp.add), axis=0, keepdims=True))
        lines.append(jnp.zeros((bias_out_ref.shape[0] - len(lines), 2 * tile), jnp.float32))
        shape = (2 * tile, tile)
        hot = class_buckets(kind, shape, 0) == lax.broadcasted_iota(jnp.int32, shape, 1)
        total = total + jnp.dot(
            jnp.concatenate(lines, axis=0), hot.astype(jnp.float32),
            precision=lax.Precision.HIGHEST, preferred_element_type=jnp.float32,
        )
    bias_out_ref[...] = total


def specs(count, space=pltpu.VMEM):
    return [pl.BlockSpec(memory_space=space) for _ in range(count)]


def attention_forward(segs, q, sources, state, rel_bias, row_count):
    rows, width = q.shape
    tiles = rows // tile
    pairs = width // tile
    near = state is None
    seg_rows = segs.reshape(3 * tiles, 1, tile)
    query_segs = mark_queries(segs, row_count).reshape(tiles, 1, tile)
    f32 = jnp.float32
    norm = jax.ShapeDtypeStruct((tiles, 8, 2 * tile), f32)
    mixed = jax.ShapeDtypeStruct((tiles, pairs, tile, tile), f32)
    count = len(sources)
    blocks = count * tiles // 2
    scratch = [
        pltpu.VMEM((count * rows, 2 * width), jnp.bfloat16),
        pltpu.VMEM((class_count, pairs, tile, 2 * tile), f32),
        pltpu.VMEM((count * tiles, tile, tile), jnp.int32),
        pltpu.VMEM((blocks, width, 2 * tile), jnp.bfloat16),
        pltpu.VMEM((blocks, pairs, 2 * tile, 2 * tile), f32),
    ]
    if not near:
        scratch.append(pltpu.VMEM((1, pairs, tile, tile), f32))
    return pl.pallas_call(
        functools.partial(forward_kernel, row_count=row_count, near=near),
        out_shape=(mixed, norm, norm)
        if near
        else (jax.ShapeDtypeStruct((rows, width), jnp.bfloat16), norm),
        in_specs=specs(1, pltpu.SMEM) + specs(1) + specs(count, pl.ANY)
        + specs(3 if near else 6),
        out_specs=tuple(specs(3 if near else 2)),
        scratch_shapes=scratch + [pltpu.SemaphoreType.DMA((2 * count,))],
        compiler_params=pltpu.CompilerParams(vmem_limit_bytes=(22 if near else 30) << 20),
        cost_estimate=cost(12),
        name="attention_near" if near else "attention_rim",
    )(segs, q, *sources, *(state or ()), seg_rows, query_segs, rel_bias)


def mark_queries(segs, row_count):
    place = jnp.arange(segs.shape[1], dtype=jnp.int32)
    return jnp.where(place < row_count, segs[1], -1)


def attention_backward(
    segs, q, do, o, before, own, after, rel_bias, lse, row_count, first_pair, pairs
):
    rows, full_width = q.shape
    tiles = rows // tile
    width = pairs * tile
    seg_rows = segs.reshape(3 * tiles, 1, tile)
    query_segs = mark_queries(segs, row_count).reshape(tiles, 1, tile)
    part = pl.BlockSpec((rows, width), lambda i: (0, first_pair // pairs))
    return pl.pallas_call(
        functools.partial(backward_kernel, row_count=row_count, first_pair=first_pair),
        grid=(1,),
        out_shape=(
            jax.ShapeDtypeStruct((rows, width), jnp.bfloat16),
            jax.ShapeDtypeStruct((rows, 2 * width), jnp.bfloat16),
            jax.ShapeDtypeStruct((rows, 2 * width), jnp.float32),
            jax.ShapeDtypeStruct((rows, 2 * width), jnp.bfloat16),
            jax.ShapeDtypeStruct((8, tile), jnp.float32),
        ),
        in_specs=specs(1, pltpu.SMEM) + [part, part, part] + specs(3, pl.ANY) + specs(4),
        out_specs=tuple(specs(5)),
        scratch_shapes=[
            pltpu.VMEM((3 * rows, 2 * width), jnp.bfloat16),
            pltpu.VMEM((class_count, pairs, tile, 2 * tile), jnp.float32),
            pltpu.VMEM((3 * tiles, tile, tile), jnp.int32),
            pltpu.VMEM((3 * tiles // 2, width, 2 * tile), jnp.bfloat16),
            pltpu.VMEM((class_count, pairs, tile, 2 * tile), jnp.float32),
            pltpu.VMEM((3 * rows, 2 * width), jnp.float32),
            pltpu.VMEM((pairs, tile, tile), jnp.float32),
            pltpu.VMEM((16, rows), jnp.float32),
            pltpu.SemaphoreType.DMA((6,)),
        ],
        compiler_params=pltpu.CompilerParams(vmem_limit_bytes=30 << 20),
        cost_estimate=cost(20),
        name="attention_backward",
    )(segs, q, do, o, before, own, after, seg_rows, query_segs, rel_bias, lse)


span = 96
id_pad = 128


def dot3(left, right, left_dim, right_dim):
    left_high, left_low = split_pair(left)
    right_high, right_low = split_pair(right)
    return (
        matmul(left_high, right_high, left_dim, right_dim)
        + matmul(left_low, right_high, left_dim, right_dim)
        + matmul(left_high, right_low, left_dim, right_dim)
    )


def block_means_grid(block_size):
    row = lax.broadcasted_iota(jnp.int32, (span, tile), 0)
    lane = lax.broadcasted_iota(jnp.int32, (span, tile), 1)
    same = (row // block_size == lane // block_size) & (lane < span)
    return jnp.where(same, 1.0 / block_size, 0.0)


def row_to_column(row):
    lane = lax.broadcasted_iota(jnp.int32, (span, tile), 1)
    place = lax.broadcasted_iota(jnp.int32, (span, tile), 0)
    return jnp.sum(jnp.where(lane == place, row, 0.0), axis=1, keepdims=True)


def column_to_row(column):
    lane = lax.broadcasted_iota(jnp.int32, (span, tile), 1)
    place = lax.broadcasted_iota(jnp.int32, (span, tile), 0)
    return jnp.sum(jnp.where(lane == place, column, 0.0), axis=0, keepdims=True)


def conv_tile(x_ref, conv_ref, base, lanes):
    taps = range(conv_width)
    return [
        sum(
            conv_ref[tap : tap + 1, i * tile : (i + 1) * tile]
            * x_ref[i, pl.ds(base + tap - conv_width // 2, span), :]
            for tap in taps
        )
        for i in range(lanes)
    ]


def gbst_forward_kernel(
    ids_ref, embed_ref, conv_ref, score_ref,
    start_ref, x_ref, mix_ref, weight_ref,
    table_ref, square_ref, wide_ref,
):
    vocab, width = embed_ref.shape
    lanes = width // tile
    id_tiles = ids_ref.shape[0]
    rows = start_ref.shape[0]
    table_ref[...] = jnp.zeros(table_ref.shape, jnp.bfloat16)
    table_ref[:vocab] = embed_ref[...]
    table_rows = table_ref.shape[0]
    rest = x_ref.shape[1] - id_tiles * tile
    for i in range(lanes):
        x_ref[i, id_tiles * tile :, :] = jnp.zeros((rest, tile), jnp.float32)

    def lookup(step, carry):
        ids = jnp.transpose(jnp.broadcast_to(ids_ref[step, 0:1, :], (tile, tile)))
        lane = lax.broadcasted_iota(jnp.int32, (tile, tile), 1)
        hot = jnp.concatenate(
            [(ids == lane + tile * i).astype(jnp.bfloat16) for i in range(table_rows // tile)], axis=1
        )
        found = matmul(hot, table_ref[...], 1, 0)
        at = pl.ds(pl.multiple_of(step * tile, tile), tile)
        for i in range(lanes):
            x_ref[i, at, :] = found[:, i * tile : (i + 1) * tile]
        return carry

    lax.fori_loop(0, id_tiles, lookup, 0)
    means = [block_means_grid(size) for size in (1, 2, 3, 4)]

    def pool(step, carry):
        base = pl.multiple_of(step * span, 8)
        conv = conv_tile(x_ref, conv_ref, base + id_pad, lanes)
        total = sum(conv[i] * score_ref[0:1, i * tile : (i + 1) * tile] for i in range(lanes))
        row = column_to_row(jnp.sum(total, axis=1, keepdims=True))
        scores = [jnp.sum(mean * row, axis=1, keepdims=True) for mean in means]
        top = functools.reduce(jnp.maximum, scores)
        exponents = [jnp.exp(score - top) for score in scores]
        inverse = 1.0 / sum(exponents)
        weights = [exponent * inverse for exponent in exponents]
        square_ref[...] = sum(weight * mean for weight, mean in zip(weights, means))
        mix = 0.5 * (
            square_ref[pl.ds(0, span // 2, stride=2), :] + square_ref[pl.ds(1, span // 2, stride=2), :]
        )
        half = pl.ds(pl.multiple_of(step * (span // 2), 8), span // 2)
        mix_ref[half, :] = mix
        lane = lax.broadcasted_iota(jnp.int32, (span, tile), 1)
        packed = jnp.zeros((span, tile), jnp.float32)
        for i in range(4):
            packed = jnp.where(lane == i, weights[i], packed)
        weight_ref[pl.ds(base, span), :] = packed
        wide_ref[half, :] = dot3(mix[:, :span], jnp.concatenate(conv, axis=1), 1, 0)
        return carry

    steps = mix_ref.shape[0] * 2 // span
    lax.fori_loop(0, steps, pool, 0, unroll=steps)
    start_ref[...] = wide_ref[:rows]


def gbst_forward(ids, embed, conv, score, row_count):
    vocab, width = embed.shape
    rows = -(-row_count // tile) * tile
    steps = -(-2 * row_count // span)
    x_rows = max(ids.shape[0] * tile, id_pad + steps * span) + 8
    f32 = jnp.float32
    return pl.pallas_call(
        gbst_forward_kernel,
        out_shape=(
            jax.ShapeDtypeStruct((rows, width), f32),
            jax.ShapeDtypeStruct((width // tile, x_rows, tile), f32),
            jax.ShapeDtypeStruct((steps * span // 2, tile), f32),
            jax.ShapeDtypeStruct((steps * span, tile), f32),
        ),
        in_specs=specs(4),
        out_specs=tuple(specs(4)),
        scratch_shapes=[
            pltpu.VMEM((-(-vocab // tile) * tile, width), jnp.bfloat16),
            pltpu.VMEM((span, tile), f32),
            pltpu.VMEM((steps * span // 2, width), f32),
        ],
        compiler_params=pltpu.CompilerParams(vmem_limit_bytes=18 << 20),
        cost_estimate=cost(12),
        name="gbst_forward",
    )(ids, embed, conv, score)


def weight_copies(place_ref, parts, pieces, full_ref, sems):
    copies = []
    rows = parts[0].shape[0]
    for i, part in enumerate(parts):
        at = pl.multiple_of(place_ref[0] * rows, rows)
        copies.append(
            pltpu.make_async_copy(part, full_ref.at[i, pl.ds(at, rows)], sems.at[len(copies)])
        )
    for number, piece in enumerate(pieces):
        share = piece.shape[1]
        at = pl.multiple_of((1 - place_ref[0]) * rows + place_ref[1 + number] * share, share)
        copies.append(
            pltpu.make_async_copy(piece, full_ref.at[:, pl.ds(at, share)], sems.at[len(copies)])
        )
    for copy in copies:
        copy.start()
    return copies


def project_kernel(place_ref, start_ref, gain_ref, *refs):
    pieces = refs[3:-5]
    first_ref, q_ref, kv_ref, weight_ref, sems = refs[-5:]
    copies = weight_copies(place_ref, refs[:3], pieces, weight_ref, sems)
    width = q_ref.shape[1]
    start = start_ref[...]
    inverse = lax.rsqrt(jnp.mean(start * start, axis=-1, keepdims=True) + epsilon)
    first = (start * inverse * gain_ref[...]).astype(jnp.bfloat16)
    first_ref[...] = first
    for copy in copies:
        copy.wait()
    q_ref[...] = matmul(first, weight_ref[0], 1, 0).astype(jnp.bfloat16)
    kv_ref[:, :width] = matmul(first, weight_ref[1], 1, 0).astype(jnp.bfloat16)
    kv_ref[:, width:] = matmul(first, weight_ref[2], 1, 0).astype(jnp.bfloat16)


def project(place, start, gain, own, pieces):
    rows, width = start.shape
    b16 = jnp.bfloat16
    return pl.pallas_call(
        project_kernel,
        out_shape=(
            jax.ShapeDtypeStruct((rows, width), b16),
            jax.ShapeDtypeStruct((rows, width), b16),
            jax.ShapeDtypeStruct((rows, 2 * width), b16),
        ),
        in_specs=specs(1, pltpu.SMEM) + specs(2) + specs(3 + len(pieces), pl.ANY),
        out_specs=tuple(specs(3)),
        scratch_shapes=[
            pltpu.VMEM((3, width, width), b16),
            pltpu.SemaphoreType.DMA((3 + len(pieces),)),
        ],
        compiler_params=pltpu.CompilerParams(vmem_limit_bytes=60 << 20),
        cost_estimate=cost(6),
        name="project",
    )(place, start, gain, *own, *pieces)


def feed_kernel(
    place_ref, order_ref, bits_ref, mixed_ref, start_ref, cot_ref, gain_ref, *refs, piece_count, tail_count
):
    (wo_ref, wg_ref, wu_ref, wd_ref), refs = refs[:4], refs[4:]
    gate_pieces, refs = refs[:piece_count], refs[piece_count:]
    tail_pieces, refs = refs[:tail_count], refs[tail_count:]
    (
        out_ref, downg_ref, gateup_ref, extra_ref, dmid_ref, dmixed_ref, outg_ref, gaing_ref,
        second_ref, turned_ref, middle_ref, scale_ref, total_ref, dsecond_ref, grad_ref,
        fullo_ref, fullg_ref, fullu_ref, fulld_ref, slot_ref, slot_sems,
    ) = refs
    step = pl.program_id(0)
    last = pl.num_programs(0) - 1
    row_count = out_ref.shape[0]
    chunk = fulld_ref.shape[0]

    def fill(full_ref, own_ref, pieces, pick, base=1):
        rows = own_ref.shape[0]
        full_ref[pl.ds(pl.multiple_of(place_ref[0] * rows, rows), rows), :] = own_ref[...]
        for number, piece in enumerate(pieces):
            block = pick(piece)
            share = block.shape[0]
            at = (1 - place_ref[0]) * rows + place_ref[base + number] * share
            full_ref[pl.ds(pl.multiple_of(at, share), share), :] = block

    @pl.when(step == 0)
    def _():
        fill(fullo_ref, wo_ref, tail_pieces, lambda piece: piece[2 * chunk :], 5)
        middle = start_ref[...] + matmul(mixed_ref[...], fullo_ref[...], 1, 0)
        middle_ref[...] = middle
        inverse = lax.rsqrt(jnp.mean(middle * middle, axis=-1, keepdims=True) + epsilon)
        scale_ref[...] = jnp.broadcast_to(inverse, scale_ref.shape)
        second = (middle * inverse * gain_ref[...]).astype(jnp.bfloat16)
        second_ref[...] = second
        turned_ref[...] = jnp.transpose(second)
        total_ref[...] = jnp.zeros(total_ref.shape, jnp.float32)
        dsecond_ref[...] = jnp.zeros(dsecond_ref.shape, jnp.float32)
        grad_ref[:row_count] = cot_ref[...]
        grad_ref[row_count:] = jnp.zeros((grad_ref.shape[0] - row_count, grad_ref.shape[1]), jnp.bfloat16)

    fill(fullg_ref, wg_ref, gate_pieces, lambda piece: piece[0])
    fill(fullu_ref, wu_ref, gate_pieces, lambda piece: piece[1])
    own_steps = pl.num_programs(0) - piece_count

    @pl.when(step < own_steps)
    def _():
        fulld_ref[...] = wd_ref[...]

    for number in range(tail_count):

        @pl.when((step >= own_steps) & ((step - own_steps) >> 1 == number))
        def _():
            at = pl.multiple_of((order_ref[step] & 1) * chunk, chunk)
            fulld_ref[...] = tail_pieces[number][pl.ds(at, chunk), :]

    second = second_ref[...]
    cot = grad_ref[...]
    gate = matmul(second, fullg_ref[...], 1, 0)
    up = matmul(second, fullu_ref[...], 1, 0)
    dhidden = matmul(cot, fulld_ref[...], 1, 1)
    root = 0.7978845608028654
    square = gate * gate
    bend = jnp.tanh(root * (gate + 0.044715 * (square * gate)))
    rise = 0.5 * (1.0 + bend)
    gelu = gate * rise
    slope = rise + 0.5 * gate * (1.0 - bend * bend) * (root * (1.0 + 3 * 0.044715 * square))
    hidden = (gelu * up).astype(jnp.bfloat16)
    dgate = (dhidden * up * slope).astype(jnp.bfloat16)
    dup = (dhidden * gelu).astype(jnp.bfloat16)
    total_ref[...] += matmul(hidden, fulld_ref[...], 1, 0)
    downg = matmul(jnp.transpose(hidden), cot, 1, 0).astype(jnp.bfloat16)
    gateg = matmul(turned_ref[...], dgate, 1, 0).astype(jnp.bfloat16)
    upg = matmul(turned_ref[...], dup, 1, 0).astype(jnp.bfloat16)
    side = downg.shape[1] // 2
    if piece_count:
        bit_core, bit_ws, bit_dp = bits_ref[0], bits_ref[1], bits_ref[2]
        number = order_ref[step]
        low, high = (number & 1) ^ bits_ref[3], ((number >> 1) & 1) ^ bits_ref[4]
        straight = bit_core == 0
        first_rows, second_rows = downg[: chunk // 2], downg[chunk // 2 :]
        kept = jnp.where(straight, first_rows, second_rows)
        sent = jnp.where(straight, second_rows, first_rows)
        for second in range(2):
            cut = slice(second * side, (second + 1) * side)
            place = (second ^ bit_dp, (number >> 2) ^ bit_ws, low, high, slice(0, chunk // 2))
            downg_ref[place] = kept[:, cut]
            outg_ref[place] = sent[:, cut]

        slot = step & 1

        def leave(target_ref, place):
            return pltpu.make_async_copy(
                slot_ref.at[slot], target_ref.at[:, :, place[0], place[1]], slot_sems.at[slot]
            )

        @pl.when(step >= 2)
        def _():
            leave(gateup_ref, (0, 0)).wait()

        for first in range(2):
            rows = slice(first * side, (first + 1) * side)
            slot_ref[slot, first ^ bit_ws, 0 ^ bit_dp] = gateg[rows]
            slot_ref[slot, first ^ bit_ws, 1 ^ bit_dp] = upg[rows]
        turn = jnp.where(step < own_steps, step >> 1, step & 1) & 1
        place = (((number >> 1) & 1) ^ bits_ref[3], (number >> 2) ^ bits_ref[4])

        @pl.when(turn == 0)
        def _():
            leave(gateup_ref, place).start()

        @pl.when(turn == 1)
        def _():
            leave(extra_ref, place).start()

    else:
        downg_ref[...] = downg
        extra_ref[...] = jnp.zeros(extra_ref.shape, jnp.bfloat16)
        gateup_ref[0, 0] = gateg
        gateup_ref[0, 1] = upg
    dsecond_ref[...] += matmul(dgate, fullg_ref[...], 1, 1) + matmul(dup, fullu_ref[...], 1, 1)

    @pl.when(step == last)
    def _():
        middle = middle_ref[...]
        inverse = scale_ref[:, 0:1]
        out_ref[...] = (middle + total_ref[...])[:row_count].astype(jnp.bfloat16)
        normed = middle * inverse
        dsecond = dsecond_ref[...]
        gaing_ref[...] = jnp.sum(dsecond * normed, axis=0, keepdims=True)
        dnormed = dsecond * gain_ref[...]
        dmid = grad_ref[...].astype(jnp.float32) + inverse * (
            dnormed - normed * jnp.mean(dnormed * normed, axis=-1, keepdims=True)
        )
        dmid_ref[...] = dmid
        dbranch = dmid.astype(jnp.bfloat16)
        dmixed_ref[...] = matmul(dbranch, fullo_ref[...], 1, 1).astype(jnp.bfloat16)
        outg = matmul(jnp.transpose(mixed_ref[...]), dbranch, 1, 0).astype(jnp.bfloat16)
        if piece_count:
            store_relative(downg_ref, outg_ref, outg, bits_ref, chunk // 2, True)
            for slot in range(2):
                pltpu.make_async_copy(
                    slot_ref.at[slot], gateup_ref.at[:, :, 0, 0], slot_sems.at[slot]
                ).wait()
        else:
            outg_ref[...] = outg


def store_relative(kept_ref, sent_ref, grad, bits_ref, at, dp_first):
    rows = grad.shape[0] // 16
    width = grad.shape[1] // 2
    bits = [bits_ref[i] for i in range(5)]
    straight = bits[0] == 0
    for number in range(8):
        group, high, low = number >> 2, (number >> 1) & 1, number & 1
        first = grad[2 * number * rows : (2 * number + 1) * rows]
        second = grad[(2 * number + 1) * rows : (2 * number + 2) * rows]
        kept = jnp.where(straight, first, second)
        sent = jnp.where(straight, second, first)
        for side in range(2):
            pair = (side ^ bits[2], group ^ bits[1])
            pair = pair if dp_first else pair[::-1]
            place = pair + (low ^ bits[3], high ^ bits[4], slice(at, at + rows))
            cut = slice(side * width, (side + 1) * width)
            kept_ref[place] = kept[:, cut]
            sent_ref[place] = sent[:, cut]


def feed_forward(place, order, bits, mixed, start, cot, gain, own, gate_pieces, tail_pieces):
    rows, width = start.shape
    row_count = cot.shape[0]
    wo, wg, wu, wd = own
    hidden = wg.shape[1]
    steps = order.shape[0]
    chunk = hidden // steps
    count = len(gate_pieces)
    own_blocks = wd.shape[0] // chunk
    f32, b16 = jnp.float32, jnp.bfloat16

    def whole(array):
        return pl.BlockSpec(array.shape, lambda f, *refs: (0,) * len(array.shape))

    def columns(array):
        if array.ndim == 3:
            shape = array.shape[:2] + (chunk,)
            return pl.BlockSpec(shape, lambda f, place, order, bits: (0, 0, order[f]))
        return pl.BlockSpec((array.shape[0], chunk), lambda f, place, order, bits: (0, order[f]))

    if count:
        gate_shape = (2,) * 4 + (width // 2, chunk)
        tail_shape = (2,) * 4 + (chunk // 2 + width // 16, width // 2)
        grad_shapes = (tail_shape, gate_shape, gate_shape)
        out_grad_shape = tail_shape

        grad_specs = [
            pl.BlockSpec(tail_shape, lambda f, *refs: (0,) * len(tail_shape)),
            pl.BlockSpec(memory_space=pl.ANY),
            pl.BlockSpec(memory_space=pl.ANY),
        ]
    else:
        grad_shapes = ((hidden, width), (steps, 2, width, chunk), (8, tile))
        out_grad_shape = (width, width)
        grad_specs = [
            pl.BlockSpec((chunk, width), lambda f, place, order, bits: (order[f], 0)),
            pl.BlockSpec((1, 2, width, chunk), lambda f, place, order, bits: (order[f], 0, 0, 0)),
            pl.BlockSpec((8, tile), lambda f, place, order, bits: (0, 0)),
        ]
    shapes = (
        jax.ShapeDtypeStruct((row_count, width), b16),
        jax.ShapeDtypeStruct(grad_shapes[0], b16),
        jax.ShapeDtypeStruct(grad_shapes[1], b16),
        jax.ShapeDtypeStruct(grad_shapes[2], b16),
        jax.ShapeDtypeStruct((rows, width), f32),
        jax.ShapeDtypeStruct((rows, width), b16),
        jax.ShapeDtypeStruct(out_grad_shape, b16),
        jax.ShapeDtypeStruct((1, width), f32),
    )
    return pl.pallas_call(
        functools.partial(feed_kernel, piece_count=count, tail_count=len(tail_pieces)),
        out_shape=shapes,
        grid_spec=pltpu.PrefetchScalarGridSpec(
            num_scalar_prefetch=3,
            grid=(steps,),
            in_specs=[whole(mixed), whole(start), whole(cot), whole(gain), whole(wo)]
            + [
                columns(wg), columns(wu),
                pl.BlockSpec(
                    (chunk, width),
                    lambda f, place, order, bits: (
                        order[jnp.minimum(f, own_blocks - 1)] & (own_blocks - 1), 0
                    ),
                ),
            ]
            + [columns(piece) for piece in gate_pieces]
            + [whole(piece) for piece in tail_pieces],
            out_specs=(
                whole(shapes[0]),
                *grad_specs,
                whole(shapes[4]), whole(shapes[5]), whole(shapes[6]), whole(shapes[7]),
            ),
            scratch_shapes=[
                pltpu.VMEM((rows, width), b16),
                pltpu.VMEM((width, rows), b16),
                pltpu.VMEM((rows, width), f32),
                pltpu.VMEM((rows, tile), f32),
                pltpu.VMEM((rows, width), f32),
                pltpu.VMEM((rows, width), f32),
                pltpu.VMEM((rows, width), b16),
                pltpu.VMEM((width, width), b16),
                pltpu.VMEM((width, chunk), b16),
                pltpu.VMEM((width, chunk), b16),
                pltpu.VMEM((chunk, width), b16),
                pltpu.VMEM((2, 2, 2, width // 2, chunk), b16),
                pltpu.SemaphoreType.DMA((2,)),
            ],
        ),
        compiler_params=pltpu.CompilerParams(vmem_limit_bytes=46 << 20),
        cost_estimate=cost(26),
        name="feed_forward",
    )(place, order, bits, mixed, start, cot, gain, *own, *gate_pieces, *tail_pieces)


def project_back_kernel(
    place_ref, bits_ref, dq0_ref, dq1_ref, own0_ref, own1_ref, after0_ref, after1_ref, before0_ref,
    before1_ref, first_ref, start_ref, dmid_ref, gain_ref, *refs
):
    pieces = refs[3:-6]
    grads_ref, sent_ref, dstart_ref, gaing_ref, weight_ref, sems = refs[-6:]
    copies = weight_copies(place_ref, refs[:3], pieces, weight_ref, sems)
    width = first_ref.shape[1]
    half = width // 2

    def total(own_ref, after_ref, before_ref):
        return (
            own_ref[...] + after_ref[...].astype(jnp.float32) + before_ref[...].astype(jnp.float32)
        ).astype(jnp.bfloat16)

    sides = (total(own0_ref, after0_ref, before0_ref), total(own1_ref, after1_ref, before1_ref))
    grads = (
        jnp.concatenate([dq0_ref[...], dq1_ref[...]], axis=1),
        jnp.concatenate([side[:, :half] for side in sides], axis=1),
        jnp.concatenate([side[:, half:] for side in sides], axis=1),
    )
    turned = jnp.transpose(first_ref[...])
    for i, grad in enumerate(grads):
        product = matmul(turned, grad, 1, 0).astype(jnp.bfloat16)
        if pieces:
            store_relative(grads_ref, sent_ref, product, bits_ref, i * (width // 16), False)
        else:
            grads_ref[i] = product
    if not pieces:
        sent_ref[...] = jnp.zeros(sent_ref.shape, jnp.bfloat16)
    start = start_ref[...]
    inverse = lax.rsqrt(jnp.mean(start * start, axis=-1, keepdims=True) + epsilon)
    normed = start * inverse
    for copy in copies:
        copy.wait()
    dfirst = sum(matmul(grad, weight_ref[i], 1, 1) for i, grad in enumerate(grads))
    gaing_ref[...] = jnp.sum(dfirst * normed, axis=0, keepdims=True)
    dnormed = dfirst * gain_ref[...]
    dstart_ref[...] = dmid_ref[...] + inverse * (
        dnormed - normed * jnp.mean(dnormed * normed, axis=-1, keepdims=True)
    )


def project_back(place, bits, halves, first, start, dmid, gain, own, pieces):
    rows, width = first.shape
    shape = (2,) * 4 + (3 * (width // 16), width // 2) if pieces else (3, width, width)
    return pl.pallas_call(
        project_back_kernel,
        out_shape=(
            jax.ShapeDtypeStruct(shape, jnp.bfloat16),
            jax.ShapeDtypeStruct(shape if pieces else (8, tile), jnp.bfloat16),
            jax.ShapeDtypeStruct((rows, width), jnp.float32),
            jax.ShapeDtypeStruct((1, width), jnp.float32),
        ),
        in_specs=specs(2, pltpu.SMEM) + specs(12) + specs(3 + len(pieces), pl.ANY),
        out_specs=tuple(specs(4)),
        scratch_shapes=[
            pltpu.VMEM((3, width, width), jnp.bfloat16),
            pltpu.SemaphoreType.DMA((3 + len(pieces),)),
        ],
        compiler_params=pltpu.CompilerParams(vmem_limit_bytes=26 << 20),
        cost_estimate=cost(10),
        name="project_back",
    )(place, bits, *halves, first, start, dmid, gain, *own, *pieces)


def unpool_kernel(
    x_ref, mix_ref, weight_ref, dstart_ref, conv_ref, score_ref,
    dconv_ref, left_ref, right_ref, convg_ref, scoreg_ref,
    wide_ref, square_ref, sums_ref, *, byte_count
):
    lanes = x_ref.shape[0]
    width = lanes * tile
    rows = dstart_ref.shape[0]
    steps = mix_ref.shape[0] * 2 // span
    lead = id_pad + 8
    wide_ref[:rows] = dstart_ref[...]
    wide_ref[rows:] = jnp.zeros((wide_ref.shape[0] - rows, width), jnp.float32)
    for i in range(lanes):
        dconv_ref[i, :lead] = jnp.zeros((lead, tile), jnp.float32)
    sums_ref[...] = jnp.zeros(sums_ref.shape, jnp.float32)
    means = [block_means_grid(size) for size in (1, 2, 3, 4)]

    def unpool(step, carry):
        base = pl.multiple_of(step * span, 8)
        half = pl.ds(pl.multiple_of(step * (span // 2), 8), span // 2)
        conv = jnp.concatenate(conv_tile(x_ref, conv_ref, base + id_pad, lanes), axis=1)
        dstart = wide_ref[half, :]
        dstart_high, dstart_low = split_pair(dstart)
        conv_high, conv_low = split_pair(conv)
        inner = (
            matmul(dstart_high, conv_high, 1, 1)
            + matmul(dstart_low, conv_high, 1, 1)
            + matmul(dstart_high, conv_low, 1, 1)
        )
        inner = jnp.concatenate([inner, jnp.zeros((span // 2, tile - span), jnp.float32)], axis=1)
        square_ref[pl.ds(0, span // 2, stride=2), :] = inner
        square_ref[pl.ds(1, span // 2, stride=2), :] = inner
        inner = square_ref[...]
        weights = [weight_ref[pl.ds(base, span), i : i + 1] for i in range(4)]
        dweights = [0.5 * jnp.sum(mean * inner, axis=1, keepdims=True) for mean in means]
        common = sum(weight * dweight for weight, dweight in zip(weights, dweights))
        dscores = [weight * (dweight - common) for weight, dweight in zip(weights, dweights)]
        row = jnp.sum(
            sum(dscore * mean for dscore, mean in zip(dscores, means)), axis=0, keepdims=True
        )
        column = row_to_column(row)
        mix_high, mix_low = split_pair(mix_ref[half, :][:, :span])
        dconv = (
            matmul(mix_high, dstart_high, 0, 0)
            + matmul(mix_low, dstart_high, 0, 0)
            + matmul(mix_high, dstart_low, 0, 0)
            + column * score_ref[...]
        )
        for i in range(lanes):
            part = dconv[:, i * tile : (i + 1) * tile]
            dconv_ref[i, pl.ds(base + lead, span), :] = part
            for tap in range(conv_width):
                moved = x_ref[i, pl.ds(base + id_pad + tap - conv_width // 2, span), :]
                sums_ref[tap, :, i * tile : (i + 1) * tile] += fold_rows(part * moved, jnp.add)
        sums_ref[conv_width] += fold_rows(column * conv, jnp.add)
        return carry

    lax.fori_loop(0, steps, unpool, 0, unroll=steps)
    for tap in range(conv_width):
        convg_ref[tap : tap + 1, :] = jnp.sum(sums_ref[tap], axis=0, keepdims=True)
    scoreg_ref[...] = jnp.sum(sums_ref[conv_width], axis=0, keepdims=True)
    left_ref[...] = spread(dconv_ref, conv_ref, lead - 8, 8)
    right_ref[...] = spread(dconv_ref, conv_ref, lead + byte_count, 8)


def spread(dconv_ref, conv_ref, base, count):
    lanes = dconv_ref.shape[0]
    parts = [
        sum(
            conv_ref[tap : tap + 1, i * tile : (i + 1) * tile]
            * dconv_ref[i, pl.ds(base + conv_width // 2 - tap, count), :]
            for tap in range(conv_width)
        )
        for i in range(lanes)
    ]
    return jnp.concatenate(parts, axis=1)


def unpool(x, mix, weight, dstart, conv, score, byte_count):
    lanes = x.shape[0]
    width = lanes * tile
    f32 = jnp.float32
    half_rows = mix.shape[0]
    return pl.pallas_call(
        functools.partial(unpool_kernel, byte_count=byte_count),
        out_shape=(
            jax.ShapeDtypeStruct((lanes, 2 * half_rows + id_pad + 8, tile), f32),
            jax.ShapeDtypeStruct((8, width), f32),
            jax.ShapeDtypeStruct((8, width), f32),
            jax.ShapeDtypeStruct((conv_width, width), f32),
            jax.ShapeDtypeStruct((1, width), f32),
        ),
        in_specs=specs(6),
        out_specs=tuple(specs(5)),
        scratch_shapes=[
            pltpu.VMEM((half_rows, width), f32),
            pltpu.VMEM((span, tile), f32),
            pltpu.VMEM((conv_width + 1, 8, width), f32),
        ],
        compiler_params=pltpu.CompilerParams(vmem_limit_bytes=10 << 20),
        cost_estimate=cost(13),
        name="unpool",
    )(x, mix, weight, dstart, conv, score)


def scatter_kernel(ids_ref, dconv_ref, conv_ref, byteg_ref, embedg_ref, total_ref):
    byte_count = byteg_ref.shape[0]
    total_ref[...] = jnp.zeros(total_ref.shape, jnp.float32)

    def scatter(step):
        grads = spread(dconv_ref, conv_ref, step * tile + 8, tile)
        ids = ids_ref[step, 0:1, :]
        place = lax.broadcasted_iota(jnp.int32, (total_ref.shape[0], tile), 0)
        hot = (place == ids).astype(jnp.bfloat16)
        grads_high, grads_low = split_pair(grads)
        total_ref[...] += matmul(hot, grads_high, 1, 0) + matmul(hot, grads_low, 1, 0)
        return grads

    scatter(0)

    def whole_tile(step, carry):
        byteg_ref[pl.ds(pl.multiple_of((step - 1) * tile, tile), tile), :] = scatter(step)
        return carry

    full = byte_count // tile
    lax.fori_loop(1, full + 1, whole_tile, 0, unroll=full)
    byteg_ref[full * tile :, :] = scatter(full + 1)[: byte_count - full * tile]
    embedg_ref[...] = total_ref[...].astype(jnp.bfloat16)


def scatter_bytes(ids, dconv, conv, byte_count, vocab):
    width = conv.shape[1]
    table_rows = -(-vocab // 32) * 32
    return pl.pallas_call(
        scatter_kernel,
        out_shape=(
            jax.ShapeDtypeStruct((byte_count, width), jnp.float32),
            jax.ShapeDtypeStruct((table_rows, width), jnp.bfloat16),
        ),
        in_specs=specs(3),
        out_specs=tuple(specs(2)),
        scratch_shapes=[pltpu.VMEM((table_rows, width), jnp.float32)],
        compiler_params=pltpu.CompilerParams(vmem_limit_bytes=8 << 20),
        cost_estimate=cost(10),
        name="scatter_bytes",
    )(ids, dconv, conv)


def edge_kernel(bytes_ref, left_ref, right_ref, out_ref, edge_ref, sems):
    places = (pl.ds(0, 8), pl.ds(out_ref.shape[0] - 8, 8))
    loads = [
        pltpu.make_async_copy(bytes_ref.at[place], edge_ref.at[i], sems.at[i])
        for i, place in enumerate(places)
    ]
    for load in loads:
        load.start()
    for load in loads:
        load.wait()
    edge_ref[0] += left_ref[...]
    edge_ref[1] += right_ref[...]
    stores = [
        pltpu.make_async_copy(edge_ref.at[i], out_ref.at[place], sems.at[i])
        for i, place in enumerate(places)
    ]
    for store in stores:
        store.start()
    for store in stores:
        store.wait()


def add_edges(grads, left, right):
    return pl.pallas_call(
        edge_kernel,
        out_shape=jax.ShapeDtypeStruct(grads.shape, grads.dtype),
        in_specs=specs(1, pl.ANY) + specs(2),
        out_specs=specs(1, pl.ANY)[0],
        scratch_shapes=[
            pltpu.VMEM((2, 8, grads.shape[1]), jnp.float32),
            pltpu.SemaphoreType.DMA((2,)),
        ],
        input_output_aliases={0: 0},
        cost_estimate=cost(1),
        name="add_edges",
    )(grads, left, right)


def finish_kernel(bits_ref, near_ref, across_ref, core_ref, both_ref, *out_refs):
    flip = bits_ref[2] == 0
    for number in range(8):
        high, low, core = number >> 2, (number >> 1) & 1, number & 1
        place = (low ^ bits_ref[3], high ^ bits_ref[4])
        same = (core ^ bits_ref[0]) == 0
        near = jnp.where(same, near_ref[place], core_ref[place]).astype(jnp.float32)
        across = jnp.where(same, across_ref[place], both_ref[place]).astype(jnp.float32)
        first, second = jnp.where(flip, near, across), jnp.where(flip, across, near)
        half = first.shape[1]
        at = 0
        for out_ref in out_refs:
            rows = out_ref.shape[0] // 8
            out_ref[number * rows : (number + 1) * rows, :half] = first[at : at + rows]
            out_ref[number * rows : (number + 1) * rows, half:] = second[at : at + rows]
            at += rows


def finish_square(bits, parts, shapes):
    return pl.pallas_call(
        finish_kernel,
        out_shape=tuple(jax.ShapeDtypeStruct(shape, jnp.float32) for shape in shapes),
        in_specs=specs(1, pltpu.SMEM) + specs(4),
        out_specs=tuple(specs(len(shapes))),
        compiler_params=pltpu.CompilerParams(vmem_limit_bytes=20 << 20),
        cost_estimate=cost(3),
        name="finish_square",
    )(bits, *parts)


def finish_feed_kernel(sum_ref, gate_ref, up_ref, down_ref, out_ref):
    blocks = sum_ref.shape[0]
    gate_rows, chunk = gate_ref.shape[0], gate_ref.shape[1] // blocks
    down_rows, out_rows = down_ref.shape[0] // blocks, out_ref.shape[0] // blocks
    half = down_ref.shape[1] // 2
    for number in range(blocks):
        at = 0
        for strip in range(chunk // tile):
            cut = slice(number * chunk + strip * tile, number * chunk + (strip + 1) * tile)
            gate_ref[:, cut] = sum_ref[number, 0, at : at + gate_rows].astype(jnp.float32)
            up_ref[:, cut] = sum_ref[number, 1, at : at + gate_rows].astype(jnp.float32)
            at += gate_rows
        for strip in range(half // tile):
            for side in range(2):
                cut = slice(side * half + strip * tile, side * half + (strip + 1) * tile)
                middle = at + down_rows
                down = sum_ref[number, side, at:middle]
                out = sum_ref[number, side, middle : middle + out_rows]
                down_ref[number * down_rows : (number + 1) * down_rows, cut] = down.astype(jnp.float32)
                out_ref[number * out_rows : (number + 1) * out_rows, cut] = out.astype(jnp.float32)
            at += down_rows + out_rows


def finish_feed(total, shapes):
    gate, up, down, out = shapes
    grid = 4
    block = pl.BlockSpec((gate[0], gate[1] // grid), lambda f: (0, f))
    return pl.pallas_call(
        finish_feed_kernel,
        grid=(grid,),
        out_shape=tuple(jax.ShapeDtypeStruct(shape, jnp.float32) for shape in shapes),
        in_specs=[pl.BlockSpec((8 // grid,) + total.shape[1:], lambda f: (f, 0, 0, 0))],
        out_specs=(
            block, block,
            pl.BlockSpec((down[0] // grid, down[1]), lambda f: (f, 0)),
            pl.BlockSpec((out[0] // grid, out[1]), lambda f: (f, 0)),
        ),
        compiler_params=pltpu.CompilerParams(vmem_limit_bytes=60 << 20),
        cost_estimate=cost(5),
        name="finish_feed",
    )(total)


def join_feed_kernel(gate_ref, gate_in_ref, tail_ref, tail_in_ref, *out_refs):
    for number, out_ref in enumerate(out_refs):
        place = (number >> 1, number & 1)
        at = 0
        for kept_ref, in_ref in ((gate_ref, gate_in_ref), (tail_ref, tail_in_ref)):
            rows, width = kept_ref.shape[2:]
            total = kept_ref[place].astype(jnp.float32) + in_ref[place].astype(jnp.float32)
            total = total.astype(jnp.bfloat16)
            for strip in range(width // tile):
                out_ref[at : at + rows] = total[:, strip * tile : (strip + 1) * tile]
                at += rows


def join_feed(gate, gate_in, tail, tail_in):
    rows = sum(block.shape[2] * block.shape[3] // tile for block in (gate, tail))
    shape = jax.ShapeDtypeStruct((rows, tile), jnp.bfloat16)
    return pl.pallas_call(
        join_feed_kernel,
        out_shape=(shape,) * 4,
        in_specs=specs(4),
        out_specs=tuple(specs(4)),
        compiler_params=pltpu.CompilerParams(vmem_limit_bytes=20 << 20),
        cost_estimate=cost(2),
        name="join_feed",
    )(gate, gate_in, tail, tail_in)


sequence_axes = ("z", "core")
copy_axes = ("z", "core", "dp")
all_axes = ("z", "core", "dp", "ws")


def neighbours(block, axes):
    count = 1
    for axis in axes:
        count *= lax.axis_size(axis)
    forward = [(i, i + 1) for i in range(count - 1)]
    backward = [(target, source) for source, target in forward]
    return lax.ppermute(block, axes, forward), lax.ppermute(block, axes, backward)


def pad_rows(block):
    return jnp.pad(block, ((0, -block.shape[0] % tile), (0, 0)))


def send_left(block, count):
    return lax.ppermute(block, sequence_axes, [(i + 1, i) for i in range(count - 1)])


def send_right(block, count):
    return lax.ppermute(block, sequence_axes, [(i, i + 1) for i in range(count - 1)])


def swap(block, axis, distance=1):
    pairs = [(i, i ^ distance) for i in range(lax.axis_size(axis))]
    return lax.ppermute(block, axis, pairs)


def ordered(near, far, place, axis):
    first = place == 0
    return jnp.concatenate([jnp.where(first, near, far), jnp.where(first, far, near)], axis=axis)


def pack(block, small):
    high, low = split_pair(small)
    rest = jnp.zeros((-2 * small.shape[0] % 16, small.shape[1]), jnp.bfloat16)
    return jnp.concatenate([block, high, low, rest])


def unpack(sent, small):
    count = small.shape[0]
    rows = sent.shape[0] - (2 * count + -2 * count % 16)
    high, low = sent[rows : rows + count], sent[rows + count : rows + 2 * count]
    return sent[:rows], small + high.astype(jnp.float32) + low.astype(jnp.float32)


def gather_columns(shard):
    axis = shard.ndim - 1
    if lax.axis_size("ws") != 2:
        return lax.all_gather(shard, "ws", axis=axis, tiled=True)
    return ordered(shard, swap(shard, "ws"), lax.axis_index("ws"), axis)


def own_share(shard, axis):
    share = shard.shape[axis] // 4
    place = lax.axis_index("dp") * 2 + lax.axis_index("core")
    return lax.dynamic_slice_in_dim(shard, place * share, share, axis)


def spread_pieces(first):
    second = swap(first, "dp")
    return first, second, swap(first, "core"), swap(second, "core")


def special_mesh():
    return lax.axis_size("ws") == 2 and lax.axis_size("dp") == 2 and lax.axis_size("z") == 4


def add(*parts):
    return sum(part.astype(jnp.float32) for part in parts).astype(parts[0].dtype)


def swap_high(block, place):
    return swap(block, "z", place[0] + 2 * place[1])


others = ((1, 0), (0, 1), (1, 1))


class Chain:
    def __init__(self, sent, kept, order):
        self.sent, self.kept = (sent,), kept
        self.order = order
        self.received = ()

    def receive(self):
        axis = self.order[0]
        if axis == "z":
            self.received = tuple(swap_high(part, place) for part, place in zip(self.sent, others))
        else:
            self.received = (swap(self.sent[0], axis),)
        self.sent = ()

    def join(self):
        if not self.received:
            self.receive()
        rest = self.order[1:]
        parts = (self.kept,) + self.received
        self.received = ()
        self.order = rest
        if not rest:
            self.sent, self.kept = (), add(*parts)
            return
        places = others if rest[0] == "z" else ((1,),)
        self.sent = tuple(add(*(part[place] for part in parts)) for place in places)
        own = (0,) * len(places[0])
        self.kept = add(*(part[own] for part in parts))

    def state(self):
        return (self.sent, self.kept, self.received)

    def set_state(self, state):
        self.sent, self.kept, self.received = state


def gather_high(part):
    return jnp.stack(
        [
            jnp.stack([part, swap_high(part, (0, 1))]),
            jnp.stack([swap_high(part, (1, 0)), swap_high(part, (1, 1))]),
        ]
    )


def collect(part):
    return lax.all_gather(part, copy_axes, axis=0).reshape((8, 2) + part.shape)


def reduce_plain(grad):
    part = lax.psum_scatter(grad, "ws", scatter_dimension=grad.ndim - 2, tiled=True)
    return lax.psum(part, copy_axes).astype(jnp.float32)


def after(value, chains):
    if not special_mesh():
        return value
    value, kept = lax.optimization_barrier((value, [chain.kept for chain in chains]))
    for chain, part in zip(chains, kept):
        chain.kept = part
    return value


def hold(value, chains=()):
    if not special_mesh():
        return value
    value, states = lax.optimization_barrier((value, [chain.state() for chain in chains]))
    for chain, state in zip(chains, states):
        chain.set_state(state)
    return value


def per_device(
    byte_ids,
    segments,
    embed,
    conv_kernel,
    score_weight,
    attn_gain,
    w_q,
    w_k,
    w_v,
    w_o,
    rel_bias,
    ff_gain,
    w_gate,
    w_up,
    w_down,
    cotangent,
):
    byte_count = byte_ids.shape[1]
    row_count = byte_count // 2
    width = w_q.shape[1]
    group_count = lax.axis_size("ws")
    cycle_count = lax.axis_size("z") * lax.axis_size("core")
    cycle_place = lax.axis_index("z") * lax.axis_size("core") + lax.axis_index("core")
    bucket_count, head_count = rel_bias.shape
    rim = conv_width // 2
    has_before = cycle_place > 0
    has_after = cycle_place < cycle_count - 1

    ids = byte_ids[0]
    row_segs = segments[0, ::2]
    note = jnp.concatenate([row_segs, ids[:rim], ids[byte_count - rim :]])
    before_note, after_note = neighbours(note, sequence_axes)
    embed_table = gather_columns(embed)
    if special_mesh():
        core, dp = lax.axis_index("core"), lax.axis_index("dp")
        place = jnp.stack(
            [
                lax.axis_index("ws"), dp * 2 + core, 2 - dp * 2 + core, dp * 2 + 1 - core,
                3 - dp * 2 - core, core, 1 - core,
            ]
        ).astype(jnp.int32)
        own_order = jnp.stack([core, core + 2, 1 - core, 3 - core])
        peer_order = jnp.stack([3 * core, 1 + core, 2 - core, 3 - 3 * core])
        order = jnp.concatenate([place[0] * 4 + own_order, (1 - place[0]) * 4 + peer_order])
        order = order.astype(jnp.int32)
        z = lax.axis_index("z")
        bits = jnp.stack([core, place[0], dp, z & 1, z >> 1]).astype(jnp.int32)
        half = w_q.shape[0] // 2
        square_share = jnp.stack(
            [lax.dynamic_slice_in_dim(weight, core * half, half, 0) for weight in (w_q, w_k, w_v)]
        )
        gate_share = jnp.stack([own_share(weight, 0) for weight in (w_gate, w_up)])
        tail_share = jnp.concatenate(
            [
                lax.dynamic_slice_in_dim(weight, core * (weight.shape[0] // 2), weight.shape[0] // 2, 0)
                for weight in (w_down, w_o)
            ]
        )
        square_first = swap(square_share, "ws")
        square_share, embed_table, before_note, after_note = lax.optimization_barrier(
            (square_share, embed_table, before_note, after_note)
        )
        square_first = swap(square_share, "ws")
        square_place = jnp.stack([place[0], core, 1 - core]).astype(jnp.int32)
        own_square, own_feed = (w_q, w_k, w_v), (w_o, w_gate, w_up, w_down)
    else:
        place = square_place = jnp.zeros((1,), jnp.int32)
        order = jnp.arange(8, dtype=jnp.int32)
        bits = jnp.zeros((5,), jnp.int32)
        square_pieces = gate_pieces = tail_pieces = ()
        own_square, own_feed = (
            tuple(lax.all_gather(weight, "ws", axis=0, tiled=True) for weight in weights)
            for weights in ((w_q, w_k, w_v), (w_o, w_gate, w_up, w_down))
        )
    segs = jnp.stack(
        [
            jnp.where(has_before, before_note[:row_count], -2),
            row_segs,
            jnp.where(has_after, after_note[:row_count], 1 << 20),
        ]
    )
    segs = jnp.pad(segs, ((0, 0), (0, -row_count % tile)), constant_values=-3)
    left_ids = jnp.where(has_before, before_note[row_count + rim :], -1)
    right_ids = jnp.where(has_after, after_note[row_count : row_count + rim], -1)
    id_rows = -(-(byte_count + rim) // tile) * tile
    id_line = jnp.concatenate(
        [
            jnp.full((tile - rim,), -1, jnp.int32),
            left_ids,
            ids,
            right_ids,
            jnp.full((id_rows - byte_count - rim,), -1, jnp.int32),
        ]
    ).reshape(-1, 1, tile)
    conv = jnp.pad(conv_kernel.astype(jnp.float32), ((0, 8 - conv_width), (0, 0)))
    score = score_weight.astype(jnp.float32)[None]
    gain_one = attn_gain[None]
    gain_two = ff_gain[None]

    special = special_mesh()
    half_pairs = width // tile // 2
    start, x_rows, mix, block_weight = gbst_forward(id_line, embed_table, conv, score, row_count)
    if special:
        start, square_first, gate_share = lax.optimization_barrier((start, square_first, gate_share))
        square_pieces = (square_first, swap(square_first, "core"))
        gate_first = swap(gate_share, "ws")
    first_in, queries, own_kv = project(square_place, start, gain_one, own_square, square_pieces)
    if special:
        queries, gate_first, tail_share = lax.optimization_barrier((queries, gate_first, tail_share))
        tail_first = swap(tail_share, "ws")
        gate_second, gate_third = swap(gate_first, "dp"), swap(gate_first, "core")
    before_kv, after_kv = neighbours(own_kv, sequence_axes)
    near_state = attention_forward(segs, queries, (own_kv,), None, rel_bias, row_count)
    if special:
        near_state, before_kv, after_kv, gate_second = lax.optimization_barrier(
            (near_state, before_kv, after_kv, gate_second)
        )
        gate_pieces = (gate_first, gate_second, gate_third, swap(gate_second, "core"))
    attended, log_norm = attention_forward(
        segs, queries, (before_kv, after_kv), near_state, rel_bias, row_count
    )
    if special:
        attended, tail_first = lax.optimization_barrier((attended, tail_first))
        tail_pieces = (tail_first, swap(tail_first, "core"))
    output, down_grad, gate_up_grad, gate_up_sent, d_middle, d_attended, out_grad, ff_gain_grad = feed_forward(
        place, order, bits, attended, start, cotangent[0], gain_two, own_feed, gate_pieces, tail_pieces
    )
    chains = []
    if special:
        gate_chain = Chain(gate_up_sent, gate_up_grad, ("core", "ws", "dp", "z"))
        tail_chain = Chain(out_grad, down_grad, ("core", "dp", "ws", "z"))
        gate_chain.join()
        chains = [gate_chain, tail_chain]
    d_attended = hold(d_attended, chains)
    halves = []
    bias_parts = []
    for part in range(2):
        d_queries, d_before, d_own, d_after, bias_sums = attention_backward(
            segs, queries, d_attended, attended, before_kv, own_kv, after_kv, rel_bias,
            log_norm,            row_count, part * half_pairs, half_pairs,
        )
        active = chains if part else chains[1:]
        d_before, d_after = after((d_before, d_after), active)
        for chain in active:
            chain.join()
        d_attended, d_before, d_after, halves = hold((d_attended, d_before, d_after, halves), active)
        from_after = lax.ppermute(
            d_before, sequence_axes, [(i + 1, i) for i in range(cycle_count - 1)]
        )
        from_before = lax.ppermute(
            d_after, sequence_axes, [(i, i + 1) for i in range(cycle_count - 1)]
        )
        halves.append((d_queries, d_own, from_after, from_before))
        bias_parts.append(jnp.transpose(bias_sums[: 2 * half_pairs, :bucket_count]))
    square_grads, square_sent, d_start, attn_gain_grad = project_back(
        square_place, bits, [part[i] for i in range(4) for part in halves], first_in, start,
        d_middle, gain_one, own_square, square_pieces,
    )
    if special:
        square_chain = Chain(square_sent, square_grads, ("core", "ws", "dp", "z"))
        d_start = after(d_start, chains)
        kept, high, low, both = join_feed(
            gate_chain.kept, swap(gate_chain.sent[0], "dp"),
            tail_chain.kept, swap(tail_chain.sent[0], "ws"),
        )
        feed_chain = Chain(None, kept, ("z",))
        feed_chain.sent = (low, high, both)
        d_start = hold(d_start, [square_chain, feed_chain])
        square_chain.join()
        d_start = hold(d_start, [square_chain])
    d_conv, left_grad, right_grad, conv_grad, score_grad = unpool(
        x_rows, mix, block_weight, d_start, conv, score, byte_count
    )
    bias_grad = jnp.concatenate(bias_parts, axis=1)
    bias_rows = jnp.pad(bias_grad.reshape(1, -1), ((0, 0), (0, width - bucket_count * head_count)))
    small = jnp.concatenate(
        [conv_grad, score_grad, attn_gain_grad, ff_gain_grad, bias_rows], axis=0
    )
    byte_grad, embed_part = scatter_bytes(id_line, d_conv, conv, byte_count, embed.shape[0])
    if special:
        rows = embed_part.shape[0] // 2
        columns = width // 2
        small = small.reshape(-1, columns)
        square_chain.receive()
        embed_part, small = hold((embed_part, small), [square_chain])
        square_chain.join()
        core_rows = lax.dynamic_slice_in_dim(embed_part, bits[0] * rows, rows, 0)
        sent_rows = lax.dynamic_slice_in_dim(embed_part, (1 - bits[0]) * rows, rows, 0)
        core_in = swap(pack(sent_rows.reshape(2 * rows, columns), small), "core")
        square_chain.receive()
        core_rows, small, core_in = hold((core_rows, small, core_in), [square_chain])
        core_rows = after(core_rows, [feed_chain])
        feed_chain.join()
        feed_sum = collect(feed_chain.kept)
        received, small = unpack(core_in, small)
        embed_part = add(core_rows, received.reshape(rows, width))
        square_chain.join()
        own_columns = lax.dynamic_slice_in_dim(embed_part, bits[1] * columns, columns, 1)
        sent_columns = lax.dynamic_slice_in_dim(embed_part, (1 - bits[1]) * columns, columns, 1)
        sent = pack(sent_columns, small)
        own_columns, small, sent, left_grad = hold(
            (own_columns, small, sent, left_grad), [square_chain]
        )
        from_right = send_left(left_grad, cycle_count)
        received, small = unpack(swap(sent, "ws"), small)
        embed_part = add(own_columns, received)
        square_chain.join()
        square_part = square_chain.kept
        sent = pack(embed_part, small)
        embed_part, small, sent, square_part, from_right, right_grad = hold(
            (embed_part, small, sent, square_part, from_right, right_grad)
        )
        from_left = send_right(right_grad, cycle_count)
        received, small = unpack(swap(sent, "dp"), small)
        embed_part = add(embed_part, received)
        square_part = gather_high(square_part)
        sent = pack(embed_part, small)
        embed_part, small, sent, square_part, from_left = hold(
            (embed_part, small, sent, square_part, from_left)
        )
        byte_grad = add_edges(byte_grad, from_left, from_right)
        parts = [embed_part]
        for place in others:
            received, small = unpack(swap_high(sent, place), small)
            parts.append(received)
        embed_part = add(*parts)
        square_across = swap(square_part, "dp")
        square_core = swap(square_part, "core")
        embed_part, small, square_across, square_core, byte_grad = hold(
            (embed_part, small, square_across, square_core, byte_grad)
        )
        square_both = swap(square_across, "core")
        embed_part = ordered(embed_part, swap(embed_part, "core"), bits[0], 0)
        square_both, embed_part, small = hold((square_both, embed_part, small))
        query_sum, key_sum, value_sum = finish_square(
            bits, (square_part, square_across, square_core, square_both), ((columns, width),) * 3
        )
        embed_part, query_sum = hold((embed_part, query_sum))
        gate_sum, up_sum, down_sum, out_sum = finish_feed(
            feed_sum,
            (
                (columns, w_gate.shape[1]), (columns, w_gate.shape[1]),
                (w_down.shape[0], width), (columns, width),
            ),
        )
        small = small.reshape(-1, width)
    else:
        small = lax.psum(small, all_axes)
        embed_part = lax.psum_scatter(embed_part, "ws", scatter_dimension=1, tiled=True)
        embed_part = lax.psum(embed_part, copy_axes)
    embed_sum = embed_part[: embed.shape[0]].astype(jnp.float32)
    if not special:
        from_right = send_left(left_grad, cycle_count)
        from_left = send_right(right_grad, cycle_count)
        byte_grad = add_edges(byte_grad, from_left, from_right)
        gate_sum, up_sum = jnp.transpose(reduce_plain(gate_up_grad), (1, 2, 0, 3)).reshape(
            2, width // group_count, -1
        )
        down_sum, out_sum = reduce_plain(down_grad), reduce_plain(out_grad)
        query_sum, key_sum, value_sum = reduce_plain(square_grads)
    return (
        output[None],
        byte_grad[None],
        embed_sum,
        small[:conv_width],
        small[conv_width],
        small[conv_width + 1],
        query_sum,
        key_sum,
        value_sum,
        out_sum,
        small[conv_width + 3, : bucket_count * head_count].reshape(bucket_count, head_count),
        small[conv_width + 2],
        gate_sum,
        up_sum,
        down_sum,
    )


def solution(mesh):
    devices = mesh.devices
    fine = Mesh(devices.reshape((devices.shape[0] // 2, 2) + devices.shape[1:]), all_axes)
    rows = P(("dp", "ws"), sequence_axes)
    split = P("ws", None)
    in_specs = (
        rows, rows, P(None, "ws"), P(), P(), P(), split, split, split, split, P(), P(),
        split, split, split, P(("dp", "ws"), sequence_axes, None),
    )
    wide = P(("dp", "ws"), sequence_axes, None)
    out_specs = (
        wide, wide, P(None, "ws"), P(), P(), P(), split, split, split, split, P(), P(),
        split, split, split,
    )
    return jax.shard_map(
        per_device, mesh=fine, in_specs=in_specs, out_specs=out_specs, check_vma=False
    )
```

```python
import functools

import jax
import jax.numpy as jnp
from jax import lax
from jax.experimental import pallas as pl
from jax.experimental.pallas import tpu as pltpu
from jax.sharding import Mesh
from jax.sharding import PartitionSpec as P

thresholds = (12, 16, 23, 32, 46, 64, 91)
negative = -1e30
epsilon = 1e-06
conv_width = 5
tile = 128
near_bases = (-128, -120, 0, 120, 128)
class_count = len(near_bases) + 2


def bucket_of(relative):
    distance = jnp.abs(relative)
    far_bucket = 8 + sum(((distance >= threshold).astype(jnp.int32) for threshold in thresholds))
    near_bucket = jnp.where(distance < 8, distance, far_bucket)
    return near_bucket + 16 * (relative > 0).astype(jnp.int32)


def matmul(left, right, left_dim, right_dim):
    return lax.dot_general(
        left, right, (((left_dim,), (right_dim,)), ((), ())), preferred_element_type=jnp.float32
    )


def split_pair(values):
    high = values.astype(jnp.bfloat16)
    return high, (values - high.astype(jnp.float32)).astype(jnp.bfloat16)


def tile_class(query_tile, key_tile):
    step = key_tile - query_tile - 4
    own = jnp.where(
        step <= -2, 0, jnp.where(step == -1, 1, jnp.where(step == 0, 3, jnp.where(step == 1, 5, 6)))
    )
    before = jnp.where(step == -1, 2, 0)
    after = jnp.where(step == 1, 4, 6)
    return jnp.where(key_tile < 4, before, jnp.where(key_tile < 8, own, after))


def key_range(seg_ref, query_tile, row_count, tiles_per_block):
    first_seg = seg_ref[1, query_tile * tile]
    last_seg = seg_ref[1, jnp.minimum(query_tile * tile + tile, row_count) - 1]
    low = jnp.int32(0)
    high = jnp.int32(0)
    for block in range(3):
        for part in range(tiles_per_block):
            key_first = seg_ref[block, part * tile]
            key_last = seg_ref[block, min(part * tile + tile, row_count) - 1]
            low = low + (key_last < first_seg).astype(jnp.int32)
            high = high + (key_first <= last_seg).astype(jnp.int32)
    return low, high


def class_buckets(kind, shape, dim):
    place = lax.broadcasted_iota(jnp.int32, shape, dim)
    swing = jnp.where(place < tile, place, place - 2 * tile)
    if kind == 0:
        return jnp.full(shape, bucket_of(jnp.int32(-4 * tile)))
    if kind == class_count - 1:
        return jnp.full(shape, bucket_of(jnp.int32(4 * tile)))
    return bucket_of(near_bases[kind - 1] - swing)


def make_bias(rel_ref, bias_ref, first_pair, pair_count):
    bucket_count = rel_ref.shape[0]
    for kind in range(class_count):
        shape = (bucket_count, 2 * tile)
        hot = class_buckets(kind, shape, 1) == lax.broadcasted_iota(jnp.int32, shape, 0)
        lines = lax.dot_general(
            rel_ref[...], hot.astype(jnp.float32), (((0,), (0,)), ((), ())),
            precision=lax.Precision.HIGHEST, preferred_element_type=jnp.float32,
        )
        for pair in range(pair_count):
            for half in range(2):
                head = 2 * (first_pair + pair) + half
                grid = jnp.broadcast_to(lines[head : head + 1], (tile, 2 * tile))
                if 0 < kind < class_count - 1:
                    grid = pltpu.roll(grid, 0, 1, stride=1, stride_axis=0)
                bias_ref[kind, pair, :, half * tile : (half + 1) * tile] = grid[:, :tile]


def cost(microseconds):
    return pl.CostEstimate(
        flops=int(microseconds * 1e7), transcendentals=0, bytes_accessed=int(microseconds * 3e4)
    )


def stack_heads(block):
    lane = lax.broadcasted_iota(jnp.int32, block.shape, 1)
    zero = jnp.zeros_like(block)
    return jnp.concatenate(
        [jnp.where(lane < tile // 2, block, zero), jnp.where(lane < tile // 2, zero, block)], axis=0
    )


def fold_rows(values, combine):
    pieces = [values[8 * i : 8 * i + 8] for i in range(values.shape[0] // 8)]
    while len(pieces) > 1:
        joined = [combine(pieces[i], pieces[i + 1]) for i in range(0, len(pieces) - 1, 2)]
        if len(pieces) % 2:
            joined.append(pieces[-1])
        pieces = joined
    return pieces[0]


def key_columns(segs_ref, column_ref, key_tile):
    row = segs_ref[key_tile, 0:1, :]
    column_ref[key_tile] = jnp.transpose(jnp.broadcast_to(row, (tile, tile)))


def start_copies(sources, window_ref, sems, first_pair):
    rows, full_width = sources[0].shape
    width = window_ref.shape[1] // 2
    copies = []
    for i, source in enumerate(sources):
        for side in range(2):
            copies.append(
                pltpu.make_async_copy(
                    source.at[:, pl.ds(side * (full_width // 2) + first_pair * tile, width)],
                    window_ref.at[pl.ds(rows * i, rows), pl.ds(side * width, width)],
                    sems.at[2 * i + side],
                )
            )
    for copy in copies:
        copy.start()
    return copies


def forward_kernel(seg_ref, q_ref, *refs, row_count, near):
    if near:
        source_refs, refs = refs[:1], refs[1:]
    else:
        source_refs, refs = refs[:2], refs[2:]
        (mixed_in_ref, top_in_ref, total_in_ref), refs = refs[:3], refs[3:]
    segs_ref, qsegs_ref, rel_ref = refs[:3]
    if near:
        mixed_ref, top_ref, total_ref = refs[3:6]
    else:
        out_ref, lse_ref = refs[3:5]
    window_ref, bias_ref, column_ref, flipped_ref, score_ref = refs[-6 if near else -7 :][:5]
    sems = refs[-1]
    if not near:
        mixed_ref = refs[-2]
    width = q_ref.shape[1]
    pair_count = width // tile
    query_tiles = q_ref.shape[0] // tile
    half = tile // 2
    middle = query_tiles // 2
    copies = start_copies(source_refs, window_ref, sems, 0)
    make_bias(rel_ref, bias_ref, 0, pair_count)

    def key_span(query_tile):
        low, high = key_range(seg_ref, query_tile, row_count, query_tiles)
        if near:
            low = jnp.maximum(low - query_tiles, 0)
            high = jnp.minimum(high - query_tiles, query_tiles)
            return low // 2, (high + 1) // 2
        return jnp.minimum(low // 2, middle), jnp.maximum((high + 1) // 2 - middle, middle)

    def global_tile(key_pair, part):
        key_tile = 2 * key_pair + part
        if near:
            return key_tile + query_tiles
        return key_tile + jnp.where(key_pair >= middle, query_tiles, 0)

    first = key_span(0)[0]
    last = key_span(query_tiles - 1)[1]
    for copy in copies:
        copy.wait()

    def prepare(key_pair, carry):
        for part in range(2):
            row = segs_ref[global_tile(key_pair, part), 0:1, :]
            column_ref[2 * key_pair + part] = jnp.transpose(jnp.broadcast_to(row, (tile, tile)))
        at = pl.multiple_of(key_pair * 2 * tile, 2 * tile)
        flipped_ref[key_pair] = jnp.transpose(window_ref[pl.ds(at, 2 * tile), width:])
        return carry

    lax.fori_loop(first, last, prepare, 0)

    def query_step(query_tile, carry):
        low, high = key_span(query_tile)
        rows = pl.ds(pl.multiple_of(query_tile * tile, tile), tile)
        lanes = [slice(pair * tile, (pair + 1) * tile) for pair in range(pair_count)]
        stacked = [stack_heads(q_ref[rows, lane]) for lane in lanes]
        query_seg = qsegs_ref[query_tile, 0:1, :]
        slot = query_tile if near else 0

        def score_step(key_pair, tops):
            keys = pl.ds(pl.multiple_of(key_pair * 2 * tile, 2 * tile), 2 * tile)
            hides = []
            kinds = []
            for part in range(2):
                hide = jnp.where(column_ref[2 * key_pair + part] == query_seg, 0.0, negative)
                hides.append(jnp.concatenate([hide, hide], axis=1))
                kinds.append(tile_class(query_tile, global_tile(key_pair, part)))
            fresh = []
            for pair in range(pair_count):
                scores = matmul(window_ref[keys, lanes[pair]], stacked[pair], 1, 1)
                top = tops[pair]
                for part in range(2):
                    cut = slice(part * tile, (part + 1) * tile)
                    piece = scores[cut] + bias_ref[kinds[part], pair] + hides[part]
                    score_ref[key_pair, pair, cut] = piece
                    top = jnp.maximum(top, fold_rows(piece, jnp.maximum))
                fresh.append(top)
            return tuple(fresh)

        tops = lax.fori_loop(
            low, high, score_step,
            tuple(jnp.full((8, 2 * tile), negative, jnp.float32) for _ in range(pair_count)),
        )
        tops = [jnp.max(top, axis=0, keepdims=True) for top in tops]
        scales = []
        for pair in range(pair_count):
            if near:
                mixed_ref[slot, pair] = jnp.zeros((tile, tile), jnp.float32)
            else:
                before = top_in_ref[query_tile, pair : pair + 1, :]
                tops[pair] = jnp.maximum(tops[pair], before)
                scale = jnp.exp(before - tops[pair])
                scales.append(scale)
                mixed_ref[slot, pair, :half] = mixed_in_ref[query_tile, pair, :half] * scale[:, :tile]
                mixed_ref[slot, pair, half:] = mixed_in_ref[query_tile, pair, half:] * scale[:, tile:]

        def mix_step(key_pair, totals):
            fresh = []
            for pair in range(pair_count):
                exponent = jnp.exp(score_ref[key_pair, pair] - tops[pair])
                fresh.append(totals[pair] + fold_rows(exponent, jnp.add))
                mixed = matmul(
                    flipped_ref[key_pair, lanes[pair], :], exponent.astype(jnp.bfloat16), 1, 0
                )
                mixed_ref[slot, pair, :half] += mixed[:half, :tile]
                mixed_ref[slot, pair, half:] += mixed[half:, tile:]
            return tuple(fresh)

        totals = lax.fori_loop(
            low, high, mix_step,
            tuple(jnp.zeros((8, 2 * tile), jnp.float32) for _ in range(pair_count)),
        )
        for pair in range(pair_count):
            total = jnp.sum(totals[pair], axis=0, keepdims=True)
            if near:
                top_ref[query_tile, pair : pair + 1, :] = tops[pair]
                total_ref[query_tile, pair : pair + 1, :] = total
                continue
            total = total + total_in_ref[query_tile, pair : pair + 1, :] * scales[pair]
            lse_ref[query_tile, pair : pair + 1, :] = tops[pair] + jnp.log(total)
            inverse = 1.0 / total
            scaled = jnp.concatenate(
                [
                    mixed_ref[slot, pair, :half] * inverse[:, :tile],
                    mixed_ref[slot, pair, half:] * inverse[:, tile:],
                ],
                axis=0,
            )
            out_ref[rows, lanes[pair]] = jnp.transpose(scaled).astype(jnp.bfloat16)
        return carry

    lax.fori_loop(0, query_tiles, query_step, 0)


def backward_kernel(
    seg_ref, q_ref, do_ref, o_ref, before_ref, own_ref, after_ref, segs_ref, qsegs_ref, rel_ref, lse_ref,
    dq_ref, dbefore_ref, down_ref, dafter_ref, bias_out_ref,
    window_ref, bias_ref, column_ref, flipped_ref, dbias_ref, dwindow_ref, dq_acc_ref, delta_ref, sems,
    *, row_count, first_pair
):
    width = dq_ref.shape[1]
    pair_count = width // tile
    query_tiles = q_ref.shape[0] // tile
    block_rows = q_ref.shape[0]
    half = tile // 2
    copies = start_copies((before_ref, own_ref, after_ref), window_ref, sems, first_pair)
    make_bias(rel_ref, bias_ref, first_pair, pair_count)
    dwindow_ref[...] = jnp.zeros(dwindow_ref.shape, jnp.float32)
    dbias_ref[...] = jnp.zeros(dbias_ref.shape, jnp.float32)
    product = do_ref[...].astype(jnp.float32) * o_ref[...].astype(jnp.float32)
    product_high, product_low = split_pair(product)
    member = (
        lax.broadcasted_iota(jnp.int32, (16, width), 1) // half
        == lax.broadcasted_iota(jnp.int32, (16, width), 0)
    ).astype(jnp.bfloat16)
    delta_ref[...] = matmul(member, product_high, 1, 1) + matmul(member, product_low, 1, 1)
    first = key_range(seg_ref, 0, row_count, query_tiles)[0]
    last = key_range(seg_ref, query_tiles - 1, row_count, query_tiles)[1]
    for copy in copies:
        copy.wait()

    def prepare(key_pair, carry):
        for part in range(2):
            key_columns(segs_ref, column_ref, 2 * key_pair + part)
        at = pl.multiple_of(key_pair * 2 * tile, 2 * tile)
        flipped_ref[key_pair] = jnp.transpose(window_ref[pl.ds(at, 2 * tile), :width])
        return carry

    lax.fori_loop(first // 2, (last + 1) // 2, prepare, 0)

    def query_step(query_tile, carry):
        low, high = key_range(seg_ref, query_tile, row_count, query_tiles)
        at = pl.multiple_of(query_tile * tile, tile)
        rows = pl.ds(at, tile)
        lanes = [slice(pair * tile, (pair + 1) * tile) for pair in range(pair_count)]
        queries = [stack_heads(q_ref[rows, lane]) for lane in lanes]
        grads = [stack_heads(do_ref[rows, lane]) for lane in lanes]
        query_seg = qsegs_ref[query_tile, 0:1, :]
        deltas = [
            jnp.concatenate(
                [delta_ref[2 * pair : 2 * pair + 1, rows], delta_ref[2 * pair + 1 : 2 * pair + 2, rows]],
                axis=1,
            )
            for pair in range(pair_count)
        ]
        norms = [
            lse_ref[query_tile, first_pair + pair : first_pair + pair + 1, :]
            for pair in range(pair_count)
        ]
        for pair in range(pair_count):
            dq_acc_ref[pair] = jnp.zeros((tile, tile), jnp.float32)

        def key_step(key_pair, carry):
            keys = pl.ds(pl.multiple_of(key_pair * 2 * tile, 2 * tile), 2 * tile)
            hides = []
            kinds = []
            for part in range(2):
                key_tile = 2 * key_pair + part
                hide = jnp.where(column_ref[key_tile] == query_seg, 0.0, negative)
                hides.append(jnp.concatenate([hide, hide], axis=1))
                kinds.append(tile_class(query_tile, key_tile))
            for pair in range(pair_count):
                lane = lanes[pair]
                value_lane = slice(width + pair * tile, width + (pair + 1) * tile)
                scores = matmul(window_ref[keys, lane], queries[pair], 1, 1)
                dprobs = matmul(window_ref[keys, value_lane], grads[pair], 1, 1)
                probs_low, dscores_low = [], []
                for part in range(2):
                    cut = slice(part * tile, (part + 1) * tile)
                    probs = jnp.exp(
                        scores[cut] + bias_ref[kinds[part], pair] + hides[part] - norms[pair]
                    )
                    dscores = probs * (dprobs[cut] - deltas[pair])
                    dbias_ref[kinds[part], pair] += dscores
                    probs_low.append(probs.astype(jnp.bfloat16))
                    dscores_low.append(dscores.astype(jnp.bfloat16))
                probs_low = jnp.concatenate(probs_low, axis=0)
                dscores_low = jnp.concatenate(dscores_low, axis=0)
                dwindow_ref[keys, lane] += matmul(dscores_low, queries[pair], 1, 0)
                dwindow_ref[keys, value_lane] += matmul(probs_low, grads[pair], 1, 0)
                dquery = matmul(flipped_ref[key_pair, lane, :], dscores_low, 1, 0)
                dq_acc_ref[pair, :half] += dquery[:half, :tile]
                dq_acc_ref[pair, half:] += dquery[half:, tile:]
            return carry

        lax.fori_loop(low // 2, (high + 1) // 2, key_step, 0)
        for pair in range(pair_count):
            dq_ref[rows, lanes[pair]] = jnp.transpose(dq_acc_ref[pair]).astype(jnp.bfloat16)
        return carry

    lax.fori_loop(0, query_tiles, query_step, 0)
    dbefore_ref[...] = dwindow_ref[:block_rows].astype(jnp.bfloat16)
    down_ref[...] = dwindow_ref[block_rows : 2 * block_rows]
    dafter_ref[...] = dwindow_ref[2 * block_rows :].astype(jnp.bfloat16)
    turn = (
        lax.broadcasted_iota(jnp.int32, (tile, tile), 0)
        + lax.broadcasted_iota(jnp.int32, (tile, tile), 1)
        == tile - 1
    ).astype(jnp.bfloat16)
    zero_half = jnp.zeros((tile, tile), jnp.float32)
    bucket_count = rel_ref.shape[0]
    total = jnp.zeros(bias_out_ref.shape, jnp.float32)
    for kind in range(class_count):
        lines = []
        for pair in range(pair_count):
            grid = dbias_ref[kind, pair]
            near = 0 < kind < class_count - 1
            if near:
                grid_high, grid_low = split_pair(grid)
                grid = matmul(turn, grid_high, 1, 0) + matmul(turn, grid_low, 1, 0)
            for side in range(2):
                part = jnp.concatenate([grid[:, side * tile : (side + 1) * tile], zero_half], axis=1)
                if near:
                    part = pltpu.roll(part, tile + 1, 1, stride=1, stride_axis=0)
                lines.append(jnp.sum(fold_rows(part, jnp.add), axis=0, keepdims=True))
        lines.append(jnp.zeros((bias_out_ref.shape[0] - len(lines), 2 * tile), jnp.float32))
        shape = (2 * tile, tile)
        hot = class_buckets(kind, shape, 0) == lax.broadcasted_iota(jnp.int32, shape, 1)
        total = total + jnp.dot(
            jnp.concatenate(lines, axis=0), hot.astype(jnp.float32),
            precision=lax.Precision.HIGHEST, preferred_element_type=jnp.float32,
        )
    bias_out_ref[...] = total


def specs(count, space=pltpu.VMEM):
    return [pl.BlockSpec(memory_space=space) for _ in range(count)]


def attention_forward(segs, q, sources, state, rel_bias, row_count):
    rows, width = q.shape
    tiles = rows // tile
    pairs = width // tile
    near = state is None
    seg_rows = segs.reshape(3 * tiles, 1, tile)
    query_segs = mark_queries(segs, row_count).reshape(tiles, 1, tile)
    f32 = jnp.float32
    norm = jax.ShapeDtypeStruct((tiles, 8, 2 * tile), f32)
    mixed = jax.ShapeDtypeStruct((tiles, pairs, tile, tile), f32)
    count = len(sources)
    blocks = count * tiles // 2
    scratch = [
        pltpu.VMEM((count * rows, 2 * width), jnp.bfloat16),
        pltpu.VMEM((class_count, pairs, tile, 2 * tile), f32),
        pltpu.VMEM((count * tiles, tile, tile), jnp.int32),
        pltpu.VMEM((blocks, width, 2 * tile), jnp.bfloat16),
        pltpu.VMEM((blocks, pairs, 2 * tile, 2 * tile), f32),
    ]
    if not near:
        scratch.append(pltpu.VMEM((1, pairs, tile, tile), f32))
    return pl.pallas_call(
        functools.partial(forward_kernel, row_count=row_count, near=near),
        out_shape=(mixed, norm, norm)
        if near
        else (jax.ShapeDtypeStruct((rows, width), jnp.bfloat16), norm),
        in_specs=specs(1, pltpu.SMEM) + specs(1) + specs(count, pl.ANY)
        + specs(3 if near else 6),
        out_specs=tuple(specs(3 if near else 2)),
        scratch_shapes=scratch + [pltpu.SemaphoreType.DMA((2 * count,))],
        compiler_params=pltpu.CompilerParams(vmem_limit_bytes=(22 if near else 30) << 20),
        cost_estimate=cost(12),
        name="attention_near" if near else "attention_rim",
    )(segs, q, *sources, *(state or ()), seg_rows, query_segs, rel_bias)


def mark_queries(segs, row_count):
    place = jnp.arange(segs.shape[1], dtype=jnp.int32)
    return jnp.where(place < row_count, segs[1], -1)


def attention_backward(
    segs, q, do, o, before, own, after, rel_bias, lse, row_count, first_pair, pairs
):
    rows, full_width = q.shape
    tiles = rows // tile
    width = pairs * tile
    seg_rows = segs.reshape(3 * tiles, 1, tile)
    query_segs = mark_queries(segs, row_count).reshape(tiles, 1, tile)
    part = pl.BlockSpec((rows, width), lambda i: (0, first_pair // pairs))
    return pl.pallas_call(
        functools.partial(backward_kernel, row_count=row_count, first_pair=first_pair),
        grid=(1,),
        out_shape=(
            jax.ShapeDtypeStruct((rows, width), jnp.bfloat16),
            jax.ShapeDtypeStruct((rows, 2 * width), jnp.bfloat16),
            jax.ShapeDtypeStruct((rows, 2 * width), jnp.float32),
            jax.ShapeDtypeStruct((rows, 2 * width), jnp.bfloat16),
            jax.ShapeDtypeStruct((8, tile), jnp.float32),
        ),
        in_specs=specs(1, pltpu.SMEM) + [part, part, part] + specs(3, pl.ANY) + specs(4),
        out_specs=tuple(specs(5)),
        scratch_shapes=[
            pltpu.VMEM((3 * rows, 2 * width), jnp.bfloat16),
            pltpu.VMEM((class_count, pairs, tile, 2 * tile), jnp.float32),
            pltpu.VMEM((3 * tiles, tile, tile), jnp.int32),
            pltpu.VMEM((3 * tiles // 2, width, 2 * tile), jnp.bfloat16),
            pltpu.VMEM((class_count, pairs, tile, 2 * tile), jnp.float32),
            pltpu.VMEM((3 * rows, 2 * width), jnp.float32),
            pltpu.VMEM((pairs, tile, tile), jnp.float32),
            pltpu.VMEM((16, rows), jnp.float32),
            pltpu.SemaphoreType.DMA((6,)),
        ],
        compiler_params=pltpu.CompilerParams(vmem_limit_bytes=30 << 20),
        cost_estimate=cost(20),
        name="attention_backward",
    )(segs, q, do, o, before, own, after, seg_rows, query_segs, rel_bias, lse)


span = 96
id_pad = 128


def dot3(left, right, left_dim, right_dim):
    left_high, left_low = split_pair(left)
    right_high, right_low = split_pair(right)
    return (
        matmul(left_high, right_high, left_dim, right_dim)
        + matmul(left_low, right_high, left_dim, right_dim)
        + matmul(left_high, right_low, left_dim, right_dim)
    )


def block_means_grid(block_size):
    row = lax.broadcasted_iota(jnp.int32, (span, tile), 0)
    lane = lax.broadcasted_iota(jnp.int32, (span, tile), 1)
    same = (row // block_size == lane // block_size) & (lane < span)
    return jnp.where(same, 1.0 / block_size, 0.0)


def row_to_column(row):
    lane = lax.broadcasted_iota(jnp.int32, (span, tile), 1)
    place = lax.broadcasted_iota(jnp.int32, (span, tile), 0)
    return jnp.sum(jnp.where(lane == place, row, 0.0), axis=1, keepdims=True)


def column_to_row(column):
    lane = lax.broadcasted_iota(jnp.int32, (span, tile), 1)
    place = lax.broadcasted_iota(jnp.int32, (span, tile), 0)
    return jnp.sum(jnp.where(lane == place, column, 0.0), axis=0, keepdims=True)


def conv_tile(x_ref, conv_ref, base, lanes):
    taps = range(conv_width)
    return [
        sum(
            conv_ref[tap : tap + 1, i * tile : (i + 1) * tile]
            * x_ref[i, pl.ds(base + tap - conv_width // 2, span), :]
            for tap in taps
        )
        for i in range(lanes)
    ]


def gbst_forward_kernel(
    ids_ref, embed_ref, conv_ref, score_ref,
    start_ref, x_ref, mix_ref, weight_ref,
    table_ref, square_ref, wide_ref,
):
    vocab, width = embed_ref.shape
    lanes = width // tile
    id_tiles = ids_ref.shape[0]
    rows = start_ref.shape[0]
    table_ref[...] = jnp.zeros(table_ref.shape, jnp.bfloat16)
    table_ref[:vocab] = embed_ref[...]
    table_rows = table_ref.shape[0]
    rest = x_ref.shape[1] - id_tiles * tile
    for i in range(lanes):
        x_ref[i, id_tiles * tile :, :] = jnp.zeros((rest, tile), jnp.float32)

    def lookup(step, carry):
        ids = jnp.transpose(jnp.broadcast_to(ids_ref[step, 0:1, :], (tile, tile)))
        lane = lax.broadcasted_iota(jnp.int32, (tile, tile), 1)
        hot = jnp.concatenate(
            [(ids == lane + tile * i).astype(jnp.bfloat16) for i in range(table_rows // tile)], axis=1
        )
        found = matmul(hot, table_ref[...], 1, 0)
        at = pl.ds(pl.multiple_of(step * tile, tile), tile)
        for i in range(lanes):
            x_ref[i, at, :] = found[:, i * tile : (i + 1) * tile]
        return carry

    lax.fori_loop(0, id_tiles, lookup, 0)
    means = [block_means_grid(size) for size in (1, 2, 3, 4)]

    def pool(step, carry):
        base = pl.multiple_of(step * span, 8)
        conv = conv_tile(x_ref, conv_ref, base + id_pad, lanes)
        total = sum(conv[i] * score_ref[0:1, i * tile : (i + 1) * tile] for i in range(lanes))
        row = column_to_row(jnp.sum(total, axis=1, keepdims=True))
        scores = [jnp.sum(mean * row, axis=1, keepdims=True) for mean in means]
        top = functools.reduce(jnp.maximum, scores)
        exponents = [jnp.exp(score - top) for score in scores]
        inverse = 1.0 / sum(exponents)
        weights = [exponent * inverse for exponent in exponents]
        square_ref[...] = sum(weight * mean for weight, mean in zip(weights, means))
        mix = 0.5 * (
            square_ref[pl.ds(0, span // 2, stride=2), :] + square_ref[pl.ds(1, span // 2, stride=2), :]
        )
        half = pl.ds(pl.multiple_of(step * (span // 2), 8), span // 2)
        mix_ref[half, :] = mix
        lane = lax.broadcasted_iota(jnp.int32, (span, tile), 1)
        packed = jnp.zeros((span, tile), jnp.float32)
        for i in range(4):
            packed = jnp.where(lane == i, weights[i], packed)
        weight_ref[pl.ds(base, span), :] = packed
        wide_ref[half, :] = dot3(mix[:, :span], jnp.concatenate(conv, axis=1), 1, 0)
        return carry

    steps = mix_ref.shape[0] * 2 // span
    lax.fori_loop(0, steps, pool, 0, unroll=steps)
    start_ref[...] = wide_ref[:rows]


def gbst_forward(ids, embed, conv, score, row_count):
    vocab, width = embed.shape
    rows = -(-row_count // tile) * tile
    steps = -(-2 * row_count // span)
    x_rows = max(ids.shape[0] * tile, id_pad + steps * span) + 8
    f32 = jnp.float32
    return pl.pallas_call(
        gbst_forward_kernel,
        out_shape=(
            jax.ShapeDtypeStruct((rows, width), f32),
            jax.ShapeDtypeStruct((width // tile, x_rows, tile), f32),
            jax.ShapeDtypeStruct((steps * span // 2, tile), f32),
            jax.ShapeDtypeStruct((steps * span, tile), f32),
        ),
        in_specs=specs(4),
        out_specs=tuple(specs(4)),
        scratch_shapes=[
            pltpu.VMEM((-(-vocab // tile) * tile, width), jnp.bfloat16),
            pltpu.VMEM((span, tile), f32),
            pltpu.VMEM((steps * span // 2, width), f32),
        ],
        compiler_params=pltpu.CompilerParams(vmem_limit_bytes=18 << 20),
        cost_estimate=cost(12),
        name="gbst_forward",
    )(ids, embed, conv, score)


def weight_copies(place_ref, parts, pieces, full_ref, sems):
    copies = []
    rows = parts[0].shape[0]
    for i, part in enumerate(parts):
        at = pl.multiple_of(place_ref[0] * rows, rows)
        copies.append(
            pltpu.make_async_copy(part, full_ref.at[i, pl.ds(at, rows)], sems.at[len(copies)])
        )
    for number, piece in enumerate(pieces):
        share = piece.shape[1]
        at = pl.multiple_of((1 - place_ref[0]) * rows + place_ref[1 + number] * share, share)
        copies.append(
            pltpu.make_async_copy(piece, full_ref.at[:, pl.ds(at, share)], sems.at[len(copies)])
        )
    for copy in copies:
        copy.start()
    return copies


def project_kernel(place_ref, start_ref, gain_ref, *refs):
    pieces = refs[3:-5]
    first_ref, q_ref, kv_ref, weight_ref, sems = refs[-5:]
    copies = weight_copies(place_ref, refs[:3], pieces, weight_ref, sems)
    width = q_ref.shape[1]
    start = start_ref[...]
    inverse = lax.rsqrt(jnp.mean(start * start, axis=-1, keepdims=True) + epsilon)
    first = (start * inverse * gain_ref[...]).astype(jnp.bfloat16)
    first_ref[...] = first
    for copy in copies:
        copy.wait()
    q_ref[...] = matmul(first, weight_ref[0], 1, 0).astype(jnp.bfloat16)
    kv_ref[:, :width] = matmul(first, weight_ref[1], 1, 0).astype(jnp.bfloat16)
    kv_ref[:, width:] = matmul(first, weight_ref[2], 1, 0).astype(jnp.bfloat16)


def project(place, start, gain, own, pieces):
    rows, width = start.shape
    b16 = jnp.bfloat16
    return pl.pallas_call(
        project_kernel,
        out_shape=(
            jax.ShapeDtypeStruct((rows, width), b16),
            jax.ShapeDtypeStruct((rows, width), b16),
            jax.ShapeDtypeStruct((rows, 2 * width), b16),
        ),
        in_specs=specs(1, pltpu.SMEM) + specs(2) + specs(3 + len(pieces), pl.ANY),
        out_specs=tuple(specs(3)),
        scratch_shapes=[
            pltpu.VMEM((3, width, width), b16),
            pltpu.SemaphoreType.DMA((3 + len(pieces),)),
        ],
        compiler_params=pltpu.CompilerParams(vmem_limit_bytes=60 << 20),
        cost_estimate=cost(6),
        name="project",
    )(place, start, gain, *own, *pieces)


def feed_kernel(
    place_ref, order_ref, bits_ref, mixed_ref, start_ref, cot_ref, gain_ref, *refs, piece_count, tail_count
):
    (wo_ref, wg_ref, wu_ref, wd_ref), refs = refs[:4], refs[4:]
    gate_pieces, refs = refs[:piece_count], refs[piece_count:]
    tail_pieces, refs = refs[:tail_count], refs[tail_count:]
    (
        out_ref, downg_ref, gateup_ref, extra_ref, dmid_ref, dmixed_ref, outg_ref, gaing_ref,
        second_ref, turned_ref, middle_ref, scale_ref, total_ref, dsecond_ref, grad_ref,
        fullo_ref, fullg_ref, fullu_ref, fulld_ref, slot_ref, slot_sems,
    ) = refs
    step = pl.program_id(0)
    last = pl.num_programs(0) - 1
    row_count = out_ref.shape[0]
    chunk = fulld_ref.shape[0]

    def fill(full_ref, own_ref, pieces, pick, base=1):
        rows = own_ref.shape[0]
        full_ref[pl.ds(pl.multiple_of(place_ref[0] * rows, rows), rows), :] = own_ref[...]
        for number, piece in enumerate(pieces):
            block = pick(piece)
            share = block.shape[0]
            at = (1 - place_ref[0]) * rows + place_ref[base + number] * share
            full_ref[pl.ds(pl.multiple_of(at, share), share), :] = block

    @pl.when(step == 0)
    def _():
        fill(fullo_ref, wo_ref, tail_pieces, lambda piece: piece[2 * chunk :], 5)
        middle = start_ref[...] + matmul(mixed_ref[...], fullo_ref[...], 1, 0)
        middle_ref[...] = middle
        inverse = lax.rsqrt(jnp.mean(middle * middle, axis=-1, keepdims=True) + epsilon)
        scale_ref[...] = jnp.broadcast_to(inverse, scale_ref.shape)
        second = (middle * inverse * gain_ref[...]).astype(jnp.bfloat16)
        second_ref[...] = second
        turned_ref[...] = jnp.transpose(second)
        total_ref[...] = jnp.zeros(total_ref.shape, jnp.float32)
        dsecond_ref[...] = jnp.zeros(dsecond_ref.shape, jnp.float32)
        grad_ref[:row_count] = cot_ref[...]
        grad_ref[row_count:] = jnp.zeros((grad_ref.shape[0] - row_count, grad_ref.shape[1]), jnp.bfloat16)

    fill(fullg_ref, wg_ref, gate_pieces, lambda piece: piece[0])
    fill(fullu_ref, wu_ref, gate_pieces, lambda piece: piece[1])
    own_steps = pl.num_programs(0) - piece_count

    @pl.when(step < own_steps)
    def _():
        fulld_ref[...] = wd_ref[...]

    for number in range(tail_count):

        @pl.when((step >= own_steps) & ((step - own_steps) >> 1 == number))
        def _():
            at = pl.multiple_of((order_ref[step] & 1) * chunk, chunk)
            fulld_ref[...] = tail_pieces[number][pl.ds(at, chunk), :]

    second = second_ref[...]
    cot = grad_ref[...]
    gate = matmul(second, fullg_ref[...], 1, 0)
    up = matmul(second, fullu_ref[...], 1, 0)
    dhidden = matmul(cot, fulld_ref[...], 1, 1)
    root = 0.7978845608028654
    square = gate * gate
    bend = jnp.tanh(root * (gate + 0.044715 * (square * gate)))
    rise = 0.5 * (1.0 + bend)
    gelu = gate * rise
    slope = rise + 0.5 * gate * (1.0 - bend * bend) * (root * (1.0 + 3 * 0.044715 * square))
    hidden = (gelu * up).astype(jnp.bfloat16)
    dgate = (dhidden * up * slope).astype(jnp.bfloat16)
    dup = (dhidden * gelu).astype(jnp.bfloat16)
    total_ref[...] += matmul(hidden, fulld_ref[...], 1, 0)
    downg = matmul(jnp.transpose(hidden), cot, 1, 0).astype(jnp.bfloat16)
    gateg = matmul(turned_ref[...], dgate, 1, 0).astype(jnp.bfloat16)
    upg = matmul(turned_ref[...], dup, 1, 0).astype(jnp.bfloat16)
    side = downg.shape[1] // 2
    if piece_count:
        bit_core, bit_ws, bit_dp = bits_ref[0], bits_ref[1], bits_ref[2]
        number = order_ref[step]
        low, high = (number & 1) ^ bits_ref[3], ((number >> 1) & 1) ^ bits_ref[4]
        straight = bit_core == 0
        first_rows, second_rows = downg[: chunk // 2], downg[chunk // 2 :]
        kept = jnp.where(straight, first_rows, second_rows)
        sent = jnp.where(straight, second_rows, first_rows)
        for second in range(2):
            cut = slice(second * side, (second + 1) * side)
            place = (second ^ bit_dp, (number >> 2) ^ bit_ws, low, high, slice(0, chunk // 2))
            downg_ref[place] = kept[:, cut]
            outg_ref[place] = sent[:, cut]

        slot = step & 1

        def leave(target_ref, place):
            return pltpu.make_async_copy(
                slot_ref.at[slot], target_ref.at[:, :, place[0], place[1]], slot_sems.at[slot]
            )

        @pl.when(step >= 2)
        def _():
            leave(gateup_ref, (0, 0)).wait()

        for first in range(2):
            rows = slice(first * side, (first + 1) * side)
            slot_ref[slot, first ^ bit_ws, 0 ^ bit_dp] = gateg[rows]
            slot_ref[slot, first ^ bit_ws, 1 ^ bit_dp] = upg[rows]
        turn = jnp.where(step < own_steps, step >> 1, step & 1) & 1
        place = (((number >> 1) & 1) ^ bits_ref[3], (number >> 2) ^ bits_ref[4])

        @pl.when(turn == 0)
        def _():
            leave(gateup_ref, place).start()

        @pl.when(turn == 1)
        def _():
            leave(extra_ref, place).start()

    else:
        downg_ref[...] = downg
        extra_ref[...] = jnp.zeros(extra_ref.shape, jnp.bfloat16)
        gateup_ref[0, 0] = gateg
        gateup_ref[0, 1] = upg
    dsecond_ref[...] += matmul(dgate, fullg_ref[...], 1, 1) + matmul(dup, fullu_ref[...], 1, 1)

    @pl.when(step == last)
    def _():
        middle = middle_ref[...]
        inverse = scale_ref[:, 0:1]
        out_ref[...] = (middle + total_ref[...])[:row_count].astype(jnp.bfloat16)
        normed = middle * inverse
        dsecond = dsecond_ref[...]
        gaing_ref[...] = jnp.sum(dsecond * normed, axis=0, keepdims=True)
        dnormed = dsecond * gain_ref[...]
        dmid = grad_ref[...].astype(jnp.float32) + inverse * (
            dnormed - normed * jnp.mean(dnormed * normed, axis=-1, keepdims=True)
        )
        dmid_ref[...] = dmid
        dbranch = dmid.astype(jnp.bfloat16)
        dmixed_ref[...] = matmul(dbranch, fullo_ref[...], 1, 1).astype(jnp.bfloat16)
        outg = matmul(jnp.transpose(mixed_ref[...]), dbranch, 1, 0).astype(jnp.bfloat16)
        if piece_count:
            store_relative(downg_ref, outg_ref, outg, bits_ref, chunk // 2, True)
            for slot in range(2):
                pltpu.make_async_copy(
                    slot_ref.at[slot], gateup_ref.at[:, :, 0, 0], slot_sems.at[slot]
                ).wait()
        else:
            outg_ref[...] = outg


def store_relative(kept_ref, sent_ref, grad, bits_ref, at, dp_first):
    rows = grad.shape[0] // 16
    width = grad.shape[1] // 2
    bits = [bits_ref[i] for i in range(5)]
    straight = bits[0] == 0
    for number in range(8):
        group, high, low = number >> 2, (number >> 1) & 1, number & 1
        first = grad[2 * number * rows : (2 * number + 1) * rows]
        second = grad[(2 * number + 1) * rows : (2 * number + 2) * rows]
        kept = jnp.where(straight, first, second)
        sent = jnp.where(straight, second, first)
        for side in range(2):
            pair = (side ^ bits[2], group ^ bits[1])
            pair = pair if dp_first else pair[::-1]
            place = pair + (low ^ bits[3], high ^ bits[4], slice(at, at + rows))
            cut = slice(side * width, (side + 1) * width)
            kept_ref[place] = kept[:, cut]
            sent_ref[place] = sent[:, cut]


def feed_forward(place, order, bits, mixed, start, cot, gain, own, gate_pieces, tail_pieces):
    rows, width = start.shape
    row_count = cot.shape[0]
    wo, wg, wu, wd = own
    hidden = wg.shape[1]
    steps = order.shape[0]
    chunk = hidden // steps
    count = len(gate_pieces)
    own_blocks = wd.shape[0] // chunk
    f32, b16 = jnp.float32, jnp.bfloat16

    def whole(array):
        return pl.BlockSpec(array.shape, lambda f, *refs: (0,) * len(array.shape))

    def columns(array):
        if array.ndim == 3:
            shape = array.shape[:2] + (chunk,)
            return pl.BlockSpec(shape, lambda f, place, order, bits: (0, 0, order[f]))
        return pl.BlockSpec((array.shape[0], chunk), lambda f, place, order, bits: (0, order[f]))

    if count:
        gate_shape = (2,) * 4 + (width // 2, chunk)
        tail_shape = (2,) * 4 + (chunk // 2 + width // 16, width // 2)
        grad_shapes = (tail_shape, gate_shape, gate_shape)
        out_grad_shape = tail_shape

        grad_specs = [
            pl.BlockSpec(tail_shape, lambda f, *refs: (0,) * len(tail_shape)),
            pl.BlockSpec(memory_space=pl.ANY),
            pl.BlockSpec(memory_space=pl.ANY),
        ]
    else:
        grad_shapes = ((hidden, width), (steps, 2, width, chunk), (8, tile))
        out_grad_shape = (width, width)
        grad_specs = [
            pl.BlockSpec((chunk, width), lambda f, place, order, bits: (order[f], 0)),
            pl.BlockSpec((1, 2, width, chunk), lambda f, place, order, bits: (order[f], 0, 0, 0)),
            pl.BlockSpec((8, tile), lambda f, place, order, bits: (0, 0)),
        ]
    shapes = (
        jax.ShapeDtypeStruct((row_count, width), b16),
        jax.ShapeDtypeStruct(grad_shapes[0], b16),
        jax.ShapeDtypeStruct(grad_shapes[1], b16),
        jax.ShapeDtypeStruct(grad_shapes[2], b16),
        jax.ShapeDtypeStruct((rows, width), f32),
        jax.ShapeDtypeStruct((rows, width), b16),
        jax.ShapeDtypeStruct(out_grad_shape, b16),
        jax.ShapeDtypeStruct((1, width), f32),
    )
    return pl.pallas_call(
        functools.partial(feed_kernel, piece_count=count, tail_count=len(tail_pieces)),
        out_shape=shapes,
        grid_spec=pltpu.PrefetchScalarGridSpec(
            num_scalar_prefetch=3,
            grid=(steps,),
            in_specs=[whole(mixed), whole(start), whole(cot), whole(gain), whole(wo)]
            + [
                columns(wg), columns(wu),
                pl.BlockSpec(
                    (chunk, width),
                    lambda f, place, order, bits: (
                        order[jnp.minimum(f, own_blocks - 1)] & (own_blocks - 1), 0
                    ),
                ),
            ]
            + [columns(piece) for piece in gate_pieces]
            + [whole(piece) for piece in tail_pieces],
            out_specs=(
                whole(shapes[0]),
                *grad_specs,
                whole(shapes[4]), whole(shapes[5]), whole(shapes[6]), whole(shapes[7]),
            ),
            scratch_shapes=[
                pltpu.VMEM((rows, width), b16),
                pltpu.VMEM((width, rows), b16),
                pltpu.VMEM((rows, width), f32),
                pltpu.VMEM((rows, tile), f32),
                pltpu.VMEM((rows, width), f32),
                pltpu.VMEM((rows, width), f32),
                pltpu.VMEM((rows, width), b16),
                pltpu.VMEM((width, width), b16),
                pltpu.VMEM((width, chunk), b16),
                pltpu.VMEM((width, chunk), b16),
                pltpu.VMEM((chunk, width), b16),
                pltpu.VMEM((2, 2, 2, width // 2, chunk), b16),
                pltpu.SemaphoreType.DMA((2,)),
            ],
        ),
        compiler_params=pltpu.CompilerParams(vmem_limit_bytes=46 << 20),
        cost_estimate=cost(26),
        name="feed_forward",
    )(place, order, bits, mixed, start, cot, gain, *own, *gate_pieces, *tail_pieces)


def project_back_kernel(
    place_ref, bits_ref, dq0_ref, dq1_ref, own0_ref, own1_ref, after0_ref, after1_ref, before0_ref,
    before1_ref, first_ref, start_ref, dmid_ref, gain_ref, *refs
):
    pieces = refs[3:-6]
    grads_ref, sent_ref, dstart_ref, gaing_ref, weight_ref, sems = refs[-6:]
    copies = weight_copies(place_ref, refs[:3], pieces, weight_ref, sems)
    width = first_ref.shape[1]
    half = width // 2

    def total(own_ref, after_ref, before_ref):
        return (
            own_ref[...] + after_ref[...].astype(jnp.float32) + before_ref[...].astype(jnp.float32)
        ).astype(jnp.bfloat16)

    sides = (total(own0_ref, after0_ref, before0_ref), total(own1_ref, after1_ref, before1_ref))
    grads = (
        jnp.concatenate([dq0_ref[...], dq1_ref[...]], axis=1),
        jnp.concatenate([side[:, :half] for side in sides], axis=1),
        jnp.concatenate([side[:, half:] for side in sides], axis=1),
    )
    turned = jnp.transpose(first_ref[...])
    for i, grad in enumerate(grads):
        product = matmul(turned, grad, 1, 0).astype(jnp.bfloat16)
        if pieces:
            store_relative(grads_ref, sent_ref, product, bits_ref, i * (width // 16), False)
        else:
            grads_ref[i] = product
    if not pieces:
        sent_ref[...] = jnp.zeros(sent_ref.shape, jnp.bfloat16)
    start = start_ref[...]
    inverse = lax.rsqrt(jnp.mean(start * start, axis=-1, keepdims=True) + epsilon)
    normed = start * inverse
    for copy in copies:
        copy.wait()
    dfirst = sum(matmul(grad, weight_ref[i], 1, 1) for i, grad in enumerate(grads))
    gaing_ref[...] = jnp.sum(dfirst * normed, axis=0, keepdims=True)
    dnormed = dfirst * gain_ref[...]
    dstart_ref[...] = dmid_ref[...] + inverse * (
        dnormed - normed * jnp.mean(dnormed * normed, axis=-1, keepdims=True)
    )


def project_back(place, bits, halves, first, start, dmid, gain, own, pieces):
    rows, width = first.shape
    shape = (2,) * 4 + (3 * (width // 16), width // 2) if pieces else (3, width, width)
    return pl.pallas_call(
        project_back_kernel,
        out_shape=(
            jax.ShapeDtypeStruct(shape, jnp.bfloat16),
            jax.ShapeDtypeStruct(shape if pieces else (8, tile), jnp.bfloat16),
            jax.ShapeDtypeStruct((rows, width), jnp.float32),
            jax.ShapeDtypeStruct((1, width), jnp.float32),
        ),
        in_specs=specs(2, pltpu.SMEM) + specs(12) + specs(3 + len(pieces), pl.ANY),
        out_specs=tuple(specs(4)),
        scratch_shapes=[
            pltpu.VMEM((3, width, width), jnp.bfloat16),
            pltpu.SemaphoreType.DMA((3 + len(pieces),)),
        ],
        compiler_params=pltpu.CompilerParams(vmem_limit_bytes=26 << 20),
        cost_estimate=cost(10),
        name="project_back",
    )(place, bits, *halves, first, start, dmid, gain, *own, *pieces)


def unpool_kernel(
    x_ref, mix_ref, weight_ref, dstart_ref, conv_ref, score_ref,
    dconv_ref, left_ref, right_ref, convg_ref, scoreg_ref,
    wide_ref, square_ref, sums_ref, *, byte_count
):
    lanes = x_ref.shape[0]
    width = lanes * tile
    rows = dstart_ref.shape[0]
    steps = mix_ref.shape[0] * 2 // span
    lead = id_pad + 8
    wide_ref[:rows] = dstart_ref[...]
    wide_ref[rows:] = jnp.zeros((wide_ref.shape[0] - rows, width), jnp.float32)
    for i in range(lanes):
        dconv_ref[i, :lead] = jnp.zeros((lead, tile), jnp.float32)
    sums_ref[...] = jnp.zeros(sums_ref.shape, jnp.float32)
    means = [block_means_grid(size) for size in (1, 2, 3, 4)]

    def unpool(step, carry):
        base = pl.multiple_of(step * span, 8)
        half = pl.ds(pl.multiple_of(step * (span // 2), 8), span // 2)
        conv = jnp.concatenate(conv_tile(x_ref, conv_ref, base + id_pad, lanes), axis=1)
        dstart = wide_ref[half, :]
        dstart_high, dstart_low = split_pair(dstart)
        conv_high, conv_low = split_pair(conv)
        inner = (
            matmul(dstart_high, conv_high, 1, 1)
            + matmul(dstart_low, conv_high, 1, 1)
            + matmul(dstart_high, conv_low, 1, 1)
        )
        inner = jnp.concatenate([inner, jnp.zeros((span // 2, tile - span), jnp.float32)], axis=1)
        square_ref[pl.ds(0, span // 2, stride=2), :] = inner
        square_ref[pl.ds(1, span // 2, stride=2), :] = inner
        inner = square_ref[...]
        weights = [weight_ref[pl.ds(base, span), i : i + 1] for i in range(4)]
        dweights = [0.5 * jnp.sum(mean * inner, axis=1, keepdims=True) for mean in means]
        common = sum(weight * dweight for weight, dweight in zip(weights, dweights))
        dscores = [weight * (dweight - common) for weight, dweight in zip(weights, dweights)]
        row = jnp.sum(
            sum(dscore * mean for dscore, mean in zip(dscores, means)), axis=0, keepdims=True
        )
        column = row_to_column(row)
        mix_high, mix_low = split_pair(mix_ref[half, :][:, :span])
        dconv = (
            matmul(mix_high, dstart_high, 0, 0)
            + matmul(mix_low, dstart_high, 0, 0)
            + matmul(mix_high, dstart_low, 0, 0)
            + column * score_ref[...]
        )
        for i in range(lanes):
            part = dconv[:, i * tile : (i + 1) * tile]
            dconv_ref[i, pl.ds(base + lead, span), :] = part
            for tap in range(conv_width):
                moved = x_ref[i, pl.ds(base + id_pad + tap - conv_width // 2, span), :]
                sums_ref[tap, :, i * tile : (i + 1) * tile] += fold_rows(part * moved, jnp.add)
        sums_ref[conv_width] += fold_rows(column * conv, jnp.add)
        return carry

    lax.fori_loop(0, steps, unpool, 0, unroll=steps)
    for tap in range(conv_width):
        convg_ref[tap : tap + 1, :] = jnp.sum(sums_ref[tap], axis=0, keepdims=True)
    scoreg_ref[...] = jnp.sum(sums_ref[conv_width], axis=0, keepdims=True)
    left_ref[...] = spread(dconv_ref, conv_ref, lead - 8, 8)
    right_ref[...] = spread(dconv_ref, conv_ref, lead + byte_count, 8)


def spread(dconv_ref, conv_ref, base, count):
    lanes = dconv_ref.shape[0]
    parts = [
        sum(
            conv_ref[tap : tap + 1, i * tile : (i + 1) * tile]
            * dconv_ref[i, pl.ds(base + conv_width // 2 - tap, count), :]
            for tap in range(conv_width)
        )
        for i in range(lanes)
    ]
    return jnp.concatenate(parts, axis=1)


def unpool(x, mix, weight, dstart, conv, score, byte_count):
    lanes = x.shape[0]
    width = lanes * tile
    f32 = jnp.float32
    half_rows = mix.shape[0]
    return pl.pallas_call(
        functools.partial(unpool_kernel, byte_count=byte_count),
        out_shape=(
            jax.ShapeDtypeStruct((lanes, 2 * half_rows + id_pad + 8, tile), f32),
            jax.ShapeDtypeStruct((8, width), f32),
            jax.ShapeDtypeStruct((8, width), f32),
            jax.ShapeDtypeStruct((conv_width, width), f32),
            jax.ShapeDtypeStruct((1, width), f32),
        ),
        in_specs=specs(6),
        out_specs=tuple(specs(5)),
        scratch_shapes=[
            pltpu.VMEM((half_rows, width), f32),
            pltpu.VMEM((span, tile), f32),
            pltpu.VMEM((conv_width + 1, 8, width), f32),
        ],
        compiler_params=pltpu.CompilerParams(vmem_limit_bytes=10 << 20),
        cost_estimate=cost(13),
        name="unpool",
    )(x, mix, weight, dstart, conv, score)


def scatter_kernel(ids_ref, dconv_ref, conv_ref, byteg_ref, embedg_ref, total_ref):
    byte_count = byteg_ref.shape[0]
    total_ref[...] = jnp.zeros(total_ref.shape, jnp.float32)

    def scatter(step):
        grads = spread(dconv_ref, conv_ref, step * tile + 8, tile)
        ids = ids_ref[step, 0:1, :]
        place = lax.broadcasted_iota(jnp.int32, (total_ref.shape[0], tile), 0)
        hot = (place == ids).astype(jnp.bfloat16)
        grads_high, grads_low = split_pair(grads)
        total_ref[...] += matmul(hot, grads_high, 1, 0) + matmul(hot, grads_low, 1, 0)
        return grads

    scatter(0)

    def whole_tile(step, carry):
        byteg_ref[pl.ds(pl.multiple_of((step - 1) * tile, tile), tile), :] = scatter(step)
        return carry

    full = byte_count // tile
    lax.fori_loop(1, full + 1, whole_tile, 0, unroll=full)
    byteg_ref[full * tile :, :] = scatter(full + 1)[: byte_count - full * tile]
    embedg_ref[...] = total_ref[...].astype(jnp.bfloat16)


def scatter_bytes(ids, dconv, conv, byte_count, vocab):
    width = conv.shape[1]
    table_rows = -(-vocab // 32) * 32
    return pl.pallas_call(
        scatter_kernel,
        out_shape=(
            jax.ShapeDtypeStruct((byte_count, width), jnp.float32),
            jax.ShapeDtypeStruct((table_rows, width), jnp.bfloat16),
        ),
        in_specs=specs(3),
        out_specs=tuple(specs(2)),
        scratch_shapes=[pltpu.VMEM((table_rows, width), jnp.float32)],
        compiler_params=pltpu.CompilerParams(vmem_limit_bytes=8 << 20),
        cost_estimate=cost(10),
        name="scatter_bytes",
    )(ids, dconv, conv)


def edge_kernel(bytes_ref, left_ref, right_ref, out_ref, edge_ref, sems):
    places = (pl.ds(0, 8), pl.ds(out_ref.shape[0] - 8, 8))
    loads = [
        pltpu.make_async_copy(bytes_ref.at[place], edge_ref.at[i], sems.at[i])
        for i, place in enumerate(places)
    ]
    for load in loads:
        load.start()
    for load in loads:
        load.wait()
    edge_ref[0] += left_ref[...]
    edge_ref[1] += right_ref[...]
    stores = [
        pltpu.make_async_copy(edge_ref.at[i], out_ref.at[place], sems.at[i])
        for i, place in enumerate(places)
    ]
    for store in stores:
        store.start()
    for store in stores:
        store.wait()


def add_edges(grads, left, right):
    return pl.pallas_call(
        edge_kernel,
        out_shape=jax.ShapeDtypeStruct(grads.shape, grads.dtype),
        in_specs=specs(1, pl.ANY) + specs(2),
        out_specs=specs(1, pl.ANY)[0],
        scratch_shapes=[
            pltpu.VMEM((2, 8, grads.shape[1]), jnp.float32),
            pltpu.SemaphoreType.DMA((2,)),
        ],
        input_output_aliases={0: 0},
        cost_estimate=cost(1),
        name="add_edges",
    )(grads, left, right)


def finish_kernel(bits_ref, near_ref, across_ref, core_ref, both_ref, *out_refs):
    flip = bits_ref[2] == 0
    for number in range(8):
        high, low, core = number >> 2, (number >> 1) & 1, number & 1
        place = (low ^ bits_ref[3], high ^ bits_ref[4])
        same = (core ^ bits_ref[0]) == 0
        near = jnp.where(same, near_ref[place], core_ref[place]).astype(jnp.float32)
        across = jnp.where(same, across_ref[place], both_ref[place]).astype(jnp.float32)
        first, second = jnp.where(flip, near, across), jnp.where(flip, across, near)
        half = first.shape[1]
        at = 0
        for out_ref in out_refs:
            rows = out_ref.shape[0] // 8
            out_ref[number * rows : (number + 1) * rows, :half] = first[at : at + rows]
            out_ref[number * rows : (number + 1) * rows, half:] = second[at : at + rows]
            at += rows


def finish_square(bits, parts, shapes):
    return pl.pallas_call(
        finish_kernel,
        out_shape=tuple(jax.ShapeDtypeStruct(shape, jnp.float32) for shape in shapes),
        in_specs=specs(1, pltpu.SMEM) + specs(4),
        out_specs=tuple(specs(len(shapes))),
        compiler_params=pltpu.CompilerParams(vmem_limit_bytes=20 << 20),
        cost_estimate=cost(3),
        name="finish_square",
    )(bits, *parts)


def finish_feed_kernel(sum_ref, gate_ref, up_ref, down_ref, out_ref):
    blocks = sum_ref.shape[0]
    gate_rows, chunk = gate_ref.shape[0], gate_ref.shape[1] // blocks
    down_rows, out_rows = down_ref.shape[0] // blocks, out_ref.shape[0] // blocks
    half = down_ref.shape[1] // 2
    for number in range(blocks):
        at = 0
        for strip in range(chunk // tile):
            cut = slice(number * chunk + strip * tile, number * chunk + (strip + 1) * tile)
            gate_ref[:, cut] = sum_ref[number, 0, at : at + gate_rows].astype(jnp.float32)
            up_ref[:, cut] = sum_ref[number, 1, at : at + gate_rows].astype(jnp.float32)
            at += gate_rows
        for strip in range(half // tile):
            for side in range(2):
                cut = slice(side * half + strip * tile, side * half + (strip + 1) * tile)
                middle = at + down_rows
                down = sum_ref[number, side, at:middle]
                out = sum_ref[number, side, middle : middle + out_rows]
                down_ref[number * down_rows : (number + 1) * down_rows, cut] = down.astype(jnp.float32)
                out_ref[number * out_rows : (number + 1) * out_rows, cut] = out.astype(jnp.float32)
            at += down_rows + out_rows


def finish_feed(total, shapes):
    gate, up, down, out = shapes
    grid = 4
    block = pl.BlockSpec((gate[0], gate[1] // grid), lambda f: (0, f))
    return pl.pallas_call(
        finish_feed_kernel,
        grid=(grid,),
        out_shape=tuple(jax.ShapeDtypeStruct(shape, jnp.float32) for shape in shapes),
        in_specs=[pl.BlockSpec((8 // grid,) + total.shape[1:], lambda f: (f, 0, 0, 0))],
        out_specs=(
            block, block,
            pl.BlockSpec((down[0] // grid, down[1]), lambda f: (f, 0)),
            pl.BlockSpec((out[0] // grid, out[1]), lambda f: (f, 0)),
        ),
        compiler_params=pltpu.CompilerParams(vmem_limit_bytes=60 << 20),
        cost_estimate=cost(5),
        name="finish_feed",
    )(total)


def join_feed_kernel(gate_ref, gate_in_ref, tail_ref, tail_in_ref, *out_refs):
    for number, out_ref in enumerate(out_refs):
        place = (number >> 1, number & 1)
        at = 0
        for kept_ref, in_ref in ((gate_ref, gate_in_ref), (tail_ref, tail_in_ref)):
            rows, width = kept_ref.shape[2:]
            total = kept_ref[place].astype(jnp.float32) + in_ref[place].astype(jnp.float32)
            total = total.astype(jnp.bfloat16)
            for strip in range(width // tile):
                out_ref[at : at + rows] = total[:, strip * tile : (strip + 1) * tile]
                at += rows


def join_feed(gate, gate_in, tail, tail_in):
    rows = sum(block.shape[2] * block.shape[3] // tile for block in (gate, tail))
    shape = jax.ShapeDtypeStruct((rows, tile), jnp.bfloat16)
    return pl.pallas_call(
        join_feed_kernel,
        out_shape=(shape,) * 4,
        in_specs=specs(4),
        out_specs=tuple(specs(4)),
        compiler_params=pltpu.CompilerParams(vmem_limit_bytes=20 << 20),
        cost_estimate=cost(2),
        name="join_feed",
    )(gate, gate_in, tail, tail_in)


sequence_axes = ("z", "core")
copy_axes = ("z", "core", "dp")
all_axes = ("z", "core", "dp", "ws")


def neighbours(block, axes):
    count = 1
    for axis in axes:
        count *= lax.axis_size(axis)
    forward = [(i, i + 1) for i in range(count - 1)]
    backward = [(target, source) for source, target in forward]
    return lax.ppermute(block, axes, forward), lax.ppermute(block, axes, backward)


def pad_rows(block):
    return jnp.pad(block, ((0, -block.shape[0] % tile), (0, 0)))


def send_left(block, count):
    return lax.ppermute(block, sequence_axes, [(i + 1, i) for i in range(count - 1)])


def send_right(block, count):
    return lax.ppermute(block, sequence_axes, [(i, i + 1) for i in range(count - 1)])


def swap(block, axis, distance=1):
    pairs = [(i, i ^ distance) for i in range(lax.axis_size(axis))]
    return lax.ppermute(block, axis, pairs)


def ordered(near, far, place, axis):
    first = place == 0
    return jnp.concatenate([jnp.where(first, near, far), jnp.where(first, far, near)], axis=axis)


def pack(block, small):
    high, low = split_pair(small)
    rest = jnp.zeros((-2 * small.shape[0] % 16, small.shape[1]), jnp.bfloat16)
    return jnp.concatenate([block, high, low, rest])


def unpack(sent, small):
    count = small.shape[0]
    rows = sent.shape[0] - (2 * count + -2 * count % 16)
    high, low = sent[rows : rows + count], sent[rows + count : rows + 2 * count]
    return sent[:rows], small + high.astype(jnp.float32) + low.astype(jnp.float32)


def gather_columns(shard):
    axis = shard.ndim - 1
    if lax.axis_size("ws") != 2:
        return lax.all_gather(shard, "ws", axis=axis, tiled=True)
    return ordered(shard, swap(shard, "ws"), lax.axis_index("ws"), axis)


def own_share(shard, axis):
    share = shard.shape[axis] // 4
    place = lax.axis_index("dp") * 2 + lax.axis_index("core")
    return lax.dynamic_slice_in_dim(shard, place * share, share, axis)


def spread_pieces(first):
    second = swap(first, "dp")
    return first, second, swap(first, "core"), swap(second, "core")


def special_mesh():
    return lax.axis_size("ws") == 2 and lax.axis_size("dp") == 2 and lax.axis_size("z") == 4


def add(*parts):
    return sum(part.astype(jnp.float32) for part in parts).astype(parts[0].dtype)


def swap_high(block, place):
    return swap(block, "z", place[0] + 2 * place[1])


others = ((1, 0), (0, 1), (1, 1))


class Chain:
    def __init__(self, sent, kept, order):
        self.sent, self.kept = (sent,), kept
        self.order = order
        self.received = ()

    def receive(self):
        axis = self.order[0]
        if axis == "z":
            self.received = tuple(swap_high(part, place) for part, place in zip(self.sent, others))
        else:
            self.received = (swap(self.sent[0], axis),)
        self.sent = ()

    def join(self):
        if not self.received:
            self.receive()
        rest = self.order[1:]
        parts = (self.kept,) + self.received
        self.received = ()
        self.order = rest
        if not rest:
            self.sent, self.kept = (), add(*parts)
            return
        places = others if rest[0] == "z" else ((1,),)
        self.sent = tuple(add(*(part[place] for part in parts)) for place in places)
        own = (0,) * len(places[0])
        self.kept = add(*(part[own] for part in parts))

    def state(self):
        return (self.sent, self.kept, self.received)

    def set_state(self, state):
        self.sent, self.kept, self.received = state


def gather_high(part):
    return jnp.stack(
        [
            jnp.stack([part, swap_high(part, (0, 1))]),
            jnp.stack([swap_high(part, (1, 0)), swap_high(part, (1, 1))]),
        ]
    )


def collect(part):
    return lax.all_gather(part, copy_axes, axis=0).reshape((8, 2) + part.shape)


def reduce_plain(grad):
    part = lax.psum_scatter(grad, "ws", scatter_dimension=grad.ndim - 2, tiled=True)
    return lax.psum(part, copy_axes).astype(jnp.float32)


def after(value, chains):
    if not special_mesh():
        return value
    value, kept = lax.optimization_barrier((value, [chain.kept for chain in chains]))
    for chain, part in zip(chains, kept):
        chain.kept = part
    return value


def hold(value, chains=()):
    if not special_mesh():
        return value
    value, states = lax.optimization_barrier((value, [chain.state() for chain in chains]))
    for chain, state in zip(chains, states):
        chain.set_state(state)
    return value


def per_device(
    byte_ids,
    segments,
    embed,
    conv_kernel,
    score_weight,
    attn_gain,
    w_q,
    w_k,
    w_v,
    w_o,
    rel_bias,
    ff_gain,
    w_gate,
    w_up,
    w_down,
    cotangent,
):
    byte_count = byte_ids.shape[1]
    row_count = byte_count // 2
    width = w_q.shape[1]
    group_count = lax.axis_size("ws")
    cycle_count = lax.axis_size("z") * lax.axis_size("core")
    cycle_place = lax.axis_index("z") * lax.axis_size("core") + lax.axis_index("core")
    bucket_count, head_count = rel_bias.shape
    rim = conv_width // 2
    has_before = cycle_place > 0
    has_after = cycle_place < cycle_count - 1

    ids = byte_ids[0]
    row_segs = segments[0, ::2]
    note = jnp.concatenate([row_segs, ids[:rim], ids[byte_count - rim :]])
    before_note, after_note = neighbours(note, sequence_axes)
    embed_table = gather_columns(embed)
    if special_mesh():
        core, dp = lax.axis_index("core"), lax.axis_index("dp")
        place = jnp.stack(
            [
                lax.axis_index("ws"), dp * 2 + core, 2 - dp * 2 + core, dp * 2 + 1 - core,
                3 - dp * 2 - core, core, 1 - core,
            ]
        ).astype(jnp.int32)
        own_order = jnp.stack([core, core + 2, 1 - core, 3 - core])
        peer_order = jnp.stack([3 * core, 1 + core, 2 - core, 3 - 3 * core])
        order = jnp.concatenate([place[0] * 4 + own_order, (1 - place[0]) * 4 + peer_order])
        order = order.astype(jnp.int32)
        z = lax.axis_index("z")
        bits = jnp.stack([core, place[0], dp, z & 1, z >> 1]).astype(jnp.int32)
        half = w_q.shape[0] // 2
        square_share = jnp.stack(
            [lax.dynamic_slice_in_dim(weight, core * half, half, 0) for weight in (w_q, w_k, w_v)]
        )
        gate_share = jnp.stack([own_share(weight, 0) for weight in (w_gate, w_up)])
        tail_share = jnp.concatenate(
            [
                lax.dynamic_slice_in_dim(weight, core * (weight.shape[0] // 2), weight.shape[0] // 2, 0)
                for weight in (w_down, w_o)
            ]
        )
        square_first = swap(square_share, "ws")
        square_share, embed_table, before_note, after_note = lax.optimization_barrier(
            (square_share, embed_table, before_note, after_note)
        )
        square_first = swap(square_share, "ws")
        square_place = jnp.stack([place[0], core, 1 - core]).astype(jnp.int32)
        own_square, own_feed = (w_q, w_k, w_v), (w_o, w_gate, w_up, w_down)
    else:
        place = square_place = jnp.zeros((1,), jnp.int32)
        order = jnp.arange(8, dtype=jnp.int32)
        bits = jnp.zeros((5,), jnp.int32)
        square_pieces = gate_pieces = tail_pieces = ()
        own_square, own_feed = (
            tuple(lax.all_gather(weight, "ws", axis=0, tiled=True) for weight in weights)
            for weights in ((w_q, w_k, w_v), (w_o, w_gate, w_up, w_down))
        )
    segs = jnp.stack(
        [
            jnp.where(has_before, before_note[:row_count], -2),
            row_segs,
            jnp.where(has_after, after_note[:row_count], 1 << 20),
        ]
    )
    segs = jnp.pad(segs, ((0, 0), (0, -row_count % tile)), constant_values=-3)
    left_ids = jnp.where(has_before, before_note[row_count + rim :], -1)
    right_ids = jnp.where(has_after, after_note[row_count : row_count + rim], -1)
    id_rows = -(-(byte_count + rim) // tile) * tile
    id_line = jnp.concatenate(
        [
            jnp.full((tile - rim,), -1, jnp.int32),
            left_ids,
            ids,
            right_ids,
            jnp.full((id_rows - byte_count - rim,), -1, jnp.int32),
        ]
    ).reshape(-1, 1, tile)
    conv = jnp.pad(conv_kernel.astype(jnp.float32), ((0, 8 - conv_width), (0, 0)))
    score = score_weight.astype(jnp.float32)[None]
    gain_one = attn_gain[None]
    gain_two = ff_gain[None]

    special = special_mesh()
    half_pairs = width // tile // 2
    start, x_rows, mix, block_weight = gbst_forward(id_line, embed_table, conv, score, row_count)
    if special:
        start, square_first, gate_share, tail_share = lax.optimization_barrier(
            (start, square_first, gate_share, tail_share)
        )
        square_pieces = (square_first, swap(square_first, "core"))
        gate_first = swap(gate_share, "ws")
    first_in, queries, own_kv = project(square_place, start, gain_one, own_square, square_pieces)
    if special:
        queries, gate_first, tail_share = lax.optimization_barrier((queries, gate_first, tail_share))
        tail_first = swap(tail_share, "ws")
        gate_second, gate_third = swap(gate_first, "dp"), swap(gate_first, "core")
    before_kv, after_kv = neighbours(own_kv, sequence_axes)
    near_state = attention_forward(segs, queries, (own_kv,), None, rel_bias, row_count)
    if special:
        near_state, before_kv, after_kv, gate_second = lax.optimization_barrier(
            (near_state, before_kv, after_kv, gate_second)
        )
        gate_pieces = (gate_first, gate_second, gate_third, swap(gate_second, "core"))
    attended, log_norm = attention_forward(
        segs, queries, (before_kv, after_kv), near_state, rel_bias, row_count
    )
    if special:
        attended, tail_first = lax.optimization_barrier((attended, tail_first))
        tail_pieces = (tail_first, swap(tail_first, "core"))
    output, down_grad, gate_up_grad, gate_up_sent, d_middle, d_attended, out_grad, ff_gain_grad = feed_forward(
        place, order, bits, attended, start, cotangent[0], gain_two, own_feed, gate_pieces, tail_pieces
    )
    chains = []
    if special:
        gate_chain = Chain(gate_up_sent, gate_up_grad, ("core", "ws", "dp", "z"))
        tail_chain = Chain(out_grad, down_grad, ("core", "dp", "ws", "z"))
        gate_chain.join()
        chains = [gate_chain, tail_chain]
    d_attended = hold(d_attended, chains)
    halves = []
    bias_parts = []
    for part in range(2):
        d_queries, d_before, d_own, d_after, bias_sums = attention_backward(
            segs, queries, d_attended, attended, before_kv, own_kv, after_kv, rel_bias,
            log_norm,            row_count, part * half_pairs, half_pairs,
        )
        active = chains if part else chains[1:]
        d_before, d_after = after((d_before, d_after), active)
        for chain in active:
            chain.join()
        d_attended, d_before, d_after, halves = hold((d_attended, d_before, d_after, halves), active)
        from_after = lax.ppermute(
            d_before, sequence_axes, [(i + 1, i) for i in range(cycle_count - 1)]
        )
        from_before = lax.ppermute(
            d_after, sequence_axes, [(i, i + 1) for i in range(cycle_count - 1)]
        )
        halves.append((d_queries, d_own, from_after, from_before))
        bias_parts.append(jnp.transpose(bias_sums[: 2 * half_pairs, :bucket_count]))
    square_grads, square_sent, d_start, attn_gain_grad = project_back(
        square_place, bits, [part[i] for i in range(4) for part in halves], first_in, start,
        d_middle, gain_one, own_square, square_pieces,
    )
    if special:
        square_chain = Chain(square_sent, square_grads, ("core", "ws", "dp", "z"))
        d_start = after(d_start, chains)
        kept, high, low, both = join_feed(
            gate_chain.kept, swap(gate_chain.sent[0], "dp"),
            tail_chain.kept, swap(tail_chain.sent[0], "ws"),
        )
        feed_chain = Chain(None, kept, ("z",))
        feed_chain.sent = (low, high, both)
        d_start = hold(d_start, [square_chain, feed_chain])
        square_chain.join()
        d_start = hold(d_start, [square_chain])
    d_conv, left_grad, right_grad, conv_grad, score_grad = unpool(
        x_rows, mix, block_weight, d_start, conv, score, byte_count
    )
    bias_grad = jnp.concatenate(bias_parts, axis=1)
    bias_rows = jnp.pad(bias_grad.reshape(1, -1), ((0, 0), (0, width - bucket_count * head_count)))
    small = jnp.concatenate(
        [conv_grad, score_grad, attn_gain_grad, ff_gain_grad, bias_rows], axis=0
    )
    byte_grad, embed_part = scatter_bytes(id_line, d_conv, conv, byte_count, embed.shape[0])
    if special:
        rows = embed_part.shape[0] // 2
        columns = width // 2
        small = small.reshape(-1, columns)
        square_chain.receive()
        embed_part, small = hold((embed_part, small), [square_chain])
        square_chain.join()
        core_rows = lax.dynamic_slice_in_dim(embed_part, bits[0] * rows, rows, 0)
        sent_rows = lax.dynamic_slice_in_dim(embed_part, (1 - bits[0]) * rows, rows, 0)
        core_in = swap(pack(sent_rows.reshape(2 * rows, columns), small), "core")
        square_chain.receive()
        core_rows, small, core_in = hold((core_rows, small, core_in), [square_chain])
        core_rows = after(core_rows, [feed_chain])
        feed_chain.join()
        feed_sum = collect(feed_chain.kept)
        received, small = unpack(core_in, small)
        embed_part = add(core_rows, received.reshape(rows, width))
        square_chain.join()
        own_columns = lax.dynamic_slice_in_dim(embed_part, bits[1] * columns, columns, 1)
        sent_columns = lax.dynamic_slice_in_dim(embed_part, (1 - bits[1]) * columns, columns, 1)
        sent = pack(sent_columns, small)
        own_columns, small, sent, left_grad = hold(
            (own_columns, small, sent, left_grad), [square_chain]
        )
        from_right = send_left(left_grad, cycle_count)
        received, small = unpack(swap(sent, "ws"), small)
        embed_part = add(own_columns, received)
        square_chain.join()
        square_part = square_chain.kept
        sent = pack(embed_part, small)
        embed_part, small, sent, square_part, from_right, right_grad = hold(
            (embed_part, small, sent, square_part, from_right, right_grad)
        )
        from_left = send_right(right_grad, cycle_count)
        received, small = unpack(swap(sent, "dp"), small)
        embed_part = add(embed_part, received)
        square_part = gather_high(square_part)
        sent = pack(embed_part, small)
        embed_part, small, sent, square_part, from_left = hold(
            (embed_part, small, sent, square_part, from_left)
        )
        byte_grad = add_edges(byte_grad, from_left, from_right)
        parts = [embed_part]
        for place in others:
            received, small = unpack(swap_high(sent, place), small)
            parts.append(received)
        embed_part = add(*parts)
        square_across = swap(square_part, "dp")
        square_core = swap(square_part, "core")
        embed_part, small, square_across, square_core, byte_grad = hold(
            (embed_part, small, square_across, square_core, byte_grad)
        )
        square_both = swap(square_across, "core")
        embed_part = ordered(embed_part, swap(embed_part, "core"), bits[0], 0)
        square_both, embed_part, small = hold((square_both, embed_part, small))
        query_sum, key_sum, value_sum = finish_square(
            bits, (square_part, square_across, square_core, square_both), ((columns, width),) * 3
        )
        embed_part, query_sum = hold((embed_part, query_sum))
        gate_sum, up_sum, down_sum, out_sum = finish_feed(
            feed_sum,
            (
                (columns, w_gate.shape[1]), (columns, w_gate.shape[1]),
                (w_down.shape[0], width), (columns, width),
            ),
        )
        small = small.reshape(-1, width)
    else:
        small = lax.psum(small, all_axes)
        embed_part = lax.psum_scatter(embed_part, "ws", scatter_dimension=1, tiled=True)
        embed_part = lax.psum(embed_part, copy_axes)
    embed_sum = embed_part[: embed.shape[0]].astype(jnp.float32)
    if not special:
        from_right = send_left(left_grad, cycle_count)
        from_left = send_right(right_grad, cycle_count)
        byte_grad = add_edges(byte_grad, from_left, from_right)
        gate_sum, up_sum = jnp.transpose(reduce_plain(gate_up_grad), (1, 2, 0, 3)).reshape(
            2, width // group_count, -1
        )
        down_sum, out_sum = reduce_plain(down_grad), reduce_plain(out_grad)
        query_sum, key_sum, value_sum = reduce_plain(square_grads)
    return (
        output[None],
        byte_grad[None],
        embed_sum,
        small[:conv_width],
        small[conv_width],
        small[conv_width + 1],
        query_sum,
        key_sum,
        value_sum,
        out_sum,
        small[conv_width + 3, : bucket_count * head_count].reshape(bucket_count, head_count),
        small[conv_width + 2],
        gate_sum,
        up_sum,
        down_sum,
    )


def solution(mesh):
    devices = mesh.devices
    fine = Mesh(devices.reshape((devices.shape[0] // 2, 2) + devices.shape[1:]), all_axes)
    rows = P(("dp", "ws"), sequence_axes)
    split = P("ws", None)
    in_specs = (
        rows, rows, P(None, "ws"), P(), P(), P(), split, split, split, split, P(), P(),
        split, split, split, P(("dp", "ws"), sequence_axes, None),
    )
    wide = P(("dp", "ws"), sequence_axes, None)
    out_specs = (
        wide, wide, P(None, "ws"), P(), P(), P(), split, split, split, split, P(), P(),
        split, split, split,
    )
    return jax.shard_map(
        per_device, mesh=fine, in_specs=in_specs, out_specs=out_specs, check_vma=False
    )
```
